32 devices in a mesh: fsdp: 8 (over z, y), ctx: 2 (over core), tp: 2 (over x).
Axes of the slice: x: 2, y: 2, z: 4, core: 2. Of those that a mesh axis runs over, the one named last changes fastest.
Arguments:
- tokens: bfloat16 [8, 320, 2048], P('fsdp', 'ctx'), may hold values from -6 to 6
- lengths: int32 [8], replicated, may hold values from 320 to 320, as said below
- weight_query: bfloat16 [2048, 2048], P('fsdp', 'tp'), may hold values from -0.125 to 0.125
- weight_key: bfloat16 [2048, 2048], P('fsdp', 'tp'), may hold values from -0.125 to 0.125
- weight_value: bfloat16 [2048, 2048], P('fsdp', 'tp'), may hold values from -0.125 to 0.125
- weight_out: bfloat16 [2048, 2048], P('fsdp', 'tp'), may hold values from -0.125 to 0.125
- weight_gate: bfloat16 [2048, 8192], P('fsdp', 'tp'), may hold values from -0.125 to 0.125
- weight_up: bfloat16 [2048, 8192], P('fsdp', 'tp'), may hold values from -0.125 to 0.125
- weight_down: bfloat16 [2048, 8192], P('fsdp', 'tp'), may hold values from -0.0625 to 0.0625
- post_attention: float32 [2048], replicated, may hold values from 0.5 to 1.5
- post_feedforward: float32 [2048], replicated, may hold values from 0.5 to 1.5
- query_norm: float32 [2048], P('tp'), may hold values from 0.1 to 1.9
- key_norm: float32 [2048], P('tp'), may hold values from 0.1 to 1.9
- cotangent: float32 [8, 320, 2048], P('fsdp', 'ctx'), may hold values from -6 to 6
Outputs:
- output: bfloat16 [8, 320, 2048], P('fsdp', 'ctx')
- grad_tokens: float32 [8, 320, 2048], P('fsdp', 'ctx')
- grad_weight_query: float32 [2048, 2048], P('fsdp', 'tp')
- grad_weight_key: float32 [2048, 2048], P('fsdp', 'tp')
- grad_weight_value: float32 [2048, 2048], P('fsdp', 'tp')
- grad_weight_out: float32 [2048, 2048], P('fsdp', 'tp')
- grad_weight_gate: float32 [2048, 8192], P('fsdp', 'tp')
- grad_weight_up: float32 [2048, 8192], P('fsdp', 'tp')
- grad_weight_down: float32 [2048, 8192], P('fsdp', 'tp')
- grad_post_attention: float32 [2048], replicated
- grad_post_feedforward: float32 [2048], replicated
- grad_query_norm: float32 [2048], P('tp')
- grad_key_norm: float32 [2048], P('tp')
- root_means: float32 [3], replicated
The draws below stay inside these ranges and needn't reach their ends.
Inputs may be any that keep to these rules, and one draw needn't show every extreme that they name: `lengths`: real tokens of each sequence, padding after them; in every draw one sequence fills its slot of 320 positions.
All inputs are finite; a program needn't handle non-finite values.
Results may differ from the reference program's by a relative error of at most 0.025.
Values may be sent and summed in bfloat16 or wider, within the bound.
A program may use at most 384 MiB of HBM per device.

```python
import math
import jax
import jax.numpy as jnp
from jax import lax

D = 2048
HEADS = 16
HD = 128
FF = 8192
SLOT = 320
SEQS = 8
LOWLEN = 320


def draw_lengths(key, part):
    drawn_lengths = jax.random.randint(jax.random.fold_in(key, 11), (SEQS,), LOWLEN, SLOT + 1)
    chosen = jax.random.randint(jax.random.fold_in(key, 12), (), 0, SEQS)
    return jnp.where(jnp.arange(SEQS) == chosen, SLOT, drawn_lengths).astype(jnp.int32)


def level_of(own_key, extent, cuts, least, high):
    level, own = 1.0, jax.random.fold_in(own_key, 6)
    for axis_at, blocks in cuts:
        heights = jnp.exp(jax.random.uniform(jax.random.fold_in(own, axis_at), (blocks,), jnp.float32, least / len(cuts), high / len(cuts)))
        level = level * jnp.repeat(heights, extent[axis_at] // blocks).reshape([-1 if axis == axis_at else 1 for axis in range(len(extent))])
    return level


def noise(own_key, shape, scale, limit, shards=(), kind=jnp.bfloat16):
    array = scale * jax.random.normal(own_key, shape, jnp.float32)
    if shards:
        array = array * level_of(own_key, shape, shards, -0.22, 0.18)
    return jnp.clip(array, -limit, limit).astype(kind)


def setup_inputs(seed: int = 0) -> dict:
    key_of = jax.random.split(jax.random.key(seed), 15)
    tokens = noise(key_of[0], (SEQS, SLOT, D), 1.0, 6.0, ((0, 8), (1, 2)))
    lengths = draw_lengths(jax.random.fold_in(key_of[14], 71), 0)
    weight_query = noise(key_of[2], (D, D), D ** -0.5, 0.125, ((0, 8), (1, 2)))
    weight_key = noise(key_of[3], (D, D), D ** -0.5, 0.125, ((0, 8), (1, 2)))
    weight_value = noise(key_of[4], (D, D), D ** -0.5, 0.125, ((0, 8), (1, 2)))
    weight_out = noise(key_of[5], (D, D), D ** -0.5, 0.125, ((0, 8), (1, 2)))
    weight_gate = noise(key_of[6], (D, FF), D ** -0.5, 0.125, ((0, 8), (1, 2)))
    weight_up = noise(key_of[7], (D, FF), D ** -0.5, 0.125, ((0, 8), (1, 2)))
    weight_down = noise(key_of[8], (D, FF), FF ** -0.5, 0.0625, ((0, 8), (1, 2)))
    post_attention = jnp.clip(1.0 + 0.1 * jax.random.normal(key_of[9], (D,), jnp.float32), 0.5, 1.5)
    post_feedforward = jnp.clip(1.0 + 0.1 * jax.random.normal(key_of[10], (D,), jnp.float32), 0.5, 1.5)
    query_norm = jnp.clip(1.0 + 0.18 * jax.random.normal(key_of[11], (D,), jnp.float32), 0.1, 1.9)
    key_norm = jnp.clip(1.0 + 0.18 * jax.random.normal(key_of[12], (D,), jnp.float32), 0.1, 1.9)
    cotangent = noise(key_of[13], (SEQS, SLOT, D), 1.0, 6.0, ((0, 8), (1, 2)), jnp.float32)
    return dict(tokens=tokens, lengths=lengths, weight_query=weight_query, weight_key=weight_key, weight_value=weight_value, weight_out=weight_out, weight_gate=weight_gate, weight_up=weight_up, weight_down=weight_down, post_attention=post_attention, post_feedforward=post_feedforward, query_norm=query_norm, key_norm=key_norm, cotangent=cotangent)


EPSILON = 1e-06
ROPE_BASE = 500000.0
NEGATIVE = -1e+30

@jax.custom_vjp
def low(v):
    return lax.optimization_barrier(v.astype(jnp.bfloat16)).astype(jnp.float32)

@jax.custom_vjp
def low_back(v):
    return v

def low_keep(v):
    return (low(v), None)

def low_pass(kept, grad):
    return (grad,)

def back_keep(v):
    return (v, None)

def back_low(kept, grad):
    return (low(grad),)
low.defvjp(low_keep, low_pass)
low_back.defvjp(back_keep, back_low)

def precise_dot(former, latter):
    return jnp.dot(former, latter, precision=lax.Precision.HIGHEST, preferred_element_type=jnp.float32)

def inverse_rms(values):
    return lax.rsqrt(lax.optimization_barrier(jnp.mean(values * values, axis=-1, keepdims=True)) + EPSILON)

def rope_tables(positions, head_size):
    half_size = head_size // 2
    exponent = jnp.arange(half_size, dtype=jnp.float32) * (2.0 / head_size)
    frequency = jnp.power(ROPE_BASE, -exponent)
    angles = positions.astype(jnp.float32)[:, None] * frequency[None, :]
    cosine = jnp.cos(angles)
    sine_table = jnp.sin(angles)
    return (jnp.concatenate([cosine, cosine], axis=-1), jnp.concatenate([sine_table, sine_table], axis=-1))

def rotate(values, cosine, sine_table):
    half_size = values.shape[-1] // 2
    turned = jnp.concatenate([-values[..., half_size:], values[..., :half_size]], axis=-1)
    return values * cosine[:, None, :] + turned * sine_table[:, None, :]

def attend_head(query_head, key_head, value_head, allowed):
    scores = low_back(precise_dot(query_head, key_head.T) * (1.0 / math.sqrt(HD)))
    scores = jnp.where(allowed, scores, NEGATIVE)
    highest = lax.optimization_barrier(jnp.max(scores, axis=-1, keepdims=True))
    exponent = jnp.exp(scores - highest)
    probability = exponent / lax.optimization_barrier(jnp.sum(exponent, axis=-1, keepdims=True))
    return precise_dot(low(probability), value_head)

def sequence_layer(tokens_row, length, params_in):
    weight_query, weight_key, weight_value, weight_out, weight_gate, weight_up, weight_down, post_attention, post_feedforward, query_norm, key_norm = params_in
    positions = jnp.arange(SLOT, dtype=jnp.int32)
    allowed = (positions[None, :] <= positions[:, None]) & (positions[None, :] < length)
    cosine, sine_table = rope_tables(positions, HD)
    query_raw = low_back(precise_dot(tokens_row, weight_query))
    key_raw = low_back(precise_dot(tokens_row, weight_key))
    value_low = low(low_back(precise_dot(tokens_row, weight_value)))
    query_normed = query_raw * inverse_rms(query_raw) * query_norm
    key_normed = key_raw * inverse_rms(key_raw) * key_norm
    queries = low(rotate(query_normed.reshape(SLOT, HEADS, HD), cosine, sine_table))
    key_rows = low(rotate(key_normed.reshape(SLOT, HEADS, HD), cosine, sine_table))
    values = value_low.reshape(SLOT, HEADS, HD)

    def one_head(operands):
        return attend_head(operands[0], operands[1], operands[2], allowed)
    per_head = lax.map(jax.checkpoint(one_head), (queries.transpose(1, 0, 2), key_rows.transpose(1, 0, 2), values.transpose(1, 0, 2)))
    attended = low(low_back(per_head.transpose(1, 0, 2).reshape(SLOT, D)))
    branch_sum = low_back(precise_dot(attended, weight_out.T))
    attention_branch = branch_sum * inverse_rms(branch_sum) * post_attention
    residual = tokens_row + attention_branch
    residual_low = low(residual)
    gate_value = low_back(precise_dot(residual_low, weight_gate))
    up_value = low_back(precise_dot(residual_low, weight_up))
    mixed_low = low(jax.nn.silu(gate_value) * up_value)
    down_sum = low_back(precise_dot(mixed_low, weight_down.T))
    feedforward_branch = down_sum * inverse_rms(down_sum) * post_feedforward
    return (residual + feedforward_branch, attention_branch, feedforward_branch)

def reference(tokens, lengths, weight_query, weight_key, weight_value, weight_out, weight_gate, weight_up, weight_down, post_attention, post_feedforward, query_norm, key_norm, cotangent):
    parameters = tuple((array_in.astype(jnp.float32) for array_in in (weight_query, weight_key, weight_value, weight_out, weight_gate, weight_up, weight_down, post_attention, post_feedforward, query_norm, key_norm)))
    tokens_float = tokens.astype(jnp.float32)

    def forward(tokens_all, params_all):

        def per_sequence(running, operands):
            tokens_row, length = operands

            def layer_call(row_in, params_in):
                return sequence_layer(row_in, length, params_in)
            outcome = jax.checkpoint(layer_call)(tokens_row, params_all)
            return (running, outcome)
        unused, outcome = lax.scan(per_sequence, jnp.zeros((), jnp.float32), (tokens_all, lengths))
        return (outcome[0], (outcome[1], outcome[2]))
    stream, pullback, branches = jax.vjp(forward, tokens_float, parameters, has_aux=True)
    valid_rows = (jnp.arange(SLOT, dtype=jnp.int32)[None, :] < lengths[:, None]).astype(jnp.float32)
    grad_tokens, grad_params = pullback(cotangent.astype(jnp.float32) * valid_rows[..., None])
    token_count = jnp.sum(lengths.astype(jnp.float32))

    def masked_rms(values):
        return jnp.sqrt(jnp.sum(valid_rows[..., None] * values * values) / (token_count * D))
    root_means = jnp.stack([masked_rms(stream), masked_rms(branches[0]), masked_rms(branches[1])])
    return (stream.astype(jnp.bfloat16), grad_tokens, grad_params[0], grad_params[1], grad_params[2], grad_params[3], grad_params[4], grad_params[5], grad_params[6], grad_params[7], grad_params[8], grad_params[9], grad_params[10], root_means)
```

```python
import math

import jax
import jax.numpy as jnp
from jax import lax
from jax.sharding import Mesh, PartitionSpec as P

HD = 128
EPSILON = 1e-06
ROPE_BASE = 500000.0
NEGATIVE = -1e30
AXES = ("z", "y", "ch", "core", "tp")
BF = jnp.bfloat16
F32 = jnp.float32


def rope_tables(positions):
    half_size = HD // 2
    exponent = jnp.arange(half_size, dtype=F32) * (2.0 / HD)
    frequency = jnp.power(ROPE_BASE, -exponent)
    angles = positions.astype(F32)[:, None] * frequency[None, :]
    cosine = jnp.cos(angles)
    sine_table = jnp.sin(angles)
    return (
        jnp.concatenate([cosine, cosine], axis=-1),
        jnp.concatenate([sine_table, sine_table], axis=-1),
    )


def rotate(values, cosine, sine_table):
    half_size = HD // 2
    turned = jnp.concatenate([-values[..., half_size:], values[..., :half_size]], axis=-1)
    return values * cosine + turned * sine_table


def rotate_back(grads_in, cosine, sine_table):
    half_size = HD // 2
    sin_part = grads_in * sine_table
    return grads_in * cosine + jnp.concatenate(
        [sin_part[..., half_size:], -sin_part[..., :half_size]], axis=-1
    )


def dot(former, latter, dims):
    return lax.dot_general(former, latter, (dims, ((), ())), preferred_element_type=F32)


def mm(a, b):
    return dot(a, b, ((1,), (0,)))


def mm_nt(a, b):
    return dot(a, b, ((1,), (1,)))


def mm_tn(a, b):
    return dot(a, b, ((0,), (0,)))


def weight_in(weight):
    rows, cols = weight.shape
    nz = lax.axis_size("z")
    part = weight.reshape(rows, nz, 2, cols // (2 * nz))
    part = lax.dynamic_index_in_dim(part, lax.axis_index("core"), 2, keepdims=False)
    part = lax.all_to_all(part.transpose(1, 0, 2), "z", 0, 0, tiled=False)
    part = lax.all_gather(part, "y", axis=1, tiled=False)
    return part.reshape(-1, cols // (2 * nz))


def grad_out(grad):
    nz = lax.axis_size("z")
    ny = lax.axis_size("y")
    cols = grad.shape[1]
    part = grad.astype(BF).reshape(nz, ny, -1, cols)
    part = lax.psum_scatter(part, "y", scatter_dimension=1, tiled=False)
    part = lax.all_to_all(part, "z", 0, 0, tiled=False)
    if lax.axis_size("ch") > 1:
        part = lax.psum(part, "ch")
    part = lax.all_gather(part, "core", axis=1, tiled=False)
    return part.transpose(2, 0, 1, 3).reshape(part.shape[2], -1).astype(F32)


def gather_tokens(rows):
    return lax.all_gather(rows, ("z", "core"), axis=0, tiled=True)


def gather_rows(rows):
    return lax.all_gather(rows, ("z", "core", "tp"), axis=0, tiled=True)


def scatter_rows(partial):
    return lax.psum_scatter(
        partial.astype(BF), ("z", "core", "tp"), scatter_dimension=0, tiled=True
    ).astype(F32)


def head_total(terms):
    return lax.psum(terms, ("z", "core", "tp"))


def all_total(terms):
    return lax.psum(terms, AXES)


def local(
    tokens,
    lengths,
    weight_query,
    weight_key,
    weight_value,
    weight_out,
    weight_gate,
    weight_up,
    weight_down,
    post_attention,
    post_feedforward,
    query_norm,
    key_norm,
    cotangent,
):
    nz, ny, nch, ntp = (lax.axis_size(a) for a in ("z", "y", "ch", "tp"))
    iz, iy, ich, icore, itp = (lax.axis_index(a) for a in AXES)
    token_rows = tokens[0]
    own_rows, width = token_rows.shape
    piece = own_rows // ntp
    seq_rows = own_rows * 2
    total_rows = seq_rows * nz
    scale_factor = 1.0 / math.sqrt(HD)
    own_head = iz * 2 + icore
    qn = lax.dynamic_slice_in_dim(query_norm, own_head * HD, HD)
    kn = lax.dynamic_slice_in_dim(key_norm, own_head * HD, HD)
    seq_lengths = lax.dynamic_index_in_dim(lengths.reshape(nz, ny), iy, 1, keepdims=False)
    positions = ich * seq_rows + jnp.arange(seq_rows, dtype=jnp.int32)
    key_positions = jnp.arange(seq_rows * nch, dtype=jnp.int32)
    cosine, sine_table = rope_tables(positions)
    allowed = (key_positions[None, None, :] <= positions[None, :, None]) & (
        key_positions[None, None, :] < seq_lengths[:, None, None]
    )
    my_tokens = lax.dynamic_slice_in_dim(token_rows, itp * piece, piece, 0)
    my_cot = lax.dynamic_slice_in_dim(cotangent[0], itp * piece, piece, 0)
    my_pos = (ich * 2 + icore) * own_rows + itp * piece + jnp.arange(piece, dtype=jnp.int32)
    my_valid = (my_pos < lengths[iz * ny + iy]).astype(F32)[:, None]

    tokens_all = gather_tokens(token_rows)
    wq, wk, wv, wo, wg, wu, wd = [
        weight_in(w)
        for w in (
            weight_query,
            weight_key,
            weight_value,
            weight_out,
            weight_gate,
            weight_up,
            weight_down,
        )
    ]
    query_raw = mm(tokens_all, wq)
    key_raw = mm(tokens_all, wk)
    value_raw = mm(tokens_all, wv)
    squares = head_total(
        jnp.stack([jnp.sum(query_raw * query_raw, axis=-1), jnp.sum(key_raw * key_raw, axis=-1)])
    )
    scales = lax.rsqrt(squares / width + EPSILON)
    query_scale = scales[0][:, None]
    key_scale = scales[1][:, None]
    by_seq = lambda a: a.reshape(nz, seq_rows, HD)
    queries = rotate(by_seq(query_raw * query_scale * qn), cosine, sine_table).astype(BF)
    keys = rotate(by_seq(key_raw * key_scale * kn), cosine, sine_table).astype(BF)
    values = by_seq(value_raw).astype(BF)
    if nch > 1:
        keys_full = lax.all_gather(keys, "ch", axis=1, tiled=True)
        values_full = lax.all_gather(values, "ch", axis=1, tiled=True)
    else:
        keys_full, values_full = keys, values
    scores = (
        jnp.einsum("btd,bsd->bts", queries, keys_full, preferred_element_type=F32) * scale_factor
    )
    scores = jnp.where(allowed, scores, NEGATIVE)
    exponent = jnp.exp(scores - jnp.max(scores, axis=-1, keepdims=True))
    probability = exponent / jnp.sum(exponent, axis=-1, keepdims=True)
    probability_low = probability.astype(BF)
    attended = jnp.einsum("bts,bsd->btd", probability_low, values_full, preferred_element_type=F32)
    attended_low = attended.reshape(total_rows, HD).astype(BF)
    branch_sum = scatter_rows(mm_nt(attended_low, wo))
    attn_scale = lax.rsqrt(jnp.mean(branch_sum * branch_sum, axis=-1, keepdims=True) + EPSILON)
    attn_normed = branch_sum * attn_scale
    attention_branch = attn_normed * post_attention
    residual = my_tokens.astype(F32) + attention_branch
    residual_all = gather_rows(residual.astype(BF))
    gate_value = mm(residual_all, wg)
    up_value = mm(residual_all, wu)
    sigmoid_gate = jax.nn.sigmoid(gate_value)
    silu_gate = gate_value * sigmoid_gate
    mixed_low = (silu_gate * up_value).astype(BF)
    down_sum = scatter_rows(mm_nt(mixed_low, wd))
    ffn_scale = lax.rsqrt(jnp.mean(down_sum * down_sum, axis=-1, keepdims=True) + EPSILON)
    ffn_normed = down_sum * ffn_scale
    feedforward_branch = ffn_normed * post_feedforward
    stream = residual + feedforward_branch
    stat_terms = jnp.stack(
        [
            jnp.sum(my_valid * stream * stream),
            jnp.sum(my_valid * attention_branch * attention_branch),
            jnp.sum(my_valid * feedforward_branch * feedforward_branch),
        ]
    )
    grad_stream = my_cot * my_valid
    grad_post_ff = jnp.sum(grad_stream * ffn_normed, axis=0)
    scaled = grad_stream * post_feedforward
    grad_down_sum = ffn_scale * (
        scaled - ffn_normed * jnp.mean(scaled * ffn_normed, axis=-1, keepdims=True)
    )
    down_all = gather_rows(grad_down_sum.astype(BF))
    grad_mixed = mm(down_all, wd)
    gate_low = (
        grad_mixed * up_value * sigmoid_gate * (1.0 + gate_value * (1.0 - sigmoid_gate))
    ).astype(BF)
    up_low = (grad_mixed * silu_gate).astype(BF)
    grad_wg = mm_tn(residual_all, gate_low)
    grad_wu = mm_tn(residual_all, up_low)
    grad_wd = mm_tn(down_all, mixed_low)
    grad_residual = grad_stream + scatter_rows(mm_nt(gate_low, wg) + mm_nt(up_low, wu))
    grad_post_attn = jnp.sum(grad_residual * attn_normed, axis=0)
    scaled_attn = grad_residual * post_attention
    grad_branch = attn_scale * (
        scaled_attn - attn_normed * jnp.mean(scaled_attn * attn_normed, axis=-1, keepdims=True)
    )
    branch_all = gather_rows(grad_branch.astype(BF))
    grad_att_low = mm(branch_all, wo).astype(BF)
    grad_wo = mm_tn(branch_all, attended_low)
    grad_att = by_seq(grad_att_low)
    grad_prob = jnp.einsum("btd,bsd->bts", grad_att, values_full, preferred_element_type=F32)
    row_dots = jnp.sum(probability * grad_prob, axis=-1, keepdims=True)
    grad_scores = (probability * (grad_prob - row_dots)).astype(BF)
    grad_queries = (
        jnp.einsum("bts,bsd->btd", grad_scores, keys_full, preferred_element_type=F32)
        * scale_factor
    )
    grad_keys = (
        jnp.einsum("bts,btd->bsd", grad_scores, queries, preferred_element_type=F32) * scale_factor
    )
    grad_values = jnp.einsum("bts,btd->bsd", probability_low, grad_att, preferred_element_type=F32)
    if nch > 1:
        grad_keys, grad_values = (
            lax.psum_scatter(g.astype(BF), "ch", scatter_dimension=1, tiled=True).astype(F32)
            for g in (grad_keys, grad_values)
        )
    value_grad_low = grad_values.reshape(total_rows, HD).astype(BF)
    grad_q_normed = rotate_back(grad_queries, cosine, sine_table).reshape(total_rows, HD)
    grad_k_normed = rotate_back(grad_keys, cosine, sine_table).reshape(total_rows, HD)
    query_weighted = grad_q_normed * qn
    key_weighted = grad_k_normed * kn
    dots = head_total(
        jnp.stack(
            [
                jnp.sum(query_weighted * query_raw, axis=-1),
                jnp.sum(key_weighted * key_raw, axis=-1),
            ]
        )
    )
    query_grad_low = (
        query_scale * (query_weighted - query_raw * query_scale**2 * (dots[0] / width)[:, None])
    ).astype(BF)
    key_grad_low = (
        key_scale * (key_weighted - key_raw * key_scale**2 * (dots[1] / width)[:, None])
    ).astype(BF)
    grad_qnorm = jnp.sum(grad_q_normed * query_raw * query_scale, axis=0)
    grad_knorm = jnp.sum(grad_k_normed * key_raw * key_scale, axis=0)
    grad_wq = mm_tn(tokens_all, query_grad_low)
    grad_wk = mm_tn(tokens_all, key_grad_low)
    grad_wv = mm_tn(tokens_all, value_grad_low)
    grad_rows = grad_residual + scatter_rows(
        mm_nt(query_grad_low, wq) + mm_nt(key_grad_low, wk) + mm_nt(value_grad_low, wv)
    )
    grad_input = lax.all_gather(grad_rows, "tp", axis=0, tiled=True)
    output = lax.all_gather(stream.astype(BF), "tp", axis=0, tiled=True)
    slot = itp * (width // ntp) + own_head * HD
    zero_row = jnp.zeros((width,), F32)
    summed = all_total(
        jnp.concatenate(
            [
                grad_post_attn,
                grad_post_ff,
                lax.dynamic_update_slice_in_dim(zero_row, grad_qnorm, slot, 0),
                lax.dynamic_update_slice_in_dim(zero_row, grad_knorm, slot, 0),
                stat_terms,
            ]
        )
    )
    half = width // ntp
    qn_sum = lax.dynamic_slice_in_dim(summed, 2 * width + itp * half, half)
    kn_sum = lax.dynamic_slice_in_dim(summed, 3 * width + itp * half, half)
    token_count = jnp.sum(lengths.astype(F32))
    root_means = jnp.sqrt(summed[4 * width :] / (token_count * width))
    return (
        output[None],
        grad_input[None],
        grad_out(grad_wq),
        grad_out(grad_wk),
        grad_out(grad_wv),
        grad_out(grad_wo),
        grad_out(grad_wg),
        grad_out(grad_wu),
        grad_out(grad_wd),
        summed[:width],
        summed[width : 2 * width],
        qn_sum,
        kn_sum,
        root_means,
    )


def solution(mesh):
    n_fsdp, n_ctx, n_tp = (mesh.shape[a] for a in ("fsdp", "ctx", "tp"))
    fine = Mesh(mesh.devices.reshape(n_fsdp // 2, 2, n_ctx // 2, 2, n_tp), AXES)
    fsdp, ctx = ("z", "y"), ("ch", "core")
    rows = P(fsdp, ctx, None)
    weight = P(fsdp, "tp")
    return jax.shard_map(
        local,
        mesh=fine,
        in_specs=(rows, P(), *([weight] * 7), P(), P(), P("tp"), P("tp"), rows),
        out_specs=(rows, rows, *([weight] * 7), P(), P(), P("tp"), P("tp"), P()),
        check_vma=False,
    )
```

```python
import functools
import math

import jax
import jax.numpy as jnp
from jax import lax
from jax.experimental import pallas as pl
from jax.experimental.pallas import tpu as pltpu
from jax.sharding import Mesh, PartitionSpec as P

HD = 128
EPSILON = 1e-06
ROPE_BASE = 500000.0
NEGATIVE = -1e30
AXES = ("z", "y", "ch", "core", "tp")
BF = jnp.bfloat16
F32 = jnp.float32


def rope_tables(positions):
    half_size = HD // 2
    exponent = jnp.arange(half_size, dtype=F32) * (2.0 / HD)
    frequency = jnp.power(ROPE_BASE, -exponent)
    angles = positions.astype(F32)[:, None] * frequency[None, :]
    cosine = jnp.cos(angles)
    sine_table = jnp.sin(angles)
    return (
        jnp.concatenate([cosine, cosine], axis=-1),
        jnp.concatenate([sine_table, sine_table], axis=-1),
    )


def rotate(values, cosine, sine_table):
    half_size = HD // 2
    turned = jnp.concatenate([-values[..., half_size:], values[..., :half_size]], axis=-1)
    return values * cosine + turned * sine_table


def rotate_back(grads_in, cosine, sine_table):
    half_size = HD // 2
    sin_part = grads_in * sine_table
    return grads_in * cosine + jnp.concatenate(
        [sin_part[..., half_size:], -sin_part[..., :half_size]], axis=-1
    )


def dot(former, latter, dims):
    return lax.dot_general(former, latter, (dims, ((), ())), preferred_element_type=F32)


def mm(a, b):
    return dot(a, b, ((1,), (0,)))


def mm_nt(a, b):
    return dot(a, b, ((1,), (1,)))


def mm_tn(a, b):
    return dot(a, b, ((0,), (0,)))


MESH = pl.DeviceIdType.MESH


def flip(axis, bits):
    me = lax.axis_index(axis)
    result, weight = me, 1
    while weight <= bits:
        if (bits // weight) % 2:
            result = result + weight * (1 - 2 * lax.rem(me // weight, 2))
        weight *= 2
    return result


def greet(partners):
    barrier = pltpu.get_barrier_semaphore()
    for partner in partners:
        pl.semaphore_signal(barrier, inc=1, device_id=partner, device_id_type=MESH)
    pl.semaphore_wait(barrier, len(partners))


def remote(src, dst, send_sem, recv_sem, partner):
    return pltpu.make_async_remote_copy(
        src_ref=src,
        dst_ref=dst,
        send_sem=send_sem,
        recv_sem=recv_sem,
        device_id=partner,
        device_id_type=MESH,
    )


def partners_of(axes):
    found = []
    for axis in axes:
        for bits in range(1, lax.axis_size(axis)):
            found.append({axis: flip(axis, bits)})
    return found


def call(kernel, identity, out_shape, in_spaces, out_spaces, scratch, limit, *operands):
    return pl.pallas_call(
        kernel,
        out_shape=out_shape,
        in_specs=[pl.BlockSpec(memory_space=s) for s in in_spaces],
        out_specs=jax.tree.map(lambda s: pl.BlockSpec(memory_space=s), out_spaces),
        scratch_shapes=scratch,
        compiler_params=pltpu.CompilerParams(
            collective_id=identity, has_side_effects=True, vmem_limit_bytes=limit * 2**20
        ),
    )(*operands)


DMA = pltpu.SemaphoreType.DMA


def gather_kernel(nz, x_ref, out_ref, own_sem, zs, zr, xs, xr, cs, cr):
    iz, ic, it = (lax.axis_index(a) for a in ("z", "core", "tp"))
    greet(partners_of(("z", "tp", "core")))
    sends = []

    def push(src, where, send_sem, recv_sem, partner):
        copy = remote(src, out_ref.at[where], send_sem, recv_sem, partner)
        copy.start()
        sends.append(copy)

    across, beside = {"tp": 1 - it}, {"core": 1 - ic}
    own = (iz, ic, it)
    for d in range(1, nz):
        push(x_ref, own, zs.at[d], zr.at[d], {"z": flip("z", d)})
    push(x_ref, own, xs.at[0], xr.at[0], across)
    push(x_ref, own, cs.at[0, 0], cr.at[0, 0], beside)
    local_copy = pltpu.make_async_copy(x_ref, out_ref.at[own], own_sem)
    local_copy.start()

    def await_at(where, sem):
        remote(out_ref.at[where], out_ref.at[where], sem, sem, across).wait_recv()

    def from_across(d):
        where = (flip("z", d), ic, 1 - it)
        await_at(where, xr.at[d])
        push(out_ref.at[where], where, cs.at[d, 1], cr.at[d, 1], beside)

    for d in range(1, nz):
        where = (flip("z", d), ic, it)
        await_at(where, zr.at[d])
        push(out_ref.at[where], where, xs.at[d], xr.at[d], across)
        push(out_ref.at[where], where, cs.at[d, 0], cr.at[d, 0], beside)
        from_across(d - 1)
    from_across(nz - 1)
    for d in range(nz):
        for half in range(2):
            side = it if half == 0 else 1 - it
            await_at((flip("z", d), 1 - ic, side), cr.at[d, half])
    for copy in sends:
        copy.wait_send()
    local_copy.wait()


def gather_rows(rows):
    piece, width = rows.shape
    nz = lax.axis_size("z")
    out = call(
        functools.partial(gather_kernel, nz),
        1,
        jax.ShapeDtypeStruct((nz, 2, 2, piece, width), rows.dtype),
        [pl.ANY],
        pl.ANY,
        [DMA, DMA((nz,)), DMA((nz,)), DMA((nz,)), DMA((nz,)), DMA((nz, 2)), DMA((nz, 2))],
        16,
        rows,
    )
    return out.reshape(-1, width)


def scatter_kernel(
    nz, p_ref, out_ref, own, cin, xout, xin, zout, zin, ls, cs, cr, xs, xr, zs, zr
):
    iz, ic, it = (lax.axis_index(a) for a in ("z", "core", "tp"))
    greet(partners_of(("z", "tp", "core")))
    across, beside = {"tp": 1 - it}, {"core": 1 - ic}
    order = list(range(nz - 1, -1, -1))
    loads, besides, acrosses, zeds = {}, {}, {}, {}
    for d in order:
        target = flip("z", d) if d else iz
        besides[d] = remote(p_ref.at[target, 1 - ic], cin.at[d], cs.at[d], cr.at[d], beside)
        besides[d].start()
        loads[d] = pltpu.make_async_copy(p_ref.at[target, ic], own.at[d], ls.at[d])
        loads[d].start()

    def add(d, side):
        return own[d, side].astype(F32) + cin[d, side].astype(F32)

    def after_across(d):
        acrosses[d].wait_recv()
        total = add(d, it) + xin[d].astype(F32)
        if d == 0:
            out_ref[...] = total
        else:
            zout[d] = total.astype(BF)
            zeds[d] = remote(zout.at[d], zin.at[d], zs.at[d], zr.at[d], {"z": flip("z", d)})
            zeds[d].start()

    for n, d in enumerate(order):
        loads[d].wait()
        besides[d].wait_recv()
        xout[d] = add(d, 1 - it).astype(BF)
        acrosses[d] = remote(xout.at[d], xin.at[d], xs.at[d], xr.at[d], across)
        acrosses[d].start()
        if n:
            after_across(order[n - 1])
    after_across(0)
    for d in order[:-1]:
        zeds[d].wait_recv()
        out_ref[...] += zin[d].astype(F32)
    for group in (besides, acrosses, zeds):
        for copy in group.values():
            copy.wait_send()


def scatter_rows(partial):
    nz = lax.axis_size("z")
    width = partial.shape[1]
    part = partial.astype(BF).reshape(nz, 2, 2, -1, width)
    piece = part.shape[3]
    sems = [DMA((nz,)) for _ in range(7)]
    return call(
        functools.partial(scatter_kernel, nz),
        2,
        jax.ShapeDtypeStruct((piece, width), F32),
        [pl.ANY],
        pltpu.VMEM,
        [
            pltpu.VMEM((nz, 2, piece, width), BF),
            pltpu.VMEM((nz, 2, piece, width), BF),
            *[pltpu.VMEM((nz, piece, width), BF) for _ in range(4)],
            *sems,
        ],
        32,
        part,
    )


def total_kernel(axes, x_ref, out_ref, *scratch):
    greet(partners_of(axes))
    value = x_ref[...]
    sends = []
    for stage, axis in enumerate(axes):
        slots, send_sems, recv_sems = scratch[3 * stage : 3 * stage + 3]
        size = lax.axis_size(axis)
        me = lax.axis_index(axis)
        slots[me] = value
        copies = []
        for d in range(1, size):
            copy = remote(
                slots.at[me], slots.at[me], send_sems.at[d], recv_sems.at[d], {axis: flip(axis, d)}
            )
            copy.start()
            copies.append(copy)
        for copy in copies:
            copy.wait_recv()
        value = slots[0]
        for n in range(1, size):
            value = value + slots[n]
        sends += copies
    out_ref[...] = value
    for copy in sends:
        copy.wait_send()


def total(terms, axes, identity):
    axes = tuple(a for a in axes if lax.axis_size(a) > 1)
    scratch = []
    for axis in axes:
        size = lax.axis_size(axis)
        scratch += [pltpu.VMEM((size, *terms.shape), F32), DMA((size,)), DMA((size,))]
    return call(
        functools.partial(total_kernel, axes),
        identity,
        jax.ShapeDtypeStruct(terms.shape, F32),
        [pltpu.VMEM],
        pltpu.VMEM,
        scratch,
        16,
        terms,
    )


def head_total(terms):
    return total(terms.reshape(-1, 128), ("core", "tp", "z"), 3).reshape(terms.shape)


def all_total(terms):
    size = terms.shape[0]
    padded = jnp.pad(terms, (0, -size % 1024)).reshape(-1, 128)
    return total(padded, ("core", "tp", "y", "z", "ch"), 4).reshape(-1)[:size]


def columns(ref, slot, count):
    return ref.at[:, pl.ds(pl.multiple_of(slot * count, 128), count)]


def intake_kernel(nz, count, tok_ref, *refs):
    w_refs, refs = refs[:count], refs[count:]
    tok_out, refs = refs[0], refs[1:]
    o_refs, refs = refs[:count], refs[count:]
    tok_buf, refs = refs[0], refs[1:]
    bufs, refs = refs[:count], refs[count:]
    tl, tzs, tzr, txs, txr, tcs, tcr, wl, wzs, wzr, wys, wyr = refs
    iz, iy, ic, it = (lax.axis_index(a) for a in ("z", "y", "core", "tp"))
    across, beside, behind = {"tp": 1 - it}, {"core": 1 - ic}, {"y": 1 - iy}
    greet(partners_of(("z", "y", "tp", "core")))
    sends = []

    def push(src, dst, send_sem, recv_sem, partner):
        copy = remote(src, dst, send_sem, recv_sem, partner)
        copy.start()
        sends.append(copy)

    def arrived(ref, sem):
        remote(ref, ref, sem, sem, across).wait_recv()

    for d in range(1, nz):
        push(tok_ref.at[it], tok_out.at[iz, ic, it], tzs.at[d], tzr.at[d], {"z": flip("z", d)})
    push(tok_ref, tok_out.at[iz, ic], tcs.at[0, 0], tcr.at[0, 0], beside)
    tok_load = pltpu.make_async_copy(tok_ref, tok_buf, tl.at[0])
    tok_load.start()
    widths = [o.shape[-1] for o in o_refs]
    loads = []
    for k, (w, o) in enumerate(zip(w_refs, o_refs)):
        own = columns(w, iz * 2 + ic, widths[k])
        push(own, o.at[iz, iy], wys.at[k, 0], wyr.at[k, 0], behind)
        for d in range(1, nz):
            other = flip("z", d)
            push(
                columns(w, other * 2 + ic, widths[k]),
                o.at[iz, iy],
                wzs.at[k, d],
                wzr.at[k, d],
                {"z": other},
            )
        load = pltpu.make_async_copy(own, bufs[k], wl.at[k])
        load.start()
        loads.append(load)
    tok_load.wait()
    stores = [pltpu.make_async_copy(tok_buf, tok_out.at[iz, ic], tl.at[1])]
    stores[0].start()
    for d in range(1, nz):
        block = tok_out.at[flip("z", d), ic, it]
        arrived(block, tzr.at[d])
        push(block, block, txs.at[d], txr.at[d], across)
        push(block, block, tcs.at[d, 0], tcr.at[d, 0], beside)

    def forward(k):
        for d in range(1, nz):
            block = o_refs[k].at[flip("z", d), iy]
            arrived(block, wzr.at[k, d])
            push(block, block, wys.at[k, d], wyr.at[k, d], behind)

    first = min(3, count)
    for k in range(first):
        forward(k)
    for d in range(1, nz):
        block = tok_out.at[flip("z", d), ic, 1 - it]
        arrived(block, txr.at[d])
        push(block, block, tcs.at[d, 1], tcr.at[d, 1], beside)
    for k, load in enumerate(loads):
        load.wait()
        store = pltpu.make_async_copy(bufs[k], o_refs[k].at[iz, iy], wl.at[k])
        store.start()
        stores.append(store)
    for k in range(first, count):
        forward(k)
    arrived(tok_out.at[iz, 1 - ic], tcr.at[0, 0])
    for d in range(1, nz):
        for half in range(2):
            side = it if half == 0 else 1 - it
            arrived(tok_out.at[flip("z", d), 1 - ic, side], tcr.at[d, half])
    for k in range(count):
        for d in range(nz):
            source = flip("z", d) if d else iz
            arrived(o_refs[k].at[source, 1 - iy], wyr.at[k, d])
    for copy in sends:
        copy.wait_send()
    for store in stores:
        store.wait()


def intake(token_rows, weights):
    nz = lax.axis_size("z")
    count = len(weights)
    own_rows, width = token_rows.shape
    rows = weights[0].shape[0]
    parts = [w.shape[1] // (2 * nz) for w in weights]
    piece = own_rows // 2
    out_shape = [jax.ShapeDtypeStruct((nz, 2, 2, piece, width), BF)] + [
        jax.ShapeDtypeStruct((nz, 2, rows, c), BF) for c in parts
    ]
    got = call(
        functools.partial(intake_kernel, nz, count),
        5,
        out_shape,
        [pl.ANY] * (count + 1),
        [pl.ANY] * (count + 1),
        [
            pltpu.VMEM((2, piece, width), BF),
            *[pltpu.VMEM((rows, c), BF) for c in parts],
            DMA((2,)),
            *[DMA((nz,)) for _ in range(4)],
            *[DMA((nz, 2)) for _ in range(2)],
            DMA((count,)),
            *[DMA((count, nz)) for _ in range(4)],
        ],
        16,
        token_rows.reshape(2, piece, width),
        *weights,
    )
    return got[0].reshape(-1, width), [g.reshape(-1, g.shape[-1]) for g in got[1:]]


def outlet_kernel(nz, count, *refs):
    g_refs, refs = refs[:count], refs[count:]
    o_refs, refs = refs[:count], refs[count:]
    own, refs = refs[:count], refs[count:]
    yin, refs = refs[:count], refs[count:]
    zout, refs = refs[:count], refs[count:]
    ls, ys, yr, zs, zr, cs, cr, os = refs
    iz, iy, ic = (lax.axis_index(a) for a in ("z", "y", "core"))
    beside, behind = {"core": 1 - ic}, {"y": 1 - iy}
    greet(partners_of(("z", "y", "core")))
    sends, loads, pairs, stores = [], {}, {}, []

    def push(src, dst, send_sem, recv_sem, partner):
        copy = remote(src, dst, send_sem, recv_sem, partner)
        copy.start()
        sends.append(copy)
        return copy

    order = [(k, d) for k in range(count) for d in range(nz - 1, -1, -1)]
    widths = [g.shape[-1] for g in g_refs]
    for k, d in order:
        target = flip("z", d) if d else iz
        pairs[k, d] = push(
            g_refs[k].at[target, 1 - iy], yin[k].at[d], ys.at[k, d], yr.at[k, d], behind
        )
        loads[k, d] = pltpu.make_async_copy(g_refs[k].at[target, iy], own[k].at[d], ls.at[k, d])
        loads[k, d].start()

    def relay(k, d):
        block = columns(o_refs[k], flip("z", d) * 2 + ic, widths[k])
        remote(block, block, zr.at[k, d], zr.at[k, d], beside).wait_recv()
        push(block, block, cs.at[k, d], cr.at[k, d], beside)

    for n, (k, d) in enumerate(order):
        loads[k, d].wait()
        pairs[k, d].wait_recv()
        zout[k][d] = (own[k][d].astype(F32) + yin[k][d].astype(F32)).astype(BF)
        mine = columns(o_refs[k], iz * 2 + ic, widths[k])
        if d:
            push(zout[k].at[d], mine, zs.at[k, d], zr.at[k, d], {"z": flip("z", d)})
        else:
            push(zout[k].at[d], mine, cs.at[k, d], cr.at[k, d], beside)
            store = pltpu.make_async_copy(zout[k].at[d], mine, os.at[k])
            store.start()
            stores.append(store)
            if k:
                for e in range(nz - 1, 0, -1):
                    relay(k - 1, e)
    for e in range(nz - 1, 0, -1):
        relay(count - 1, e)
    for k, d in order:
        source = flip("z", d) if d else iz
        block = columns(o_refs[k], source * 2 + 1 - ic, widths[k])
        remote(block, block, cr.at[k, d], cr.at[k, d], beside).wait_recv()
    for copy in sends:
        copy.wait_send()
    for store in stores:
        store.wait()


def outlet(grads, identity=6):
    nz = lax.axis_size("z")
    count = len(grads)
    parts = [g.shape[1] for g in grads]
    blocks = [g.astype(BF).reshape(nz, 2, -1, g.shape[1]) for g in grads]
    rows = blocks[0].shape[2]
    got = call(
        functools.partial(outlet_kernel, nz, count),
        identity,
        [jax.ShapeDtypeStruct((rows, 2 * nz * c), BF) for c in parts],
        [pl.ANY] * count,
        [pl.ANY] * count,
        [
            *[pltpu.VMEM((nz, rows, c), BF) for _ in range(3) for c in parts],
            *[DMA((count, nz)) for _ in range(7)],
            DMA((count,)),
        ],
        32,
        *blocks,
    )
    if lax.axis_size("ch") > 1:
        got = lax.psum(tuple(got), "ch")
    return [g.astype(F32) for g in got]


def local(
    tokens,
    lengths,
    weight_query,
    weight_key,
    weight_value,
    weight_out,
    weight_gate,
    weight_up,
    weight_down,
    post_attention,
    post_feedforward,
    query_norm,
    key_norm,
    cotangent,
):
    nz, ny, nch, ntp = (lax.axis_size(a) for a in ("z", "y", "ch", "tp"))
    iz, iy, ich, icore, itp = (lax.axis_index(a) for a in AXES)
    token_rows = tokens[0]
    own_rows, width = token_rows.shape
    piece = own_rows // ntp
    seq_rows = own_rows * 2
    total_rows = seq_rows * nz
    scale_factor = 1.0 / math.sqrt(HD)
    own_head = iz * 2 + icore
    qn = lax.dynamic_slice_in_dim(query_norm, own_head * HD, HD)
    kn = lax.dynamic_slice_in_dim(key_norm, own_head * HD, HD)
    seq_lengths = lax.dynamic_index_in_dim(lengths.reshape(nz, ny), iy, 1, keepdims=False)
    positions = ich * seq_rows + jnp.arange(seq_rows, dtype=jnp.int32)
    key_positions = jnp.arange(seq_rows * nch, dtype=jnp.int32)
    cosine, sine_table = rope_tables(positions)
    allowed = (key_positions[None, None, :] <= positions[None, :, None]) & (
        key_positions[None, None, :] < seq_lengths[:, None, None]
    )
    my_tokens = lax.dynamic_slice_in_dim(token_rows, itp * piece, piece, 0)
    my_cot = lax.dynamic_slice_in_dim(cotangent[0], itp * piece, piece, 0)
    my_pos = (ich * 2 + icore) * own_rows + itp * piece + jnp.arange(piece, dtype=jnp.int32)
    my_valid = (my_pos < lengths[iz * ny + iy]).astype(F32)[:, None]

    tokens_all, (wq, wk, wv, wo, wg, wu, wd) = intake(
        token_rows,
        (
            weight_query,
            weight_key,
            weight_value,
            weight_out,
            weight_gate,
            weight_up,
            weight_down,
        ),
    )
    query_raw = mm(tokens_all, wq)
    key_raw = mm(tokens_all, wk)
    value_raw = mm(tokens_all, wv)
    squares = head_total(
        jnp.stack([jnp.sum(query_raw * query_raw, axis=-1), jnp.sum(key_raw * key_raw, axis=-1)])
    )
    scales = lax.rsqrt(squares / width + EPSILON)
    query_scale = scales[0][:, None]
    key_scale = scales[1][:, None]
    by_seq = lambda a: a.reshape(nz, seq_rows, HD)
    queries = rotate(by_seq(query_raw * query_scale * qn), cosine, sine_table).astype(BF)
    keys = rotate(by_seq(key_raw * key_scale * kn), cosine, sine_table).astype(BF)
    values = by_seq(value_raw).astype(BF)
    if nch > 1:
        keys_full = lax.all_gather(keys, "ch", axis=1, tiled=True)
        values_full = lax.all_gather(values, "ch", axis=1, tiled=True)
    else:
        keys_full, values_full = keys, values
    scores = (
        jnp.einsum("btd,bsd->bts", queries, keys_full, preferred_element_type=F32) * scale_factor
    )
    scores = jnp.where(allowed, scores, NEGATIVE)
    exponent = jnp.exp(scores - jnp.max(scores, axis=-1, keepdims=True))
    probability = exponent / jnp.sum(exponent, axis=-1, keepdims=True)
    probability_low = probability.astype(BF)
    attended = jnp.einsum("bts,bsd->btd", probability_low, values_full, preferred_element_type=F32)
    attended_low = attended.reshape(total_rows, HD).astype(BF)
    branch_sum = scatter_rows(mm_nt(attended_low, wo))
    attn_scale = lax.rsqrt(jnp.mean(branch_sum * branch_sum, axis=-1, keepdims=True) + EPSILON)
    attn_normed = branch_sum * attn_scale
    attention_branch = attn_normed * post_attention
    residual = my_tokens.astype(F32) + attention_branch
    residual_all = gather_rows(residual.astype(BF))
    gate_value = mm(residual_all, wg)
    up_value = mm(residual_all, wu)
    sigmoid_gate = jax.nn.sigmoid(gate_value)
    silu_gate = gate_value * sigmoid_gate
    mixed_low = (silu_gate * up_value).astype(BF)
    down_sum = scatter_rows(mm_nt(mixed_low, wd))
    ffn_scale = lax.rsqrt(jnp.mean(down_sum * down_sum, axis=-1, keepdims=True) + EPSILON)
    ffn_normed = down_sum * ffn_scale
    feedforward_branch = ffn_normed * post_feedforward
    stream = residual + feedforward_branch
    stat_terms = jnp.stack(
        [
            jnp.sum(my_valid * stream * stream),
            jnp.sum(my_valid * attention_branch * attention_branch),
            jnp.sum(my_valid * feedforward_branch * feedforward_branch),
        ]
    )
    grad_stream = my_cot * my_valid
    grad_post_ff = jnp.sum(grad_stream * ffn_normed, axis=0)
    scaled = grad_stream * post_feedforward
    grad_down_sum = ffn_scale * (
        scaled - ffn_normed * jnp.mean(scaled * ffn_normed, axis=-1, keepdims=True)
    )
    down_all = gather_rows(grad_down_sum.astype(BF))
    grad_mixed = mm(down_all, wd)
    gate_low = (
        grad_mixed * up_value * sigmoid_gate * (1.0 + gate_value * (1.0 - sigmoid_gate))
    ).astype(BF)
    up_low = (grad_mixed * silu_gate).astype(BF)
    grad_wg = mm_tn(residual_all, gate_low)
    grad_wu = mm_tn(residual_all, up_low)
    grad_wd = mm_tn(down_all, mixed_low)
    grad_residual = grad_stream + scatter_rows(mm_nt(gate_low, wg) + mm_nt(up_low, wu))
    grad_post_attn = jnp.sum(grad_residual * attn_normed, axis=0)
    scaled_attn = grad_residual * post_attention
    grad_branch = attn_scale * (
        scaled_attn - attn_normed * jnp.mean(scaled_attn * attn_normed, axis=-1, keepdims=True)
    )
    branch_all = gather_rows(grad_branch.astype(BF))
    grad_att_low = mm(branch_all, wo).astype(BF)
    grad_wo = mm_tn(branch_all, attended_low)
    grad_att = by_seq(grad_att_low)
    grad_prob = jnp.einsum("btd,bsd->bts", grad_att, values_full, preferred_element_type=F32)
    row_dots = jnp.sum(probability * grad_prob, axis=-1, keepdims=True)
    grad_scores = (probability * (grad_prob - row_dots)).astype(BF)
    grad_queries = (
        jnp.einsum("bts,bsd->btd", grad_scores, keys_full, preferred_element_type=F32)
        * scale_factor
    )
    grad_keys = (
        jnp.einsum("bts,btd->bsd", grad_scores, queries, preferred_element_type=F32) * scale_factor
    )
    grad_values = jnp.einsum("bts,btd->bsd", probability_low, grad_att, preferred_element_type=F32)
    if nch > 1:
        grad_keys, grad_values = (
            lax.psum_scatter(g.astype(BF), "ch", scatter_dimension=1, tiled=True).astype(F32)
            for g in (grad_keys, grad_values)
        )
    value_grad_low = grad_values.reshape(total_rows, HD).astype(BF)
    grad_q_normed = rotate_back(grad_queries, cosine, sine_table).reshape(total_rows, HD)
    grad_k_normed = rotate_back(grad_keys, cosine, sine_table).reshape(total_rows, HD)
    query_weighted = grad_q_normed * qn
    key_weighted = grad_k_normed * kn
    dots = head_total(
        jnp.stack(
            [
                jnp.sum(query_weighted * query_raw, axis=-1),
                jnp.sum(key_weighted * key_raw, axis=-1),
            ]
        )
    )
    query_grad_low = (
        query_scale * (query_weighted - query_raw * query_scale**2 * (dots[0] / width)[:, None])
    ).astype(BF)
    key_grad_low = (
        key_scale * (key_weighted - key_raw * key_scale**2 * (dots[1] / width)[:, None])
    ).astype(BF)
    grad_qnorm = jnp.sum(grad_q_normed * query_raw * query_scale, axis=0)
    grad_knorm = jnp.sum(grad_k_normed * key_raw * key_scale, axis=0)
    grad_wq = mm_tn(tokens_all, query_grad_low)
    grad_wk = mm_tn(tokens_all, key_grad_low)
    grad_wv = mm_tn(tokens_all, value_grad_low)
    grad_rows = grad_residual + scatter_rows(
        mm_nt(query_grad_low, wq) + mm_nt(key_grad_low, wk) + mm_nt(value_grad_low, wv)
    )
    weight_grads = outlet((grad_wq, grad_wk, grad_wv, grad_wo, grad_wg, grad_wu, grad_wd))
    grad_input = lax.all_gather(grad_rows, "tp", axis=0, tiled=True)
    output = lax.all_gather(stream.astype(BF), "tp", axis=0, tiled=True)
    slot = itp * (width // ntp) + own_head * HD
    zero_row = jnp.zeros((width,), F32)
    summed = all_total(
        jnp.concatenate(
            [
                grad_post_attn,
                grad_post_ff,
                lax.dynamic_update_slice_in_dim(zero_row, grad_qnorm, slot, 0),
                lax.dynamic_update_slice_in_dim(zero_row, grad_knorm, slot, 0),
                stat_terms,
            ]
        )
    )
    half = width // ntp
    qn_sum = lax.dynamic_slice_in_dim(summed, 2 * width + itp * half, half)
    kn_sum = lax.dynamic_slice_in_dim(summed, 3 * width + itp * half, half)
    token_count = jnp.sum(lengths.astype(F32))
    root_means = jnp.sqrt(summed[4 * width :] / (token_count * width))
    return (
        output[None],
        grad_input[None],
        *weight_grads,
        summed[:width],
        summed[width : 2 * width],
        qn_sum,
        kn_sum,
        root_means,
    )


def solution(mesh):
    n_fsdp, n_ctx, n_tp = (mesh.shape[a] for a in ("fsdp", "ctx", "tp"))
    fine = Mesh(mesh.devices.reshape(n_fsdp // 2, 2, n_ctx // 2, 2, n_tp), AXES)
    fsdp, ctx = ("z", "y"), ("ch", "core")
    rows = P(fsdp, ctx, None)
    weight = P(fsdp, "tp")
    return jax.shard_map(
        local,
        mesh=fine,
        in_specs=(rows, P(), *([weight] * 7), P(), P(), P("tp"), P("tp"), rows),
        out_specs=(rows, rows, *([weight] * 7), P(), P(), P("tp"), P("tp"), P()),
        check_vma=False,
    )
```

```python
import functools
import math
import types

import jax
import jax.numpy as jnp
from jax import lax
from jax.experimental import pallas as pl
from jax.experimental.pallas import tpu as pltpu
from jax.sharding import Mesh, PartitionSpec as P

HD = 128
EPSILON = 1e-06
ROPE_BASE = 500000.0
NEGATIVE = -1e30
AXES = ("z", "y", "ch", "core", "tp")
BF = jnp.bfloat16
F32 = jnp.float32


def rope_tables(positions):
    half_size = HD // 2
    exponent = jnp.arange(half_size, dtype=F32) * (2.0 / HD)
    frequency = jnp.power(ROPE_BASE, -exponent)
    angles = positions.astype(F32)[:, None] * frequency[None, :]
    cosine = jnp.cos(angles)
    sine_table = jnp.sin(angles)
    return (
        jnp.concatenate([cosine, cosine], axis=-1),
        jnp.concatenate([sine_table, sine_table], axis=-1),
    )


def rotate(values, cosine, sine_table):
    half_size = HD // 2
    turned = jnp.concatenate([-values[..., half_size:], values[..., :half_size]], axis=-1)
    return values * cosine + turned * sine_table


def rotate_back(grads_in, cosine, sine_table):
    half_size = HD // 2
    sin_part = grads_in * sine_table
    return grads_in * cosine + jnp.concatenate(
        [sin_part[..., half_size:], -sin_part[..., :half_size]], axis=-1
    )


def dot(former, latter, dims):
    return lax.dot_general(former, latter, (dims, ((), ())), preferred_element_type=F32)


def mm(a, b):
    return dot(a, b, ((1,), (0,)))


def mm_nt(a, b):
    return dot(a, b, ((1,), (1,)))


def mm_tn(a, b):
    return dot(a, b, ((0,), (0,)))


MESH = pl.DeviceIdType.MESH


def flip(axis, bits):
    me = lax.axis_index(axis)
    result, weight = me, 1
    while weight <= bits:
        if (bits // weight) % 2:
            result = result + weight * (1 - 2 * lax.rem(me // weight, 2))
        weight *= 2
    return result


def greet(partners):
    barrier = pltpu.get_barrier_semaphore()
    for partner in partners:
        pl.semaphore_signal(barrier, inc=1, device_id=partner, device_id_type=MESH)
    pl.semaphore_wait(barrier, len(partners))


def remote(src, dst, send_sem, recv_sem, partner):
    return pltpu.make_async_remote_copy(
        src_ref=src,
        dst_ref=dst,
        send_sem=send_sem,
        recv_sem=recv_sem,
        device_id=partner,
        device_id_type=MESH,
    )


def partners_of(axes):
    found = []
    for axis in axes:
        for bits in range(1, lax.axis_size(axis)):
            found.append({axis: flip(axis, bits)})
    return found


def call(kernel, identity, out_shape, in_spaces, out_spaces, scratch, limit, *operands):
    return pl.pallas_call(
        kernel,
        out_shape=out_shape,
        in_specs=[pl.BlockSpec(memory_space=s) for s in in_spaces],
        out_specs=jax.tree.map(lambda s: pl.BlockSpec(memory_space=s), out_spaces),
        scratch_shapes=scratch,
        compiler_params=pltpu.CompilerParams(
            collective_id=identity, has_side_effects=True, vmem_limit_bytes=limit * 2**20
        ),
    )(*operands)


DMA = pltpu.SemaphoreType.DMA


def gather_kernel(nz, x_ref, out_ref, own_sem, zs, zr, xs, xr, cs, cr):
    iz, ic, it = (lax.axis_index(a) for a in ("z", "core", "tp"))
    greet(partners_of(("z", "tp", "core")))
    sends = []

    def push(src, where, send_sem, recv_sem, partner):
        copy = remote(src, out_ref.at[where], send_sem, recv_sem, partner)
        copy.start()
        sends.append(copy)

    across, beside = {"tp": 1 - it}, {"core": 1 - ic}
    own = (iz, ic, it)
    for d in range(1, nz):
        push(x_ref, own, zs.at[d], zr.at[d], {"z": flip("z", d)})
    push(x_ref, own, xs.at[0], xr.at[0], across)
    push(x_ref, own, cs.at[0, 0], cr.at[0, 0], beside)
    local_copy = pltpu.make_async_copy(x_ref, out_ref.at[own], own_sem)
    local_copy.start()

    def await_at(where, sem):
        remote(out_ref.at[where], out_ref.at[where], sem, sem, across).wait_recv()

    def from_across(d):
        where = (flip("z", d), ic, 1 - it)
        await_at(where, xr.at[d])
        push(out_ref.at[where], where, cs.at[d, 1], cr.at[d, 1], beside)

    for d in range(1, nz):
        where = (flip("z", d), ic, it)
        await_at(where, zr.at[d])
        push(out_ref.at[where], where, xs.at[d], xr.at[d], across)
        push(out_ref.at[where], where, cs.at[d, 0], cr.at[d, 0], beside)
        from_across(d - 1)
    from_across(nz - 1)
    for d in range(nz):
        for half in range(2):
            side = it if half == 0 else 1 - it
            await_at((flip("z", d), 1 - ic, side), cr.at[d, half])
    for copy in sends:
        copy.wait_send()
    local_copy.wait()


def gather_rows(rows):
    piece, width = rows.shape
    nz = lax.axis_size("z")
    out = call(
        functools.partial(gather_kernel, nz),
        1,
        jax.ShapeDtypeStruct((nz, 2, 2, piece, width), rows.dtype),
        [pl.ANY],
        pl.ANY,
        [DMA, DMA((nz,)), DMA((nz,)), DMA((nz,)), DMA((nz,)), DMA((nz, 2)), DMA((nz, 2))],
        16,
        rows,
    )
    return out.reshape(-1, width)


def scatter_kernel(
    nz, p_ref, out_ref, own, cin, xout, xin, zout, zin, ls, cs, cr, xs, xr, zs, zr
):
    iz, ic, it = (lax.axis_index(a) for a in ("z", "core", "tp"))
    greet(partners_of(("z", "tp", "core")))
    across, beside = {"tp": 1 - it}, {"core": 1 - ic}
    order = list(range(nz - 1, -1, -1))
    loads, besides, acrosses, zeds = {}, {}, {}, {}
    for d in order:
        target = flip("z", d) if d else iz
        besides[d] = remote(p_ref.at[target, 1 - ic], cin.at[d], cs.at[d], cr.at[d], beside)
        besides[d].start()
        loads[d] = pltpu.make_async_copy(p_ref.at[target, ic], own.at[d], ls.at[d])
        loads[d].start()

    def add(d, side):
        return own[d, side].astype(F32) + cin[d, side].astype(F32)

    def after_across(d):
        acrosses[d].wait_recv()
        total = add(d, it) + xin[d].astype(F32)
        if d == 0:
            out_ref[...] = total
        else:
            zout[d] = total.astype(BF)
            zeds[d] = remote(zout.at[d], zin.at[d], zs.at[d], zr.at[d], {"z": flip("z", d)})
            zeds[d].start()

    for n, d in enumerate(order):
        loads[d].wait()
        besides[d].wait_recv()
        xout[d] = add(d, 1 - it).astype(BF)
        acrosses[d] = remote(xout.at[d], xin.at[d], xs.at[d], xr.at[d], across)
        acrosses[d].start()
        if n:
            after_across(order[n - 1])
    after_across(0)
    for d in order[:-1]:
        zeds[d].wait_recv()
        out_ref[...] += zin[d].astype(F32)
    for group in (besides, acrosses, zeds):
        for copy in group.values():
            copy.wait_send()


def scatter_rows(partial):
    nz = lax.axis_size("z")
    width = partial.shape[1]
    part = partial.astype(BF).reshape(nz, 2, 2, -1, width)
    piece = part.shape[3]
    sems = [DMA((nz,)) for _ in range(7)]
    return call(
        functools.partial(scatter_kernel, nz),
        2,
        jax.ShapeDtypeStruct((piece, width), F32),
        [pl.ANY],
        pltpu.VMEM,
        [
            pltpu.VMEM((nz, 2, piece, width), BF),
            pltpu.VMEM((nz, 2, piece, width), BF),
            *[pltpu.VMEM((nz, piece, width), BF) for _ in range(4)],
            *sems,
        ],
        32,
        part,
    )


def total_kernel(axes, x_ref, out_ref, *scratch):
    greet(partners_of(axes))
    value = x_ref[...]
    sends = []
    for stage, axis in enumerate(axes):
        slots, send_sems, recv_sems = scratch[3 * stage : 3 * stage + 3]
        size = lax.axis_size(axis)
        me = lax.axis_index(axis)
        slots[me] = value
        copies = []
        for d in range(1, size):
            copy = remote(
                slots.at[me], slots.at[me], send_sems.at[d], recv_sems.at[d], {axis: flip(axis, d)}
            )
            copy.start()
            copies.append(copy)
        for copy in copies:
            copy.wait_recv()
        value = slots[0]
        for n in range(1, size):
            value = value + slots[n]
        sends += copies
    out_ref[...] = value
    for copy in sends:
        copy.wait_send()


def total(terms, axes, identity):
    axes = tuple(a for a in axes if lax.axis_size(a) > 1)
    scratch = []
    for axis in axes:
        size = lax.axis_size(axis)
        scratch += [pltpu.VMEM((size, *terms.shape), F32), DMA((size,)), DMA((size,))]
    return call(
        functools.partial(total_kernel, axes),
        identity,
        jax.ShapeDtypeStruct(terms.shape, F32),
        [pltpu.VMEM],
        pltpu.VMEM,
        scratch,
        16,
        terms,
    )


def head_total(terms):
    return total(terms.reshape(-1, 128), ("core", "tp", "z"), 3).reshape(terms.shape)


def all_total(terms):
    size = terms.shape[0]
    padded = jnp.pad(terms, (0, -size % 1024)).reshape(-1, 128)
    return total(padded, ("core", "tp", "y", "z", "ch"), 4).reshape(-1)[:size]


def columns(ref, slot, count):
    return ref.at[:, pl.ds(pl.multiple_of(slot * count, 128), count)]


def intake_kernel(nz, count, tok_ref, *refs):
    w_refs, refs = refs[:count], refs[count:]
    tok_out, refs = refs[0], refs[1:]
    o_refs, refs = refs[:count], refs[count:]
    tok_buf, refs = refs[0], refs[1:]
    bufs, refs = refs[:count], refs[count:]
    tl, tzs, tzr, txs, txr, tcs, tcr, wl, wzs, wzr, wys, wyr = refs
    iz, iy, ic, it = (lax.axis_index(a) for a in ("z", "y", "core", "tp"))
    across, beside, behind = {"tp": 1 - it}, {"core": 1 - ic}, {"y": 1 - iy}
    greet(partners_of(("z", "y", "tp", "core")))
    sends = []

    def push(src, dst, send_sem, recv_sem, partner):
        copy = remote(src, dst, send_sem, recv_sem, partner)
        copy.start()
        sends.append(copy)

    def arrived(ref, sem):
        remote(ref, ref, sem, sem, across).wait_recv()

    for d in range(1, nz):
        push(tok_ref.at[it], tok_out.at[iz, ic, it], tzs.at[d], tzr.at[d], {"z": flip("z", d)})
    push(tok_ref, tok_out.at[iz, ic], tcs.at[0, 0], tcr.at[0, 0], beside)
    tok_load = pltpu.make_async_copy(tok_ref, tok_buf, tl.at[0])
    tok_load.start()
    widths = [o.shape[-1] for o in o_refs]
    loads = []
    for k, (w, o) in enumerate(zip(w_refs, o_refs)):
        own = columns(w, iz * 2 + ic, widths[k])
        push(own, o.at[iz, iy], wys.at[k, 0], wyr.at[k, 0], behind)
        for d in range(1, nz):
            other = flip("z", d)
            push(
                columns(w, other * 2 + ic, widths[k]),
                o.at[iz, iy],
                wzs.at[k, d],
                wzr.at[k, d],
                {"z": other},
            )
        load = pltpu.make_async_copy(own, bufs[k], wl.at[k])
        load.start()
        loads.append(load)
    tok_load.wait()
    stores = [pltpu.make_async_copy(tok_buf, tok_out.at[iz, ic], tl.at[1])]
    stores[0].start()
    for d in range(1, nz):
        block = tok_out.at[flip("z", d), ic, it]
        arrived(block, tzr.at[d])
        push(block, block, txs.at[d], txr.at[d], across)
        push(block, block, tcs.at[d, 0], tcr.at[d, 0], beside)

    def forward(k):
        for d in range(1, nz):
            block = o_refs[k].at[flip("z", d), iy]
            arrived(block, wzr.at[k, d])
            push(block, block, wys.at[k, d], wyr.at[k, d], behind)

    first = min(3, count)
    for k in range(first):
        forward(k)
    for d in range(1, nz):
        block = tok_out.at[flip("z", d), ic, 1 - it]
        arrived(block, txr.at[d])
        push(block, block, tcs.at[d, 1], tcr.at[d, 1], beside)
    for k, load in enumerate(loads):
        load.wait()
        store = pltpu.make_async_copy(bufs[k], o_refs[k].at[iz, iy], wl.at[k])
        store.start()
        stores.append(store)
    for k in range(first, count):
        forward(k)
    arrived(tok_out.at[iz, 1 - ic], tcr.at[0, 0])
    for d in range(1, nz):
        for half in range(2):
            side = it if half == 0 else 1 - it
            arrived(tok_out.at[flip("z", d), 1 - ic, side], tcr.at[d, half])
    for k in range(count):
        for d in range(nz):
            source = flip("z", d) if d else iz
            arrived(o_refs[k].at[source, 1 - iy], wyr.at[k, d])
    for copy in sends:
        copy.wait_send()
    for store in stores:
        store.wait()


def intake(token_rows, weights):
    nz = lax.axis_size("z")
    count = len(weights)
    own_rows, width = token_rows.shape
    rows = weights[0].shape[0]
    parts = [w.shape[1] // (2 * nz) for w in weights]
    piece = own_rows // 2
    out_shape = [jax.ShapeDtypeStruct((nz, 2, 2, piece, width), BF)] + [
        jax.ShapeDtypeStruct((nz, 2, rows, c), BF) for c in parts
    ]
    got = call(
        functools.partial(intake_kernel, nz, count),
        5,
        out_shape,
        [pl.ANY] * (count + 1),
        [pl.ANY] * (count + 1),
        [
            pltpu.VMEM((2, piece, width), BF),
            *[pltpu.VMEM((rows, c), BF) for c in parts],
            DMA((2,)),
            *[DMA((nz,)) for _ in range(4)],
            *[DMA((nz, 2)) for _ in range(2)],
            DMA((count,)),
            *[DMA((count, nz)) for _ in range(4)],
        ],
        16,
        token_rows.reshape(2, piece, width),
        *weights,
    )
    return got[0].reshape(-1, width), [g.reshape(-1, g.shape[-1]) for g in got[1:]]


def outlet_kernel(nz, count, *refs):
    g_refs, refs = refs[:count], refs[count:]
    o_refs, refs = refs[:count], refs[count:]
    own, refs = refs[:count], refs[count:]
    yin, refs = refs[:count], refs[count:]
    zout, refs = refs[:count], refs[count:]
    ls, ys, yr, zs, zr, cs, cr, os = refs
    iz, iy, ic = (lax.axis_index(a) for a in ("z", "y", "core"))
    beside, behind = {"core": 1 - ic}, {"y": 1 - iy}
    greet(partners_of(("z", "y", "core")))
    sends, loads, pairs, stores = [], {}, {}, []

    def push(src, dst, send_sem, recv_sem, partner):
        copy = remote(src, dst, send_sem, recv_sem, partner)
        copy.start()
        sends.append(copy)
        return copy

    order = [(k, d) for k in range(count) for d in range(nz - 1, -1, -1)]
    widths = [g.shape[-1] for g in g_refs]
    for k, d in order:
        target = flip("z", d) if d else iz
        pairs[k, d] = push(
            g_refs[k].at[target, 1 - iy], yin[k].at[d], ys.at[k, d], yr.at[k, d], behind
        )
        loads[k, d] = pltpu.make_async_copy(g_refs[k].at[target, iy], own[k].at[d], ls.at[k, d])
        loads[k, d].start()

    def relay(k, d):
        block = columns(o_refs[k], flip("z", d) * 2 + ic, widths[k])
        remote(block, block, zr.at[k, d], zr.at[k, d], beside).wait_recv()
        push(block, block, cs.at[k, d], cr.at[k, d], beside)

    for n, (k, d) in enumerate(order):
        loads[k, d].wait()
        pairs[k, d].wait_recv()
        zout[k][d] = (own[k][d].astype(F32) + yin[k][d].astype(F32)).astype(BF)
        mine = columns(o_refs[k], iz * 2 + ic, widths[k])
        if d:
            push(zout[k].at[d], mine, zs.at[k, d], zr.at[k, d], {"z": flip("z", d)})
        else:
            push(zout[k].at[d], mine, cs.at[k, d], cr.at[k, d], beside)
            store = pltpu.make_async_copy(zout[k].at[d], mine, os.at[k])
            store.start()
            stores.append(store)
            if k:
                for e in range(nz - 1, 0, -1):
                    relay(k - 1, e)
    for e in range(nz - 1, 0, -1):
        relay(count - 1, e)
    for k, d in order:
        source = flip("z", d) if d else iz
        block = columns(o_refs[k], source * 2 + 1 - ic, widths[k])
        remote(block, block, cr.at[k, d], cr.at[k, d], beside).wait_recv()
    for copy in sends:
        copy.wait_send()
    for store in stores:
        store.wait()


def outlet(grads, identity=6):
    nz = lax.axis_size("z")
    count = len(grads)
    parts = [g.shape[1] for g in grads]
    blocks = [g.astype(BF).reshape(nz, 2, -1, g.shape[1]) for g in grads]
    rows = blocks[0].shape[2]
    got = call(
        functools.partial(outlet_kernel, nz, count),
        identity,
        [jax.ShapeDtypeStruct((rows, 2 * nz * c), BF) for c in parts],
        [pl.ANY] * count,
        [pl.ANY] * count,
        [
            *[pltpu.VMEM((nz, rows, c), BF) for _ in range(3) for c in parts],
            *[DMA((count, nz)) for _ in range(7)],
            DMA((count,)),
        ],
        32,
        *blocks,
    )
    if lax.axis_size("ch") > 1:
        got = lax.psum(tuple(got), "ch")
    return [g.astype(F32) for g in got]


class Kernel:
    def __init__(self):
        self.ins, self.outs, self.scratch = [], [], []

    def inp(self, name, array, space=pl.ANY):
        self.ins.append((name, array, space))

    def out(self, name, shape, dtype, space=pl.ANY):
        self.outs.append((name, jax.ShapeDtypeStruct(shape, dtype), space))

    def mem(self, name, shape, dtype):
        self.scratch.append((name, pltpu.VMEM(shape, dtype)))

    def sem(self, name, *shape):
        self.scratch.append((name, DMA(shape)))

    def run(self, identity, body, limit):
        names = [n for n, *_ in self.ins + self.outs + self.scratch]

        def kernel(*refs):
            body(types.SimpleNamespace(**dict(zip(names, refs))))

        got = call(
            kernel,
            identity,
            [shape for _, shape, _ in self.outs],
            [space for *_, space in self.ins],
            [space for *_, space in self.outs],
            [made for _, made in self.scratch],
            limit,
            *[array for _, array, _ in self.ins],
        )
        return {n: g for (n, *_), g in zip(self.outs, got)}


class Flow:
    def __init__(self):
        self.sends = []
        self.iz, self.iy, self.ic, self.it = (
            lax.axis_index(a) for a in ("z", "y", "core", "tp")
        )
        self.across = {"tp": 1 - self.it}
        self.beside = {"core": 1 - self.ic}
        self.behind = {"y": 1 - self.iy}

    def at(self, d):
        return flip("z", d) if d else self.iz

    def push(self, src, dst, send_sem, recv_sem, partner):
        copy = remote(src, dst, send_sem, recv_sem, partner)
        copy.start()
        self.sends.append(copy)
        return copy

    def arrived(self, ref, sem):
        remote(ref, ref, sem, sem, self.across).wait_recv()

    def finish(self):
        for copy in self.sends:
            copy.wait_send()
        self.sends = []


def stripe(ref, z, core, tp, piece):
    start = pl.multiple_of((core * 2 + tp) * piece, piece)
    return ref.at[z, pl.ds(start, piece)]


class Gather(Flow):
    @staticmethod
    def setup(k, name, rows, nz):
        piece, width = rows.shape
        k.inp(name + "_x", rows)
        k.mem(name, (nz, 4 * piece, width), rows.dtype)
        k.sem(name + "_own")
        for s in ("_zs", "_zr", "_xs", "_xr"):
            k.sem(name + s, nz)
        k.sem(name + "_cs", nz, 2)
        k.sem(name + "_cr", nz, 2)

    def __init__(self, r, name, nz):
        super().__init__()
        self.nz = nz
        self.x, self.buf = getattr(r, name + "_x"), getattr(r, name)
        self.own_sem, self.zs, self.zr, self.xs, self.xr, self.cs, self.cr = (
            getattr(r, name + s) for s in ("_own", "_zs", "_zr", "_xs", "_xr", "_cs", "_cr")
        )
        self.piece = self.x.shape[0]

    def block(self, z, core, tp):
        return stripe(self.buf, z, core, tp, self.piece)

    def start(self):
        own = self.block(self.iz, self.ic, self.it)
        for d in range(1, self.nz):
            self.push(self.x, own, self.zs.at[d], self.zr.at[d], {"z": self.at(d)})
        self.push(self.x, own, self.xs.at[0], self.xr.at[0], self.across)
        self.push(self.x, own, self.cs.at[0, 0], self.cr.at[0, 0], self.beside)
        self.local = pltpu.make_async_copy(self.x, own, self.own_sem)
        self.local.start()

    def from_across(self, d):
        block = self.block(self.at(d), self.ic, 1 - self.it)
        self.arrived(block, self.xr.at[d])
        self.push(block, block, self.cs.at[d, 1], self.cr.at[d, 1], self.beside)

    def advance(self, d):
        if d < self.nz:
            block = self.block(self.at(d), self.ic, self.it)
            self.arrived(block, self.zr.at[d])
            self.push(block, block, self.xs.at[d], self.xr.at[d], self.across)
            self.push(block, block, self.cs.at[d, 0], self.cr.at[d, 0], self.beside)
        self.from_across(d - 1)

    def ready(self, d):
        if d == 0:
            self.local.wait()
        for half in range(2):
            side = self.it if half == 0 else 1 - self.it
            self.arrived(self.block(self.at(d), 1 - self.ic, side), self.cr.at[d, half])


class Scatter(Flow):
    @staticmethod
    def setup(k, name, piece, width, nz):
        k.mem(name + "_p", (nz, 4 * piece, width), BF)
        k.mem(name + "_c", (nz, 2 * piece, width), BF)
        for s in ("_xo", "_xi", "_zo", "_zi"):
            k.mem(name + s, (nz, piece, width), BF)
        for s in ("_cs", "_cr", "_xs", "_xr", "_zs", "_zr"):
            k.sem(name + s, nz)

    def __init__(self, r, name, nz, out):
        super().__init__()
        self.nz, self.out = nz, out
        self.p, self.c, self.xo, self.xi, self.zo, self.zi = (
            getattr(r, name + s) for s in ("_p", "_c", "_xo", "_xi", "_zo", "_zi")
        )
        self.cs, self.cr, self.xs, self.xr, self.zs, self.zr = (
            getattr(r, name + s) for s in ("_cs", "_cr", "_xs", "_xr", "_zs", "_zr")
        )
        self.piece = self.xo.shape[1]
        self.core_copy, self.across_copy, self.z_copy = {}, {}, {}

    def begin(self, d):
        rows = pl.ds(pl.multiple_of((1 - self.ic) * 2 * self.piece, 2 * self.piece), 2 * self.piece)
        src = self.p.at[d, rows]
        self.core_copy[d] = self.push(
            src, self.c.at[d], self.cs.at[d], self.cr.at[d], self.beside
        )

    def add(self, d, side):
        start = pl.multiple_of((self.ic * 2 + side) * self.piece, self.piece)
        rows = pl.ds(pl.multiple_of(side * self.piece, self.piece), self.piece)
        return self.p[d, pl.ds(start, self.piece)].astype(F32) + self.c[d, rows].astype(F32)

    def cross(self, d):
        self.core_copy[d].wait_recv()
        self.xo[d] = self.add(d, 1 - self.it).astype(BF)
        self.across_copy[d] = self.push(
            self.xo.at[d], self.xi.at[d], self.xs.at[d], self.xr.at[d], self.across
        )

    def leave(self, d):
        self.across_copy[d].wait_recv()
        value = self.add(d, self.it) + self.xi[d].astype(F32)
        if d == 0:
            self.out[...] = value
        else:
            self.zo[d] = value.astype(BF)
            self.z_copy[d] = self.push(
                self.zo.at[d], self.zi.at[d], self.zs.at[d], self.zr.at[d], {"z": self.at(d)}
            )

    def end(self):
        for d in range(self.nz - 1, 0, -1):
            self.z_copy[d].wait_recv()
            self.out[...] += self.zi[d].astype(F32)


class Total(Flow):
    @staticmethod
    def setup(k, name, shape, axes):
        for axis in axes:
            size = lax.axis_size(axis)
            k.mem(f"{name}_{axis}", (size, *shape), F32)
            k.sem(f"{name}_{axis}_s", size)
            k.sem(f"{name}_{axis}_r", size)

    def __init__(self, r, name):
        super().__init__()
        self.r, self.name = r, name

    def send(self, axis, value):
        slots, ss, rs = (getattr(self.r, f"{self.name}_{axis}{s}") for s in ("", "_s", "_r"))
        me = lax.axis_index(axis)
        slots[me] = value
        self.copies = [
            self.push(slots.at[me], slots.at[me], ss.at[d], rs.at[d], {axis: flip(axis, d)})
            for d in range(1, lax.axis_size(axis))
        ]
        self.slots = slots

    def receive(self):
        for copy in self.copies:
            copy.wait_recv()
        value = self.slots[0]
        for n in range(1, self.slots.shape[0]):
            value = value + self.slots[n]
        return value


class Outlet(Flow):
    @staticmethod
    def setup(k, name, grads, nz):
        for n, grad in enumerate(grads):
            rows, cols = grad.shape[0] // (2 * nz), grad.shape[1]
            k.inp(f"{name}_g{n}", grad.astype(BF).reshape(nz, 2, rows, cols))
            k.out(f"{name}_o{n}", (rows, 2 * nz * cols), BF)
            for s in ("own", "yin", "zout"):
                k.mem(f"{name}_{s}{n}", (nz, rows, cols), BF)
        for s in ("ls", "ys", "yr", "zs", "zr", "cs", "cr"):
            k.sem(f"{name}_{s}", len(grads), nz)
        k.sem(f"{name}_os", len(grads))

    def __init__(self, r, name, count, nz):
        super().__init__()
        self.nz, self.count = nz, count
        self.g, self.o, self.own, self.yin, self.zout = (
            [getattr(r, f"{name}_{s}{n}") for n in range(count)]
            for s in ("g", "o", "own", "yin", "zout")
        )
        self.ls, self.ys, self.yr, self.zs, self.zr, self.cs, self.cr, self.os = (
            getattr(r, f"{name}_{s}") for s in ("ls", "ys", "yr", "zs", "zr", "cs", "cr", "os")
        )
        self.loads, self.pairs, self.stores = {}, {}, []

    def slot(self, k, z, core):
        return columns(self.o[k], z * 2 + core, self.g[k].shape[-1])

    def start(self, k):
        for d in range(self.nz - 1, -1, -1):
            target = self.at(d)
            self.pairs[k, d] = self.push(
                self.g[k].at[target, 1 - self.iy],
                self.yin[k].at[d],
                self.ys.at[k, d],
                self.yr.at[k, d],
                self.behind,
            )
            self.loads[k, d] = pltpu.make_async_copy(
                self.g[k].at[target, self.iy], self.own[k].at[d], self.ls.at[k, d]
            )
            self.loads[k, d].start()

    def combine(self, k):
        mine = self.slot(k, self.iz, self.ic)
        for d in range(self.nz - 1, -1, -1):
            self.loads[k, d].wait()
            self.pairs[k, d].wait_recv()
            self.zout[k][d] = (
                self.own[k][d].astype(F32) + self.yin[k][d].astype(F32)
            ).astype(BF)
            src = self.zout[k].at[d]
            if d:
                self.push(src, mine, self.zs.at[k, d], self.zr.at[k, d], {"z": self.at(d)})
            else:
                self.push(src, mine, self.cs.at[k, d], self.cr.at[k, d], self.beside)
                store = pltpu.make_async_copy(src, mine, self.os.at[k])
                store.start()
                self.stores.append(store)

    def relay(self, k):
        for d in range(1, self.nz):
            block = self.slot(k, self.at(d), self.ic)
            self.arrived(block, self.zr.at[k, d])
            self.push(block, block, self.cs.at[k, d], self.cr.at[k, d], self.beside)

    def end(self):
        for k in range(self.count):
            for d in range(self.nz):
                self.arrived(self.slot(k, self.at(d), 1 - self.ic), self.cr.at[k, d])
        for store in self.stores:
            store.wait()
        self.finish()


def exact(a, b, dims):
    return lax.dot_general(
        a, b, (dims, ((), ())), precision=lax.Precision.HIGHEST, preferred_element_type=F32
    )


def picker(width):
    row = lax.broadcasted_iota(jnp.int32, (8, width), 0)
    part = lax.broadcasted_iota(jnp.int32, (8, width), 1) // HD
    return jnp.where(row == part, 1.0, 0.0).astype(F32)


def row_sums(first, second):
    both = jnp.concatenate([first, second], axis=1)
    return exact(picker(2 * HD), both, ((1,), (1,)))


def spread(sums, which):
    row = lax.broadcasted_iota(jnp.int32, (8, HD), 0)
    one = jnp.where(row == which, 1.0, 0.0).astype(F32)
    return exact(sums, one, ((0,), (0,)))


def softmax_rows(query, key, length):
    count = query.shape[0]
    row = lax.broadcasted_iota(jnp.int32, (count, count), 0)
    col = lax.broadcasted_iota(jnp.int32, (count, count), 1)
    scores = mm_nt(query, key) * (1.0 / math.sqrt(HD))
    scores = jnp.where((col <= row) & (col < length), scores, NEGATIVE)
    exponent = jnp.exp(scores - jnp.max(scores, axis=-1, keepdims=True))
    return exponent / jnp.sum(exponent, axis=-1, keepdims=True)


def load_all(pairs, sems):
    copies = []
    for n, (src, dst) in enumerate(pairs):
        copy = pltpu.make_async_copy(src, dst, sems.at[n])
        copy.start()
        copies.append(copy)
    return copies


def attention_back(branch, wide, wo, wqkv, saved, gains, tables, seq_lengths):
    nz = lax.axis_size("z")
    piece, width = branch.shape
    rows = 4 * piece
    k = Kernel()
    Gather.setup(k, "ball", branch, nz)
    Outlet.setup(k, "wide", wide, nz)
    Scatter.setup(k, "rs", piece, width, nz)
    Total.setup(k, "tot", (nz, 8, rows), ("core", "tp", "z"))
    k.inp("wo", wo)
    k.inp("wqkv", wqkv)
    names = ("q", "k", "v", "nq", "nk", "qs", "ks")
    for name, array in zip(names, saved):
        k.inp(name, array)
        k.mem(name + "_m", array.shape, array.dtype)
    k.mem("wo_m", wo.shape, BF)
    k.mem("wqkv_m", wqkv.shape, BF)
    k.sem("ld", len(names) + 2)
    k.inp("gains", gains, pltpu.VMEM)
    k.inp("tables", tables, pltpu.VMEM)
    k.inp("lens", seq_lengths, pltpu.SMEM)
    k.mem("wqk", (nz, 2, rows, HD), F32)
    k.mem("low_m", (nz, rows, 3 * HD), BF)
    k.mem("dots", (nz, 8, rows), F32)
    k.sem("st", 2, nz)
    k.out("grad", (piece, width), F32, pltpu.VMEM)
    k.out("norms", (2, HD), F32, pltpu.VMEM)
    k.out("low", (nz, rows, 3 * HD), BF)
    k.out("branch_all", (nz, rows, width), BF)

    def body(r):
        greet(partners_of(("z", "y", "tp", "core")))
        gather, outlet_flow = Gather(r, "ball", nz), Outlet(r, "wide", len(wide), nz)
        scatter, total_flow = Scatter(r, "rs", nz, r.grad), Total(r, "tot")
        gather.start()
        for n in range(len(wide)):
            outlet_flow.start(n)
        loads = load_all(
            [(getattr(r, n), getattr(r, n + "_m")) for n in ("wo", "wqkv", *names)], r.ld
        )
        scale = 1.0 / math.sqrt(HD)
        cosine, sine = r.tables[0], r.tables[1]
        gather.advance(1)
        for copy in loads:
            copy.wait()
        stores = []
        r.norms[...] = jnp.zeros_like(r.norms)

        def save(n, src, dst, d):
            copy = pltpu.make_async_copy(src, dst, r.st.at[n, d])
            copy.start()
            stores.append(copy)

        def compute(z):
            grad_low = mm(r.ball[z], r.wo_m[...]).astype(BF)
            query, key, value = r.q_m[z], r.k_m[z], r.v_m[z]
            probability = softmax_rows(query, key, r.lens[z])
            grad_prob = mm_nt(grad_low, value)
            row_dots = jnp.sum(probability * grad_prob, axis=-1, keepdims=True)
            grad_scores = (probability * (grad_prob - row_dots)).astype(BF)
            grad_q = rotate_back(mm(grad_scores, key) * scale, cosine, sine)
            grad_k = rotate_back(mm_tn(grad_scores, query) * scale, cosine, sine)
            grad_v = mm_tn(probability.astype(BF), grad_low)
            r.low_m[z, :, 2 * HD :] = grad_v.astype(BF)
            nq, nk = r.nq_m[z], r.nk_m[z]
            r.norms[0:1] += jnp.sum(grad_q * nq, axis=0, keepdims=True)
            r.norms[1:2] += jnp.sum(grad_k * nk, axis=0, keepdims=True)
            wq, wk = grad_q * r.gains[0:1], grad_k * r.gains[1:2]
            r.wqk[z, 0] = wq
            r.wqk[z, 1] = wk
            r.dots[z] = row_sums(wq * nq, wk * nk)

        for d in range(nz):
            if d + 2 <= nz:
                gather.advance(d + 2)
            gather.ready(d)
            z = gather.at(d)
            save(0, r.ball.at[z], r.branch_all.at[z], d)
            compute(z)
            if d == nz - 2:
                outlet_flow.combine(0)
        total_flow.send("core", r.dots[...])
        value = total_flow.receive()
        total_flow.send("tp", value)
        value = total_flow.receive()
        total_flow.send("z", value)
        for n in range(1, len(wide)):
            outlet_flow.combine(n)
        r.dots[...] = total_flow.receive()
        order = list(range(nz - 1, -1, -1))
        for n, d in enumerate(order):
            z = gather.at(d)
            sums = r.dots[z] * (1.0 / width)
            for j, (normed, factor) in enumerate(((r.nq_m, r.qs_m), (r.nk_m, r.ks_m))):
                low = factor[z] * (r.wqk[z, j] - normed[z] * spread(sums, j))
                r.low_m[z, :, j * HD : (j + 1) * HD] = low.astype(BF)
            save(1, r.low_m.at[z], r.low.at[z], d)
            r.rs_p[d] = mm_nt(r.low_m[z], r.wqkv_m[...]).astype(BF)
            scatter.begin(d)
            if n:
                scatter.cross(order[n - 1])
            if n > 1:
                scatter.leave(order[n - 2])
        scatter.cross(0)
        if nz > 1:
            scatter.leave(order[-2])
        scatter.leave(0)
        for n in range(len(wide)):
            outlet_flow.relay(n)
        scatter.end()
        outlet_flow.end()
        for flow in (gather, scatter, total_flow):
            flow.finish()
        for copy in stores:
            copy.wait()

    return k.run(7, body, 60)


def last_exchange(grads, grad_rows, stream_rows, terms):
    nz = lax.axis_size("z")
    axes = tuple(a for a in ("core", "tp", "y", "z") if lax.axis_size(a) > 1)
    piece, width = grad_rows.shape
    size = terms.shape[0]
    padded = jnp.pad(terms, (0, -size % 1024)).reshape(-1, 128)
    k = Kernel()
    Outlet.setup(k, "g", grads, nz)
    Total.setup(k, "tot", padded.shape, axes)
    k.inp("terms", padded, pltpu.VMEM)
    k.out("terms_out", padded.shape, F32, pltpu.VMEM)
    for name, array in (("grad", grad_rows), ("stream", stream_rows)):
        k.inp(name, array)
        k.out(name + "_out", (2, piece, width), array.dtype)
        k.mem(name + "_m", (piece, width), array.dtype)
    k.sem("xs", 2)
    k.sem("xr", 2)
    k.sem("ls", 2)
    k.sem("ss", 2)

    def body(r):
        greet(partners_of(("z", "y", "tp", "core")))
        flow, own, total_flow = Outlet(r, "g", len(grads), nz), Flow(), Total(r, "tot")
        for n in range(len(grads)):
            flow.start(n)
        loads = load_all([(r.grad, r.grad_m), (r.stream, r.stream_m)], r.ls)
        value = r.terms[...]
        total_flow.send(axes[0], value)
        for n, name in enumerate(("grad", "stream")):
            out = getattr(r, name + "_out")
            own.push(getattr(r, name), out.at[own.it], r.xs.at[n], r.xr.at[n], own.across)
        value = total_flow.receive()
        for load in loads:
            load.wait()
        stores = []
        for n, name in enumerate(("grad", "stream")):
            src, dst = getattr(r, name + "_m"), getattr(r, name + "_out").at[own.it]
            stores.append(pltpu.make_async_copy(src, dst, r.ss.at[n]))
            stores[-1].start()
        for n, axis in enumerate(axes[1:]):
            total_flow.send(axis, value)
            if n < len(grads):
                flow.combine(n)
            value = total_flow.receive()
        for n in range(len(axes) - 1, len(grads)):
            flow.combine(n)
        r.terms_out[...] = value
        for n in range(len(grads)):
            flow.relay(n)
        flow.end()
        for n, name in enumerate(("grad", "stream")):
            own.arrived(getattr(r, name + "_out").at[1 - own.it], r.xr.at[n])
        own.finish()
        total_flow.finish()
        for store in stores:
            store.wait()

    got = k.run(8, body, 32)
    return (
        [got[f"g_o{n}"].astype(F32) for n in range(len(grads))],
        got["grad_out"].reshape(-1, width),
        got["stream_out"].reshape(-1, width),
        got["terms_out"].reshape(-1)[:size],
    )


def attention_front(token_rows, weights, gains, tables, seq_lengths):
    nz = lax.axis_size("z")
    own_rows, width = token_rows.shape
    piece, rows = own_rows // 2, own_rows * 2
    w_rows = weights[0].shape[0]
    count = len(weights)
    parts = [w.shape[1] // (2 * nz) for w in weights]
    k = Kernel()
    Scatter.setup(k, "rs", piece, width, nz)
    Total.setup(k, "tot", (nz, 8, rows), ("core", "tp", "z"))
    k.inp("tok", token_rows)
    for n, weight in enumerate(weights):
        k.inp(f"w{n}", weight)
    k.inp("gains", gains, pltpu.VMEM)
    k.inp("tables", tables, pltpu.VMEM)
    k.inp("lens", seq_lengths, pltpu.SMEM)
    k.mem("tall", (nz, rows, width), BF)
    k.mem("qkv", (nz, 2, w_rows, 3 * HD), BF)
    k.mem("wo", (nz, 2, w_rows, parts[3]), BF)
    for n in range(4, count):
        k.mem(f"b{n}", (w_rows, parts[n]), BF)
        k.out(f"o{n}", (nz, 2, w_rows, parts[n]), BF)
    k.mem("raw", (nz, rows, 3 * HD), F32)
    k.mem("dots", (nz, 8, rows), F32)
    saved = (("q", BF), ("k", BF), ("v", BF), ("nq", F32), ("nk", F32), ("qs", F32), ("ks", F32), ("att", BF))
    for name, kind in saved:
        k.mem(name + "_m", (nz, rows, HD), kind)
        k.out(name, (nz, rows, HD), kind)
    k.out("branch", (piece, width), F32, pltpu.VMEM)
    k.out("tokens", (nz, rows, width), BF)
    k.out("qkv_out", (nz, 2, w_rows, 3 * HD), BF)
    k.out("wo_out", (nz, 2, w_rows, parts[3]), BF)
    k.sem("tl")
    for s in ("tzs", "tzr", "txs", "txr"):
        k.sem(s, nz)
    k.sem("tcs", nz, 2)
    k.sem("tcr", nz, 2)
    k.sem("wl", 2, count)
    for s in ("wzs", "wzr", "wys", "wyr"):
        k.sem(s, count, nz)
    k.sem("st", len(saved) + 1, nz)
    k.sem("sw", 2)

    def body(r):
        greet(partners_of(("z", "y", "tp", "core")))
        flow = Flow()
        iz, iy, ic, it = flow.iz, flow.iy, flow.ic, flow.it
        scatter, total_flow = Scatter(r, "rs", nz, r.branch), Total(r, "tot")

        def block(z, core, tp):
            return stripe(r.tall, z, core, tp, piece)

        def pair(z, core):
            start = pl.multiple_of(core * own_rows, own_rows)
            return r.tall.at[z, pl.ds(start, own_rows)]

        tok_half = r.tok.at[pl.ds(pl.multiple_of(it * piece, piece), piece)]
        for d in range(1, nz):
            flow.push(tok_half, block(iz, ic, it), r.tzs.at[d], r.tzr.at[d], {"z": flow.at(d)})
        flow.push(r.tok, pair(iz, ic), r.tcs.at[0, 0], r.tcr.at[0, 0], flow.beside)
        tok_load = pltpu.make_async_copy(r.tok, pair(iz, ic), r.tl)
        tok_load.start()
        loads = {}

        def landing(n, z, y):
            if n < 3:
                return r.qkv.at[z, y, :, n * HD : (n + 1) * HD]
            return r.wo.at[z, y] if n == 3 else getattr(r, f"o{n}").at[z, y]

        def bring(n):
            weight = getattr(r, f"w{n}")
            own = columns(weight, iz * 2 + ic, parts[n])
            for d in range(nz - 1, 0, -1):
                other = flow.at(d)
                flow.push(
                    columns(weight, other * 2 + ic, parts[n]),
                    landing(n, iz, iy),
                    r.wzs.at[n, d],
                    r.wzr.at[n, d],
                    {"z": other},
                )
            flow.push(own, landing(n, iz, iy), r.wys.at[n, 0], r.wyr.at[n, 0], flow.behind)
            dst = landing(n, iz, iy) if n < 4 else getattr(r, f"b{n}")
            loads[n] = pltpu.make_async_copy(own, dst, r.wl.at[0, n])
            loads[n].start()

        def forward(n):
            for d in range(1, nz):
                here = landing(n, flow.at(d), iy)
                flow.arrived(here, r.wzr.at[n, d])
                flow.push(here, here, r.wys.at[n, d], r.wyr.at[n, d], flow.behind)

        def complete(n):
            for d in range(nz):
                flow.arrived(landing(n, flow.at(d), 1 - iy), r.wyr.at[n, d])

        for n in range(min(5, count)):
            bring(n)
        for d in range(1, nz):
            here = block(flow.at(d), ic, it)
            flow.arrived(here, r.tzr.at[d])
            flow.push(here, here, r.txs.at[d], r.txr.at[d], flow.across)
            flow.push(here, here, r.tcs.at[d, 0], r.tcr.at[d, 0], flow.beside)
        for n in range(3):
            forward(n)
        for d in range(1, nz):
            here = block(flow.at(d), ic, 1 - it)
            flow.arrived(here, r.txr.at[d])
            flow.push(here, here, r.tcs.at[d, 1], r.tcr.at[d, 1], flow.beside)
        stores = []

        def save(n, src, dst, d):
            copy = pltpu.make_async_copy(src, dst, r.st.at[n, d])
            copy.start()
            stores.append(copy)

        for n in range(4):
            loads[n].wait()
        for n in range(3):
            complete(n)
        tok_load.wait()
        for d in range(nz):
            z = flow.at(d)
            if d == 0:
                flow.arrived(pair(iz, 1 - ic), r.tcr.at[0, 0])
            else:
                for half in range(2):
                    side = it if half == 0 else 1 - it
                    flow.arrived(block(z, 1 - ic, side), r.tcr.at[d, half])
            save(0, r.tall.at[z], r.tokens.at[z], d)
            raw = mm(r.tall[z], r.qkv[...].reshape(2 * nz * w_rows, 3 * HD))
            r.raw[z] = raw
            query, key = raw[:, :HD], raw[:, HD : 2 * HD]
            r.dots[z] = row_sums(query * query, key * key)
        total_flow.send("core", r.dots[...])
        forward(3)
        value = total_flow.receive()
        total_flow.send("tp", value)
        value = total_flow.receive()
        total_flow.send("z", value)
        for n in range(5, count):
            bring(n)
        for n in range(4, count):
            loads[n].wait()
            copy = pltpu.make_async_copy(getattr(r, f"b{n}"), landing(n, iz, iy), r.wl.at[1, n])
            copy.start()
            stores.append(copy)
        complete(3)
        for n, (src, dst) in enumerate(((r.qkv, r.qkv_out), (r.wo, r.wo_out))):
            copy = pltpu.make_async_copy(src, dst, r.sw.at[n])
            copy.start()
            stores.append(copy)
        r.dots[...] = lax.rsqrt(total_flow.receive() * (1.0 / width) + EPSILON)
        cosine, sine = r.tables[0], r.tables[1]
        order = list(range(nz - 1, -1, -1))
        for n, d in enumerate(order):
            z = flow.at(d)
            sums = r.dots[z]
            r.qs_m[z] = spread(sums, 0)
            r.ks_m[z] = spread(sums, 1)
            r.nq_m[z] = r.raw[z, :, :HD] * r.qs_m[z]
            r.nk_m[z] = r.raw[z, :, HD : 2 * HD] * r.ks_m[z]
            query = rotate(r.nq_m[z] * r.gains[0:1], cosine, sine).astype(BF)
            key = rotate(r.nk_m[z] * r.gains[1:2], cosine, sine).astype(BF)
            value = r.raw[z, :, 2 * HD :].astype(BF)
            r.q_m[z] = query
            r.k_m[z] = key
            r.v_m[z] = value
            probability = softmax_rows(query, key, r.lens[z]).astype(BF)
            r.att_m[z] = mm(probability, value).astype(BF)
            for m, (name, _) in enumerate(saved):
                save(m + 1, getattr(r, name + "_m").at[z], getattr(r, name).at[z], d)
            wo = r.wo[...].reshape(2 * nz * w_rows, parts[3])
            r.rs_p[d] = mm_nt(r.att_m[z], wo).astype(BF)
            scatter.begin(d)
            if n:
                scatter.cross(order[n - 1])
            if n > 1:
                scatter.leave(order[n - 2])
        scatter.cross(0)
        scatter.leave(order[-2])
        scatter.leave(0)
        for n in range(4, count):
            forward(n)
        scatter.end()
        for n in range(4, count):
            complete(n)
        for f in (flow, scatter, total_flow):
            f.finish()
        for copy in stores:
            copy.wait()

    return k.run(9, body, 60)


def local(
    tokens,
    lengths,
    weight_query,
    weight_key,
    weight_value,
    weight_out,
    weight_gate,
    weight_up,
    weight_down,
    post_attention,
    post_feedforward,
    query_norm,
    key_norm,
    cotangent,
):
    nz, ny, nch, ntp = (lax.axis_size(a) for a in ("z", "y", "ch", "tp"))
    iz, iy, ich, icore, itp = (lax.axis_index(a) for a in AXES)
    token_rows = tokens[0]
    own_rows, width = token_rows.shape
    piece = own_rows // ntp
    seq_rows = own_rows * 2
    total_rows = seq_rows * nz
    scale_factor = 1.0 / math.sqrt(HD)
    own_head = iz * 2 + icore
    qn = lax.dynamic_slice_in_dim(query_norm, own_head * HD, HD)
    kn = lax.dynamic_slice_in_dim(key_norm, own_head * HD, HD)
    seq_lengths = lax.dynamic_index_in_dim(lengths.reshape(nz, ny), iy, 1, keepdims=False)
    positions = ich * seq_rows + jnp.arange(seq_rows, dtype=jnp.int32)
    key_positions = jnp.arange(seq_rows * nch, dtype=jnp.int32)
    cosine, sine_table = rope_tables(positions)
    allowed = (key_positions[None, None, :] <= positions[None, :, None]) & (
        key_positions[None, None, :] < seq_lengths[:, None, None]
    )
    my_tokens = lax.dynamic_slice_in_dim(token_rows, itp * piece, piece, 0)
    my_cot = lax.dynamic_slice_in_dim(cotangent[0], itp * piece, piece, 0)
    my_pos = (ich * 2 + icore) * own_rows + itp * piece + jnp.arange(piece, dtype=jnp.int32)
    my_valid = (my_pos < lengths[iz * ny + iy]).astype(F32)[:, None]

    weights = (
        weight_query,
        weight_key,
        weight_value,
        weight_out,
        weight_gate,
        weight_up,
        weight_down,
    )
    fused = nch == 1
    by_seq = lambda a: a.reshape(nz, seq_rows, HD)
    gains, tables = jnp.stack([qn, kn]), jnp.stack([cosine, sine_table])
    if fused:
        front = attention_front(token_rows, weights, gains, tables, seq_lengths)
        branch_sum = front["branch"]
        wg, wu, wd = (front[f"o{n}"].reshape(width, -1) for n in (4, 5, 6))
    else:
        tokens_all, (wq, wk, wv, wo, wg, wu, wd) = intake(token_rows, weights)
        query_raw = mm(tokens_all, wq)
        key_raw = mm(tokens_all, wk)
        value_raw = mm(tokens_all, wv)
        squares = head_total(
            jnp.stack([jnp.sum(query_raw * query_raw, axis=-1), jnp.sum(key_raw * key_raw, axis=-1)])
        )
        scales = lax.rsqrt(squares / width + EPSILON)
        query_scale = scales[0][:, None]
        key_scale = scales[1][:, None]
        queries = rotate(by_seq(query_raw * query_scale * qn), cosine, sine_table).astype(BF)
        keys = rotate(by_seq(key_raw * key_scale * kn), cosine, sine_table).astype(BF)
        values = by_seq(value_raw).astype(BF)
        if nch > 1:
            keys_full = lax.all_gather(keys, "ch", axis=1, tiled=True)
            values_full = lax.all_gather(values, "ch", axis=1, tiled=True)
        else:
            keys_full, values_full = keys, values
        scores = (
            jnp.einsum("btd,bsd->bts", queries, keys_full, preferred_element_type=F32) * scale_factor
        )
        scores = jnp.where(allowed, scores, NEGATIVE)
        exponent = jnp.exp(scores - jnp.max(scores, axis=-1, keepdims=True))
        probability = exponent / jnp.sum(exponent, axis=-1, keepdims=True)
        probability_low = probability.astype(BF)
        attended = jnp.einsum("bts,bsd->btd", probability_low, values_full, preferred_element_type=F32)
        attended_low = attended.reshape(total_rows, HD).astype(BF)
        branch_sum = scatter_rows(mm_nt(attended_low, wo))
    attn_scale = lax.rsqrt(jnp.mean(branch_sum * branch_sum, axis=-1, keepdims=True) + EPSILON)
    attn_normed = branch_sum * attn_scale
    attention_branch = attn_normed * post_attention
    residual = my_tokens.astype(F32) + attention_branch
    residual_all = gather_rows(residual.astype(BF))
    gate_value = mm(residual_all, wg)
    up_value = mm(residual_all, wu)
    sigmoid_gate = jax.nn.sigmoid(gate_value)
    silu_gate = gate_value * sigmoid_gate
    mixed_low = (silu_gate * up_value).astype(BF)
    down_sum = scatter_rows(mm_nt(mixed_low, wd))
    ffn_scale = lax.rsqrt(jnp.mean(down_sum * down_sum, axis=-1, keepdims=True) + EPSILON)
    ffn_normed = down_sum * ffn_scale
    feedforward_branch = ffn_normed * post_feedforward
    stream = residual + feedforward_branch
    stat_terms = jnp.stack(
        [
            jnp.sum(my_valid * stream * stream),
            jnp.sum(my_valid * attention_branch * attention_branch),
            jnp.sum(my_valid * feedforward_branch * feedforward_branch),
        ]
    )
    grad_stream = my_cot * my_valid
    grad_post_ff = jnp.sum(grad_stream * ffn_normed, axis=0)
    scaled = grad_stream * post_feedforward
    grad_down_sum = ffn_scale * (
        scaled - ffn_normed * jnp.mean(scaled * ffn_normed, axis=-1, keepdims=True)
    )
    down_all = gather_rows(grad_down_sum.astype(BF))
    grad_mixed = mm(down_all, wd)
    gate_low = (
        grad_mixed * up_value * sigmoid_gate * (1.0 + gate_value * (1.0 - sigmoid_gate))
    ).astype(BF)
    up_low = (grad_mixed * silu_gate).astype(BF)
    grad_wg = mm_tn(residual_all, gate_low)
    grad_wu = mm_tn(residual_all, up_low)
    grad_wd = mm_tn(down_all, mixed_low)
    grad_residual = grad_stream + scatter_rows(mm_nt(gate_low, wg) + mm_nt(up_low, wu))
    grad_post_attn = jnp.sum(grad_residual * attn_normed, axis=0)
    scaled_attn = grad_residual * post_attention
    grad_branch = attn_scale * (
        scaled_attn - attn_normed * jnp.mean(scaled_attn * attn_normed, axis=-1, keepdims=True)
    )
    if fused:
        saved = tuple(front[n] for n in ("q", "k", "v", "nq", "nk", "qs", "ks"))
        wqkv, wo = front["qkv_out"].reshape(width, -1), front["wo_out"].reshape(width, -1)
        back = attention_back(
            grad_branch.astype(BF),
            (grad_wd, grad_wg, grad_wu),
            wo,
            wqkv,
            saved,
            gains,
            tables,
            seq_lengths,
        )
        grad_qkv = mm_tn(front["tokens"].reshape(total_rows, -1), back["low"].reshape(total_rows, -1))
        grad_wo = mm_tn(
            back["branch_all"].reshape(total_rows, -1), front["att"].reshape(total_rows, -1)
        )
        grad_rows = grad_residual + back["grad"]
        grad_qnorm, grad_knorm = back["norms"][0], back["norms"][1]
    else:
        branch_all = gather_rows(grad_branch.astype(BF))
        grad_att_low = mm(branch_all, wo).astype(BF)
        grad_wo = mm_tn(branch_all, attended_low)
        grad_att = by_seq(grad_att_low)
        grad_prob = jnp.einsum("btd,bsd->bts", grad_att, values_full, preferred_element_type=F32)
        row_dots = jnp.sum(probability * grad_prob, axis=-1, keepdims=True)
        grad_scores = (probability * (grad_prob - row_dots)).astype(BF)
        grad_queries = (
            jnp.einsum("bts,bsd->btd", grad_scores, keys_full, preferred_element_type=F32)
            * scale_factor
        )
        grad_keys = (
            jnp.einsum("bts,btd->bsd", grad_scores, queries, preferred_element_type=F32) * scale_factor
        )
        grad_values = jnp.einsum("bts,btd->bsd", probability_low, grad_att, preferred_element_type=F32)
        if nch > 1:
            grad_keys, grad_values = (
                lax.psum_scatter(g.astype(BF), "ch", scatter_dimension=1, tiled=True).astype(F32)
                for g in (grad_keys, grad_values)
            )
        value_grad_low = grad_values.reshape(total_rows, HD).astype(BF)
        grad_q_normed = rotate_back(grad_queries, cosine, sine_table).reshape(total_rows, HD)
        grad_k_normed = rotate_back(grad_keys, cosine, sine_table).reshape(total_rows, HD)
        query_weighted = grad_q_normed * qn
        key_weighted = grad_k_normed * kn
        dots = head_total(
            jnp.stack(
                [
                    jnp.sum(query_weighted * query_raw, axis=-1),
                    jnp.sum(key_weighted * key_raw, axis=-1),
                ]
            )
        )
        query_grad_low = (
            query_scale * (query_weighted - query_raw * query_scale**2 * (dots[0] / width)[:, None])
        ).astype(BF)
        key_grad_low = (
            key_scale * (key_weighted - key_raw * key_scale**2 * (dots[1] / width)[:, None])
        ).astype(BF)
        grad_qnorm = jnp.sum(grad_q_normed * query_raw * query_scale, axis=0)
        grad_knorm = jnp.sum(grad_k_normed * key_raw * key_scale, axis=0)
        grad_wq = mm_tn(tokens_all, query_grad_low)
        grad_wk = mm_tn(tokens_all, key_grad_low)
        grad_wv = mm_tn(tokens_all, value_grad_low)
        grad_rows = grad_residual + scatter_rows(
            mm_nt(query_grad_low, wq) + mm_nt(key_grad_low, wk) + mm_nt(value_grad_low, wv)
        )
    slot = itp * (width // ntp) + own_head * HD
    zero_row = jnp.zeros((width,), F32)
    terms = jnp.concatenate(
        [
            grad_post_attn,
            grad_post_ff,
            lax.dynamic_update_slice_in_dim(zero_row, grad_qnorm, slot, 0),
            lax.dynamic_update_slice_in_dim(zero_row, grad_knorm, slot, 0),
            stat_terms,
        ]
    )
    if fused:
        narrow, grad_input, output, summed = last_exchange(
            (*(grad_qkv[:, n * HD : (n + 1) * HD] for n in range(3)), grad_wo),
            grad_rows,
            stream.astype(BF),
            terms,
        )
        weight_grads = narrow + [back[f"wide_o{n}"].astype(F32) for n in (1, 2, 0)]
    else:
        weight_grads = outlet((grad_wq, grad_wk, grad_wv, grad_wo, grad_wg, grad_wu, grad_wd))
        grad_input = lax.all_gather(grad_rows, "tp", axis=0, tiled=True)
        output = lax.all_gather(stream.astype(BF), "tp", axis=0, tiled=True)
        summed = all_total(terms)
    half = width // ntp
    qn_sum = lax.dynamic_slice_in_dim(summed, 2 * width + itp * half, half)
    kn_sum = lax.dynamic_slice_in_dim(summed, 3 * width + itp * half, half)
    token_count = jnp.sum(lengths.astype(F32))
    root_means = jnp.sqrt(summed[4 * width :] / (token_count * width))
    return (
        output[None],
        grad_input[None],
        *weight_grads,
        summed[:width],
        summed[width : 2 * width],
        qn_sum,
        kn_sum,
        root_means,
    )


def solution(mesh):
    n_fsdp, n_ctx, n_tp = (mesh.shape[a] for a in ("fsdp", "ctx", "tp"))
    fine = Mesh(mesh.devices.reshape(n_fsdp // 2, 2, n_ctx // 2, 2, n_tp), AXES)
    fsdp, ctx = ("z", "y"), ("ch", "core")
    rows = P(fsdp, ctx, None)
    weight = P(fsdp, "tp")
    return jax.shard_map(
        local,
        mesh=fine,
        in_specs=(rows, P(), *([weight] * 7), P(), P(), P("tp"), P("tp"), rows),
        out_specs=(rows, rows, *([weight] * 7), P(), P(), P("tp"), P("tp"), P()),
        check_vma=False,
    )
```

```python
import functools
import math
import types

import jax
import jax.numpy as jnp
from jax import lax
from jax.experimental import pallas as pl
from jax.experimental.pallas import tpu as pltpu
from jax.sharding import Mesh, PartitionSpec as P

HD = 128
EPSILON = 1e-06
ROPE_BASE = 500000.0
NEGATIVE = -1e30
AXES = ("z", "y", "ch", "core", "tp")
BF = jnp.bfloat16
F32 = jnp.float32


def rope_tables(positions):
    half_size = HD // 2
    exponent = jnp.arange(half_size, dtype=F32) * (2.0 / HD)
    frequency = jnp.power(ROPE_BASE, -exponent)
    angles = positions.astype(F32)[:, None] * frequency[None, :]
    cosine = jnp.cos(angles)
    sine_table = jnp.sin(angles)
    return (
        jnp.concatenate([cosine, cosine], axis=-1),
        jnp.concatenate([sine_table, sine_table], axis=-1),
    )


def rotate(values, cosine, sine_table):
    half_size = HD // 2
    turned = jnp.concatenate([-values[..., half_size:], values[..., :half_size]], axis=-1)
    return values * cosine + turned * sine_table


def rotate_back(grads_in, cosine, sine_table):
    half_size = HD // 2
    sin_part = grads_in * sine_table
    return grads_in * cosine + jnp.concatenate(
        [sin_part[..., half_size:], -sin_part[..., :half_size]], axis=-1
    )


def dot(former, latter, dims):
    return lax.dot_general(former, latter, (dims, ((), ())), preferred_element_type=F32)


def mm(a, b):
    return dot(a, b, ((1,), (0,)))


def mm_nt(a, b):
    return dot(a, b, ((1,), (1,)))


def mm_tn(a, b):
    return dot(a, b, ((0,), (0,)))


MESH = pl.DeviceIdType.MESH


def flip(axis, bits):
    me = lax.axis_index(axis)
    result, weight = me, 1
    while weight <= bits:
        if (bits // weight) % 2:
            result = result + weight * (1 - 2 * lax.rem(me // weight, 2))
        weight *= 2
    return result


def greet(partners):
    barrier = pltpu.get_barrier_semaphore()
    for partner in partners:
        pl.semaphore_signal(barrier, inc=1, device_id=partner, device_id_type=MESH)
    pl.semaphore_wait(barrier, len(partners))


def remote(src, dst, send_sem, recv_sem, partner):
    return pltpu.make_async_remote_copy(
        src_ref=src,
        dst_ref=dst,
        send_sem=send_sem,
        recv_sem=recv_sem,
        device_id=partner,
        device_id_type=MESH,
    )


def partners_of(axes):
    found = []
    for axis in axes:
        for bits in range(1, lax.axis_size(axis)):
            found.append({axis: flip(axis, bits)})
    return found


def call(kernel, identity, out_shape, in_spaces, out_spaces, scratch, limit, *operands):
    return pl.pallas_call(
        kernel,
        out_shape=out_shape,
        in_specs=[pl.BlockSpec(memory_space=s) for s in in_spaces],
        out_specs=jax.tree.map(lambda s: pl.BlockSpec(memory_space=s), out_spaces),
        scratch_shapes=scratch,
        compiler_params=pltpu.CompilerParams(
            collective_id=identity, has_side_effects=True, vmem_limit_bytes=limit * 2**20
        ),
    )(*operands)


DMA = pltpu.SemaphoreType.DMA


def gather_kernel(nz, x_ref, out_ref, own_sem, zs, zr, xs, xr, cs, cr):
    iz, ic, it = (lax.axis_index(a) for a in ("z", "core", "tp"))
    greet(partners_of(("z", "tp", "core")))
    sends = []

    def push(src, where, send_sem, recv_sem, partner):
        copy = remote(src, out_ref.at[where], send_sem, recv_sem, partner)
        copy.start()
        sends.append(copy)

    across, beside = {"tp": 1 - it}, {"core": 1 - ic}
    own = (iz, ic, it)
    for d in range(1, nz):
        push(x_ref, own, zs.at[d], zr.at[d], {"z": flip("z", d)})
    push(x_ref, own, xs.at[0], xr.at[0], across)
    push(x_ref, own, cs.at[0, 0], cr.at[0, 0], beside)
    local_copy = pltpu.make_async_copy(x_ref, out_ref.at[own], own_sem)
    local_copy.start()

    def await_at(where, sem):
        remote(out_ref.at[where], out_ref.at[where], sem, sem, across).wait_recv()

    def from_across(d):
        where = (flip("z", d), ic, 1 - it)
        await_at(where, xr.at[d])
        push(out_ref.at[where], where, cs.at[d, 1], cr.at[d, 1], beside)

    for d in range(1, nz):
        where = (flip("z", d), ic, it)
        await_at(where, zr.at[d])
        push(out_ref.at[where], where, xs.at[d], xr.at[d], across)
        push(out_ref.at[where], where, cs.at[d, 0], cr.at[d, 0], beside)
        from_across(d - 1)
    from_across(nz - 1)
    for d in range(nz):
        for half in range(2):
            side = it if half == 0 else 1 - it
            await_at((flip("z", d), 1 - ic, side), cr.at[d, half])
    for copy in sends:
        copy.wait_send()
    local_copy.wait()


def gather_rows(rows):
    piece, width = rows.shape
    nz = lax.axis_size("z")
    out = call(
        functools.partial(gather_kernel, nz),
        1,
        jax.ShapeDtypeStruct((nz, 2, 2, piece, width), rows.dtype),
        [pl.ANY],
        pl.ANY,
        [DMA, DMA((nz,)), DMA((nz,)), DMA((nz,)), DMA((nz,)), DMA((nz, 2)), DMA((nz, 2))],
        16,
        rows,
    )
    return out.reshape(-1, width)


def scatter_kernel(
    nz, p_ref, out_ref, own, cin, xout, xin, zout, zin, ls, cs, cr, xs, xr, zs, zr
):
    iz, ic, it = (lax.axis_index(a) for a in ("z", "core", "tp"))
    greet(partners_of(("z", "tp", "core")))
    across, beside = {"tp": 1 - it}, {"core": 1 - ic}
    order = list(range(nz - 1, -1, -1))
    loads, besides, acrosses, zeds = {}, {}, {}, {}
    for d in order:
        target = flip("z", d) if d else iz
        besides[d] = remote(p_ref.at[target, 1 - ic], cin.at[d], cs.at[d], cr.at[d], beside)
        besides[d].start()
        loads[d] = pltpu.make_async_copy(p_ref.at[target, ic], own.at[d], ls.at[d])
        loads[d].start()

    def add(d, side):
        return own[d, side].astype(F32) + cin[d, side].astype(F32)

    def after_across(d):
        acrosses[d].wait_recv()
        total = add(d, it) + xin[d].astype(F32)
        if d == 0:
            out_ref[...] = total
        else:
            zout[d] = total.astype(BF)
            zeds[d] = remote(zout.at[d], zin.at[d], zs.at[d], zr.at[d], {"z": flip("z", d)})
            zeds[d].start()

    for n, d in enumerate(order):
        loads[d].wait()
        besides[d].wait_recv()
        xout[d] = add(d, 1 - it).astype(BF)
        acrosses[d] = remote(xout.at[d], xin.at[d], xs.at[d], xr.at[d], across)
        acrosses[d].start()
        if n:
            after_across(order[n - 1])
    after_across(0)
    for d in order[:-1]:
        zeds[d].wait_recv()
        out_ref[...] += zin[d].astype(F32)
    for group in (besides, acrosses, zeds):
        for copy in group.values():
            copy.wait_send()


def scatter_rows(partial):
    nz = lax.axis_size("z")
    width = partial.shape[1]
    part = partial.astype(BF).reshape(nz, 2, 2, -1, width)
    piece = part.shape[3]
    sems = [DMA((nz,)) for _ in range(7)]
    return call(
        functools.partial(scatter_kernel, nz),
        2,
        jax.ShapeDtypeStruct((piece, width), F32),
        [pl.ANY],
        pltpu.VMEM,
        [
            pltpu.VMEM((nz, 2, piece, width), BF),
            pltpu.VMEM((nz, 2, piece, width), BF),
            *[pltpu.VMEM((nz, piece, width), BF) for _ in range(4)],
            *sems,
        ],
        32,
        part,
    )


def total_kernel(axes, x_ref, out_ref, *scratch):
    greet(partners_of(axes))
    value = x_ref[...]
    sends = []
    for stage, axis in enumerate(axes):
        slots, send_sems, recv_sems = scratch[3 * stage : 3 * stage + 3]
        size = lax.axis_size(axis)
        me = lax.axis_index(axis)
        slots[me] = value
        copies = []
        for d in range(1, size):
            copy = remote(
                slots.at[me], slots.at[me], send_sems.at[d], recv_sems.at[d], {axis: flip(axis, d)}
            )
            copy.start()
            copies.append(copy)
        for copy in copies:
            copy.wait_recv()
        value = slots[0]
        for n in range(1, size):
            value = value + slots[n]
        sends += copies
    out_ref[...] = value
    for copy in sends:
        copy.wait_send()


def total(terms, axes, identity):
    axes = tuple(a for a in axes if lax.axis_size(a) > 1)
    scratch = []
    for axis in axes:
        size = lax.axis_size(axis)
        scratch += [pltpu.VMEM((size, *terms.shape), F32), DMA((size,)), DMA((size,))]
    return call(
        functools.partial(total_kernel, axes),
        identity,
        jax.ShapeDtypeStruct(terms.shape, F32),
        [pltpu.VMEM],
        pltpu.VMEM,
        scratch,
        16,
        terms,
    )


def head_total(terms):
    return total(terms.reshape(-1, 128), ("core", "tp", "z"), 3).reshape(terms.shape)


def all_total(terms):
    size = terms.shape[0]
    padded = jnp.pad(terms, (0, -size % 1024)).reshape(-1, 128)
    return total(padded, ("core", "tp", "y", "z", "ch"), 4).reshape(-1)[:size]


def columns(ref, slot, count):
    return ref.at[:, pl.ds(pl.multiple_of(slot * count, 128), count)]


def intake_kernel(nz, count, tok_ref, *refs):
    w_refs, refs = refs[:count], refs[count:]
    tok_out, refs = refs[0], refs[1:]
    o_refs, refs = refs[:count], refs[count:]
    tok_buf, refs = refs[0], refs[1:]
    bufs, refs = refs[:count], refs[count:]
    tl, tzs, tzr, txs, txr, tcs, tcr, wl, wzs, wzr, wys, wyr = refs
    iz, iy, ic, it = (lax.axis_index(a) for a in ("z", "y", "core", "tp"))
    across, beside, behind = {"tp": 1 - it}, {"core": 1 - ic}, {"y": 1 - iy}
    greet(partners_of(("z", "y", "tp", "core")))
    sends = []

    def push(src, dst, send_sem, recv_sem, partner):
        copy = remote(src, dst, send_sem, recv_sem, partner)
        copy.start()
        sends.append(copy)

    def arrived(ref, sem):
        remote(ref, ref, sem, sem, across).wait_recv()

    for d in range(1, nz):
        push(tok_ref.at[it], tok_out.at[iz, ic, it], tzs.at[d], tzr.at[d], {"z": flip("z", d)})
    push(tok_ref, tok_out.at[iz, ic], tcs.at[0, 0], tcr.at[0, 0], beside)
    tok_load = pltpu.make_async_copy(tok_ref, tok_buf, tl.at[0])
    tok_load.start()
    widths = [o.shape[-1] for o in o_refs]
    loads = []
    for k, (w, o) in enumerate(zip(w_refs, o_refs)):
        own = columns(w, iz * 2 + ic, widths[k])
        push(own, o.at[iz, iy], wys.at[k, 0], wyr.at[k, 0], behind)
        for d in range(1, nz):
            other = flip("z", d)
            push(
                columns(w, other * 2 + ic, widths[k]),
                o.at[iz, iy],
                wzs.at[k, d],
                wzr.at[k, d],
                {"z": other},
            )
        load = pltpu.make_async_copy(own, bufs[k], wl.at[k])
        load.start()
        loads.append(load)
    tok_load.wait()
    stores = [pltpu.make_async_copy(tok_buf, tok_out.at[iz, ic], tl.at[1])]
    stores[0].start()
    for d in range(1, nz):
        block = tok_out.at[flip("z", d), ic, it]
        arrived(block, tzr.at[d])
        push(block, block, txs.at[d], txr.at[d], across)
        push(block, block, tcs.at[d, 0], tcr.at[d, 0], beside)

    def forward(k):
        for d in range(1, nz):
            block = o_refs[k].at[flip("z", d), iy]
            arrived(block, wzr.at[k, d])
            push(block, block, wys.at[k, d], wyr.at[k, d], behind)

    first = min(3, count)
    for k in range(first):
        forward(k)
    for d in range(1, nz):
        block = tok_out.at[flip("z", d), ic, 1 - it]
        arrived(block, txr.at[d])
        push(block, block, tcs.at[d, 1], tcr.at[d, 1], beside)
    for k, load in enumerate(loads):
        load.wait()
        store = pltpu.make_async_copy(bufs[k], o_refs[k].at[iz, iy], wl.at[k])
        store.start()
        stores.append(store)
    for k in range(first, count):
        forward(k)
    arrived(tok_out.at[iz, 1 - ic], tcr.at[0, 0])
    for d in range(1, nz):
        for half in range(2):
            side = it if half == 0 else 1 - it
            arrived(tok_out.at[flip("z", d), 1 - ic, side], tcr.at[d, half])
    for k in range(count):
        for d in range(nz):
            source = flip("z", d) if d else iz
            arrived(o_refs[k].at[source, 1 - iy], wyr.at[k, d])
    for copy in sends:
        copy.wait_send()
    for store in stores:
        store.wait()


def intake(token_rows, weights):
    nz = lax.axis_size("z")
    count = len(weights)
    own_rows, width = token_rows.shape
    rows = weights[0].shape[0]
    parts = [w.shape[1] // (2 * nz) for w in weights]
    piece = own_rows // 2
    out_shape = [jax.ShapeDtypeStruct((nz, 2, 2, piece, width), BF)] + [
        jax.ShapeDtypeStruct((nz, 2, rows, c), BF) for c in parts
    ]
    got = call(
        functools.partial(intake_kernel, nz, count),
        5,
        out_shape,
        [pl.ANY] * (count + 1),
        [pl.ANY] * (count + 1),
        [
            pltpu.VMEM((2, piece, width), BF),
            *[pltpu.VMEM((rows, c), BF) for c in parts],
            DMA((2,)),
            *[DMA((nz,)) for _ in range(4)],
            *[DMA((nz, 2)) for _ in range(2)],
            DMA((count,)),
            *[DMA((count, nz)) for _ in range(4)],
        ],
        16,
        token_rows.reshape(2, piece, width),
        *weights,
    )
    return got[0].reshape(-1, width), [g.reshape(-1, g.shape[-1]) for g in got[1:]]


def outlet_kernel(nz, count, *refs):
    g_refs, refs = refs[:count], refs[count:]
    o_refs, refs = refs[:count], refs[count:]
    own, refs = refs[:count], refs[count:]
    yin, refs = refs[:count], refs[count:]
    zout, refs = refs[:count], refs[count:]
    ls, ys, yr, zs, zr, cs, cr, os = refs
    iz, iy, ic = (lax.axis_index(a) for a in ("z", "y", "core"))
    beside, behind = {"core": 1 - ic}, {"y": 1 - iy}
    greet(partners_of(("z", "y", "core")))
    sends, loads, pairs, stores = [], {}, {}, []

    def push(src, dst, send_sem, recv_sem, partner):
        copy = remote(src, dst, send_sem, recv_sem, partner)
        copy.start()
        sends.append(copy)
        return copy

    order = [(k, d) for k in range(count) for d in range(nz - 1, -1, -1)]
    widths = [g.shape[-1] for g in g_refs]
    for k, d in order:
        target = flip("z", d) if d else iz
        pairs[k, d] = push(
            g_refs[k].at[target, 1 - iy], yin[k].at[d], ys.at[k, d], yr.at[k, d], behind
        )
        loads[k, d] = pltpu.make_async_copy(g_refs[k].at[target, iy], own[k].at[d], ls.at[k, d])
        loads[k, d].start()

    def relay(k, d):
        block = columns(o_refs[k], flip("z", d) * 2 + ic, widths[k])
        remote(block, block, zr.at[k, d], zr.at[k, d], beside).wait_recv()
        push(block, block, cs.at[k, d], cr.at[k, d], beside)

    for n, (k, d) in enumerate(order):
        loads[k, d].wait()
        pairs[k, d].wait_recv()
        zout[k][d] = (own[k][d].astype(F32) + yin[k][d].astype(F32)).astype(BF)
        mine = columns(o_refs[k], iz * 2 + ic, widths[k])
        if d:
            push(zout[k].at[d], mine, zs.at[k, d], zr.at[k, d], {"z": flip("z", d)})
        else:
            push(zout[k].at[d], mine, cs.at[k, d], cr.at[k, d], beside)
            store = pltpu.make_async_copy(zout[k].at[d], mine, os.at[k])
            store.start()
            stores.append(store)
            if k:
                for e in range(nz - 1, 0, -1):
                    relay(k - 1, e)
    for e in range(nz - 1, 0, -1):
        relay(count - 1, e)
    for k, d in order:
        source = flip("z", d) if d else iz
        block = columns(o_refs[k], source * 2 + 1 - ic, widths[k])
        remote(block, block, cr.at[k, d], cr.at[k, d], beside).wait_recv()
    for copy in sends:
        copy.wait_send()
    for store in stores:
        store.wait()


def outlet(grads, identity=6):
    nz = lax.axis_size("z")
    count = len(grads)
    parts = [g.shape[1] for g in grads]
    blocks = [g.astype(BF).reshape(nz, 2, -1, g.shape[1]) for g in grads]
    rows = blocks[0].shape[2]
    got = call(
        functools.partial(outlet_kernel, nz, count),
        identity,
        [jax.ShapeDtypeStruct((rows, 2 * nz * c), BF) for c in parts],
        [pl.ANY] * count,
        [pl.ANY] * count,
        [
            *[pltpu.VMEM((nz, rows, c), BF) for _ in range(3) for c in parts],
            *[DMA((count, nz)) for _ in range(7)],
            DMA((count,)),
        ],
        32,
        *blocks,
    )
    if lax.axis_size("ch") > 1:
        got = lax.psum(tuple(got), "ch")
    return [g.astype(F32) for g in got]


class Kernel:
    def __init__(self):
        self.ins, self.outs, self.scratch = [], [], []

    def inp(self, name, array, space=pl.ANY):
        self.ins.append((name, array, space))

    def out(self, name, shape, dtype, space=pl.ANY):
        self.outs.append((name, jax.ShapeDtypeStruct(shape, dtype), space))

    def mem(self, name, shape, dtype):
        self.scratch.append((name, pltpu.VMEM(shape, dtype)))

    def sem(self, name, *shape):
        self.scratch.append((name, DMA(shape)))

    def run(self, identity, body, limit):
        names = [n for n, *_ in self.ins + self.outs + self.scratch]

        def kernel(*refs):
            body(types.SimpleNamespace(**dict(zip(names, refs))))

        got = call(
            kernel,
            identity,
            [shape for _, shape, _ in self.outs],
            [space for *_, space in self.ins],
            [space for *_, space in self.outs],
            [made for _, made in self.scratch],
            limit,
            *[array for _, array, _ in self.ins],
        )
        return {n: g for (n, *_), g in zip(self.outs, got)}


class Flow:
    def __init__(self):
        self.sends = []
        self.iz, self.iy, self.ic, self.it = (
            lax.axis_index(a) for a in ("z", "y", "core", "tp")
        )
        self.across = {"tp": 1 - self.it}
        self.beside = {"core": 1 - self.ic}
        self.behind = {"y": 1 - self.iy}

    def at(self, d):
        return flip("z", d) if d else self.iz

    def push(self, src, dst, send_sem, recv_sem, partner):
        copy = remote(src, dst, send_sem, recv_sem, partner)
        copy.start()
        self.sends.append(copy)
        return copy

    def arrived(self, ref, sem):
        remote(ref, ref, sem, sem, self.across).wait_recv()

    def finish(self):
        for copy in self.sends:
            copy.wait_send()
        self.sends = []


def stripe(ref, z, core, tp, piece):
    start = pl.multiple_of((core * 2 + tp) * piece, piece)
    return ref.at[z, pl.ds(start, piece)]


class Gather(Flow):
    @staticmethod
    def setup(k, name, rows, nz):
        piece, width = rows.shape
        k.inp(name + "_x", rows)
        k.mem(name, (nz, 4 * piece, width), rows.dtype)
        k.sem(name + "_own")
        for s in ("_zs", "_zr", "_xs", "_xr"):
            k.sem(name + s, nz)
        k.sem(name + "_cs", nz, 2)
        k.sem(name + "_cr", nz, 2)

    def __init__(self, r, name, nz):
        super().__init__()
        self.nz = nz
        self.x, self.buf = getattr(r, name + "_x"), getattr(r, name)
        self.own_sem, self.zs, self.zr, self.xs, self.xr, self.cs, self.cr = (
            getattr(r, name + s) for s in ("_own", "_zs", "_zr", "_xs", "_xr", "_cs", "_cr")
        )
        self.piece = self.x.shape[0]

    def block(self, z, core, tp):
        return stripe(self.buf, z, core, tp, self.piece)

    def start(self):
        own = self.block(self.iz, self.ic, self.it)
        for d in range(1, self.nz):
            self.push(self.x, own, self.zs.at[d], self.zr.at[d], {"z": self.at(d)})
        self.push(self.x, own, self.xs.at[0], self.xr.at[0], self.across)
        self.push(self.x, own, self.cs.at[0, 0], self.cr.at[0, 0], self.beside)
        self.local = pltpu.make_async_copy(self.x, own, self.own_sem)
        self.local.start()

    def from_across(self, d):
        block = self.block(self.at(d), self.ic, 1 - self.it)
        self.arrived(block, self.xr.at[d])
        self.push(block, block, self.cs.at[d, 1], self.cr.at[d, 1], self.beside)

    def advance(self, d):
        if d < self.nz:
            block = self.block(self.at(d), self.ic, self.it)
            self.arrived(block, self.zr.at[d])
            self.push(block, block, self.xs.at[d], self.xr.at[d], self.across)
            self.push(block, block, self.cs.at[d, 0], self.cr.at[d, 0], self.beside)
        self.from_across(d - 1)

    def ready(self, d):
        if d == 0:
            self.local.wait()
        for half in range(2):
            side = self.it if half == 0 else 1 - self.it
            self.arrived(self.block(self.at(d), 1 - self.ic, side), self.cr.at[d, half])


class Scatter(Flow):
    @staticmethod
    def setup(k, name, piece, width, nz):
        k.mem(name + "_p", (nz, 4 * piece, width), BF)
        k.mem(name + "_c", (nz, 2 * piece, width), BF)
        for s in ("_xo", "_xi", "_zo", "_zi"):
            k.mem(name + s, (nz, piece, width), BF)
        for s in ("_cs", "_cr", "_xs", "_xr", "_zs", "_zr"):
            k.sem(name + s, nz)

    def __init__(self, r, name, nz, out):
        super().__init__()
        self.nz, self.out = nz, out
        self.p, self.c, self.xo, self.xi, self.zo, self.zi = (
            getattr(r, name + s) for s in ("_p", "_c", "_xo", "_xi", "_zo", "_zi")
        )
        self.cs, self.cr, self.xs, self.xr, self.zs, self.zr = (
            getattr(r, name + s) for s in ("_cs", "_cr", "_xs", "_xr", "_zs", "_zr")
        )
        self.piece = self.xo.shape[1]
        self.core_copy, self.across_copy, self.z_copy = {}, {}, {}

    def begin(self, d):
        rows = pl.ds(pl.multiple_of((1 - self.ic) * 2 * self.piece, 2 * self.piece), 2 * self.piece)
        src = self.p.at[d, rows]
        self.core_copy[d] = self.push(
            src, self.c.at[d], self.cs.at[d], self.cr.at[d], self.beside
        )

    def add(self, d, side):
        start = pl.multiple_of((self.ic * 2 + side) * self.piece, self.piece)
        rows = pl.ds(pl.multiple_of(side * self.piece, self.piece), self.piece)
        return self.p[d, pl.ds(start, self.piece)].astype(F32) + self.c[d, rows].astype(F32)

    def cross(self, d):
        self.core_copy[d].wait_recv()
        self.xo[d] = self.add(d, 1 - self.it).astype(BF)
        self.across_copy[d] = self.push(
            self.xo.at[d], self.xi.at[d], self.xs.at[d], self.xr.at[d], self.across
        )

    def leave(self, d):
        self.across_copy[d].wait_recv()
        value = self.add(d, self.it) + self.xi[d].astype(F32)
        if d == 0:
            self.out[...] = value
        else:
            self.zo[d] = value.astype(BF)
            self.z_copy[d] = self.push(
                self.zo.at[d], self.zi.at[d], self.zs.at[d], self.zr.at[d], {"z": self.at(d)}
            )

    def end(self):
        for d in range(self.nz - 1, 0, -1):
            self.z_copy[d].wait_recv()
            self.out[...] += self.zi[d].astype(F32)


class Total(Flow):
    @staticmethod
    def setup(k, name, shape, axes):
        for axis in axes:
            size = lax.axis_size(axis)
            k.mem(f"{name}_{axis}", (size, *shape), F32)
            k.sem(f"{name}_{axis}_s", size)
            k.sem(f"{name}_{axis}_r", size)

    def __init__(self, r, name):
        super().__init__()
        self.r, self.name = r, name

    def send(self, axis, value):
        slots, ss, rs = (getattr(self.r, f"{self.name}_{axis}{s}") for s in ("", "_s", "_r"))
        me = lax.axis_index(axis)
        slots[me] = value
        self.copies = [
            self.push(slots.at[me], slots.at[me], ss.at[d], rs.at[d], {axis: flip(axis, d)})
            for d in range(1, lax.axis_size(axis))
        ]
        self.slots = slots

    def receive(self):
        for copy in self.copies:
            copy.wait_recv()
        value = self.slots[0]
        for n in range(1, self.slots.shape[0]):
            value = value + self.slots[n]
        return value


class Outlet(Flow):
    @staticmethod
    def setup(k, name, grads, nz, inside=False):
        for n, grad in enumerate(grads):
            rows, cols = grad.shape[0] // (2 * nz), grad.shape[1]
            if inside:
                k.mem(f"{name}_g{n}", (nz, 2, rows, cols), BF)
            else:
                k.inp(f"{name}_g{n}", grad.astype(BF).reshape(nz, 2, rows, cols))
                k.mem(f"{name}_own{n}", (nz, rows, cols), BF)
            k.out(f"{name}_o{n}", (rows, 2 * nz * cols), BF)
            for s in ("yin", "zout"):
                k.mem(f"{name}_{s}{n}", (nz, rows, cols), BF)
        for s in ("ls", "ys", "yr", "zs", "zr", "cs", "cr"):
            k.sem(f"{name}_{s}", len(grads), nz)
        k.sem(f"{name}_os", len(grads))

    def __init__(self, r, name, count, nz):
        super().__init__()
        self.nz, self.count = nz, count
        self.g, self.o, self.own, self.yin, self.zout = (
            [getattr(r, f"{name}_{s}{n}", None) for n in range(count)]
            for s in ("g", "o", "own", "yin", "zout")
        )
        self.ls, self.ys, self.yr, self.zs, self.zr, self.cs, self.cr, self.os = (
            getattr(r, f"{name}_{s}") for s in ("ls", "ys", "yr", "zs", "zr", "cs", "cr", "os")
        )
        self.loads, self.pairs, self.stores = {}, {}, []

    def slot(self, k, z, core):
        return columns(self.o[k], z * 2 + core, self.g[k].shape[-1])

    def start(self, k):
        for d in range(self.nz - 1, -1, -1):
            target = self.at(d)
            self.pairs[k, d] = self.push(
                self.g[k].at[target, 1 - self.iy],
                self.yin[k].at[d],
                self.ys.at[k, d],
                self.yr.at[k, d],
                self.behind,
            )
            if self.own[k] is not None:
                self.loads[k, d] = pltpu.make_async_copy(
                    self.g[k].at[target, self.iy], self.own[k].at[d], self.ls.at[k, d]
                )
                self.loads[k, d].start()

    def combine(self, k):
        mine = self.slot(k, self.iz, self.ic)
        for d in range(self.nz - 1, -1, -1):
            self.pairs[k, d].wait_recv()
            if self.own[k] is not None:
                self.loads[k, d].wait()
                own = self.own[k][d]
            else:
                own = self.g[k][self.at(d), self.iy]
            self.zout[k][d] = (own.astype(F32) + self.yin[k][d].astype(F32)).astype(BF)
            src = self.zout[k].at[d]
            if d:
                self.push(src, mine, self.zs.at[k, d], self.zr.at[k, d], {"z": self.at(d)})
            else:
                self.push(src, mine, self.cs.at[k, d], self.cr.at[k, d], self.beside)
                store = pltpu.make_async_copy(src, mine, self.os.at[k])
                store.start()
                self.stores.append(store)

    def relay(self, k):
        for d in range(1, self.nz):
            block = self.slot(k, self.at(d), self.ic)
            self.arrived(block, self.zr.at[k, d])
            self.push(block, block, self.cs.at[k, d], self.cr.at[k, d], self.beside)

    def end(self):
        for k in range(self.count):
            for d in range(self.nz):
                self.arrived(self.slot(k, self.at(d), 1 - self.ic), self.cr.at[k, d])
        for store in self.stores:
            store.wait()
        self.finish()


def exact(a, b, dims):
    return lax.dot_general(
        a, b, (dims, ((), ())), precision=lax.Precision.HIGHEST, preferred_element_type=F32
    )


def picker(width):
    row = lax.broadcasted_iota(jnp.int32, (8, width), 0)
    part = lax.broadcasted_iota(jnp.int32, (8, width), 1) // HD
    return jnp.where(row == part, 1.0, 0.0).astype(F32)


def row_sums(first, second):
    both = jnp.concatenate([first, second], axis=1)
    return exact(picker(2 * HD), both, ((1,), (1,)))


def spread(sums, which):
    row = lax.broadcasted_iota(jnp.int32, (8, HD), 0)
    one = jnp.where(row == which, 1.0, 0.0).astype(F32)
    return exact(sums, one, ((0,), (0,)))


def softmax_rows(query, key, length):
    count = query.shape[0]
    row = lax.broadcasted_iota(jnp.int32, (count, count), 0)
    col = lax.broadcasted_iota(jnp.int32, (count, count), 1)
    scores = mm_nt(query, key) * (1.0 / math.sqrt(HD))
    scores = jnp.where((col <= row) & (col < length), scores, NEGATIVE)
    exponent = jnp.exp(scores - jnp.max(scores, axis=-1, keepdims=True))
    return exponent / jnp.sum(exponent, axis=-1, keepdims=True)


def load_all(pairs, sems):
    copies = []
    for n, (src, dst) in enumerate(pairs):
        copy = pltpu.make_async_copy(src, dst, sems.at[n])
        copy.start()
        copies.append(copy)
    return copies


def attention_back(
    branch, wide, wo, wqkv, saved, tokens_all, residual_grad, stream_rows, terms, gains, tables,
    seq_lengths,
):
    nz = lax.axis_size("z")
    piece, width = branch.shape
    rows = 4 * piece
    block = width // (2 * nz)
    padded = jnp.pad(terms, (0, -terms.shape[0] % 1024)).reshape(-1, 128)
    lanes = width // 128
    sum_axes = ("core", "tp", "y", "z")
    k = Kernel()
    Gather.setup(k, "ball", branch, nz)
    Outlet.setup(k, "wide", wide, nz)
    slim = [jax.ShapeDtypeStruct((width, HD), BF)] * 4
    Outlet.setup(k, "slim", slim, nz, inside=True)
    Scatter.setup(k, "rs", piece, width, nz)
    Total.setup(k, "tot", (nz, 8, rows), ("core", "tp", "z"))
    Total.setup(k, "sum", padded.shape, sum_axes)
    k.inp("wo", wo)
    k.inp("wqkv", wqkv)
    k.inp("tokens", tokens_all)
    k.mem("tokens_m", tokens_all.shape, BF)
    names = ("q", "k", "v", "att", "nq", "nk", "qs", "ks")
    for name, array in zip(names, saved):
        k.inp(name, array)
        k.mem(name + "_m", array.shape, array.dtype)
    k.mem("wo_m", wo.shape, BF)
    k.mem("wqkv_m", wqkv.shape, BF)
    k.inp("res", residual_grad)
    k.mem("res_m", (piece, width), F32)
    k.inp("stream", stream_rows)
    k.mem("stream_m", (piece, width), BF)
    k.sem("ld", len(names) + 5)
    k.inp("terms", padded, pltpu.VMEM)
    k.mem("terms_m", padded.shape, F32)
    k.out("terms_out", padded.shape, F32, pltpu.VMEM)
    k.inp("gains", gains, pltpu.VMEM)
    k.inp("tables", tables, pltpu.VMEM)
    k.inp("lens", seq_lengths, pltpu.SMEM)
    k.mem("wqk", (nz, 2, rows, HD), F32)
    k.mem("low", (nz, rows, 3 * HD), BF)
    k.mem("dots", (nz, 8, rows), F32)
    k.mem("norms", (2, HD), F32)
    k.mem("grad", (piece, width), F32)
    k.out("grad_out", (2, piece, width), F32)
    k.out("stream_out", (2, piece, width), BF)
    k.sem("xs", 2)
    k.sem("xr", 2)
    k.sem("ss", 2)

    def body(r):
        greet(partners_of(("z", "y", "tp", "core")))
        gather, outlet_flow = Gather(r, "ball", nz), Outlet(r, "wide", len(wide), nz)
        slim_flow, own = Outlet(r, "slim", len(slim), nz), Flow()
        scatter, total_flow = Scatter(r, "rs", nz, r.grad), Total(r, "tot")
        sum_flow = Total(r, "sum")
        gather.start()
        for n in range(len(wide)):
            outlet_flow.start(n)
        names_in = ("wo", "wqkv", *names, "tokens", "res", "stream")
        loads = load_all([(getattr(r, n), getattr(r, n + "_m")) for n in names_in], r.ld)
        scale = 1.0 / math.sqrt(HD)
        cosine, sine = r.tables[0], r.tables[1]
        gather.advance(1)
        for copy in loads:
            copy.wait()
        r.norms[...] = jnp.zeros_like(r.norms)

        def compute(z):
            grad_low = mm(r.ball[z], r.wo_m[...]).astype(BF)
            query, key, value = r.q_m[z], r.k_m[z], r.v_m[z]
            probability = softmax_rows(query, key, r.lens[z])
            grad_prob = mm_nt(grad_low, value)
            row_dots = jnp.sum(probability * grad_prob, axis=-1, keepdims=True)
            grad_scores = (probability * (grad_prob - row_dots)).astype(BF)
            grad_q = rotate_back(mm(grad_scores, key) * scale, cosine, sine)
            grad_k = rotate_back(mm_tn(grad_scores, query) * scale, cosine, sine)
            grad_v = mm_tn(probability.astype(BF), grad_low)
            r.low[z, :, 2 * HD :] = grad_v.astype(BF)
            nq, nk = r.nq_m[z], r.nk_m[z]
            r.norms[0:1] += jnp.sum(grad_q * nq, axis=0, keepdims=True)
            r.norms[1:2] += jnp.sum(grad_k * nk, axis=0, keepdims=True)
            wq, wk = grad_q * r.gains[0:1], grad_k * r.gains[1:2]
            r.wqk[z, 0] = wq
            r.wqk[z, 1] = wk
            r.dots[z] = row_sums(wq * nq, wk * nk)

        def weight_blocks(left, right, place):
            @pl.loop(0, 2 * nz)
            def _(f):
                cols = pl.ds(pl.multiple_of(f * block, block), block)
                made = mm_tn(left[0, :, cols], right[0])
                for z in range(1, nz):
                    made = made + mm_tn(left[z, :, cols], right[z])
                made = made.astype(BF)
                for n, grad in enumerate(place):
                    grad[f // 2, lax.rem(f, 2)] = made[:, n * HD : (n + 1) * HD]

        for d in range(nz):
            if d + 2 <= nz:
                gather.advance(d + 2)
            if d == nz - 2:
                own.push(
                    r.stream, r.stream_out.at[own.it], r.xs.at[0], r.xr.at[0], own.across
                )
            gather.ready(d)
            compute(gather.at(d))
            if d == nz - 2:
                outlet_flow.combine(0)
        r.terms_m[...] = r.terms[...]
        slot = 2 * lanes + own.it * (lanes // 2) + own.iz * 2 + own.ic
        for n in range(2):
            r.terms_m[pl.ds(slot + n * lanes, 1)] = r.norms[n : n + 1]
        total_flow.send("core", r.dots[...])
        sum_flow.send("core", r.terms_m[...])
        value, other = total_flow.receive(), sum_flow.receive()
        total_flow.send("tp", value)
        sum_flow.send("tp", other)
        value, other = total_flow.receive(), sum_flow.receive()
        total_flow.send("z", value)
        sum_flow.send("y", other)
        outlet_flow.combine(1)
        weight_blocks(r.ball, r.att_m, [slim_flow.g[3]])
        slim_flow.start(3)
        r.dots[...] = total_flow.receive()
        order = list(range(nz - 1, -1, -1))
        for n, d in enumerate(order):
            z = gather.at(d)
            sums = r.dots[z] * (1.0 / width)
            for j, (normed, factor) in enumerate(((r.nq_m, r.qs_m), (r.nk_m, r.ks_m))):
                low = factor[z] * (r.wqk[z, j] - normed[z] * spread(sums, j))
                r.low[z, :, j * HD : (j + 1) * HD] = low.astype(BF)
            r.rs_p[d] = mm_nt(r.low[z], r.wqkv_m[...]).astype(BF)
            scatter.begin(d)
            if n:
                scatter.cross(order[n - 1])
            if n > 1:
                scatter.leave(order[n - 2])
        scatter.cross(0)
        scatter.leave(1)
        scatter.leave(0)
        outlet_flow.combine(2)
        weight_blocks(r.tokens_m, r.low, slim_flow.g[:3])
        for n in range(3):
            slim_flow.start(n)
        sum_flow.send("z", sum_flow.receive())
        slim_flow.combine(3)
        outlet_flow.relay(0)
        outlet_flow.relay(1)
        scatter.end()
        r.res_m[...] += r.grad[...]
        own.push(r.res_m, r.grad_out.at[own.it], r.xs.at[1], r.xr.at[1], own.across)
        stores = []
        for n, (src, out) in enumerate(((r.stream_m, r.stream_out), (r.res_m, r.grad_out))):
            stores.append(pltpu.make_async_copy(src, out.at[own.it], r.ss.at[n]))
            stores[-1].start()
        for n in range(3):
            slim_flow.combine(n)
        r.terms_out[...] = sum_flow.receive()
        outlet_flow.relay(2)
        slim_flow.relay(3)
        for n in range(3):
            slim_flow.relay(n)
        outlet_flow.end()
        slim_flow.end()
        for n, out in enumerate((r.stream_out, r.grad_out)):
            own.arrived(out.at[1 - own.it], r.xr.at[n])
        for flow in (gather, scatter, total_flow, sum_flow, own):
            flow.finish()
        for copy in stores:
            copy.wait()

    got = k.run(7, body, 60)
    return (
        [got[f"slim_o{n}"].astype(F32) for n in range(4)]
        + [got[f"wide_o{n}"].astype(F32) for n in range(len(wide))],
        got["grad_out"].reshape(-1, width),
        got["stream_out"].reshape(-1, width),
        got["terms_out"].reshape(-1)[: terms.shape[0]],
    )


def attention_front(token_rows, weights, gains, tables, seq_lengths):
    nz = lax.axis_size("z")
    own_rows, width = token_rows.shape
    piece, rows = own_rows // 2, own_rows * 2
    w_rows = weights[0].shape[0]
    count = len(weights)
    parts = [w.shape[1] // (2 * nz) for w in weights]
    k = Kernel()
    Scatter.setup(k, "rs", piece, width, nz)
    Total.setup(k, "tot", (nz, 8, rows), ("core", "tp", "z"))
    k.inp("tok", token_rows)
    for n, weight in enumerate(weights):
        k.inp(f"w{n}", weight)
    k.inp("gains", gains, pltpu.VMEM)
    k.inp("tables", tables, pltpu.VMEM)
    k.inp("lens", seq_lengths, pltpu.SMEM)
    k.mem("tall", (nz, rows, width), BF)
    k.mem("qkv", (nz, 2, w_rows, 3 * HD), BF)
    k.mem("wo", (nz, 2, w_rows, parts[3]), BF)
    for n in range(4, count):
        k.mem(f"b{n}", (w_rows, parts[n]), BF)
        k.out(f"o{n}", (nz, 2, w_rows, parts[n]), BF)
    k.mem("raw", (nz, rows, 3 * HD), F32)
    k.mem("dots", (nz, 8, rows), F32)
    saved = (("q", BF), ("k", BF), ("v", BF), ("nq", F32), ("nk", F32), ("qs", F32), ("ks", F32), ("att", BF))
    for name, kind in saved:
        k.mem(name + "_m", (nz, rows, HD), kind)
        k.out(name, (nz, rows, HD), kind)
    k.out("branch", (piece, width), F32, pltpu.VMEM)
    k.out("tokens", (nz, rows, width), BF)
    k.out("qkv_out", (nz, 2, w_rows, 3 * HD), BF)
    k.out("wo_out", (nz, 2, w_rows, parts[3]), BF)
    k.sem("tl")
    for s in ("tzs", "tzr", "txs", "txr"):
        k.sem(s, nz)
    k.sem("tcs", nz, 2)
    k.sem("tcr", nz, 2)
    k.sem("wl", 2, count)
    for s in ("wzs", "wzr", "wys", "wyr"):
        k.sem(s, count, nz)
    k.sem("st", len(saved) + 1, nz)
    k.sem("sw", 2)

    def body(r):
        greet(partners_of(("z", "y", "tp", "core")))
        flow = Flow()
        iz, iy, ic, it = flow.iz, flow.iy, flow.ic, flow.it
        scatter, total_flow = Scatter(r, "rs", nz, r.branch), Total(r, "tot")

        def block(z, core, tp):
            return stripe(r.tall, z, core, tp, piece)

        def pair(z, core):
            start = pl.multiple_of(core * own_rows, own_rows)
            return r.tall.at[z, pl.ds(start, own_rows)]

        tok_half = r.tok.at[pl.ds(pl.multiple_of(it * piece, piece), piece)]
        for d in range(1, nz):
            flow.push(tok_half, block(iz, ic, it), r.tzs.at[d], r.tzr.at[d], {"z": flow.at(d)})
        flow.push(r.tok, pair(iz, ic), r.tcs.at[0, 0], r.tcr.at[0, 0], flow.beside)
        tok_load = pltpu.make_async_copy(r.tok, pair(iz, ic), r.tl)
        tok_load.start()
        loads = {}

        def landing(n, z, y):
            if n < 3:
                return r.qkv.at[z, y, :, n * HD : (n + 1) * HD]
            return r.wo.at[z, y] if n == 3 else getattr(r, f"o{n}").at[z, y]

        def bring(n):
            weight = getattr(r, f"w{n}")
            own = columns(weight, iz * 2 + ic, parts[n])
            for d in range(nz - 1, 0, -1):
                other = flow.at(d)
                flow.push(
                    columns(weight, other * 2 + ic, parts[n]),
                    landing(n, iz, iy),
                    r.wzs.at[n, d],
                    r.wzr.at[n, d],
                    {"z": other},
                )
            flow.push(own, landing(n, iz, iy), r.wys.at[n, 0], r.wyr.at[n, 0], flow.behind)
            dst = landing(n, iz, iy) if n < 4 else getattr(r, f"b{n}")
            loads[n] = pltpu.make_async_copy(own, dst, r.wl.at[0, n])
            loads[n].start()

        def forward(n):
            for d in range(1, nz):
                here = landing(n, flow.at(d), iy)
                flow.arrived(here, r.wzr.at[n, d])
                flow.push(here, here, r.wys.at[n, d], r.wyr.at[n, d], flow.behind)

        def complete(n):
            for d in range(nz):
                flow.arrived(landing(n, flow.at(d), 1 - iy), r.wyr.at[n, d])

        for n in range(min(5, count)):
            bring(n)
        for d in range(1, nz):
            here = block(flow.at(d), ic, it)
            flow.arrived(here, r.tzr.at[d])
            flow.push(here, here, r.txs.at[d], r.txr.at[d], flow.across)
            flow.push(here, here, r.tcs.at[d, 0], r.tcr.at[d, 0], flow.beside)
        for n in range(3):
            forward(n)
        for d in range(1, nz):
            here = block(flow.at(d), ic, 1 - it)
            flow.arrived(here, r.txr.at[d])
            flow.push(here, here, r.tcs.at[d, 1], r.tcr.at[d, 1], flow.beside)
        stores = []

        def save(n, src, dst, d):
            copy = pltpu.make_async_copy(src, dst, r.st.at[n, d])
            copy.start()
            stores.append(copy)

        for n in range(4):
            loads[n].wait()
        for n in range(3):
            complete(n)
        tok_load.wait()
        for d in range(nz):
            z = flow.at(d)
            if d == 0:
                flow.arrived(pair(iz, 1 - ic), r.tcr.at[0, 0])
            else:
                for half in range(2):
                    side = it if half == 0 else 1 - it
                    flow.arrived(block(z, 1 - ic, side), r.tcr.at[d, half])
            save(0, r.tall.at[z], r.tokens.at[z], d)
            raw = mm(r.tall[z], r.qkv[...].reshape(2 * nz * w_rows, 3 * HD))
            r.raw[z] = raw
            query, key = raw[:, :HD], raw[:, HD : 2 * HD]
            r.dots[z] = row_sums(query * query, key * key)
        total_flow.send("core", r.dots[...])
        forward(3)
        value = total_flow.receive()
        total_flow.send("tp", value)
        value = total_flow.receive()
        total_flow.send("z", value)
        for n in range(5, count):
            bring(n)
        for n in range(4, count):
            loads[n].wait()
            copy = pltpu.make_async_copy(getattr(r, f"b{n}"), landing(n, iz, iy), r.wl.at[1, n])
            copy.start()
            stores.append(copy)
        complete(3)
        for n, (src, dst) in enumerate(((r.qkv, r.qkv_out), (r.wo, r.wo_out))):
            copy = pltpu.make_async_copy(src, dst, r.sw.at[n])
            copy.start()
            stores.append(copy)
        r.dots[...] = lax.rsqrt(total_flow.receive() * (1.0 / width) + EPSILON)
        cosine, sine = r.tables[0], r.tables[1]
        order = list(range(nz - 1, -1, -1))
        for n, d in enumerate(order):
            z = flow.at(d)
            sums = r.dots[z]
            r.qs_m[z] = spread(sums, 0)
            r.ks_m[z] = spread(sums, 1)
            r.nq_m[z] = r.raw[z, :, :HD] * r.qs_m[z]
            r.nk_m[z] = r.raw[z, :, HD : 2 * HD] * r.ks_m[z]
            query = rotate(r.nq_m[z] * r.gains[0:1], cosine, sine).astype(BF)
            key = rotate(r.nk_m[z] * r.gains[1:2], cosine, sine).astype(BF)
            value = r.raw[z, :, 2 * HD :].astype(BF)
            r.q_m[z] = query
            r.k_m[z] = key
            r.v_m[z] = value
            probability = softmax_rows(query, key, r.lens[z]).astype(BF)
            r.att_m[z] = mm(probability, value).astype(BF)
            for m, (name, _) in enumerate(saved):
                save(m + 1, getattr(r, name + "_m").at[z], getattr(r, name).at[z], d)
            wo = r.wo[...].reshape(2 * nz * w_rows, parts[3])
            r.rs_p[d] = mm_nt(r.att_m[z], wo).astype(BF)
            scatter.begin(d)
            if n:
                scatter.cross(order[n - 1])
            if n > 1:
                scatter.leave(order[n - 2])
            if n == 0:
                forward(4)
        scatter.cross(0)
        forward(5)
        scatter.leave(1)
        scatter.leave(0)
        forward(6)
        scatter.end()
        for n in range(4, count):
            complete(n)
        for f in (flow, scatter, total_flow):
            f.finish()
        for copy in stores:
            copy.wait()

    return k.run(9, body, 60)


def local(
    tokens,
    lengths,
    weight_query,
    weight_key,
    weight_value,
    weight_out,
    weight_gate,
    weight_up,
    weight_down,
    post_attention,
    post_feedforward,
    query_norm,
    key_norm,
    cotangent,
):
    nz, ny, nch, ntp = (lax.axis_size(a) for a in ("z", "y", "ch", "tp"))
    iz, iy, ich, icore, itp = (lax.axis_index(a) for a in AXES)
    token_rows = tokens[0]
    own_rows, width = token_rows.shape
    piece = own_rows // ntp
    seq_rows = own_rows * 2
    total_rows = seq_rows * nz
    scale_factor = 1.0 / math.sqrt(HD)
    own_head = iz * 2 + icore
    qn = lax.dynamic_slice_in_dim(query_norm, own_head * HD, HD)
    kn = lax.dynamic_slice_in_dim(key_norm, own_head * HD, HD)
    seq_lengths = lax.dynamic_index_in_dim(lengths.reshape(nz, ny), iy, 1, keepdims=False)
    positions = ich * seq_rows + jnp.arange(seq_rows, dtype=jnp.int32)
    key_positions = jnp.arange(seq_rows * nch, dtype=jnp.int32)
    cosine, sine_table = rope_tables(positions)
    allowed = (key_positions[None, None, :] <= positions[None, :, None]) & (
        key_positions[None, None, :] < seq_lengths[:, None, None]
    )
    my_tokens = lax.dynamic_slice_in_dim(token_rows, itp * piece, piece, 0)
    my_cot = lax.dynamic_slice_in_dim(cotangent[0], itp * piece, piece, 0)
    my_pos = (ich * 2 + icore) * own_rows + itp * piece + jnp.arange(piece, dtype=jnp.int32)
    my_valid = (my_pos < lengths[iz * ny + iy]).astype(F32)[:, None]

    weights = (
        weight_query,
        weight_key,
        weight_value,
        weight_out,
        weight_gate,
        weight_up,
        weight_down,
    )
    fused = nch == 1
    by_seq = lambda a: a.reshape(nz, seq_rows, HD)
    gains, tables = jnp.stack([qn, kn]), jnp.stack([cosine, sine_table])
    if fused:
        front = attention_front(token_rows, weights, gains, tables, seq_lengths)
        branch_sum = front["branch"]
        wg, wu, wd = (front[f"o{n}"].reshape(width, -1) for n in (4, 5, 6))
    else:
        tokens_all, (wq, wk, wv, wo, wg, wu, wd) = intake(token_rows, weights)
        query_raw = mm(tokens_all, wq)
        key_raw = mm(tokens_all, wk)
        value_raw = mm(tokens_all, wv)
        squares = head_total(
            jnp.stack([jnp.sum(query_raw * query_raw, axis=-1), jnp.sum(key_raw * key_raw, axis=-1)])
        )
        scales = lax.rsqrt(squares / width + EPSILON)
        query_scale = scales[0][:, None]
        key_scale = scales[1][:, None]
        queries = rotate(by_seq(query_raw * query_scale * qn), cosine, sine_table).astype(BF)
        keys = rotate(by_seq(key_raw * key_scale * kn), cosine, sine_table).astype(BF)
        values = by_seq(value_raw).astype(BF)
        if nch > 1:
            keys_full = lax.all_gather(keys, "ch", axis=1, tiled=True)
            values_full = lax.all_gather(values, "ch", axis=1, tiled=True)
        else:
            keys_full, values_full = keys, values
        scores = (
            jnp.einsum("btd,bsd->bts", queries, keys_full, preferred_element_type=F32) * scale_factor
        )
        scores = jnp.where(allowed, scores, NEGATIVE)
        exponent = jnp.exp(scores - jnp.max(scores, axis=-1, keepdims=True))
        probability = exponent / jnp.sum(exponent, axis=-1, keepdims=True)
        probability_low = probability.astype(BF)
        attended = jnp.einsum("bts,bsd->btd", probability_low, values_full, preferred_element_type=F32)
        attended_low = attended.reshape(total_rows, HD).astype(BF)
        branch_sum = scatter_rows(mm_nt(attended_low, wo))
    attn_scale = lax.rsqrt(jnp.mean(branch_sum * branch_sum, axis=-1, keepdims=True) + EPSILON)
    attn_normed = branch_sum * attn_scale
    attention_branch = attn_normed * post_attention
    residual = my_tokens.astype(F32) + attention_branch
    residual_all = gather_rows(residual.astype(BF))
    gate_value = mm(residual_all, wg)
    up_value = mm(residual_all, wu)
    sigmoid_gate = jax.nn.sigmoid(gate_value)
    silu_gate = gate_value * sigmoid_gate
    mixed_low = (silu_gate * up_value).astype(BF)
    down_sum = scatter_rows(mm_nt(mixed_low, wd))
    ffn_scale = lax.rsqrt(jnp.mean(down_sum * down_sum, axis=-1, keepdims=True) + EPSILON)
    ffn_normed = down_sum * ffn_scale
    feedforward_branch = ffn_normed * post_feedforward
    stream = residual + feedforward_branch
    stat_terms = jnp.stack(
        [
            jnp.sum(my_valid * stream * stream),
            jnp.sum(my_valid * attention_branch * attention_branch),
            jnp.sum(my_valid * feedforward_branch * feedforward_branch),
        ]
    )
    grad_stream = my_cot * my_valid
    grad_post_ff = jnp.sum(grad_stream * ffn_normed, axis=0)
    scaled = grad_stream * post_feedforward
    grad_down_sum = ffn_scale * (
        scaled - ffn_normed * jnp.mean(scaled * ffn_normed, axis=-1, keepdims=True)
    )
    down_all = gather_rows(grad_down_sum.astype(BF))
    grad_mixed = mm(down_all, wd)
    gate_low = (
        grad_mixed * up_value * sigmoid_gate * (1.0 + gate_value * (1.0 - sigmoid_gate))
    ).astype(BF)
    up_low = (grad_mixed * silu_gate).astype(BF)
    grad_wg = mm_tn(residual_all, gate_low)
    grad_wu = mm_tn(residual_all, up_low)
    grad_wd = mm_tn(down_all, mixed_low)
    grad_residual = grad_stream + scatter_rows(mm_nt(gate_low, wg) + mm_nt(up_low, wu))
    grad_post_attn = jnp.sum(grad_residual * attn_normed, axis=0)
    scaled_attn = grad_residual * post_attention
    grad_branch = attn_scale * (
        scaled_attn - attn_normed * jnp.mean(scaled_attn * attn_normed, axis=-1, keepdims=True)
    )
    if not fused:
        branch_all = gather_rows(grad_branch.astype(BF))
        grad_att_low = mm(branch_all, wo).astype(BF)
        grad_wo = mm_tn(branch_all, attended_low)
        grad_att = by_seq(grad_att_low)
        grad_prob = jnp.einsum("btd,bsd->bts", grad_att, values_full, preferred_element_type=F32)
        row_dots = jnp.sum(probability * grad_prob, axis=-1, keepdims=True)
        grad_scores = (probability * (grad_prob - row_dots)).astype(BF)
        grad_queries = (
            jnp.einsum("bts,bsd->btd", grad_scores, keys_full, preferred_element_type=F32)
            * scale_factor
        )
        grad_keys = (
            jnp.einsum("bts,btd->bsd", grad_scores, queries, preferred_element_type=F32) * scale_factor
        )
        grad_values = jnp.einsum("bts,btd->bsd", probability_low, grad_att, preferred_element_type=F32)
        if nch > 1:
            grad_keys, grad_values = (
                lax.psum_scatter(g.astype(BF), "ch", scatter_dimension=1, tiled=True).astype(F32)
                for g in (grad_keys, grad_values)
            )
        value_grad_low = grad_values.reshape(total_rows, HD).astype(BF)
        grad_q_normed = rotate_back(grad_queries, cosine, sine_table).reshape(total_rows, HD)
        grad_k_normed = rotate_back(grad_keys, cosine, sine_table).reshape(total_rows, HD)
        query_weighted = grad_q_normed * qn
        key_weighted = grad_k_normed * kn
        dots = head_total(
            jnp.stack(
                [
                    jnp.sum(query_weighted * query_raw, axis=-1),
                    jnp.sum(key_weighted * key_raw, axis=-1),
                ]
            )
        )
        query_grad_low = (
            query_scale * (query_weighted - query_raw * query_scale**2 * (dots[0] / width)[:, None])
        ).astype(BF)
        key_grad_low = (
            key_scale * (key_weighted - key_raw * key_scale**2 * (dots[1] / width)[:, None])
        ).astype(BF)
        grad_qnorm = jnp.sum(grad_q_normed * query_raw * query_scale, axis=0)
        grad_knorm = jnp.sum(grad_k_normed * key_raw * key_scale, axis=0)
        grad_wq = mm_tn(tokens_all, query_grad_low)
        grad_wk = mm_tn(tokens_all, key_grad_low)
        grad_wv = mm_tn(tokens_all, value_grad_low)
        grad_rows = grad_residual + scatter_rows(
            mm_nt(query_grad_low, wq) + mm_nt(key_grad_low, wk) + mm_nt(value_grad_low, wv)
        )
    if fused:
        saved = tuple(front[n] for n in ("q", "k", "v", "att", "nq", "nk", "qs", "ks"))
        norms_wide = jnp.zeros((2 * width,), F32)
    else:
        slot = itp * (width // ntp) + own_head * HD
        zero_row = jnp.zeros((width,), F32)
        norms_wide = jnp.concatenate(
            [
                lax.dynamic_update_slice_in_dim(zero_row, grad_qnorm, slot, 0),
                lax.dynamic_update_slice_in_dim(zero_row, grad_knorm, slot, 0),
            ]
        )
    terms = jnp.concatenate([grad_post_attn, grad_post_ff, norms_wide, stat_terms])
    if fused:
        weight_grads, grad_input, output, summed = attention_back(
            grad_branch.astype(BF),
            (grad_wd, grad_wg, grad_wu),
            front["wo_out"].reshape(width, -1),
            front["qkv_out"].reshape(width, -1),
            saved,
            front["tokens"],
            grad_residual,
            stream.astype(BF),
            terms,
            gains,
            tables,
            seq_lengths,
        )
        weight_grads = [weight_grads[n] for n in (0, 1, 2, 3, 5, 6, 4)]
    else:
        weight_grads = outlet((grad_wq, grad_wk, grad_wv, grad_wo, grad_wg, grad_wu, grad_wd))
        grad_input = lax.all_gather(grad_rows, "tp", axis=0, tiled=True)
        output = lax.all_gather(stream.astype(BF), "tp", axis=0, tiled=True)
        summed = all_total(terms)
    half = width // ntp
    qn_sum = lax.dynamic_slice_in_dim(summed, 2 * width + itp * half, half)
    kn_sum = lax.dynamic_slice_in_dim(summed, 3 * width + itp * half, half)
    token_count = jnp.sum(lengths.astype(F32))
    root_means = jnp.sqrt(summed[4 * width :] / (token_count * width))
    return (
        output[None],
        grad_input[None],
        *weight_grads,
        summed[:width],
        summed[width : 2 * width],
        qn_sum,
        kn_sum,
        root_means,
    )


def solution(mesh):
    n_fsdp, n_ctx, n_tp = (mesh.shape[a] for a in ("fsdp", "ctx", "tp"))
    fine = Mesh(mesh.devices.reshape(n_fsdp // 2, 2, n_ctx // 2, 2, n_tp), AXES)
    fsdp, ctx = ("z", "y"), ("ch", "core")
    rows = P(fsdp, ctx, None)
    weight = P(fsdp, "tp")
    return jax.shard_map(
        local,
        mesh=fine,
        in_specs=(rows, P(), *([weight] * 7), P(), P(), P("tp"), P("tp"), rows),
        out_specs=(rows, rows, *([weight] * 7), P(), P(), P("tp"), P("tp"), P()),
        check_vma=False,
    )
```

```python
import functools
import math
import types

import jax
import jax.numpy as jnp
from jax import lax
from jax.experimental import pallas as pl
from jax.experimental.pallas import tpu as pltpu
from jax.sharding import Mesh, PartitionSpec as P

HD = 128
EPSILON = 1e-06
ROPE_BASE = 500000.0
NEGATIVE = -1e30
CORE, TP = "core", "tp"
SCORE = "btd,bsd->bts"
APPLY = "bts,bsd->btd"
AXES = ("z", "y", "ch", CORE, TP)
BF = jnp.bfloat16
F32 = jnp.float32


def rope_tables(positions):
    half_size = HD // 2
    exponent = jnp.arange(half_size, dtype=F32) * (2.0 / HD)
    frequency = jnp.power(ROPE_BASE, -exponent)
    angles = positions.astype(F32)[:, None] * frequency[None, :]
    cosine = jnp.cos(angles)
    sine_table = jnp.sin(angles)
    return (
        jnp.concatenate([cosine, cosine], axis=-1),
        jnp.concatenate([sine_table, sine_table], axis=-1),
    )


def rotate(values, cosine, sine_table):
    half_size = HD // 2
    turned = jnp.concatenate([-values[..., half_size:], values[..., :half_size]], axis=-1)
    return values * cosine + turned * sine_table


def rotate_back(grads_in, cosine, sine_table):
    half_size = HD // 2
    sin_part = grads_in * sine_table
    return grads_in * cosine + jnp.concatenate(
        [sin_part[..., half_size:], -sin_part[..., :half_size]], axis=-1
    )


def dot(former, latter, dims):
    return lax.dot_general(former, latter, (dims, ((), ())), preferred_element_type=F32)


def mm(a, b):
    return dot(a, b, ((1,), (0,)))


def mm_nt(a, b):
    return dot(a, b, ((1,), (1,)))


def mm_tn(a, b):
    return dot(a, b, ((0,), (0,)))


MESH = pl.DeviceIdType.MESH


def flip(axis, bits):
    me = lax.axis_index(axis)
    result, weight = me, 1
    while weight <= bits:
        if (bits // weight) % 2:
            result = result + weight * (1 - 2 * lax.rem(me // weight, 2))
        weight *= 2
    return result


def greet(partners):
    barrier = pltpu.get_barrier_semaphore()
    for partner in partners:
        pl.semaphore_signal(barrier, inc=1, device_id=partner, device_id_type=MESH)
    pl.semaphore_wait(barrier, len(partners))


def remote(src, dst, send_sem, recv_sem, partner):
    return pltpu.make_async_remote_copy(
        src_ref=src,
        dst_ref=dst,
        send_sem=send_sem,
        recv_sem=recv_sem,
        device_id=partner,
        device_id_type=MESH,
    )


def partners_of(axes):
    found = []
    for axis in axes:
        for bits in range(1, lax.axis_size(axis)):
            found.append({axis: flip(axis, bits)})
    return found


def call(kernel, identity, out_shape, in_spaces, out_spaces, scratch, limit, *operands):
    return pl.pallas_call(
        kernel,
        out_shape=out_shape,
        in_specs=[pl.BlockSpec(memory_space=s) for s in in_spaces],
        out_specs=jax.tree.map(lambda s: pl.BlockSpec(memory_space=s), out_spaces),
        scratch_shapes=scratch,
        compiler_params=pltpu.CompilerParams(
            collective_id=identity, has_side_effects=True, vmem_limit_bytes=limit * 2**20
        ),
    )(*operands)


DMA = pltpu.SemaphoreType.DMA


def gather_kernel(nz, x_ref, out_ref, own_sem, zs, zr, xs, xr, cs, cr):
    iz, ic, it = (lax.axis_index(a) for a in ("z", CORE, TP))
    greet(partners_of(("z", TP, CORE)))
    sends = []

    def push(src, where, send_sem, recv_sem, partner):
        copy = remote(src, out_ref.at[where], send_sem, recv_sem, partner)
        copy.start()
        sends.append(copy)

    across, beside = {TP: 1 - it}, {CORE: 1 - ic}
    own = (iz, ic, it)
    for d in range(1, nz):
        push(x_ref, own, zs.at[d], zr.at[d], {"z": flip("z", d)})
    push(x_ref, own, xs.at[0], xr.at[0], across)
    push(x_ref, own, cs.at[0, 0], cr.at[0, 0], beside)
    local_copy = pltpu.make_async_copy(x_ref, out_ref.at[own], own_sem)
    local_copy.start()

    def await_at(where, sem):
        remote(out_ref.at[where], out_ref.at[where], sem, sem, across).wait_recv()

    def from_across(d):
        where = (flip("z", d), ic, 1 - it)
        await_at(where, xr.at[d])
        push(out_ref.at[where], where, cs.at[d, 1], cr.at[d, 1], beside)

    for d in range(1, nz):
        where = (flip("z", d), ic, it)
        await_at(where, zr.at[d])
        push(out_ref.at[where], where, xs.at[d], xr.at[d], across)
        push(out_ref.at[where], where, cs.at[d, 0], cr.at[d, 0], beside)
        from_across(d - 1)
    from_across(nz - 1)
    for d in range(nz):
        for half in range(2):
            side = it if half == 0 else 1 - it
            await_at((flip("z", d), 1 - ic, side), cr.at[d, half])
    for copy in sends:
        copy.wait_send()
    local_copy.wait()


def gather_rows(rows):
    piece, width = rows.shape
    nz = lax.axis_size("z")
    out = call(
        functools.partial(gather_kernel, nz),
        1,
        jax.ShapeDtypeStruct((nz, 2, 2, piece, width), rows.dtype),
        [pl.ANY],
        pl.ANY,
        [DMA, DMA((nz,)), DMA((nz,)), DMA((nz,)), DMA((nz,)), DMA((nz, 2)), DMA((nz, 2))],
        16,
        rows,
    )
    return out.reshape(-1, width)


def scatter_kernel(
    nz, p_ref, out_ref, own, cin, xout, xin, zout, zin, ls, cs, cr, xs, xr, zs, zr
):
    iz, ic, it = (lax.axis_index(a) for a in ("z", CORE, TP))
    greet(partners_of(("z", TP, CORE)))
    across, beside = {TP: 1 - it}, {CORE: 1 - ic}
    order = list(range(nz - 1, -1, -1))
    loads, besides, acrosses, zeds = {}, {}, {}, {}
    for d in order:
        target = flip("z", d) if d else iz
        besides[d] = remote(p_ref.at[target, 1 - ic], cin.at[d], cs.at[d], cr.at[d], beside)
        besides[d].start()
        loads[d] = pltpu.make_async_copy(p_ref.at[target, ic], own.at[d], ls.at[d])
        loads[d].start()

    def add(d, side):
        return own[d, side].astype(F32) + cin[d, side].astype(F32)

    def after_across(d):
        acrosses[d].wait_recv()
        total = add(d, it) + xin[d].astype(F32)
        if d == 0:
            out_ref[...] = total
        else:
            zout[d] = total.astype(BF)
            zeds[d] = remote(zout.at[d], zin.at[d], zs.at[d], zr.at[d], {"z": flip("z", d)})
            zeds[d].start()

    for n, d in enumerate(order):
        loads[d].wait()
        besides[d].wait_recv()
        xout[d] = add(d, 1 - it).astype(BF)
        acrosses[d] = remote(xout.at[d], xin.at[d], xs.at[d], xr.at[d], across)
        acrosses[d].start()
        if n:
            after_across(order[n - 1])
    after_across(0)
    for d in order[:-1]:
        zeds[d].wait_recv()
        out_ref[...] += zin[d].astype(F32)
    for group in (besides, acrosses, zeds):
        for copy in group.values():
            copy.wait_send()


def scatter_rows(partial):
    nz = lax.axis_size("z")
    width = partial.shape[1]
    part = partial.astype(BF).reshape(nz, 2, 2, -1, width)
    piece = part.shape[3]
    sems = [DMA((nz,)) for _ in range(7)]
    return call(
        functools.partial(scatter_kernel, nz),
        2,
        jax.ShapeDtypeStruct((piece, width), F32),
        [pl.ANY],
        pltpu.VMEM,
        [
            pltpu.VMEM((nz, 2, piece, width), BF),
            pltpu.VMEM((nz, 2, piece, width), BF),
            *[pltpu.VMEM((nz, piece, width), BF) for _ in range(4)],
            *sems,
        ],
        32,
        part,
    )


def total_kernel(axes, x_ref, out_ref, *scratch):
    greet(partners_of(axes))
    value = x_ref[...]
    sends = []
    for stage, axis in enumerate(axes):
        slots, send_sems, recv_sems = scratch[3 * stage : 3 * stage + 3]
        size = lax.axis_size(axis)
        me = lax.axis_index(axis)
        slots[me] = value
        copies = []
        for d in range(1, size):
            copy = remote(
                slots.at[me], slots.at[me], send_sems.at[d], recv_sems.at[d], {axis: flip(axis, d)}
            )
            copy.start()
            copies.append(copy)
        for copy in copies:
            copy.wait_recv()
        value = slots[0]
        for n in range(1, size):
            value = value + slots[n]
        sends += copies
    out_ref[...] = value
    for copy in sends:
        copy.wait_send()


def total(terms, axes, identity):
    axes = tuple(a for a in axes if lax.axis_size(a) > 1)
    scratch = []
    for axis in axes:
        size = lax.axis_size(axis)
        scratch += [pltpu.VMEM((size, *terms.shape), F32), DMA((size,)), DMA((size,))]
    return call(
        functools.partial(total_kernel, axes),
        identity,
        jax.ShapeDtypeStruct(terms.shape, F32),
        [pltpu.VMEM],
        pltpu.VMEM,
        scratch,
        16,
        terms,
    )


def head_total(terms):
    return total(terms.reshape(-1, 128), (CORE, TP, "z"), 3).reshape(terms.shape)


def all_total(terms):
    size = terms.shape[0]
    padded = jnp.pad(terms, (0, -size % 1024)).reshape(-1, 128)
    return total(padded, (CORE, TP, "y", "z", "ch"), 4).reshape(-1)[:size]


def columns(ref, slot, count):
    return ref.at[:, pl.ds(pl.multiple_of(slot * count, 128), count)]


def intake_kernel(nz, count, tok_ref, *refs):
    w_refs, refs = refs[:count], refs[count:]
    tok_out, refs = refs[0], refs[1:]
    o_refs, refs = refs[:count], refs[count:]
    tok_buf, refs = refs[0], refs[1:]
    bufs, refs = refs[:count], refs[count:]
    tl, tzs, tzr, txs, txr, tcs, tcr, wl, wzs, wzr, wys, wyr = refs
    iz, iy, ic, it = (lax.axis_index(a) for a in ("z", "y", CORE, TP))
    across, beside, behind = {TP: 1 - it}, {CORE: 1 - ic}, {"y": 1 - iy}
    greet(partners_of(("z", "y", TP, CORE)))
    sends = []

    def push(src, dst, send_sem, recv_sem, partner):
        copy = remote(src, dst, send_sem, recv_sem, partner)
        copy.start()
        sends.append(copy)

    def arrived(ref, sem):
        remote(ref, ref, sem, sem, across).wait_recv()

    for d in range(1, nz):
        push(tok_ref.at[it], tok_out.at[iz, ic, it], tzs.at[d], tzr.at[d], {"z": flip("z", d)})
    push(tok_ref, tok_out.at[iz, ic], tcs.at[0, 0], tcr.at[0, 0], beside)
    tok_load = pltpu.make_async_copy(tok_ref, tok_buf, tl.at[0])
    tok_load.start()
    widths = [o.shape[-1] for o in o_refs]
    loads = []
    for k, (w, o) in enumerate(zip(w_refs, o_refs)):
        own = columns(w, iz * 2 + ic, widths[k])
        push(own, o.at[iz, iy], wys.at[k, 0], wyr.at[k, 0], behind)
        for d in range(1, nz):
            other = flip("z", d)
            push(
                columns(w, other * 2 + ic, widths[k]),
                o.at[iz, iy],
                wzs.at[k, d],
                wzr.at[k, d],
                {"z": other},
            )
        load = pltpu.make_async_copy(own, bufs[k], wl.at[k])
        load.start()
        loads.append(load)
    tok_load.wait()
    stores = [pltpu.make_async_copy(tok_buf, tok_out.at[iz, ic], tl.at[1])]
    stores[0].start()
    for d in range(1, nz):
        block = tok_out.at[flip("z", d), ic, it]
        arrived(block, tzr.at[d])
        push(block, block, txs.at[d], txr.at[d], across)
        push(block, block, tcs.at[d, 0], tcr.at[d, 0], beside)

    def forward(k):
        for d in range(1, nz):
            block = o_refs[k].at[flip("z", d), iy]
            arrived(block, wzr.at[k, d])
            push(block, block, wys.at[k, d], wyr.at[k, d], behind)

    first = min(3, count)
    for k in range(first):
        forward(k)
    for d in range(1, nz):
        block = tok_out.at[flip("z", d), ic, 1 - it]
        arrived(block, txr.at[d])
        push(block, block, tcs.at[d, 1], tcr.at[d, 1], beside)
    for k, load in enumerate(loads):
        load.wait()
        store = pltpu.make_async_copy(bufs[k], o_refs[k].at[iz, iy], wl.at[k])
        store.start()
        stores.append(store)
    for k in range(first, count):
        forward(k)
    arrived(tok_out.at[iz, 1 - ic], tcr.at[0, 0])
    for d in range(1, nz):
        for half in range(2):
            side = it if half == 0 else 1 - it
            arrived(tok_out.at[flip("z", d), 1 - ic, side], tcr.at[d, half])
    for k in range(count):
        for d in range(nz):
            source = flip("z", d) if d else iz
            arrived(o_refs[k].at[source, 1 - iy], wyr.at[k, d])
    for copy in sends:
        copy.wait_send()
    for store in stores:
        store.wait()


def intake(token_rows, weights):
    nz = lax.axis_size("z")
    count = len(weights)
    own_rows, width = token_rows.shape
    rows = weights[0].shape[0]
    parts = [w.shape[1] // (2 * nz) for w in weights]
    piece = own_rows // 2
    out_shape = [jax.ShapeDtypeStruct((nz, 2, 2, piece, width), BF)] + [
        jax.ShapeDtypeStruct((nz, 2, rows, c), BF) for c in parts
    ]
    got = call(
        functools.partial(intake_kernel, nz, count),
        5,
        out_shape,
        [pl.ANY] * (count + 1),
        [pl.ANY] * (count + 1),
        [
            pltpu.VMEM((2, piece, width), BF),
            *[pltpu.VMEM((rows, c), BF) for c in parts],
            DMA((2,)),
            *[DMA((nz,)) for _ in range(4)],
            *[DMA((nz, 2)) for _ in range(2)],
            DMA((count,)),
            *[DMA((count, nz)) for _ in range(4)],
        ],
        16,
        token_rows.reshape(2, piece, width),
        *weights,
    )
    return got[0].reshape(-1, width), [g.reshape(-1, g.shape[-1]) for g in got[1:]]


def outlet_kernel(nz, count, *refs):
    g_refs, refs = refs[:count], refs[count:]
    o_refs, refs = refs[:count], refs[count:]
    own, refs = refs[:count], refs[count:]
    yin, refs = refs[:count], refs[count:]
    zout, refs = refs[:count], refs[count:]
    ls, ys, yr, zs, zr, cs, cr, os = refs
    iz, iy, ic = (lax.axis_index(a) for a in ("z", "y", CORE))
    beside, behind = {CORE: 1 - ic}, {"y": 1 - iy}
    greet(partners_of(("z", "y", CORE)))
    sends, loads, pairs, stores = [], {}, {}, []

    def push(src, dst, send_sem, recv_sem, partner):
        copy = remote(src, dst, send_sem, recv_sem, partner)
        copy.start()
        sends.append(copy)
        return copy

    order = [(k, d) for k in range(count) for d in range(nz - 1, -1, -1)]
    widths = [g.shape[-1] for g in g_refs]
    for k, d in order:
        target = flip("z", d) if d else iz
        pairs[k, d] = push(
            g_refs[k].at[target, 1 - iy], yin[k].at[d], ys.at[k, d], yr.at[k, d], behind
        )
        loads[k, d] = pltpu.make_async_copy(g_refs[k].at[target, iy], own[k].at[d], ls.at[k, d])
        loads[k, d].start()

    def relay(k, d):
        block = columns(o_refs[k], flip("z", d) * 2 + ic, widths[k])
        remote(block, block, zr.at[k, d], zr.at[k, d], beside).wait_recv()
        push(block, block, cs.at[k, d], cr.at[k, d], beside)

    for n, (k, d) in enumerate(order):
        loads[k, d].wait()
        pairs[k, d].wait_recv()
        zout[k][d] = (own[k][d].astype(F32) + yin[k][d].astype(F32)).astype(BF)
        mine = columns(o_refs[k], iz * 2 + ic, widths[k])
        if d:
            push(zout[k].at[d], mine, zs.at[k, d], zr.at[k, d], {"z": flip("z", d)})
        else:
            push(zout[k].at[d], mine, cs.at[k, d], cr.at[k, d], beside)
            store = pltpu.make_async_copy(zout[k].at[d], mine, os.at[k])
            store.start()
            stores.append(store)
            if k:
                for e in range(nz - 1, 0, -1):
                    relay(k - 1, e)
    for e in range(nz - 1, 0, -1):
        relay(count - 1, e)
    for k, d in order:
        source = flip("z", d) if d else iz
        block = columns(o_refs[k], source * 2 + 1 - ic, widths[k])
        remote(block, block, cr.at[k, d], cr.at[k, d], beside).wait_recv()
    for copy in sends:
        copy.wait_send()
    for store in stores:
        store.wait()


def outlet(grads, identity=6):
    nz = lax.axis_size("z")
    count = len(grads)
    parts = [g.shape[1] for g in grads]
    blocks = [g.astype(BF).reshape(nz, 2, -1, g.shape[1]) for g in grads]
    rows = blocks[0].shape[2]
    got = call(
        functools.partial(outlet_kernel, nz, count),
        identity,
        [jax.ShapeDtypeStruct((rows, 2 * nz * c), BF) for c in parts],
        [pl.ANY] * count,
        [pl.ANY] * count,
        [
            *[pltpu.VMEM((nz, rows, c), BF) for _ in range(3) for c in parts],
            *[DMA((count, nz)) for _ in range(7)],
            DMA((count,)),
        ],
        32,
        *blocks,
    )
    if lax.axis_size("ch") > 1:
        got = lax.psum(tuple(got), "ch")
    return [g.astype(F32) for g in got]


class Kernel:
    def __init__(self):
        self.ins, self.outs, self.scratch = [], [], []

    def inp(self, name, array, space=pl.ANY):
        self.ins.append((name, array, space))

    def out(self, name, shape, dtype, space=pl.ANY):
        self.outs.append((name, jax.ShapeDtypeStruct(shape, dtype), space))

    def mem(self, name, shape, dtype):
        self.scratch.append((name, pltpu.VMEM(shape, dtype)))

    def sem(self, name, *shape):
        self.scratch.append((name, DMA(shape)))

    def run(self, identity, body, limit):
        names = [n for n, *_ in self.ins + self.outs + self.scratch]

        def kernel(*refs):
            body(types.SimpleNamespace(**dict(zip(names, refs))))

        got = call(
            kernel,
            identity,
            [shape for _, shape, _ in self.outs],
            [space for *_, space in self.ins],
            [space for *_, space in self.outs],
            [made for _, made in self.scratch],
            limit,
            *[array for _, array, _ in self.ins],
        )
        return {n: g for (n, *_), g in zip(self.outs, got)}


class Flow:
    def __init__(self):
        self.sends, self.inner_sends = [], []
        self.iz, self.iy, self.ic, self.it = (
            lax.axis_index(a) for a in ("z", "y", CORE, TP)
        )
        self.across = {TP: 1 - self.it}
        self.beside = {CORE: 1 - self.ic}
        self.behind = {"y": 1 - self.iy}
        self.near, self.mid = {"z": flip("z", 1)}, {"z": 3 - self.iz}
        self.role = lax.rem((self.iz + 1) // 2, 2)
        self.inner = self.role == 1

    def at(self, d):
        return flip("z", d) if d else self.iz

    def line(self, s):
        side = self.iz // 2
        return (self.iz, self.near["z"], 2 - side, 3 - 3 * side)[s]

    def push(self, src, dst, send_sem, recv_sem, partner):
        copy = remote(src, dst, send_sem, recv_sem, partner)
        copy.start()
        self.sends.append(copy)
        return copy

    def push_inner(self, src, dst, send_sem, recv_sem, partner):
        copy = remote(src, dst, send_sem, recv_sem, partner)
        pl.when(self.inner)(copy.start)
        self.inner_sends.append(copy)

    def pass_on(self, s, block, send_sems, recv_sems):
        partner, number = ((self.mid, 3), (self.near, 2), (self.near, 3))[s - 1]
        self.push_inner(block, block, send_sems.at[s + 2], recv_sems.at[number], partner)

    def arrived(self, ref, sem):
        remote(ref, ref, sem, sem, self.across).wait_recv()

    def finish(self):
        for copy in self.sends:
            copy.wait_send()
        if self.inner_sends:

            @pl.when(self.inner)
            def _():
                for copy in self.inner_sends:
                    copy.wait_send()

        self.sends, self.inner_sends = [], []


def greet_line():
    flow = Flow()
    barrier = pltpu.get_barrier_semaphore()
    for partner in (flow.near, flow.across, flow.beside):
        pl.semaphore_signal(barrier, inc=1, device_id=partner, device_id_type=MESH)

    @pl.when(flow.inner)
    def _():
        pl.semaphore_signal(barrier, inc=1, device_id=flow.mid, device_id_type=MESH)

    pl.semaphore_wait(barrier, 3 + flow.role)


def stripe(ref, z, core, tp, piece):
    start = pl.multiple_of((core * 2 + tp) * piece, piece)
    return ref.at[z, pl.ds(start, piece)]


class Gather(Flow):
    @staticmethod
    def setup(k, name, rows, out=False):
        piece, width = rows.shape
        k.inp(name + "_x", rows)
        (k.out if out else k.mem)(name, (4, 4 * piece, width), rows.dtype)
        k.sem(name + "_own")
        k.sem(name + "_zs", 6)
        for s in ("_zr", "_xs", "_xr"):
            k.sem(name + s, 4)
        k.sem(name + "_cs", 4, 2)
        k.sem(name + "_cr", 4, 2)

    def __init__(self, r, name):
        super().__init__()
        self.x, self.buf = getattr(r, name + "_x"), getattr(r, name)
        self.own_sem, self.zs, self.zr, self.xs, self.xr, self.cs, self.cr = (
            getattr(r, name + s) for s in ("_own", "_zs", "_zr", "_xs", "_xr", "_cs", "_cr")
        )
        self.piece = self.x.shape[0]

    def block(self, z, core, tp):
        return stripe(self.buf, z, core, tp, self.piece)

    def start(self):
        own = self.block(self.iz, self.ic, self.it)
        self.push(self.x, own, self.zs.at[1], self.zr.at[1], self.near)
        self.push_inner(self.x, own, self.zs.at[2], self.zr.at[2], self.mid)
        self.push(self.x, own, self.xs.at[0], self.xr.at[0], self.across)
        self.push(self.x, own, self.cs.at[0, 0], self.cr.at[0, 0], self.beside)
        self.local = pltpu.make_async_copy(self.x, own, self.own_sem)
        self.local.start()

    def from_across(self, s):
        block = self.block(self.line(s), self.ic, 1 - self.it)
        self.arrived(block, self.xr.at[s])
        self.push(block, block, self.cs.at[s, 1], self.cr.at[s, 1], self.beside)

    def advance(self, s):
        if s < 4:
            block = self.block(self.line(s), self.ic, self.it)
            self.arrived(block, self.zr.at[s])
            self.pass_on(s, block, self.zs, self.zr)
            self.push(block, block, self.xs.at[s], self.xr.at[s], self.across)
            self.push(block, block, self.cs.at[s, 0], self.cr.at[s, 0], self.beside)
        self.from_across(s - 1)

    def ready(self, s):
        if s == 0:
            self.local.wait()
        for half in range(2):
            side = self.it if half == 0 else 1 - self.it
            self.arrived(self.block(self.line(s), 1 - self.ic, side), self.cr.at[s, half])


class Scatter(Flow):
    @staticmethod
    def setup(k, name, piece, width, partial=None):
        if partial is None:
            k.mem(name + "_p", (4, 4 * piece, width), BF)
        else:
            k.inp(name + "_p", partial)
            k.mem(name + "_m", (4, 2 * piece, width), BF)
            k.sem(name + "_ls", 4)
        k.mem(name + "_c", (4, 2 * piece, width), BF)
        for s in ("_xo", "_xi", "_zo"):
            k.mem(name + s, (4, piece, width), BF)
        k.mem(name + "_zi", (6, piece, width), BF)
        for s in ("_cs", "_cr", "_xs", "_xr", "_zs"):
            k.sem(name + s, 4)
        k.sem(name + "_zr", 6)

    def __init__(self, r, name, out):
        super().__init__()
        self.out = out
        self.p, self.c, self.xo, self.xi, self.zo, self.zi = (
            getattr(r, name + s) for s in ("_p", "_c", "_xo", "_xi", "_zo", "_zi")
        )
        self.cs, self.cr, self.xs, self.xr, self.zs, self.zr = (
            getattr(r, name + s) for s in ("_cs", "_cr", "_xs", "_xr", "_zs", "_zr")
        )
        self.m, self.ls = getattr(r, name + "_m", None), getattr(r, name + "_ls", None)
        self.piece = self.xo.shape[1]
        self.core_copy, self.across_copy, self.loads = {}, {}, {}

    def rows(self, core):
        return pl.ds(pl.multiple_of(core * 2 * self.piece, 2 * self.piece), 2 * self.piece)

    def begin(self, s):
        part = s if self.m is None else self.line(s)
        self.core_copy[s] = self.push(
            self.p.at[part, self.rows(1 - self.ic)],
            self.c.at[s],
            self.cs.at[s],
            self.cr.at[s],
            self.beside,
        )
        if self.m is not None:
            self.loads[s] = pltpu.make_async_copy(
                self.p.at[part, self.rows(self.ic)], self.m.at[s], self.ls.at[s]
            )
            self.loads[s].start()

    def add(self, s, side):
        rows = pl.ds(pl.multiple_of(side * self.piece, self.piece), self.piece)
        if self.m is not None:
            own = self.m[s, rows]
        else:
            start = pl.multiple_of((self.ic * 2 + side) * self.piece, self.piece)
            own = self.p[s, pl.ds(start, self.piece)]
        return own.astype(F32) + self.c[s, rows].astype(F32)

    def cross(self, s):
        if s in self.loads:
            self.loads[s].wait()
        self.core_copy[s].wait_recv()
        self.xo[s] = self.add(s, 1 - self.it).astype(BF)
        self.across_copy[s] = self.push(
            self.xo.at[s], self.xi.at[s], self.xs.at[s], self.xr.at[s], self.across
        )

    def leave(self, s):
        self.across_copy[s].wait_recv()

        def value():
            return self.add(s, self.it) + self.xi[s].astype(F32)

        if s == 0:
            self.out[...] = value()
            return
        came = (None, 4, 2, 3)[s]

        @pl.when(self.inner)
        def _():
            self.arrived(self.zi.at[came], self.zr.at[came])
            self.zo[s] = (value() + self.zi[came].astype(F32)).astype(BF)

        @pl.when(self.role == 0)
        def _():
            self.zo[s] = value().astype(BF)

        place = s + self.role * (None, -1, 3, 1)[s]
        partner = self.near["z"]
        if s > 1:
            partner = partner + self.role * (self.mid["z"] - partner)
        self.push(
            self.zo.at[s], self.zi.at[place], self.zs.at[s], self.zr.at[place], {"z": partner}
        )

    def end(self):
        @pl.when(self.inner)
        def _():
            for place in (1, 5):
                self.arrived(self.zi.at[place], self.zr.at[place])
                self.out[...] += self.zi[place].astype(F32)

        @pl.when(self.role == 0)
        def _():
            self.arrived(self.zi.at[0], self.zr.at[0])
            self.out[...] += self.zi[0].astype(F32)


class Total(Flow):
    @staticmethod
    def setup(k, name, shape, axes):
        for axis in axes:
            size = lax.axis_size(axis)
            k.mem(f"{name}_{axis}", (size, *shape), F32)
            k.sem(f"{name}_{axis}_s", size)
            k.sem(f"{name}_{axis}_r", size)

    def __init__(self, r, name):
        super().__init__()
        self.r, self.name = r, name

    def send(self, axis, value):
        slots, ss, rs = (getattr(self.r, f"{self.name}_{axis}{s}") for s in ("", "_s", "_r"))
        me = lax.axis_index(axis)
        slots[me] = value
        self.copies = [
            self.push(slots.at[me], slots.at[me], ss.at[d], rs.at[d], {axis: flip(axis, d)})
            for d in range(1, lax.axis_size(axis))
        ]
        self.slots = slots

    def receive(self):
        for copy in self.copies:
            copy.wait_recv()
        value = self.slots[0]
        for n in range(1, self.slots.shape[0]):
            value = value + self.slots[n]
        return value


class Outlet(Flow):
    @staticmethod
    def setup(k, name, grads, nz, inside=False):
        for n, grad in enumerate(grads):
            rows, cols = grad.shape[0] // (2 * nz), grad.shape[1]
            if inside:
                k.mem(f"{name}_g{n}", (nz, 2, rows, cols), BF)
            else:
                k.inp(f"{name}_g{n}", grad.astype(BF).reshape(nz, 2, rows, cols))
                k.mem(f"{name}_own{n}", (nz, rows, cols), BF)
            k.out(f"{name}_o{n}", (rows, 2 * nz * cols), BF)
            for s in ("yin", "zout"):
                k.mem(f"{name}_{s}{n}", (nz, rows, cols), BF)
        for s in ("ls", "ys", "yr", "zs", "zr", "cs", "cr"):
            k.sem(f"{name}_{s}", len(grads), nz)
        k.sem(f"{name}_os", len(grads))

    def __init__(self, r, name, count, nz):
        super().__init__()
        self.nz, self.count = nz, count
        self.g, self.o, self.own, self.yin, self.zout = (
            [getattr(r, f"{name}_{s}{n}", None) for n in range(count)]
            for s in ("g", "o", "own", "yin", "zout")
        )
        self.ls, self.ys, self.yr, self.zs, self.zr, self.cs, self.cr, self.os = (
            getattr(r, f"{name}_{s}") for s in ("ls", "ys", "yr", "zs", "zr", "cs", "cr", "os")
        )
        self.loads, self.pairs, self.stores = {}, {}, []

    def slot(self, k, z, core):
        return columns(self.o[k], z * 2 + core, self.g[k].shape[-1])

    def start(self, k):
        for d in range(self.nz - 1, -1, -1):
            target = self.at(d)
            self.pairs[k, d] = self.push(
                self.g[k].at[target, 1 - self.iy],
                self.yin[k].at[d],
                self.ys.at[k, d],
                self.yr.at[k, d],
                self.behind,
            )
            if self.own[k] is not None:
                self.loads[k, d] = pltpu.make_async_copy(
                    self.g[k].at[target, self.iy], self.own[k].at[d], self.ls.at[k, d]
                )
                self.loads[k, d].start()

    def combine(self, k):
        mine = self.slot(k, self.iz, self.ic)
        for d in range(self.nz - 1, -1, -1):
            self.pairs[k, d].wait_recv()
            if self.own[k] is not None:
                self.loads[k, d].wait()
                own = self.own[k][d]
            else:
                own = self.g[k][self.at(d), self.iy]
            self.zout[k][d] = (own.astype(F32) + self.yin[k][d].astype(F32)).astype(BF)
            src = self.zout[k].at[d]
            if d:
                self.push(src, mine, self.zs.at[k, d], self.zr.at[k, d], {"z": self.at(d)})
            else:
                self.push(src, mine, self.cs.at[k, d], self.cr.at[k, d], self.beside)
                store = pltpu.make_async_copy(src, mine, self.os.at[k])
                store.start()
                self.stores.append(store)

    def relay(self, k):
        for d in range(1, self.nz):
            block = self.slot(k, self.at(d), self.ic)
            self.arrived(block, self.zr.at[k, d])
            self.push(block, block, self.cs.at[k, d], self.cr.at[k, d], self.beside)

    def end(self):
        for k in range(self.count):
            for d in range(self.nz):
                self.arrived(self.slot(k, self.at(d), 1 - self.ic), self.cr.at[k, d])
        for store in self.stores:
            store.wait()
        self.finish()


def gather_line(rows):
    k = Kernel()
    Gather.setup(k, "all", rows, out=True)

    def body(r):
        greet_line()
        gather = Gather(r, "all")
        gather.start()
        for s in range(1, 5):
            gather.advance(s)
        for s in range(4):
            gather.ready(s)
        gather.finish()

    return k.run(1, body, 16)["all"].reshape(-1, rows.shape[1])


def scatter_line(partial):
    width = partial.shape[1]
    piece = partial.shape[0] // 16
    k = Kernel()
    Scatter.setup(k, "rs", piece, width, partial.astype(BF).reshape(4, 4 * piece, width))
    k.out("sum", (piece, width), F32, pltpu.VMEM)

    def body(r):
        greet_line()
        scatter = Scatter(r, "rs", r.sum)
        order = (3, 2, 1, 0)
        for s in order:
            scatter.begin(s)
        for s in order:
            scatter.cross(s)
        for s in order:
            scatter.leave(s)
        scatter.end()
        scatter.finish()

    return k.run(2, body, 32)["sum"]


def exact(a, b, dims):
    return lax.dot_general(
        a, b, (dims, ((), ())), precision=lax.Precision.HIGHEST, preferred_element_type=F32
    )


def picker(width):
    row = lax.broadcasted_iota(jnp.int32, (8, width), 0)
    part = lax.broadcasted_iota(jnp.int32, (8, width), 1) // HD
    return jnp.where(row == part, 1.0, 0.0).astype(F32)


def row_sums(first, second):
    both = jnp.concatenate([first, second], axis=1)
    return exact(picker(2 * HD), both, ((1,), (1,)))


def spread(sums, which):
    row = lax.broadcasted_iota(jnp.int32, (8, HD), 0)
    one = jnp.where(row == which, 1.0, 0.0).astype(F32)
    return exact(sums, one, ((0,), (0,)))


def softmax_rows(query, key, length):
    count = query.shape[0]
    row = lax.broadcasted_iota(jnp.int32, (count, count), 0)
    col = lax.broadcasted_iota(jnp.int32, (count, count), 1)
    scores = mm_nt(query, key) * (1.0 / math.sqrt(HD))
    scores = jnp.where((col <= row) & (col < length), scores, NEGATIVE)
    exponent = jnp.exp(scores - jnp.max(scores, axis=-1, keepdims=True))
    return exponent / jnp.sum(exponent, axis=-1, keepdims=True)


def load_all(pairs, sems):
    copies = []
    for n, (src, dst) in enumerate(pairs):
        copy = pltpu.make_async_copy(src, dst, sems.at[n])
        copy.start()
        copies.append(copy)
    return copies


def attention_back(
    branch, wide, wo, wqkv, saved, tokens_all, residual_grad, stream_rows, terms, gains, tables,
    seq_lengths,
):
    nz = lax.axis_size("z")
    piece, width = branch.shape
    rows = 4 * piece
    block = width // (2 * nz)
    padded = jnp.pad(terms, (0, -terms.shape[0] % 1024)).reshape(-1, 128)
    lanes = width // 128
    sum_axes = (CORE, TP, "y", "z")
    k = Kernel()
    Gather.setup(k, "ball", branch)
    Outlet.setup(k, "wide", wide, nz)
    slim = [jax.ShapeDtypeStruct((width, HD), BF)] * 4
    Outlet.setup(k, "slim", slim, nz, inside=True)
    Scatter.setup(k, "rs", piece, width)
    Total.setup(k, "tot", (nz, 8, rows), (CORE, TP, "z"))
    Total.setup(k, "sum", padded.shape, sum_axes)
    k.inp("wo", wo)
    k.inp("wqkv", wqkv)
    k.inp("tokens", tokens_all)
    k.mem("tokens_m", tokens_all.shape, BF)
    names = ("q", "k", "v", "att", "nq", "nk", "qs", "ks")
    for name, array in zip(names, saved):
        k.inp(name, array)
        k.mem(name + "_m", array.shape, array.dtype)
    k.mem("wo_m", wo.shape, BF)
    k.mem("wqkv_m", wqkv.shape, BF)
    k.inp("res", residual_grad)
    k.mem("res_m", (piece, width), F32)
    k.inp("stream", stream_rows)
    k.mem("stream_m", (piece, width), BF)
    k.sem("ld", len(names) + 5)
    k.inp("terms", padded, pltpu.VMEM)
    k.mem("terms_m", padded.shape, F32)
    k.out("terms_out", padded.shape, F32, pltpu.VMEM)
    k.inp("gains", gains, pltpu.VMEM)
    k.inp("tables", tables, pltpu.VMEM)
    k.inp("lens", seq_lengths, pltpu.SMEM)
    k.mem("wqk", (nz, 2, rows, HD), F32)
    k.mem("low", (nz, rows, 3 * HD), BF)
    k.mem("dots", (nz, 8, rows), F32)
    k.mem("norms", (2, HD), F32)
    k.mem("grad", (piece, width), F32)
    k.out("grad_out", (2, piece, width), F32)
    k.out("stream_out", (2, piece, width), BF)
    k.sem("xs", 2)
    k.sem("xr", 2)
    k.sem("ss", 2)

    def body(r):
        greet(partners_of(("z", "y", TP, CORE)))
        gather, outlet_flow = Gather(r, "ball"), Outlet(r, "wide", len(wide), nz)
        slim_flow, own = Outlet(r, "slim", len(slim), nz), Flow()
        scatter, total_flow = Scatter(r, "rs", r.grad), Total(r, "tot")
        sum_flow = Total(r, "sum")
        gather.start()
        for n in range(len(wide)):
            outlet_flow.start(n)
        names_in = ("wo", "wqkv", *names, "tokens", "res", "stream")
        loads = load_all([(getattr(r, n), getattr(r, n + "_m")) for n in names_in], r.ld)
        scale = 1.0 / math.sqrt(HD)
        cosine, sine = r.tables[0], r.tables[1]
        gather.advance(1)
        for copy in loads:
            copy.wait()
        r.norms[...] = jnp.zeros_like(r.norms)

        def compute(z):
            grad_low = mm(r.ball[z], r.wo_m[...]).astype(BF)
            query, key, value = r.q_m[z], r.k_m[z], r.v_m[z]
            probability = softmax_rows(query, key, r.lens[z])
            grad_prob = mm_nt(grad_low, value)
            row_dots = jnp.sum(probability * grad_prob, axis=-1, keepdims=True)
            grad_scores = (probability * (grad_prob - row_dots)).astype(BF)
            grad_q = rotate_back(mm(grad_scores, key) * scale, cosine, sine)
            grad_k = rotate_back(mm_tn(grad_scores, query) * scale, cosine, sine)
            grad_v = mm_tn(probability.astype(BF), grad_low)
            r.low[z, :, 2 * HD :] = grad_v.astype(BF)
            nq, nk = r.nq_m[z], r.nk_m[z]
            r.norms[0:1] += jnp.sum(grad_q * nq, axis=0, keepdims=True)
            r.norms[1:2] += jnp.sum(grad_k * nk, axis=0, keepdims=True)
            wq, wk = grad_q * r.gains[0:1], grad_k * r.gains[1:2]
            r.wqk[z, 0] = wq
            r.wqk[z, 1] = wk
            r.dots[z] = row_sums(wq * nq, wk * nk)

        def weight_blocks(left, right, place):
            @pl.loop(0, 2 * nz)
            def _(f):
                cols = pl.ds(pl.multiple_of(f * block, block), block)
                made = mm_tn(left[0, :, cols], right[0])
                for z in range(1, nz):
                    made = made + mm_tn(left[z, :, cols], right[z])
                made = made.astype(BF)
                for n, grad in enumerate(place):
                    grad[f // 2, lax.rem(f, 2)] = made[:, n * HD : (n + 1) * HD]

        for d in range(nz):
            if d + 2 <= nz:
                gather.advance(d + 2)
            if d == nz - 2:
                own.push(
                    r.stream, r.stream_out.at[own.it], r.xs.at[0], r.xr.at[0], own.across
                )
            gather.ready(d)
            compute(gather.line(d))
            if d == nz - 2:
                outlet_flow.combine(0)
        r.terms_m[...] = r.terms[...]
        slot = 2 * lanes + own.it * (lanes // 2) + own.iz * 2 + own.ic
        for n in range(2):
            r.terms_m[pl.ds(slot + n * lanes, 1)] = r.norms[n : n + 1]
        total_flow.send(CORE, r.dots[...])
        sum_flow.send(CORE, r.terms_m[...])
        value, other = total_flow.receive(), sum_flow.receive()
        total_flow.send(TP, value)
        sum_flow.send(TP, other)
        value, other = total_flow.receive(), sum_flow.receive()
        total_flow.send("z", value)
        sum_flow.send("y", other)
        outlet_flow.combine(1)
        weight_blocks(r.ball, r.att_m, [slim_flow.g[3]])
        slim_flow.start(3)
        r.dots[...] = total_flow.receive()
        order = list(range(nz - 1, -1, -1))
        for n, d in enumerate(order):
            z = gather.line(d)
            sums = r.dots[z] * (1.0 / width)
            for j, (normed, factor) in enumerate(((r.nq_m, r.qs_m), (r.nk_m, r.ks_m))):
                low = factor[z] * (r.wqk[z, j] - normed[z] * spread(sums, j))
                r.low[z, :, j * HD : (j + 1) * HD] = low.astype(BF)
            r.rs_p[d] = mm_nt(r.low[z], r.wqkv_m[...]).astype(BF)
            scatter.begin(d)
            if n:
                scatter.cross(order[n - 1])
            if n > 1:
                scatter.leave(order[n - 2])
        scatter.cross(0)
        scatter.leave(1)
        scatter.leave(0)
        outlet_flow.combine(2)
        weight_blocks(r.tokens_m, r.low, slim_flow.g[:3])
        for n in range(3):
            slim_flow.start(n)
        sum_flow.send("z", sum_flow.receive())
        slim_flow.combine(3)
        outlet_flow.relay(0)
        outlet_flow.relay(1)
        scatter.end()
        r.res_m[...] += r.grad[...]
        own.push(r.res_m, r.grad_out.at[own.it], r.xs.at[1], r.xr.at[1], own.across)
        stores = []
        for n, (src, out) in enumerate(((r.stream_m, r.stream_out), (r.res_m, r.grad_out))):
            stores.append(pltpu.make_async_copy(src, out.at[own.it], r.ss.at[n]))
            stores[-1].start()
        for n in range(3):
            slim_flow.combine(n)
        r.terms_out[...] = sum_flow.receive()
        outlet_flow.relay(2)
        slim_flow.relay(3)
        for n in range(3):
            slim_flow.relay(n)
        outlet_flow.end()
        slim_flow.end()
        for n, out in enumerate((r.stream_out, r.grad_out)):
            own.arrived(out.at[1 - own.it], r.xr.at[n])
        for flow in (gather, scatter, total_flow, sum_flow, own):
            flow.finish()
        for copy in stores:
            copy.wait()

    got = k.run(7, body, 60)
    return (
        [got[f"slim_o{n}"].astype(F32) for n in range(4)]
        + [got[f"wide_o{n}"].astype(F32) for n in range(len(wide))],
        got["grad_out"].reshape(-1, width),
        got["stream_out"].reshape(-1, width),
        got["terms_out"].reshape(-1)[: terms.shape[0]],
    )


def attention_front(token_rows, weights, gains, tables, seq_lengths):
    nz = lax.axis_size("z")
    own_rows, width = token_rows.shape
    piece, rows = own_rows // 2, own_rows * 2
    w_rows = weights[0].shape[0]
    count = len(weights)
    parts = [w.shape[1] // (2 * nz) for w in weights]
    k = Kernel()
    Scatter.setup(k, "rs", piece, width)
    Total.setup(k, "tot", (nz, 8, rows), (CORE, TP, "z"))
    k.inp("tok", token_rows)
    for n, weight in enumerate(weights):
        k.inp(f"w{n}", weight)
    k.inp("gains", gains, pltpu.VMEM)
    k.inp("tables", tables, pltpu.VMEM)
    k.inp("lens", seq_lengths, pltpu.SMEM)
    k.mem("tall", (nz, rows, width), BF)
    k.mem("qkv", (nz, 2, w_rows, 3 * HD), BF)
    k.mem("wo", (nz, 2, w_rows, parts[3]), BF)
    for n in range(4, count):
        k.mem(f"b{n}", (w_rows, parts[n]), BF)
        k.out(f"o{n}", (nz, 2, w_rows, parts[n]), BF)
    k.mem("raw", (nz, rows, 3 * HD), F32)
    k.mem("dots", (nz, 8, rows), F32)
    saved = (("q", BF), ("k", BF), ("v", BF), ("nq", F32), ("nk", F32), ("qs", F32), ("ks", F32), ("att", BF))
    for name, kind in saved:
        k.mem(name + "_m", (nz, rows, HD), kind)
        k.out(name, (nz, rows, HD), kind)
    k.out("branch", (piece, width), F32, pltpu.VMEM)
    k.out("tokens", (nz, rows, width), BF)
    k.out("qkv_out", (nz, 2, w_rows, 3 * HD), BF)
    k.out("wo_out", (nz, 2, w_rows, parts[3]), BF)
    k.sem("tl")
    k.sem("tzs", 6)
    for s in ("tzr", "txs", "txr"):
        k.sem(s, nz)
    k.sem("tcs", nz, 2)
    k.sem("tcr", nz, 2)
    k.sem("wl", 2, count)
    for s in ("wzs", "wzr", "wys", "wyr"):
        k.sem(s, count, nz)
    k.sem("st", len(saved) + 1, nz)
    k.sem("sw", 2)

    def body(r):
        greet(partners_of(("z", "y", TP, CORE)))
        flow = Flow()
        iz, iy, ic, it = flow.iz, flow.iy, flow.ic, flow.it
        scatter, total_flow = Scatter(r, "rs", r.branch), Total(r, "tot")

        def block(z, core, tp):
            return stripe(r.tall, z, core, tp, piece)

        def pair(z, core):
            start = pl.multiple_of(core * own_rows, own_rows)
            return r.tall.at[z, pl.ds(start, own_rows)]

        tok_half = r.tok.at[pl.ds(pl.multiple_of(it * piece, piece), piece)]
        flow.push(tok_half, block(iz, ic, it), r.tzs.at[1], r.tzr.at[1], flow.near)
        flow.push_inner(tok_half, block(iz, ic, it), r.tzs.at[2], r.tzr.at[2], flow.mid)
        flow.push(r.tok, pair(iz, ic), r.tcs.at[0, 0], r.tcr.at[0, 0], flow.beside)
        tok_load = pltpu.make_async_copy(r.tok, pair(iz, ic), r.tl)
        tok_load.start()
        loads = {}

        def landing(n, z, y):
            if n < 3:
                return r.qkv.at[z, y, :, n * HD : (n + 1) * HD]
            return r.wo.at[z, y] if n == 3 else getattr(r, f"o{n}").at[z, y]

        def bring(n):
            weight = getattr(r, f"w{n}")
            own = columns(weight, iz * 2 + ic, parts[n])
            for d in range(nz - 1, 0, -1):
                other = flow.at(d)
                flow.push(
                    columns(weight, other * 2 + ic, parts[n]),
                    landing(n, iz, iy),
                    r.wzs.at[n, d],
                    r.wzr.at[n, d],
                    {"z": other},
                )
            flow.push(own, landing(n, iz, iy), r.wys.at[n, 0], r.wyr.at[n, 0], flow.behind)
            dst = landing(n, iz, iy) if n < 4 else getattr(r, f"b{n}")
            loads[n] = pltpu.make_async_copy(own, dst, r.wl.at[0, n])
            loads[n].start()

        def forward(n):
            for d in range(1, nz):
                here = landing(n, flow.at(d), iy)
                flow.arrived(here, r.wzr.at[n, d])
                flow.push(here, here, r.wys.at[n, d], r.wyr.at[n, d], flow.behind)

        def complete(n):
            for d in range(nz):
                flow.arrived(landing(n, flow.at(d), 1 - iy), r.wyr.at[n, d])

        for n in range(min(5, count)):
            bring(n)
        for d in range(1, nz):
            here = block(flow.line(d), ic, it)
            flow.arrived(here, r.tzr.at[d])
            flow.pass_on(d, here, r.tzs, r.tzr)
            flow.push(here, here, r.txs.at[d], r.txr.at[d], flow.across)
            flow.push(here, here, r.tcs.at[d, 0], r.tcr.at[d, 0], flow.beside)
        for n in range(3):
            forward(n)
        for d in range(1, nz):
            here = block(flow.line(d), ic, 1 - it)
            flow.arrived(here, r.txr.at[d])
            flow.push(here, here, r.tcs.at[d, 1], r.tcr.at[d, 1], flow.beside)
        stores = []

        def save(n, src, dst, d):
            copy = pltpu.make_async_copy(src, dst, r.st.at[n, d])
            copy.start()
            stores.append(copy)

        for n in range(4):
            loads[n].wait()
        for n in range(3):
            complete(n)
        tok_load.wait()
        for d in range(nz):
            z = flow.line(d)
            if d == 0:
                flow.arrived(pair(iz, 1 - ic), r.tcr.at[0, 0])
            else:
                for half in range(2):
                    side = it if half == 0 else 1 - it
                    flow.arrived(block(z, 1 - ic, side), r.tcr.at[d, half])
            save(0, r.tall.at[z], r.tokens.at[z], d)
            raw = mm(r.tall[z], r.qkv[...].reshape(2 * nz * w_rows, 3 * HD))
            r.raw[z] = raw
            query, key = raw[:, :HD], raw[:, HD : 2 * HD]
            r.dots[z] = row_sums(query * query, key * key)
        total_flow.send(CORE, r.dots[...])
        forward(3)
        value = total_flow.receive()
        total_flow.send(TP, value)
        value = total_flow.receive()
        total_flow.send("z", value)
        for n in range(5, count):
            bring(n)
        for n in range(4, count):
            loads[n].wait()
            copy = pltpu.make_async_copy(getattr(r, f"b{n}"), landing(n, iz, iy), r.wl.at[1, n])
            copy.start()
            stores.append(copy)
        complete(3)
        for n, (src, dst) in enumerate(((r.qkv, r.qkv_out), (r.wo, r.wo_out))):
            copy = pltpu.make_async_copy(src, dst, r.sw.at[n])
            copy.start()
            stores.append(copy)
        r.dots[...] = lax.rsqrt(total_flow.receive() * (1.0 / width) + EPSILON)
        cosine, sine = r.tables[0], r.tables[1]
        order = list(range(nz - 1, -1, -1))
        for n, d in enumerate(order):
            z = flow.line(d)
            sums = r.dots[z]
            r.qs_m[z] = spread(sums, 0)
            r.ks_m[z] = spread(sums, 1)
            r.nq_m[z] = r.raw[z, :, :HD] * r.qs_m[z]
            r.nk_m[z] = r.raw[z, :, HD : 2 * HD] * r.ks_m[z]
            query = rotate(r.nq_m[z] * r.gains[0:1], cosine, sine).astype(BF)
            key = rotate(r.nk_m[z] * r.gains[1:2], cosine, sine).astype(BF)
            value = r.raw[z, :, 2 * HD :].astype(BF)
            r.q_m[z] = query
            r.k_m[z] = key
            r.v_m[z] = value
            probability = softmax_rows(query, key, r.lens[z]).astype(BF)
            r.att_m[z] = mm(probability, value).astype(BF)
            for m, (name, _) in enumerate(saved):
                save(m + 1, getattr(r, name + "_m").at[z], getattr(r, name).at[z], d)
            wo = r.wo[...].reshape(2 * nz * w_rows, parts[3])
            r.rs_p[d] = mm_nt(r.att_m[z], wo).astype(BF)
            scatter.begin(d)
            if n:
                scatter.cross(order[n - 1])
            if n > 1:
                scatter.leave(order[n - 2])
            if n == 0:
                forward(4)
        scatter.cross(0)
        forward(5)
        scatter.leave(1)
        scatter.leave(0)
        forward(6)
        scatter.end()
        for n in range(4, count):
            complete(n)
        for f in (flow, scatter, total_flow):
            f.finish()
        for copy in stores:
            copy.wait()

    return k.run(9, body, 60)


def local(
    tokens,
    lengths,
    weight_query,
    weight_key,
    weight_value,
    weight_out,
    weight_gate,
    weight_up,
    weight_down,
    post_attention,
    post_feedforward,
    query_norm,
    key_norm,
    cotangent,
):
    nz, ny, nch, ntp = (lax.axis_size(a) for a in ("z", "y", "ch", TP))
    iz, iy, ich, icore, itp = (lax.axis_index(a) for a in AXES)
    token_rows = tokens[0]
    own_rows, width = token_rows.shape
    piece = own_rows // ntp
    seq_rows = own_rows * 2
    total_rows = seq_rows * nz
    scale_factor = 1.0 / math.sqrt(HD)
    own_head = iz * 2 + icore
    qn = lax.dynamic_slice_in_dim(query_norm, own_head * HD, HD)
    kn = lax.dynamic_slice_in_dim(key_norm, own_head * HD, HD)
    seq_lengths = lax.dynamic_index_in_dim(lengths.reshape(nz, ny), iy, 1, keepdims=False)
    positions = ich * seq_rows + jnp.arange(seq_rows, dtype=jnp.int32)
    key_positions = jnp.arange(seq_rows * nch, dtype=jnp.int32)
    cosine, sine_table = rope_tables(positions)
    allowed = (key_positions[None, None, :] <= positions[None, :, None]) & (
        key_positions[None, None, :] < seq_lengths[:, None, None]
    )
    my_tokens = lax.dynamic_slice_in_dim(token_rows, itp * piece, piece, 0)
    my_cot = lax.dynamic_slice_in_dim(cotangent[0], itp * piece, piece, 0)
    my_pos = (ich * 2 + icore) * own_rows + itp * piece + jnp.arange(piece, dtype=jnp.int32)
    my_valid = (my_pos < lengths[iz * ny + iy]).astype(F32)[:, None]

    weights = (
        weight_query,
        weight_key,
        weight_value,
        weight_out,
        weight_gate,
        weight_up,
        weight_down,
    )
    fused = nch == 1 and nz == 4
    gather, scatter = (gather_line, scatter_line) if fused else (gather_rows, scatter_rows)
    by_seq = lambda a: a.reshape(nz, seq_rows, HD)
    gains, tables = jnp.stack([qn, kn]), jnp.stack([cosine, sine_table])
    if fused:
        front = attention_front(token_rows, weights, gains, tables, seq_lengths)
        branch_sum = front["branch"]
        wg, wu, wd = (front[f"o{n}"].reshape(width, -1) for n in (4, 5, 6))
    else:
        tokens_all, (wq, wk, wv, wo, wg, wu, wd) = intake(token_rows, weights)
        query_raw = mm(tokens_all, wq)
        key_raw = mm(tokens_all, wk)
        value_raw = mm(tokens_all, wv)
        squares = head_total(
            jnp.stack([jnp.sum(query_raw * query_raw, axis=-1), jnp.sum(key_raw * key_raw, axis=-1)])
        )
        scales = lax.rsqrt(squares / width + EPSILON)
        query_scale = scales[0][:, None]
        key_scale = scales[1][:, None]
        queries = rotate(by_seq(query_raw * query_scale * qn), cosine, sine_table).astype(BF)
        keys = rotate(by_seq(key_raw * key_scale * kn), cosine, sine_table).astype(BF)
        values = by_seq(value_raw).astype(BF)
        if nch > 1:
            keys_full = lax.all_gather(keys, "ch", axis=1, tiled=True)
            values_full = lax.all_gather(values, "ch", axis=1, tiled=True)
        else:
            keys_full, values_full = keys, values
        scores = (
            jnp.einsum(SCORE, queries, keys_full, preferred_element_type=F32) * scale_factor
        )
        scores = jnp.where(allowed, scores, NEGATIVE)
        exponent = jnp.exp(scores - jnp.max(scores, axis=-1, keepdims=True))
        probability = exponent / jnp.sum(exponent, axis=-1, keepdims=True)
        probability_low = probability.astype(BF)
        attended = jnp.einsum(APPLY, probability_low, values_full, preferred_element_type=F32)
        attended_low = attended.reshape(total_rows, HD).astype(BF)
        branch_sum = scatter_rows(mm_nt(attended_low, wo))
    attn_scale = lax.rsqrt(jnp.mean(branch_sum * branch_sum, axis=-1, keepdims=True) + EPSILON)
    attn_normed = branch_sum * attn_scale
    attention_branch = attn_normed * post_attention
    residual = my_tokens.astype(F32) + attention_branch
    residual_all = gather(residual.astype(BF))
    gate_value = mm(residual_all, wg)
    up_value = mm(residual_all, wu)
    sigmoid_gate = jax.nn.sigmoid(gate_value)
    silu_gate = gate_value * sigmoid_gate
    mixed_low = (silu_gate * up_value).astype(BF)
    down_sum = scatter(mm_nt(mixed_low, wd))
    ffn_scale = lax.rsqrt(jnp.mean(down_sum * down_sum, axis=-1, keepdims=True) + EPSILON)
    ffn_normed = down_sum * ffn_scale
    feedforward_branch = ffn_normed * post_feedforward
    stream = residual + feedforward_branch
    stat_terms = jnp.stack(
        [
            jnp.sum(my_valid * stream * stream),
            jnp.sum(my_valid * attention_branch * attention_branch),
            jnp.sum(my_valid * feedforward_branch * feedforward_branch),
        ]
    )
    grad_stream = my_cot * my_valid
    grad_post_ff = jnp.sum(grad_stream * ffn_normed, axis=0)
    scaled = grad_stream * post_feedforward
    grad_down_sum = ffn_scale * (
        scaled - ffn_normed * jnp.mean(scaled * ffn_normed, axis=-1, keepdims=True)
    )
    down_all = gather(grad_down_sum.astype(BF))
    grad_mixed = mm(down_all, wd)
    gate_low = (
        grad_mixed * up_value * sigmoid_gate * (1.0 + gate_value * (1.0 - sigmoid_gate))
    ).astype(BF)
    up_low = (grad_mixed * silu_gate).astype(BF)
    grad_wg = mm_tn(residual_all, gate_low)
    grad_wu = mm_tn(residual_all, up_low)
    grad_wd = mm_tn(down_all, mixed_low)
    grad_residual = grad_stream + scatter(mm_nt(gate_low, wg) + mm_nt(up_low, wu))
    grad_post_attn = jnp.sum(grad_residual * attn_normed, axis=0)
    scaled_attn = grad_residual * post_attention
    grad_branch = attn_scale * (
        scaled_attn - attn_normed * jnp.mean(scaled_attn * attn_normed, axis=-1, keepdims=True)
    )
    if not fused:
        branch_all = gather_rows(grad_branch.astype(BF))
        grad_att_low = mm(branch_all, wo).astype(BF)
        grad_wo = mm_tn(branch_all, attended_low)
        grad_att = by_seq(grad_att_low)
        grad_prob = jnp.einsum(SCORE, grad_att, values_full, preferred_element_type=F32)
        row_dots = jnp.sum(probability * grad_prob, axis=-1, keepdims=True)
        grad_scores = (probability * (grad_prob - row_dots)).astype(BF)
        grad_queries = (
            jnp.einsum(APPLY, grad_scores, keys_full, preferred_element_type=F32)
            * scale_factor
        )
        grad_keys = (
            jnp.einsum("bts,btd->bsd", grad_scores, queries, preferred_element_type=F32) * scale_factor
        )
        grad_values = jnp.einsum("bts,btd->bsd", probability_low, grad_att, preferred_element_type=F32)
        if nch > 1:
            grad_keys, grad_values = (
                lax.psum_scatter(g.astype(BF), "ch", scatter_dimension=1, tiled=True).astype(F32)
                for g in (grad_keys, grad_values)
            )
        value_grad_low = grad_values.reshape(total_rows, HD).astype(BF)
        grad_q_normed = rotate_back(grad_queries, cosine, sine_table).reshape(total_rows, HD)
        grad_k_normed = rotate_back(grad_keys, cosine, sine_table).reshape(total_rows, HD)
        query_weighted = grad_q_normed * qn
        key_weighted = grad_k_normed * kn
        dots = head_total(
            jnp.stack(
                [
                    jnp.sum(query_weighted * query_raw, axis=-1),
                    jnp.sum(key_weighted * key_raw, axis=-1),
                ]
            )
        )
        query_grad_low = (
            query_scale * (query_weighted - query_raw * query_scale**2 * (dots[0] / width)[:, None])
        ).astype(BF)
        key_grad_low = (
            key_scale * (key_weighted - key_raw * key_scale**2 * (dots[1] / width)[:, None])
        ).astype(BF)
        grad_qnorm = jnp.sum(grad_q_normed * query_raw * query_scale, axis=0)
        grad_knorm = jnp.sum(grad_k_normed * key_raw * key_scale, axis=0)
        grad_wq = mm_tn(tokens_all, query_grad_low)
        grad_wk = mm_tn(tokens_all, key_grad_low)
        grad_wv = mm_tn(tokens_all, value_grad_low)
        grad_rows = grad_residual + scatter_rows(
            mm_nt(query_grad_low, wq) + mm_nt(key_grad_low, wk) + mm_nt(value_grad_low, wv)
        )
    if fused:
        saved = tuple(front[n] for n in ("q", "k", "v", "att", "nq", "nk", "qs", "ks"))
        norms_wide = jnp.zeros((2 * width,), F32)
    else:
        slot = itp * (width // ntp) + own_head * HD
        zero_row = jnp.zeros((width,), F32)
        norms_wide = jnp.concatenate(
            [
                lax.dynamic_update_slice_in_dim(zero_row, grad_qnorm, slot, 0),
                lax.dynamic_update_slice_in_dim(zero_row, grad_knorm, slot, 0),
            ]
        )
    terms = jnp.concatenate([grad_post_attn, grad_post_ff, norms_wide, stat_terms])
    if fused:
        weight_grads, grad_input, output, summed = attention_back(
            grad_branch.astype(BF),
            (grad_wd, grad_wg, grad_wu),
            front["wo_out"].reshape(width, -1),
            front["qkv_out"].reshape(width, -1),
            saved,
            front["tokens"],
            grad_residual,
            stream.astype(BF),
            terms,
            gains,
            tables,
            seq_lengths,
        )
        weight_grads = [weight_grads[n] for n in (0, 1, 2, 3, 5, 6, 4)]
    else:
        weight_grads = outlet((grad_wq, grad_wk, grad_wv, grad_wo, grad_wg, grad_wu, grad_wd))
        grad_input = lax.all_gather(grad_rows, TP, axis=0, tiled=True)
        output = lax.all_gather(stream.astype(BF), TP, axis=0, tiled=True)
        summed = all_total(terms)
    half = width // ntp
    qn_sum = lax.dynamic_slice_in_dim(summed, 2 * width + itp * half, half)
    kn_sum = lax.dynamic_slice_in_dim(summed, 3 * width + itp * half, half)
    token_count = jnp.sum(lengths.astype(F32))
    root_means = jnp.sqrt(summed[4 * width :] / (token_count * width))
    return (
        output[None],
        grad_input[None],
        *weight_grads,
        summed[:width],
        summed[width : 2 * width],
        qn_sum,
        kn_sum,
        root_means,
    )


def solution(mesh):
    n_fsdp, n_ctx, n_tp = (mesh.shape[a] for a in ("fsdp", "ctx", TP))
    fine = Mesh(mesh.devices.reshape(n_fsdp // 2, 2, n_ctx // 2, 2, n_tp), AXES)
    fsdp, ctx = ("z", "y"), ("ch", CORE)
    rows = P(fsdp, ctx, None)
    weight = P(fsdp, TP)
    return jax.shard_map(
        local,
        mesh=fine,
        in_specs=(rows, P(), *([weight] * 7), P(), P(), P(TP), P(TP), rows),
        out_specs=(rows, rows, *([weight] * 7), P(), P(), P(TP), P(TP), P()),
        check_vma=False,
    )
```

```python
import functools
import math
import types

import jax
import jax.numpy as jnp
from jax import lax
from jax.experimental import pallas as pl
from jax.experimental.pallas import tpu as pltpu
from jax.sharding import Mesh, PartitionSpec as P

HD = 128
EPSILON = 1e-06
ROPE_BASE = 500000.0
NEGATIVE = -1e30
CORE, TP = "core", "tp"
SCORE = "btd,bsd->bts"
APPLY = "bts,bsd->btd"
AXES = ("z", "y", "ch", CORE, TP)
BF = jnp.bfloat16
F32 = jnp.float32


def rope_tables(positions):
    half_size = HD // 2
    exponent = jnp.arange(half_size, dtype=F32) * (2.0 / HD)
    frequency = jnp.power(ROPE_BASE, -exponent)
    angles = positions.astype(F32)[:, None] * frequency[None, :]
    cosine = jnp.cos(angles)
    sine_table = jnp.sin(angles)
    return (
        jnp.concatenate([cosine, cosine], axis=-1),
        jnp.concatenate([sine_table, sine_table], axis=-1),
    )


def rotate(values, cosine, sine_table):
    half_size = HD // 2
    turned = jnp.concatenate([-values[..., half_size:], values[..., :half_size]], axis=-1)
    return values * cosine + turned * sine_table


def rotate_back(grads_in, cosine, sine_table):
    half_size = HD // 2
    sin_part = grads_in * sine_table
    return grads_in * cosine + jnp.concatenate(
        [sin_part[..., half_size:], -sin_part[..., :half_size]], axis=-1
    )


def dot(former, latter, dims):
    return lax.dot_general(former, latter, (dims, ((), ())), preferred_element_type=F32)


def mm(a, b):
    return dot(a, b, ((1,), (0,)))


def mm_nt(a, b):
    return dot(a, b, ((1,), (1,)))


def mm_tn(a, b):
    return dot(a, b, ((0,), (0,)))


MESH = pl.DeviceIdType.MESH


def flip(axis, bits):
    me = lax.axis_index(axis)
    result, weight = me, 1
    while weight <= bits:
        if (bits // weight) % 2:
            result = result + weight * (1 - 2 * lax.rem(me // weight, 2))
        weight *= 2
    return result


def greet(partners):
    barrier = pltpu.get_barrier_semaphore()
    for partner in partners:
        pl.semaphore_signal(barrier, inc=1, device_id=partner, device_id_type=MESH)
    pl.semaphore_wait(barrier, len(partners))


def remote(src, dst, send_sem, recv_sem, partner):
    return pltpu.make_async_remote_copy(
        src_ref=src,
        dst_ref=dst,
        send_sem=send_sem,
        recv_sem=recv_sem,
        device_id=partner,
        device_id_type=MESH,
    )


def partners_of(axes):
    found = []
    for axis in axes:
        for bits in range(1, lax.axis_size(axis)):
            found.append({axis: flip(axis, bits)})
    return found


def call(kernel, identity, out_shape, in_spaces, out_spaces, scratch, limit, *operands):
    return pl.pallas_call(
        kernel,
        out_shape=out_shape,
        in_specs=[pl.BlockSpec(memory_space=s) for s in in_spaces],
        out_specs=jax.tree.map(lambda s: pl.BlockSpec(memory_space=s), out_spaces),
        scratch_shapes=scratch,
        compiler_params=pltpu.CompilerParams(
            collective_id=identity, has_side_effects=True, vmem_limit_bytes=limit * 2**20
        ),
    )(*operands)


DMA = pltpu.SemaphoreType.DMA


def gather_kernel(nz, x_ref, out_ref, own_sem, zs, zr, xs, xr, cs, cr):
    iz, ic, it = (lax.axis_index(a) for a in ("z", CORE, TP))
    greet(partners_of(("z", TP, CORE)))
    sends = []

    def push(src, where, send_sem, recv_sem, partner):
        copy = remote(src, out_ref.at[where], send_sem, recv_sem, partner)
        copy.start()
        sends.append(copy)

    across, beside = {TP: 1 - it}, {CORE: 1 - ic}
    own = (iz, ic, it)
    for d in range(1, nz):
        push(x_ref, own, zs.at[d], zr.at[d], {"z": flip("z", d)})
    push(x_ref, own, xs.at[0], xr.at[0], across)
    push(x_ref, own, cs.at[0, 0], cr.at[0, 0], beside)
    local_copy = pltpu.make_async_copy(x_ref, out_ref.at[own], own_sem)
    local_copy.start()

    def await_at(where, sem):
        remote(out_ref.at[where], out_ref.at[where], sem, sem, across).wait_recv()

    def from_across(d):
        where = (flip("z", d), ic, 1 - it)
        await_at(where, xr.at[d])
        push(out_ref.at[where], where, cs.at[d, 1], cr.at[d, 1], beside)

    for d in range(1, nz):
        where = (flip("z", d), ic, it)
        await_at(where, zr.at[d])
        push(out_ref.at[where], where, xs.at[d], xr.at[d], across)
        push(out_ref.at[where], where, cs.at[d, 0], cr.at[d, 0], beside)
        from_across(d - 1)
    from_across(nz - 1)
    for d in range(nz):
        for half in range(2):
            side = it if half == 0 else 1 - it
            await_at((flip("z", d), 1 - ic, side), cr.at[d, half])
    for copy in sends:
        copy.wait_send()
    local_copy.wait()


def gather_rows(rows):
    piece, width = rows.shape
    nz = lax.axis_size("z")
    out = call(
        functools.partial(gather_kernel, nz),
        1,
        jax.ShapeDtypeStruct((nz, 2, 2, piece, width), rows.dtype),
        [pl.ANY],
        pl.ANY,
        [DMA, DMA((nz,)), DMA((nz,)), DMA((nz,)), DMA((nz,)), DMA((nz, 2)), DMA((nz, 2))],
        16,
        rows,
    )
    return out.reshape(-1, width)


def scatter_kernel(
    nz, p_ref, out_ref, own, cin, xout, xin, zout, zin, ls, cs, cr, xs, xr, zs, zr
):
    iz, ic, it = (lax.axis_index(a) for a in ("z", CORE, TP))
    greet(partners_of(("z", TP, CORE)))
    across, beside = {TP: 1 - it}, {CORE: 1 - ic}
    order = list(range(nz - 1, -1, -1))
    loads, besides, acrosses, zeds = {}, {}, {}, {}
    for d in order:
        target = flip("z", d) if d else iz
        besides[d] = remote(p_ref.at[target, 1 - ic], cin.at[d], cs.at[d], cr.at[d], beside)
        besides[d].start()
        loads[d] = pltpu.make_async_copy(p_ref.at[target, ic], own.at[d], ls.at[d])
        loads[d].start()

    def add(d, side):
        return own[d, side].astype(F32) + cin[d, side].astype(F32)

    def after_across(d):
        acrosses[d].wait_recv()
        total = add(d, it) + xin[d].astype(F32)
        if d == 0:
            out_ref[...] = total
        else:
            zout[d] = total.astype(BF)
            zeds[d] = remote(zout.at[d], zin.at[d], zs.at[d], zr.at[d], {"z": flip("z", d)})
            zeds[d].start()

    for n, d in enumerate(order):
        loads[d].wait()
        besides[d].wait_recv()
        xout[d] = add(d, 1 - it).astype(BF)
        acrosses[d] = remote(xout.at[d], xin.at[d], xs.at[d], xr.at[d], across)
        acrosses[d].start()
        if n:
            after_across(order[n - 1])
    after_across(0)
    for d in order[:-1]:
        zeds[d].wait_recv()
        out_ref[...] += zin[d].astype(F32)
    for group in (besides, acrosses, zeds):
        for copy in group.values():
            copy.wait_send()


def scatter_rows(partial):
    nz = lax.axis_size("z")
    width = partial.shape[1]
    part = partial.astype(BF).reshape(nz, 2, 2, -1, width)
    piece = part.shape[3]
    sems = [DMA((nz,)) for _ in range(7)]
    return call(
        functools.partial(scatter_kernel, nz),
        2,
        jax.ShapeDtypeStruct((piece, width), F32),
        [pl.ANY],
        pltpu.VMEM,
        [
            pltpu.VMEM((nz, 2, piece, width), BF),
            pltpu.VMEM((nz, 2, piece, width), BF),
            *[pltpu.VMEM((nz, piece, width), BF) for _ in range(4)],
            *sems,
        ],
        32,
        part,
    )


def total_kernel(axes, x_ref, out_ref, *scratch):
    greet(partners_of(axes))
    value = x_ref[...]
    sends = []
    for stage, axis in enumerate(axes):
        slots, send_sems, recv_sems = scratch[3 * stage : 3 * stage + 3]
        size = lax.axis_size(axis)
        me = lax.axis_index(axis)
        slots[me] = value
        copies = []
        for d in range(1, size):
            copy = remote(
                slots.at[me], slots.at[me], send_sems.at[d], recv_sems.at[d], {axis: flip(axis, d)}
            )
            copy.start()
            copies.append(copy)
        for copy in copies:
            copy.wait_recv()
        value = slots[0]
        for n in range(1, size):
            value = value + slots[n]
        sends += copies
    out_ref[...] = value
    for copy in sends:
        copy.wait_send()


def total(terms, axes, identity):
    axes = tuple(a for a in axes if lax.axis_size(a) > 1)
    scratch = []
    for axis in axes:
        size = lax.axis_size(axis)
        scratch += [pltpu.VMEM((size, *terms.shape), F32), DMA((size,)), DMA((size,))]
    return call(
        functools.partial(total_kernel, axes),
        identity,
        jax.ShapeDtypeStruct(terms.shape, F32),
        [pltpu.VMEM],
        pltpu.VMEM,
        scratch,
        16,
        terms,
    )


def head_total(terms):
    return total(terms.reshape(-1, 128), (CORE, TP, "z"), 3).reshape(terms.shape)


def all_total(terms):
    size = terms.shape[0]
    padded = jnp.pad(terms, (0, -size % 1024)).reshape(-1, 128)
    return total(padded, (CORE, TP, "y", "z", "ch"), 4).reshape(-1)[:size]


def columns(ref, slot, count):
    return ref.at[:, pl.ds(pl.multiple_of(slot * count, 128), count)]


def intake_kernel(nz, count, tok_ref, *refs):
    w_refs, refs = refs[:count], refs[count:]
    tok_out, refs = refs[0], refs[1:]
    o_refs, refs = refs[:count], refs[count:]
    tok_buf, refs = refs[0], refs[1:]
    bufs, refs = refs[:count], refs[count:]
    tl, tzs, tzr, txs, txr, tcs, tcr, wl, wzs, wzr, wys, wyr = refs
    iz, iy, ic, it = (lax.axis_index(a) for a in ("z", "y", CORE, TP))
    across, beside, behind = {TP: 1 - it}, {CORE: 1 - ic}, {"y": 1 - iy}
    greet(partners_of(("z", "y", TP, CORE)))
    sends = []

    def push(src, dst, send_sem, recv_sem, partner):
        copy = remote(src, dst, send_sem, recv_sem, partner)
        copy.start()
        sends.append(copy)

    def arrived(ref, sem):
        remote(ref, ref, sem, sem, across).wait_recv()

    for d in range(1, nz):
        push(tok_ref.at[it], tok_out.at[iz, ic, it], tzs.at[d], tzr.at[d], {"z": flip("z", d)})
    push(tok_ref, tok_out.at[iz, ic], tcs.at[0, 0], tcr.at[0, 0], beside)
    tok_load = pltpu.make_async_copy(tok_ref, tok_buf, tl.at[0])
    tok_load.start()
    widths = [o.shape[-1] for o in o_refs]
    loads = []
    for k, (w, o) in enumerate(zip(w_refs, o_refs)):
        own = columns(w, iz * 2 + ic, widths[k])
        push(own, o.at[iz, iy], wys.at[k, 0], wyr.at[k, 0], behind)
        for d in range(1, nz):
            other = flip("z", d)
            push(
                columns(w, other * 2 + ic, widths[k]),
                o.at[iz, iy],
                wzs.at[k, d],
                wzr.at[k, d],
                {"z": other},
            )
        load = pltpu.make_async_copy(own, bufs[k], wl.at[k])
        load.start()
        loads.append(load)
    tok_load.wait()
    stores = [pltpu.make_async_copy(tok_buf, tok_out.at[iz, ic], tl.at[1])]
    stores[0].start()
    for d in range(1, nz):
        block = tok_out.at[flip("z", d), ic, it]
        arrived(block, tzr.at[d])
        push(block, block, txs.at[d], txr.at[d], across)
        push(block, block, tcs.at[d, 0], tcr.at[d, 0], beside)

    def forward(k):
        for d in range(1, nz):
            block = o_refs[k].at[flip("z", d), iy]
            arrived(block, wzr.at[k, d])
            push(block, block, wys.at[k, d], wyr.at[k, d], behind)

    first = min(3, count)
    for k in range(first):
        forward(k)
    for d in range(1, nz):
        block = tok_out.at[flip("z", d), ic, 1 - it]
        arrived(block, txr.at[d])
        push(block, block, tcs.at[d, 1], tcr.at[d, 1], beside)
    for k, load in enumerate(loads):
        load.wait()
        store = pltpu.make_async_copy(bufs[k], o_refs[k].at[iz, iy], wl.at[k])
        store.start()
        stores.append(store)
    for k in range(first, count):
        forward(k)
    arrived(tok_out.at[iz, 1 - ic], tcr.at[0, 0])
    for d in range(1, nz):
        for half in range(2):
            side = it if half == 0 else 1 - it
            arrived(tok_out.at[flip("z", d), 1 - ic, side], tcr.at[d, half])
    for k in range(count):
        for d in range(nz):
            source = flip("z", d) if d else iz
            arrived(o_refs[k].at[source, 1 - iy], wyr.at[k, d])
    for copy in sends:
        copy.wait_send()
    for store in stores:
        store.wait()


def intake(token_rows, weights):
    nz = lax.axis_size("z")
    count = len(weights)
    own_rows, width = token_rows.shape
    rows = weights[0].shape[0]
    parts = [w.shape[1] // (2 * nz) for w in weights]
    piece = own_rows // 2
    out_shape = [jax.ShapeDtypeStruct((nz, 2, 2, piece, width), BF)] + [
        jax.ShapeDtypeStruct((nz, 2, rows, c), BF) for c in parts
    ]
    got = call(
        functools.partial(intake_kernel, nz, count),
        5,
        out_shape,
        [pl.ANY] * (count + 1),
        [pl.ANY] * (count + 1),
        [
            pltpu.VMEM((2, piece, width), BF),
            *[pltpu.VMEM((rows, c), BF) for c in parts],
            DMA((2,)),
            *[DMA((nz,)) for _ in range(4)],
            *[DMA((nz, 2)) for _ in range(2)],
            DMA((count,)),
            *[DMA((count, nz)) for _ in range(4)],
        ],
        16,
        token_rows.reshape(2, piece, width),
        *weights,
    )
    return got[0].reshape(-1, width), [g.reshape(-1, g.shape[-1]) for g in got[1:]]


def outlet_kernel(nz, count, *refs):
    g_refs, refs = refs[:count], refs[count:]
    o_refs, refs = refs[:count], refs[count:]
    own, refs = refs[:count], refs[count:]
    yin, refs = refs[:count], refs[count:]
    zout, refs = refs[:count], refs[count:]
    ls, ys, yr, zs, zr, cs, cr, os = refs
    iz, iy, ic = (lax.axis_index(a) for a in ("z", "y", CORE))
    beside, behind = {CORE: 1 - ic}, {"y": 1 - iy}
    greet(partners_of(("z", "y", CORE)))
    sends, loads, pairs, stores = [], {}, {}, []

    def push(src, dst, send_sem, recv_sem, partner):
        copy = remote(src, dst, send_sem, recv_sem, partner)
        copy.start()
        sends.append(copy)
        return copy

    order = [(k, d) for k in range(count) for d in range(nz - 1, -1, -1)]
    widths = [g.shape[-1] for g in g_refs]
    for k, d in order:
        target = flip("z", d) if d else iz
        pairs[k, d] = push(
            g_refs[k].at[target, 1 - iy], yin[k].at[d], ys.at[k, d], yr.at[k, d], behind
        )
        loads[k, d] = pltpu.make_async_copy(g_refs[k].at[target, iy], own[k].at[d], ls.at[k, d])
        loads[k, d].start()

    def relay(k, d):
        block = columns(o_refs[k], flip("z", d) * 2 + ic, widths[k])
        remote(block, block, zr.at[k, d], zr.at[k, d], beside).wait_recv()
        push(block, block, cs.at[k, d], cr.at[k, d], beside)

    for n, (k, d) in enumerate(order):
        loads[k, d].wait()
        pairs[k, d].wait_recv()
        zout[k][d] = (own[k][d].astype(F32) + yin[k][d].astype(F32)).astype(BF)
        mine = columns(o_refs[k], iz * 2 + ic, widths[k])
        if d:
            push(zout[k].at[d], mine, zs.at[k, d], zr.at[k, d], {"z": flip("z", d)})
        else:
            push(zout[k].at[d], mine, cs.at[k, d], cr.at[k, d], beside)
            store = pltpu.make_async_copy(zout[k].at[d], mine, os.at[k])
            store.start()
            stores.append(store)
            if k:
                for e in range(nz - 1, 0, -1):
                    relay(k - 1, e)
    for e in range(nz - 1, 0, -1):
        relay(count - 1, e)
    for k, d in order:
        source = flip("z", d) if d else iz
        block = columns(o_refs[k], source * 2 + 1 - ic, widths[k])
        remote(block, block, cr.at[k, d], cr.at[k, d], beside).wait_recv()
    for copy in sends:
        copy.wait_send()
    for store in stores:
        store.wait()


def outlet(grads, identity=6):
    nz = lax.axis_size("z")
    count = len(grads)
    parts = [g.shape[1] for g in grads]
    blocks = [g.astype(BF).reshape(nz, 2, -1, g.shape[1]) for g in grads]
    rows = blocks[0].shape[2]
    got = call(
        functools.partial(outlet_kernel, nz, count),
        identity,
        [jax.ShapeDtypeStruct((rows, 2 * nz * c), BF) for c in parts],
        [pl.ANY] * count,
        [pl.ANY] * count,
        [
            *[pltpu.VMEM((nz, rows, c), BF) for _ in range(3) for c in parts],
            *[DMA((count, nz)) for _ in range(7)],
            DMA((count,)),
        ],
        32,
        *blocks,
    )
    if lax.axis_size("ch") > 1:
        got = lax.psum(tuple(got), "ch")
    return [g.astype(F32) for g in got]


class Kernel:
    def __init__(self):
        self.ins, self.outs, self.scratch = [], [], []

    def inp(self, name, array, space=pl.ANY):
        self.ins.append((name, array, space))

    def out(self, name, shape, dtype, space=pl.ANY):
        self.outs.append((name, jax.ShapeDtypeStruct(shape, dtype), space))

    def mem(self, name, shape, dtype):
        self.scratch.append((name, pltpu.VMEM(shape, dtype)))

    def sem(self, name, *shape):
        self.scratch.append((name, DMA(shape)))

    def run(self, identity, body, limit):
        names = [n for n, *_ in self.ins + self.outs + self.scratch]

        def kernel(*refs):
            body(types.SimpleNamespace(**dict(zip(names, refs))))

        got = call(
            kernel,
            identity,
            [shape for _, shape, _ in self.outs],
            [space for *_, space in self.ins],
            [space for *_, space in self.outs],
            [made for _, made in self.scratch],
            limit,
            *[array for _, array, _ in self.ins],
        )
        return {n: g for (n, *_), g in zip(self.outs, got)}


class Flow:
    def __init__(self):
        self.sends, self.inner_sends = [], []
        self.iz, self.iy, self.ic, self.it = (
            lax.axis_index(a) for a in ("z", "y", CORE, TP)
        )
        self.across = {TP: 1 - self.it}
        self.beside = {CORE: 1 - self.ic}
        self.behind = {"y": 1 - self.iy}
        self.near, self.mid = {"z": flip("z", 1)}, {"z": 3 - self.iz}
        self.role = lax.rem((self.iz + 1) // 2, 2)
        self.inner = self.role == 1

    def at(self, d):
        return flip("z", d) if d else self.iz

    def line(self, s):
        side = self.iz // 2
        return (self.iz, self.near["z"], 2 - side, 3 - 3 * side)[s]

    def push(self, src, dst, send_sem, recv_sem, partner):
        copy = remote(src, dst, send_sem, recv_sem, partner)
        copy.start()
        self.sends.append(copy)
        return copy

    def push_inner(self, src, dst, send_sem, recv_sem, partner):
        copy = remote(src, dst, send_sem, recv_sem, partner)
        pl.when(self.inner)(copy.start)
        self.inner_sends.append(copy)

    def pass_on(self, s, block, send_sems, recv_sems):
        partner, number = ((self.mid, 3), (self.near, 2), (self.near, 3))[s - 1]
        self.push_inner(block, block, send_sems.at[s + 2], recv_sems.at[number], partner)

    def arrived(self, ref, sem):
        remote(ref, ref, sem, sem, self.across).wait_recv()

    def finish(self):
        for copy in self.sends:
            copy.wait_send()
        if self.inner_sends:

            @pl.when(self.inner)
            def _():
                for copy in self.inner_sends:
                    copy.wait_send()

        self.sends, self.inner_sends = [], []


def greet_line():
    flow = Flow()
    barrier = pltpu.get_barrier_semaphore()
    for partner in (flow.near, flow.across, flow.beside):
        pl.semaphore_signal(barrier, inc=1, device_id=partner, device_id_type=MESH)

    @pl.when(flow.inner)
    def _():
        pl.semaphore_signal(barrier, inc=1, device_id=flow.mid, device_id_type=MESH)

    pl.semaphore_wait(barrier, 3 + flow.role)


def stripe(ref, z, core, tp, piece):
    start = pl.multiple_of((core * 2 + tp) * piece, piece)
    return ref.at[z, pl.ds(start, piece)]


class Gather(Flow):
    @staticmethod
    def setup(k, name, rows, out=False, inside=False):
        piece, width = rows.shape
        if inside:
            k.mem(name + "_x", rows.shape, rows.dtype)
        else:
            k.inp(name + "_x", rows)
        (k.out if out else k.mem)(name, (4, 4 * piece, width), rows.dtype)
        k.sem(name + "_own")
        k.sem(name + "_zs", 6)
        for s in ("_zr", "_xs", "_xr"):
            k.sem(name + s, 4)
        k.sem(name + "_cs", 4, 2)
        k.sem(name + "_cr", 4, 2)

    def __init__(self, r, name):
        super().__init__()
        self.x, self.buf = getattr(r, name + "_x"), getattr(r, name)
        self.own_sem, self.zs, self.zr, self.xs, self.xr, self.cs, self.cr = (
            getattr(r, name + s) for s in ("_own", "_zs", "_zr", "_xs", "_xr", "_cs", "_cr")
        )
        self.piece = self.x.shape[0]

    def block(self, z, core, tp):
        return stripe(self.buf, z, core, tp, self.piece)

    def start(self):
        own = self.block(self.iz, self.ic, self.it)
        self.push(self.x, own, self.zs.at[1], self.zr.at[1], self.near)
        self.push_inner(self.x, own, self.zs.at[2], self.zr.at[2], self.mid)
        self.push(self.x, own, self.xs.at[0], self.xr.at[0], self.across)
        self.push(self.x, own, self.cs.at[0, 0], self.cr.at[0, 0], self.beside)
        self.local = pltpu.make_async_copy(self.x, own, self.own_sem)
        self.local.start()

    def from_across(self, s):
        block = self.block(self.line(s), self.ic, 1 - self.it)
        self.arrived(block, self.xr.at[s])
        self.push(block, block, self.cs.at[s, 1], self.cr.at[s, 1], self.beside)

    def advance(self, s):
        if s < 4:
            block = self.block(self.line(s), self.ic, self.it)
            self.arrived(block, self.zr.at[s])
            self.pass_on(s, block, self.zs, self.zr)
            self.push(block, block, self.xs.at[s], self.xr.at[s], self.across)
            self.push(block, block, self.cs.at[s, 0], self.cr.at[s, 0], self.beside)
        self.from_across(s - 1)

    def ready(self, s):
        if s == 0:
            self.local.wait()
        for half in range(2):
            side = self.it if half == 0 else 1 - self.it
            self.arrived(self.block(self.line(s), 1 - self.ic, side), self.cr.at[s, half])


class Scatter(Flow):
    @staticmethod
    def setup(k, name, piece, width, partial=None):
        if partial is None:
            k.mem(name + "_p", (4, 4 * piece, width), BF)
        else:
            k.inp(name + "_p", partial)
            k.mem(name + "_m", (4, 2 * piece, width), BF)
            k.sem(name + "_ls", 4)
        k.mem(name + "_c", (4, 2 * piece, width), BF)
        for s in ("_xo", "_xi", "_zo"):
            k.mem(name + s, (4, piece, width), BF)
        k.mem(name + "_zi", (6, piece, width), BF)
        for s in ("_cs", "_cr", "_xs", "_xr", "_zs"):
            k.sem(name + s, 4)
        k.sem(name + "_zr", 6)

    def __init__(self, r, name, out):
        super().__init__()
        self.out = out
        self.p, self.c, self.xo, self.xi, self.zo, self.zi = (
            getattr(r, name + s) for s in ("_p", "_c", "_xo", "_xi", "_zo", "_zi")
        )
        self.cs, self.cr, self.xs, self.xr, self.zs, self.zr = (
            getattr(r, name + s) for s in ("_cs", "_cr", "_xs", "_xr", "_zs", "_zr")
        )
        self.m, self.ls = getattr(r, name + "_m", None), getattr(r, name + "_ls", None)
        self.piece = self.xo.shape[1]
        self.core_copy, self.across_copy, self.loads = {}, {}, {}

    def rows(self, core):
        return pl.ds(pl.multiple_of(core * 2 * self.piece, 2 * self.piece), 2 * self.piece)

    def begin(self, s):
        part = s if self.m is None else self.line(s)
        self.core_copy[s] = self.push(
            self.p.at[part, self.rows(1 - self.ic)],
            self.c.at[s],
            self.cs.at[s],
            self.cr.at[s],
            self.beside,
        )
        if self.m is not None:
            self.loads[s] = pltpu.make_async_copy(
                self.p.at[part, self.rows(self.ic)], self.m.at[s], self.ls.at[s]
            )
            self.loads[s].start()

    def add(self, s, side):
        rows = pl.ds(pl.multiple_of(side * self.piece, self.piece), self.piece)
        if self.m is not None:
            own = self.m[s, rows]
        else:
            start = pl.multiple_of((self.ic * 2 + side) * self.piece, self.piece)
            own = self.p[s, pl.ds(start, self.piece)]
        return own.astype(F32) + self.c[s, rows].astype(F32)

    def cross(self, s):
        if s in self.loads:
            self.loads[s].wait()
        self.core_copy[s].wait_recv()
        self.xo[s] = self.add(s, 1 - self.it).astype(BF)
        self.across_copy[s] = self.push(
            self.xo.at[s], self.xi.at[s], self.xs.at[s], self.xr.at[s], self.across
        )

    def leave(self, s):
        self.across_copy[s].wait_recv()

        def value():
            return self.add(s, self.it) + self.xi[s].astype(F32)

        if s == 0:
            self.out[...] = value()
            return
        came = (None, 4, 2, 3)[s]

        @pl.when(self.inner)
        def _():
            self.arrived(self.zi.at[came], self.zr.at[came])
            self.zo[s] = (value() + self.zi[came].astype(F32)).astype(BF)

        @pl.when(self.role == 0)
        def _():
            self.zo[s] = value().astype(BF)

        place = s + self.role * (None, -1, 3, 1)[s]
        partner = self.near["z"]
        if s > 1:
            partner = partner + self.role * (self.mid["z"] - partner)
        self.push(
            self.zo.at[s], self.zi.at[place], self.zs.at[s], self.zr.at[place], {"z": partner}
        )

    def end(self):
        @pl.when(self.inner)
        def _():
            for place in (1, 5):
                self.arrived(self.zi.at[place], self.zr.at[place])
                self.out[...] += self.zi[place].astype(F32)

        @pl.when(self.role == 0)
        def _():
            self.arrived(self.zi.at[0], self.zr.at[0])
            self.out[...] += self.zi[0].astype(F32)


class Total(Flow):
    @staticmethod
    def setup(k, name, shape, axes):
        for axis in axes:
            size = lax.axis_size(axis)
            k.mem(f"{name}_{axis}", (size, *shape), F32)
            k.sem(f"{name}_{axis}_s", size)
            k.sem(f"{name}_{axis}_r", size)

    def __init__(self, r, name):
        super().__init__()
        self.r, self.name = r, name

    def send(self, axis, value):
        slots, ss, rs = (getattr(self.r, f"{self.name}_{axis}{s}") for s in ("", "_s", "_r"))
        me = lax.axis_index(axis)
        slots[me] = value
        self.copies = [
            self.push(slots.at[me], slots.at[me], ss.at[d], rs.at[d], {axis: flip(axis, d)})
            for d in range(1, lax.axis_size(axis))
        ]
        self.slots = slots

    def receive(self):
        for copy in self.copies:
            copy.wait_recv()
        value = self.slots[0]
        for n in range(1, self.slots.shape[0]):
            value = value + self.slots[n]
        return value


class Outlet(Flow):
    @staticmethod
    def setup(k, name, grads, nz, inside=False):
        for n, grad in enumerate(grads):
            rows, cols = grad.shape[0] // (2 * nz), grad.shape[1]
            if inside:
                k.mem(f"{name}_g{n}", (nz, 2, rows, cols), BF)
            else:
                k.inp(f"{name}_g{n}", grad.astype(BF).reshape(nz, 2, rows, cols))
                k.mem(f"{name}_own{n}", (nz, rows, cols), BF)
            k.out(f"{name}_o{n}", (rows, 2 * nz * cols), BF)
            for s in ("yin", "zout"):
                k.mem(f"{name}_{s}{n}", (nz, rows, cols), BF)
        for s in ("ls", "ys", "yr", "zs", "zr", "cs", "cr"):
            k.sem(f"{name}_{s}", len(grads), nz)
        k.sem(f"{name}_os", len(grads))

    def __init__(self, r, name, count, nz):
        super().__init__()
        self.nz, self.count = nz, count
        self.g, self.o, self.own, self.yin, self.zout = (
            [getattr(r, f"{name}_{s}{n}", None) for n in range(count)]
            for s in ("g", "o", "own", "yin", "zout")
        )
        self.ls, self.ys, self.yr, self.zs, self.zr, self.cs, self.cr, self.os = (
            getattr(r, f"{name}_{s}") for s in ("ls", "ys", "yr", "zs", "zr", "cs", "cr", "os")
        )
        self.loads, self.pairs, self.stores = {}, {}, []

    def slot(self, k, z, core):
        return columns(self.o[k], z * 2 + core, self.g[k].shape[-1])

    def start(self, k):
        for d in range(self.nz - 1, -1, -1):
            target = self.at(d)
            self.pairs[k, d] = self.push(
                self.g[k].at[target, 1 - self.iy],
                self.yin[k].at[d],
                self.ys.at[k, d],
                self.yr.at[k, d],
                self.behind,
            )
            if self.own[k] is not None:
                self.loads[k, d] = pltpu.make_async_copy(
                    self.g[k].at[target, self.iy], self.own[k].at[d], self.ls.at[k, d]
                )
                self.loads[k, d].start()

    def combine(self, k):
        mine = self.slot(k, self.iz, self.ic)
        for d in range(self.nz - 1, -1, -1):
            self.pairs[k, d].wait_recv()
            if self.own[k] is not None:
                self.loads[k, d].wait()
                own = self.own[k][d]
            else:
                own = self.g[k][self.at(d), self.iy]
            self.zout[k][d] = (own.astype(F32) + self.yin[k][d].astype(F32)).astype(BF)
            src = self.zout[k].at[d]
            if d:
                self.push(src, mine, self.zs.at[k, d], self.zr.at[k, d], {"z": self.at(d)})
            else:
                self.push(src, mine, self.cs.at[k, d], self.cr.at[k, d], self.beside)
                store = pltpu.make_async_copy(src, mine, self.os.at[k])
                store.start()
                self.stores.append(store)

    def relay(self, k):
        for d in range(1, self.nz):
            block = self.slot(k, self.at(d), self.ic)
            self.arrived(block, self.zr.at[k, d])
            self.push(block, block, self.cs.at[k, d], self.cr.at[k, d], self.beside)

    def end(self):
        for k in range(self.count):
            for d in range(self.nz):
                self.arrived(self.slot(k, self.at(d), 1 - self.ic), self.cr.at[k, d])
        for store in self.stores:
            store.wait()
        self.finish()


def gather_line(rows):
    k = Kernel()
    Gather.setup(k, "all", rows, out=True)

    def body(r):
        greet_line()
        gather = Gather(r, "all")
        gather.start()
        for s in range(1, 5):
            gather.advance(s)
        for s in range(4):
            gather.ready(s)
        gather.finish()

    return k.run(1, body, 16)["all"].reshape(-1, rows.shape[1])


def scatter_line(partial):
    width = partial.shape[1]
    piece = partial.shape[0] // 16
    k = Kernel()
    Scatter.setup(k, "rs", piece, width, partial.astype(BF).reshape(4, 4 * piece, width))
    k.out("sum", (piece, width), F32, pltpu.VMEM)

    def body(r):
        greet_line()
        scatter = Scatter(r, "rs", r.sum)
        order = (3, 2, 1, 0)
        for s in order:
            scatter.begin(s)
        for s in order:
            scatter.cross(s)
        for s in order:
            scatter.leave(s)
        scatter.end()
        scatter.finish()

    return k.run(2, body, 32)["sum"]


def exact(a, b, dims):
    return lax.dot_general(
        a, b, (dims, ((), ())), precision=lax.Precision.HIGHEST, preferred_element_type=F32
    )


def picker(width):
    row = lax.broadcasted_iota(jnp.int32, (8, width), 0)
    part = lax.broadcasted_iota(jnp.int32, (8, width), 1) // HD
    return jnp.where(row == part, 1.0, 0.0).astype(F32)


def row_sums(first, second):
    both = jnp.concatenate([first, second], axis=1)
    return exact(picker(2 * HD), both, ((1,), (1,)))


def spread(sums, which):
    row = lax.broadcasted_iota(jnp.int32, (8, HD), 0)
    one = jnp.where(row == which, 1.0, 0.0).astype(F32)
    return exact(sums, one, ((0,), (0,)))


def softmax_rows(query, key, length):
    count = query.shape[0]
    row = lax.broadcasted_iota(jnp.int32, (count, count), 0)
    col = lax.broadcasted_iota(jnp.int32, (count, count), 1)
    scores = mm_nt(query, key) * (1.0 / math.sqrt(HD))
    scores = jnp.where((col <= row) & (col < length), scores, NEGATIVE)
    exponent = jnp.exp(scores - jnp.max(scores, axis=-1, keepdims=True))
    return exponent / jnp.sum(exponent, axis=-1, keepdims=True)


def load_all(pairs, sems):
    copies = []
    for n, (src, dst) in enumerate(pairs):
        copy = pltpu.make_async_copy(src, dst, sems.at[n])
        copy.start()
        copies.append(copy)
    return copies


def attention_back(
    branch, wide, wo, wqkv, saved, tokens_all, residual_grad, stream_rows, terms, gains, tables,
    seq_lengths,
):
    nz = lax.axis_size("z")
    piece, width = branch.shape
    rows = 4 * piece
    block = width // (2 * nz)
    padded = jnp.pad(terms, (0, -terms.shape[0] % 1024)).reshape(-1, 128)
    lanes = width // 128
    sum_axes = (CORE, TP, "y", "z")
    k = Kernel()
    Gather.setup(k, "ball", branch)
    Outlet.setup(k, "wide", wide, nz)
    slim = [jax.ShapeDtypeStruct((width, HD), BF)] * 4
    Outlet.setup(k, "slim", slim, nz, inside=True)
    Scatter.setup(k, "rs", piece, width)
    Total.setup(k, "tot", (nz, 8, rows), (CORE, TP, "z"))
    Total.setup(k, "sum", padded.shape, sum_axes)
    k.inp("wo", wo)
    k.inp("wqkv", wqkv)
    k.inp("tokens", tokens_all)
    k.mem("tokens_m", tokens_all.shape, BF)
    names = ("q", "k", "v", "att", "nq", "nk", "qs", "ks")
    for name, array in zip(names, saved):
        k.inp(name, array)
        k.mem(name + "_m", array.shape, array.dtype)
    k.mem("wo_m", wo.shape, BF)
    k.mem("wqkv_m", wqkv.shape, BF)
    k.inp("res", residual_grad)
    k.mem("res_m", (piece, width), F32)
    k.inp("stream", stream_rows)
    k.mem("stream_m", (piece, width), BF)
    k.sem("ld", len(names) + 5)
    k.inp("terms", padded, pltpu.VMEM)
    k.mem("terms_m", padded.shape, F32)
    k.out("terms_out", padded.shape, F32, pltpu.VMEM)
    k.inp("gains", gains, pltpu.VMEM)
    k.inp("tables", tables, pltpu.VMEM)
    k.inp("lens", seq_lengths, pltpu.SMEM)
    k.mem("wqk", (nz, 2, rows, HD), F32)
    k.mem("low", (nz, rows, 3 * HD), BF)
    k.mem("dots", (nz, 8, rows), F32)
    k.mem("norms", (2, HD), F32)
    k.mem("grad", (piece, width), F32)
    k.out("grad_out", (2, piece, width), F32)
    k.out("stream_out", (2, piece, width), BF)
    k.sem("xs", 2)
    k.sem("xr", 2)
    k.sem("ss", 2)

    def body(r):
        greet(partners_of(("z", "y", TP, CORE)))
        gather, outlet_flow = Gather(r, "ball"), Outlet(r, "wide", len(wide), nz)
        slim_flow, own = Outlet(r, "slim", len(slim), nz), Flow()
        scatter, total_flow = Scatter(r, "rs", r.grad), Total(r, "tot")
        sum_flow = Total(r, "sum")
        gather.start()
        for n in range(len(wide)):
            outlet_flow.start(n)
        names_in = ("wo", "wqkv", *names, "tokens", "res", "stream")
        loads = load_all([(getattr(r, n), getattr(r, n + "_m")) for n in names_in], r.ld)
        scale = 1.0 / math.sqrt(HD)
        cosine, sine = r.tables[0], r.tables[1]
        gather.advance(1)
        for copy in loads:
            copy.wait()
        r.norms[...] = jnp.zeros_like(r.norms)

        def compute(z):
            grad_low = mm(r.ball[z], r.wo_m[...]).astype(BF)
            query, key, value = r.q_m[z], r.k_m[z], r.v_m[z]
            probability = softmax_rows(query, key, r.lens[z])
            grad_prob = mm_nt(grad_low, value)
            row_dots = jnp.sum(probability * grad_prob, axis=-1, keepdims=True)
            grad_scores = (probability * (grad_prob - row_dots)).astype(BF)
            grad_q = rotate_back(mm(grad_scores, key) * scale, cosine, sine)
            grad_k = rotate_back(mm_tn(grad_scores, query) * scale, cosine, sine)
            grad_v = mm_tn(probability.astype(BF), grad_low)
            r.low[z, :, 2 * HD :] = grad_v.astype(BF)
            nq, nk = r.nq_m[z], r.nk_m[z]
            r.norms[0:1] += jnp.sum(grad_q * nq, axis=0, keepdims=True)
            r.norms[1:2] += jnp.sum(grad_k * nk, axis=0, keepdims=True)
            wq, wk = grad_q * r.gains[0:1], grad_k * r.gains[1:2]
            r.wqk[z, 0] = wq
            r.wqk[z, 1] = wk
            r.dots[z] = row_sums(wq * nq, wk * nk)

        def weight_blocks(left, right, place):
            @pl.loop(0, 2 * nz)
            def _(f):
                cols = pl.ds(pl.multiple_of(f * block, block), block)
                made = mm_tn(left[0, :, cols], right[0])
                for z in range(1, nz):
                    made = made + mm_tn(left[z, :, cols], right[z])
                made = made.astype(BF)
                for n, grad in enumerate(place):
                    grad[f // 2, lax.rem(f, 2)] = made[:, n * HD : (n + 1) * HD]

        for d in range(nz):
            if d + 2 <= nz:
                gather.advance(d + 2)
            if d == nz - 2:
                own.push(
                    r.stream, r.stream_out.at[own.it], r.xs.at[0], r.xr.at[0], own.across
                )
            gather.ready(d)
            compute(gather.line(d))
            if d == nz - 2:
                outlet_flow.combine(0)
        r.terms_m[...] = r.terms[...]
        slot = 2 * lanes + own.it * (lanes // 2) + own.iz * 2 + own.ic
        for n in range(2):
            r.terms_m[pl.ds(slot + n * lanes, 1)] = r.norms[n : n + 1]
        total_flow.send(CORE, r.dots[...])
        sum_flow.send(CORE, r.terms_m[...])
        value, other = total_flow.receive(), sum_flow.receive()
        total_flow.send(TP, value)
        sum_flow.send(TP, other)
        value, other = total_flow.receive(), sum_flow.receive()
        total_flow.send("z", value)
        sum_flow.send("y", other)
        outlet_flow.combine(1)
        weight_blocks(r.ball, r.att_m, [slim_flow.g[3]])
        slim_flow.start(3)
        r.dots[...] = total_flow.receive()
        order = list(range(nz - 1, -1, -1))
        for n, d in enumerate(order):
            z = gather.line(d)
            sums = r.dots[z] * (1.0 / width)
            for j, (normed, factor) in enumerate(((r.nq_m, r.qs_m), (r.nk_m, r.ks_m))):
                low = factor[z] * (r.wqk[z, j] - normed[z] * spread(sums, j))
                r.low[z, :, j * HD : (j + 1) * HD] = low.astype(BF)
            r.rs_p[d] = mm_nt(r.low[z], r.wqkv_m[...]).astype(BF)
            scatter.begin(d)
            if n:
                scatter.cross(order[n - 1])
            if n > 1:
                scatter.leave(order[n - 2])
        scatter.cross(0)
        scatter.leave(1)
        scatter.leave(0)
        outlet_flow.combine(2)
        weight_blocks(r.tokens_m, r.low, slim_flow.g[:3])
        for n in range(3):
            slim_flow.start(n)
        sum_flow.send("z", sum_flow.receive())
        slim_flow.combine(3)
        outlet_flow.relay(0)
        outlet_flow.relay(1)
        scatter.end()
        r.res_m[...] += r.grad[...]
        own.push(r.res_m, r.grad_out.at[own.it], r.xs.at[1], r.xr.at[1], own.across)
        stores = []
        for n, (src, out) in enumerate(((r.stream_m, r.stream_out), (r.res_m, r.grad_out))):
            stores.append(pltpu.make_async_copy(src, out.at[own.it], r.ss.at[n]))
            stores[-1].start()
        for n in range(3):
            slim_flow.combine(n)
        r.terms_out[...] = sum_flow.receive()
        outlet_flow.relay(2)
        slim_flow.relay(3)
        for n in range(3):
            slim_flow.relay(n)
        outlet_flow.end()
        slim_flow.end()
        for n, out in enumerate((r.stream_out, r.grad_out)):
            own.arrived(out.at[1 - own.it], r.xr.at[n])
        for flow in (gather, scatter, total_flow, sum_flow, own):
            flow.finish()
        for copy in stores:
            copy.wait()

    got = k.run(7, body, 60)
    return (
        [got[f"slim_o{n}"].astype(F32) for n in range(4)]
        + [got[f"wide_o{n}"].astype(F32) for n in range(len(wide))],
        got["grad_out"].reshape(-1, width),
        got["stream_out"].reshape(-1, width),
        got["terms_out"].reshape(-1)[: terms.shape[0]],
    )


def attention_front(token_rows, weights, gains, tables, seq_lengths, post_attention):
    nz = lax.axis_size("z")
    own_rows, width = token_rows.shape
    piece, rows = own_rows // 2, own_rows * 2
    w_rows = weights[0].shape[0]
    count = len(weights)
    parts = [w.shape[1] // (2 * nz) for w in weights]
    k = Kernel()
    Scatter.setup(k, "rs", piece, width)
    Total.setup(k, "tot", (nz, 8, rows), (CORE, TP, "z"))
    k.inp("tok", token_rows)
    for n, weight in enumerate(weights):
        k.inp(f"w{n}", weight)
    k.inp("gains", gains, pltpu.VMEM)
    k.inp("tables", tables, pltpu.VMEM)
    k.inp("lens", seq_lengths, pltpu.SMEM)
    k.mem("tall", (nz, rows, width), BF)
    k.mem("qkv", (nz, 2, w_rows, 3 * HD), BF)
    k.mem("wo", (nz, 2, w_rows, parts[3]), BF)
    for n in range(4, count):
        k.mem(f"b{n}", (w_rows, parts[n]), BF)
        k.out(f"o{n}", (nz, 2, w_rows, parts[n]), BF)
    k.mem("raw", (nz, rows, 3 * HD), F32)
    k.mem("dots", (nz, 8, rows), F32)
    saved = (("q", BF), ("k", BF), ("v", BF), ("nq", F32), ("nk", F32), ("qs", F32), ("ks", F32), ("att", BF))
    for name, kind in saved:
        k.mem(name + "_m", (nz, rows, HD), kind)
        k.out(name, (nz, rows, HD), kind)
    k.mem("branch", (piece, width), F32)
    k.inp("post", post_attention[None], pltpu.VMEM)
    for name in ("normed", "residual"):
        k.out(name, (piece, width), F32, pltpu.VMEM)
    k.out("scale", (piece, 128), F32, pltpu.VMEM)
    Gather.setup(k, "all", jax.ShapeDtypeStruct((piece, width), BF), inside=True)
    k.out("wide", (nz, rows, width), BF)
    k.out("tokens", (nz, rows, width), BF)
    k.out("qkv_out", (nz, 2, w_rows, 3 * HD), BF)
    k.out("wo_out", (nz, 2, w_rows, parts[3]), BF)
    k.sem("tl")
    k.sem("tzs", 6)
    for s in ("tzr", "txs", "txr"):
        k.sem(s, nz)
    k.sem("tcs", nz, 2)
    k.sem("tcr", nz, 2)
    k.sem("wl", 2, count)
    for s in ("wzs", "wzr", "wys", "wyr"):
        k.sem(s, count, nz)
    k.sem("st", len(saved) + 2, nz)
    k.sem("sw", 2)

    def body(r):
        greet(partners_of(("z", "y", TP, CORE)))
        flow = Flow()
        iz, iy, ic, it = flow.iz, flow.iy, flow.ic, flow.it
        scatter, total_flow = Scatter(r, "rs", r.branch), Total(r, "tot")
        gather = Gather(r, "all")

        def block(z, core, tp):
            return stripe(r.tall, z, core, tp, piece)

        def pair(z, core):
            start = pl.multiple_of(core * own_rows, own_rows)
            return r.tall.at[z, pl.ds(start, own_rows)]

        tok_half = r.tok.at[pl.ds(pl.multiple_of(it * piece, piece), piece)]
        flow.push(tok_half, block(iz, ic, it), r.tzs.at[1], r.tzr.at[1], flow.near)
        flow.push_inner(tok_half, block(iz, ic, it), r.tzs.at[2], r.tzr.at[2], flow.mid)
        flow.push(r.tok, pair(iz, ic), r.tcs.at[0, 0], r.tcr.at[0, 0], flow.beside)
        tok_load = pltpu.make_async_copy(r.tok, pair(iz, ic), r.tl)
        tok_load.start()
        loads = {}

        def landing(n, z, y):
            if n < 3:
                return r.qkv.at[z, y, :, n * HD : (n + 1) * HD]
            return r.wo.at[z, y] if n == 3 else getattr(r, f"o{n}").at[z, y]

        def bring(n, parts_of_z=(3, 2, 1), own_part=True):
            weight = getattr(r, f"w{n}")
            own = columns(weight, iz * 2 + ic, parts[n])
            for d in parts_of_z:
                other = flow.at(d)
                flow.push(
                    columns(weight, other * 2 + ic, parts[n]),
                    landing(n, iz, iy),
                    r.wzs.at[n, d],
                    r.wzr.at[n, d],
                    {"z": other},
                )
            if own_part:
                flow.push(own, landing(n, iz, iy), r.wys.at[n, 0], r.wyr.at[n, 0], flow.behind)
                dst = landing(n, iz, iy) if n < 4 else getattr(r, f"b{n}")
                loads[n] = pltpu.make_async_copy(own, dst, r.wl.at[0, n])
                loads[n].start()

        def forward(n, parts_of_z=(3, 1, 2)):
            for d in parts_of_z:
                here = landing(n, flow.at(d), iy)
                flow.arrived(here, r.wzr.at[n, d])
                flow.push(here, here, r.wys.at[n, d], r.wyr.at[n, d], flow.behind)

        def keep(n):
            loads[n].wait()
            copy = pltpu.make_async_copy(getattr(r, f"b{n}"), landing(n, iz, iy), r.wl.at[1, n])
            copy.start()
            stores.append(copy)

        def complete(n):
            for d in range(nz):
                flow.arrived(landing(n, flow.at(d), 1 - iy), r.wyr.at[n, d])

        for n in range(min(5, count)):
            bring(n)
        for d in range(1, nz):
            here = block(flow.line(d), ic, it)
            flow.arrived(here, r.tzr.at[d])
            flow.pass_on(d, here, r.tzs, r.tzr)
            flow.push(here, here, r.txs.at[d], r.txr.at[d], flow.across)
            flow.push(here, here, r.tcs.at[d, 0], r.tcr.at[d, 0], flow.beside)
        for n in range(3):
            forward(n)
        for d in range(1, nz):
            here = block(flow.line(d), ic, 1 - it)
            flow.arrived(here, r.txr.at[d])
            flow.push(here, here, r.tcs.at[d, 1], r.tcr.at[d, 1], flow.beside)
        stores = []

        def save(n, src, dst, d):
            copy = pltpu.make_async_copy(src, dst, r.st.at[n, d])
            copy.start()
            stores.append(copy)

        for n in range(4):
            loads[n].wait()
        for n in range(3):
            complete(n)
        tok_load.wait()
        for d in range(nz):
            z = flow.line(d)
            if d == 0:
                flow.arrived(pair(iz, 1 - ic), r.tcr.at[0, 0])
            else:
                for half in range(2):
                    side = it if half == 0 else 1 - it
                    flow.arrived(block(z, 1 - ic, side), r.tcr.at[d, half])
            save(0, r.tall.at[z], r.tokens.at[z], d)
            raw = mm(r.tall[z], r.qkv[...].reshape(2 * nz * w_rows, 3 * HD))
            r.raw[z] = raw
            query, key = raw[:, :HD], raw[:, HD : 2 * HD]
            r.dots[z] = row_sums(query * query, key * key)
        total_flow.send(CORE, r.dots[...])
        forward(3)
        value = total_flow.receive()
        total_flow.send(TP, value)
        value = total_flow.receive()
        total_flow.send("z", value)
        bring(5)
        for n in (4, 5):
            keep(n)
        complete(3)
        for n, (src, dst) in enumerate(((r.qkv, r.qkv_out), (r.wo, r.wo_out))):
            copy = pltpu.make_async_copy(src, dst, r.sw.at[n])
            copy.start()
            stores.append(copy)
        r.dots[...] = lax.rsqrt(total_flow.receive() * (1.0 / width) + EPSILON)
        cosine, sine = r.tables[0], r.tables[1]
        order = list(range(nz - 1, -1, -1))
        for n, d in enumerate(order):
            z = flow.line(d)
            sums = r.dots[z]
            r.qs_m[z] = spread(sums, 0)
            r.ks_m[z] = spread(sums, 1)
            r.nq_m[z] = r.raw[z, :, :HD] * r.qs_m[z]
            r.nk_m[z] = r.raw[z, :, HD : 2 * HD] * r.ks_m[z]
            query = rotate(r.nq_m[z] * r.gains[0:1], cosine, sine).astype(BF)
            key = rotate(r.nk_m[z] * r.gains[1:2], cosine, sine).astype(BF)
            value = r.raw[z, :, 2 * HD :].astype(BF)
            r.q_m[z] = query
            r.k_m[z] = key
            r.v_m[z] = value
            probability = softmax_rows(query, key, r.lens[z]).astype(BF)
            r.att_m[z] = mm(probability, value).astype(BF)
            for m, (name, _) in enumerate(saved):
                save(m + 1, getattr(r, name + "_m").at[z], getattr(r, name).at[z], d)
            wo = r.wo[...].reshape(2 * nz * w_rows, parts[3])
            r.rs_p[d] = mm_nt(r.att_m[z], wo).astype(BF)
            scatter.begin(d)
            if n:
                scatter.cross(order[n - 1])
            if n > 1:
                scatter.leave(order[n - 2])
            if n == 0:
                forward(4)
        scatter.cross(0)
        scatter.leave(1)
        bring(6, (3,))
        scatter.leave(0)
        forward(5)
        keep(6)
        scatter.end()
        branch = r.branch[...]
        scale = lax.rsqrt(jnp.mean(branch * branch, axis=-1, keepdims=True) + EPSILON)
        r.normed[...] = branch * scale
        r.scale[...] = jnp.broadcast_to(scale, r.scale.shape)
        start = pl.multiple_of((ic * 2 + it) * piece, piece)
        mine = r.tall[iz, pl.ds(start, piece)].astype(F32)
        r.residual[...] = mine + r.normed[...] * r.post[...]
        r.all_x[...] = r.residual[...].astype(BF)
        gather.start()
        gather.advance(1)
        bring(6, (2, 1), False)
        for d in range(2, 5):
            gather.advance(d)
        forward(6, (3,))
        for d in range(nz):
            gather.ready(d)
            z = gather.line(d)
            save(len(saved) + 1, gather.buf.at[z], r.wide.at[z], d)
        forward(6, (1, 2))
        for n in range(4, count):
            complete(n)
        for f in (flow, scatter, total_flow, gather):
            f.finish()
        for copy in stores:
            copy.wait()

    return k.run(9, body, 60)


def local(
    tokens,
    lengths,
    weight_query,
    weight_key,
    weight_value,
    weight_out,
    weight_gate,
    weight_up,
    weight_down,
    post_attention,
    post_feedforward,
    query_norm,
    key_norm,
    cotangent,
):
    nz, ny, nch, ntp = (lax.axis_size(a) for a in ("z", "y", "ch", TP))
    iz, iy, ich, icore, itp = (lax.axis_index(a) for a in AXES)
    token_rows = tokens[0]
    own_rows, width = token_rows.shape
    piece = own_rows // ntp
    seq_rows = own_rows * 2
    total_rows = seq_rows * nz
    scale_factor = 1.0 / math.sqrt(HD)
    own_head = iz * 2 + icore
    qn = lax.dynamic_slice_in_dim(query_norm, own_head * HD, HD)
    kn = lax.dynamic_slice_in_dim(key_norm, own_head * HD, HD)
    seq_lengths = lax.dynamic_index_in_dim(lengths.reshape(nz, ny), iy, 1, keepdims=False)
    positions = ich * seq_rows + jnp.arange(seq_rows, dtype=jnp.int32)
    key_positions = jnp.arange(seq_rows * nch, dtype=jnp.int32)
    cosine, sine_table = rope_tables(positions)
    allowed = (key_positions[None, None, :] <= positions[None, :, None]) & (
        key_positions[None, None, :] < seq_lengths[:, None, None]
    )
    my_tokens = lax.dynamic_slice_in_dim(token_rows, itp * piece, piece, 0)
    my_cot = lax.dynamic_slice_in_dim(cotangent[0], itp * piece, piece, 0)
    my_pos = (ich * 2 + icore) * own_rows + itp * piece + jnp.arange(piece, dtype=jnp.int32)
    my_valid = (my_pos < lengths[iz * ny + iy]).astype(F32)[:, None]

    weights = (
        weight_query,
        weight_key,
        weight_value,
        weight_out,
        weight_gate,
        weight_up,
        weight_down,
    )
    fused = nch == 1 and nz == 4
    gather, scatter = (gather_line, scatter_line) if fused else (gather_rows, scatter_rows)
    by_seq = lambda a: a.reshape(nz, seq_rows, HD)
    gains, tables = jnp.stack([qn, kn]), jnp.stack([cosine, sine_table])
    if fused:
        front = attention_front(
            token_rows, weights, gains, tables, seq_lengths, post_attention
        )
        wg, wu, wd = (front[f"o{n}"].reshape(width, -1) for n in (4, 5, 6))
    else:
        tokens_all, (wq, wk, wv, wo, wg, wu, wd) = intake(token_rows, weights)
        query_raw = mm(tokens_all, wq)
        key_raw = mm(tokens_all, wk)
        value_raw = mm(tokens_all, wv)
        squares = head_total(
            jnp.stack([jnp.sum(query_raw * query_raw, axis=-1), jnp.sum(key_raw * key_raw, axis=-1)])
        )
        scales = lax.rsqrt(squares / width + EPSILON)
        query_scale = scales[0][:, None]
        key_scale = scales[1][:, None]
        queries = rotate(by_seq(query_raw * query_scale * qn), cosine, sine_table).astype(BF)
        keys = rotate(by_seq(key_raw * key_scale * kn), cosine, sine_table).astype(BF)
        values = by_seq(value_raw).astype(BF)
        if nch > 1:
            keys_full = lax.all_gather(keys, "ch", axis=1, tiled=True)
            values_full = lax.all_gather(values, "ch", axis=1, tiled=True)
        else:
            keys_full, values_full = keys, values
        scores = (
            jnp.einsum(SCORE, queries, keys_full, preferred_element_type=F32) * scale_factor
        )
        scores = jnp.where(allowed, scores, NEGATIVE)
        exponent = jnp.exp(scores - jnp.max(scores, axis=-1, keepdims=True))
        probability = exponent / jnp.sum(exponent, axis=-1, keepdims=True)
        probability_low = probability.astype(BF)
        attended = jnp.einsum(APPLY, probability_low, values_full, preferred_element_type=F32)
        attended_low = attended.reshape(total_rows, HD).astype(BF)
        branch_sum = scatter_rows(mm_nt(attended_low, wo))
    if fused:
        attn_normed, residual = front["normed"], front["residual"]
        attn_scale = front["scale"][:, :1]
        residual_all = front["wide"].reshape(-1, width)
    else:
        attn_scale = lax.rsqrt(jnp.mean(branch_sum * branch_sum, axis=-1, keepdims=True) + EPSILON)
        attn_normed = branch_sum * attn_scale
        residual = my_tokens.astype(F32) + attn_normed * post_attention
        residual_all = gather(residual.astype(BF))
    attention_branch = attn_normed * post_attention
    gate_value = mm(residual_all, wg)
    up_value = mm(residual_all, wu)
    sigmoid_gate = jax.nn.sigmoid(gate_value)
    silu_gate = gate_value * sigmoid_gate
    mixed_low = (silu_gate * up_value).astype(BF)
    down_sum = scatter(mm_nt(mixed_low, wd))
    ffn_scale = lax.rsqrt(jnp.mean(down_sum * down_sum, axis=-1, keepdims=True) + EPSILON)
    ffn_normed = down_sum * ffn_scale
    feedforward_branch = ffn_normed * post_feedforward
    stream = residual + feedforward_branch
    stat_terms = jnp.stack(
        [
            jnp.sum(my_valid * stream * stream),
            jnp.sum(my_valid * attention_branch * attention_branch),
            jnp.sum(my_valid * feedforward_branch * feedforward_branch),
        ]
    )
    grad_stream = my_cot * my_valid
    grad_post_ff = jnp.sum(grad_stream * ffn_normed, axis=0)
    scaled = grad_stream * post_feedforward
    grad_down_sum = ffn_scale * (
        scaled - ffn_normed * jnp.mean(scaled * ffn_normed, axis=-1, keepdims=True)
    )
    down_all = gather(grad_down_sum.astype(BF))
    grad_mixed = mm(down_all, wd)
    gate_low = (
        grad_mixed * up_value * sigmoid_gate * (1.0 + gate_value * (1.0 - sigmoid_gate))
    ).astype(BF)
    up_low = (grad_mixed * silu_gate).astype(BF)
    grad_wg = mm_tn(residual_all, gate_low)
    grad_wu = mm_tn(residual_all, up_low)
    grad_wd = mm_tn(down_all, mixed_low)
    grad_residual = grad_stream + scatter(mm_nt(gate_low, wg) + mm_nt(up_low, wu))
    grad_post_attn = jnp.sum(grad_residual * attn_normed, axis=0)
    scaled_attn = grad_residual * post_attention
    grad_branch = attn_scale * (
        scaled_attn - attn_normed * jnp.mean(scaled_attn * attn_normed, axis=-1, keepdims=True)
    )
    if not fused:
        branch_all = gather_rows(grad_branch.astype(BF))
        grad_att_low = mm(branch_all, wo).astype(BF)
        grad_wo = mm_tn(branch_all, attended_low)
        grad_att = by_seq(grad_att_low)
        grad_prob = jnp.einsum(SCORE, grad_att, values_full, preferred_element_type=F32)
        row_dots = jnp.sum(probability * grad_prob, axis=-1, keepdims=True)
        grad_scores = (probability * (grad_prob - row_dots)).astype(BF)
        grad_queries = (
            jnp.einsum(APPLY, grad_scores, keys_full, preferred_element_type=F32)
            * scale_factor
        )
        grad_keys = (
            jnp.einsum("bts,btd->bsd", grad_scores, queries, preferred_element_type=F32) * scale_factor
        )
        grad_values = jnp.einsum("bts,btd->bsd", probability_low, grad_att, preferred_element_type=F32)
        if nch > 1:
            grad_keys, grad_values = (
                lax.psum_scatter(g.astype(BF), "ch", scatter_dimension=1, tiled=True).astype(F32)
                for g in (grad_keys, grad_values)
            )
        value_grad_low = grad_values.reshape(total_rows, HD).astype(BF)
        grad_q_normed = rotate_back(grad_queries, cosine, sine_table).reshape(total_rows, HD)
        grad_k_normed = rotate_back(grad_keys, cosine, sine_table).reshape(total_rows, HD)
        query_weighted = grad_q_normed * qn
        key_weighted = grad_k_normed * kn
        dots = head_total(
            jnp.stack(
                [
                    jnp.sum(query_weighted * query_raw, axis=-1),
                    jnp.sum(key_weighted * key_raw, axis=-1),
                ]
            )
        )
        query_grad_low = (
            query_scale * (query_weighted - query_raw * query_scale**2 * (dots[0] / width)[:, None])
        ).astype(BF)
        key_grad_low = (
            key_scale * (key_weighted - key_raw * key_scale**2 * (dots[1] / width)[:, None])
        ).astype(BF)
        grad_qnorm = jnp.sum(grad_q_normed * query_raw * query_scale, axis=0)
        grad_knorm = jnp.sum(grad_k_normed * key_raw * key_scale, axis=0)
        grad_wq = mm_tn(tokens_all, query_grad_low)
        grad_wk = mm_tn(tokens_all, key_grad_low)
        grad_wv = mm_tn(tokens_all, value_grad_low)
        grad_rows = grad_residual + scatter_rows(
            mm_nt(query_grad_low, wq) + mm_nt(key_grad_low, wk) + mm_nt(value_grad_low, wv)
        )
    if fused:
        saved = tuple(front[n] for n in ("q", "k", "v", "att", "nq", "nk", "qs", "ks"))
        norms_wide = jnp.zeros((2 * width,), F32)
    else:
        slot = itp * (width // ntp) + own_head * HD
        zero_row = jnp.zeros((width,), F32)
        norms_wide = jnp.concatenate(
            [
                lax.dynamic_update_slice_in_dim(zero_row, grad_qnorm, slot, 0),
                lax.dynamic_update_slice_in_dim(zero_row, grad_knorm, slot, 0),
            ]
        )
    terms = jnp.concatenate([grad_post_attn, grad_post_ff, norms_wide, stat_terms])
    if fused:
        weight_grads, grad_input, output, summed = attention_back(
            grad_branch.astype(BF),
            (grad_wd, grad_wg, grad_wu),
            front["wo_out"].reshape(width, -1),
            front["qkv_out"].reshape(width, -1),
            saved,
            front["tokens"],
            grad_residual,
            stream.astype(BF),
            terms,
            gains,
            tables,
            seq_lengths,
        )
        weight_grads = [weight_grads[n] for n in (0, 1, 2, 3, 5, 6, 4)]
    else:
        weight_grads = outlet((grad_wq, grad_wk, grad_wv, grad_wo, grad_wg, grad_wu, grad_wd))
        grad_input = lax.all_gather(grad_rows, TP, axis=0, tiled=True)
        output = lax.all_gather(stream.astype(BF), TP, axis=0, tiled=True)
        summed = all_total(terms)
    half = width // ntp
    qn_sum = lax.dynamic_slice_in_dim(summed, 2 * width + itp * half, half)
    kn_sum = lax.dynamic_slice_in_dim(summed, 3 * width + itp * half, half)
    token_count = jnp.sum(lengths.astype(F32))
    root_means = jnp.sqrt(summed[4 * width :] / (token_count * width))
    return (
        output[None],
        grad_input[None],
        *weight_grads,
        summed[:width],
        summed[width : 2 * width],
        qn_sum,
        kn_sum,
        root_means,
    )


def solution(mesh):
    n_fsdp, n_ctx, n_tp = (mesh.shape[a] for a in ("fsdp", "ctx", TP))
    fine = Mesh(mesh.devices.reshape(n_fsdp // 2, 2, n_ctx // 2, 2, n_tp), AXES)
    fsdp, ctx = ("z", "y"), ("ch", CORE)
    rows = P(fsdp, ctx, None)
    weight = P(fsdp, TP)
    return jax.shard_map(
        local,
        mesh=fine,
        in_specs=(rows, P(), *([weight] * 7), P(), P(), P(TP), P(TP), rows),
        out_specs=(rows, rows, *([weight] * 7), P(), P(), P(TP), P(TP), P()),
        check_vma=False,
    )
```

```python
import functools
import math
import types

import jax
import jax.numpy as jnp
from jax import lax
from jax.experimental import pallas as pl
from jax.experimental.pallas import tpu as pltpu
from jax.sharding import Mesh, PartitionSpec as P

HD = 128
EPSILON = 1e-06
ROPE_BASE = 500000.0
NEGATIVE = -1e30
CORE, TP = "core", "tp"
SCORE = "btd,bsd->bts"
APPLY = "bts,bsd->btd"
AXES = ("z", "y", "ch", CORE, TP)
BF = jnp.bfloat16
F32 = jnp.float32


def rope_tables(positions):
    half_size = HD // 2
    exponent = jnp.arange(half_size, dtype=F32) * (2.0 / HD)
    frequency = jnp.power(ROPE_BASE, -exponent)
    angles = positions.astype(F32)[:, None] * frequency[None, :]
    cosine = jnp.cos(angles)
    sine_table = jnp.sin(angles)
    return (
        jnp.concatenate([cosine, cosine], axis=-1),
        jnp.concatenate([sine_table, sine_table], axis=-1),
    )


def rotate(values, cosine, sine_table):
    half_size = HD // 2
    turned = jnp.concatenate([-values[..., half_size:], values[..., :half_size]], axis=-1)
    return values * cosine + turned * sine_table


def rotate_back(grads_in, cosine, sine_table):
    half_size = HD // 2
    sin_part = grads_in * sine_table
    return grads_in * cosine + jnp.concatenate(
        [sin_part[..., half_size:], -sin_part[..., :half_size]], axis=-1
    )


def dot(former, latter, dims):
    return lax.dot_general(former, latter, (dims, ((), ())), preferred_element_type=F32)


def mm(a, b):
    return dot(a, b, ((1,), (0,)))


def mm_nt(a, b):
    return dot(a, b, ((1,), (1,)))


def mm_tn(a, b):
    return dot(a, b, ((0,), (0,)))


MESH = pl.DeviceIdType.MESH


def flip(axis, bits):
    me = lax.axis_index(axis)
    result, weight = me, 1
    while weight <= bits:
        if (bits // weight) % 2:
            result = result + weight * (1 - 2 * lax.rem(me // weight, 2))
        weight *= 2
    return result


def greet(partners):
    barrier = pltpu.get_barrier_semaphore()
    for partner in partners:
        pl.semaphore_signal(barrier, inc=1, device_id=partner, device_id_type=MESH)
    pl.semaphore_wait(barrier, len(partners))


def remote(src, dst, send_sem, recv_sem, partner):
    return pltpu.make_async_remote_copy(
        src_ref=src,
        dst_ref=dst,
        send_sem=send_sem,
        recv_sem=recv_sem,
        device_id=partner,
        device_id_type=MESH,
    )


def partners_of(axes):
    found = []
    for axis in axes:
        for bits in range(1, lax.axis_size(axis)):
            found.append({axis: flip(axis, bits)})
    return found


def call(kernel, identity, out_shape, in_spaces, out_spaces, scratch, limit, *operands):
    return pl.pallas_call(
        kernel,
        out_shape=out_shape,
        in_specs=[pl.BlockSpec(memory_space=s) for s in in_spaces],
        out_specs=jax.tree.map(lambda s: pl.BlockSpec(memory_space=s), out_spaces),
        scratch_shapes=scratch,
        compiler_params=pltpu.CompilerParams(
            collective_id=identity, has_side_effects=True, vmem_limit_bytes=limit * 2**20
        ),
    )(*operands)


DMA = pltpu.SemaphoreType.DMA


def gather_kernel(nz, x_ref, out_ref, own_sem, zs, zr, xs, xr, cs, cr):
    iz, ic, it = (lax.axis_index(a) for a in ("z", CORE, TP))
    greet(partners_of(("z", TP, CORE)))
    sends = []

    def push(src, where, send_sem, recv_sem, partner):
        copy = remote(src, out_ref.at[where], send_sem, recv_sem, partner)
        copy.start()
        sends.append(copy)

    across, beside = {TP: 1 - it}, {CORE: 1 - ic}
    own = (iz, ic, it)
    for d in range(1, nz):
        push(x_ref, own, zs.at[d], zr.at[d], {"z": flip("z", d)})
    push(x_ref, own, xs.at[0], xr.at[0], across)
    push(x_ref, own, cs.at[0, 0], cr.at[0, 0], beside)
    local_copy = pltpu.make_async_copy(x_ref, out_ref.at[own], own_sem)
    local_copy.start()

    def await_at(where, sem):
        remote(out_ref.at[where], out_ref.at[where], sem, sem, across).wait_recv()

    def from_across(d):
        where = (flip("z", d), ic, 1 - it)
        await_at(where, xr.at[d])
        push(out_ref.at[where], where, cs.at[d, 1], cr.at[d, 1], beside)

    for d in range(1, nz):
        where = (flip("z", d), ic, it)
        await_at(where, zr.at[d])
        push(out_ref.at[where], where, xs.at[d], xr.at[d], across)
        push(out_ref.at[where], where, cs.at[d, 0], cr.at[d, 0], beside)
        from_across(d - 1)
    from_across(nz - 1)
    for d in range(nz):
        for half in range(2):
            side = it if half == 0 else 1 - it
            await_at((flip("z", d), 1 - ic, side), cr.at[d, half])
    for copy in sends:
        copy.wait_send()
    local_copy.wait()


def gather_rows(rows):
    piece, width = rows.shape
    nz = lax.axis_size("z")
    out = call(
        functools.partial(gather_kernel, nz),
        1,
        jax.ShapeDtypeStruct((nz, 2, 2, piece, width), rows.dtype),
        [pl.ANY],
        pl.ANY,
        [DMA, DMA((nz,)), DMA((nz,)), DMA((nz,)), DMA((nz,)), DMA((nz, 2)), DMA((nz, 2))],
        16,
        rows,
    )
    return out.reshape(-1, width)


def scatter_kernel(
    nz, p_ref, out_ref, own, cin, xout, xin, zout, zin, ls, cs, cr, xs, xr, zs, zr
):
    iz, ic, it = (lax.axis_index(a) for a in ("z", CORE, TP))
    greet(partners_of(("z", TP, CORE)))
    across, beside = {TP: 1 - it}, {CORE: 1 - ic}
    order = list(range(nz - 1, -1, -1))
    loads, besides, acrosses, zeds = {}, {}, {}, {}
    for d in order:
        target = flip("z", d) if d else iz
        besides[d] = remote(p_ref.at[target, 1 - ic], cin.at[d], cs.at[d], cr.at[d], beside)
        besides[d].start()
        loads[d] = pltpu.make_async_copy(p_ref.at[target, ic], own.at[d], ls.at[d])
        loads[d].start()

    def add(d, side):
        return own[d, side].astype(F32) + cin[d, side].astype(F32)

    def after_across(d):
        acrosses[d].wait_recv()
        total = add(d, it) + xin[d].astype(F32)
        if d == 0:
            out_ref[...] = total
        else:
            zout[d] = total.astype(BF)
            zeds[d] = remote(zout.at[d], zin.at[d], zs.at[d], zr.at[d], {"z": flip("z", d)})
            zeds[d].start()

    for n, d in enumerate(order):
        loads[d].wait()
        besides[d].wait_recv()
        xout[d] = add(d, 1 - it).astype(BF)
        acrosses[d] = remote(xout.at[d], xin.at[d], xs.at[d], xr.at[d], across)
        acrosses[d].start()
        if n:
            after_across(order[n - 1])
    after_across(0)
    for d in order[:-1]:
        zeds[d].wait_recv()
        out_ref[...] += zin[d].astype(F32)
    for group in (besides, acrosses, zeds):
        for copy in group.values():
            copy.wait_send()


def scatter_rows(partial):
    nz = lax.axis_size("z")
    width = partial.shape[1]
    part = partial.astype(BF).reshape(nz, 2, 2, -1, width)
    piece = part.shape[3]
    sems = [DMA((nz,)) for _ in range(7)]
    return call(
        functools.partial(scatter_kernel, nz),
        2,
        jax.ShapeDtypeStruct((piece, width), F32),
        [pl.ANY],
        pltpu.VMEM,
        [
            pltpu.VMEM((nz, 2, piece, width), BF),
            pltpu.VMEM((nz, 2, piece, width), BF),
            *[pltpu.VMEM((nz, piece, width), BF) for _ in range(4)],
            *sems,
        ],
        32,
        part,
    )


def total_kernel(axes, x_ref, out_ref, *scratch):
    greet(partners_of(axes))
    value = x_ref[...]
    sends = []
    for stage, axis in enumerate(axes):
        slots, send_sems, recv_sems = scratch[3 * stage : 3 * stage + 3]
        size = lax.axis_size(axis)
        me = lax.axis_index(axis)
        slots[me] = value
        copies = []
        for d in range(1, size):
            copy = remote(
                slots.at[me], slots.at[me], send_sems.at[d], recv_sems.at[d], {axis: flip(axis, d)}
            )
            copy.start()
            copies.append(copy)
        for copy in copies:
            copy.wait_recv()
        value = slots[0]
        for n in range(1, size):
            value = value + slots[n]
        sends += copies
    out_ref[...] = value
    for copy in sends:
        copy.wait_send()


def total(terms, axes, identity):
    axes = tuple(a for a in axes if lax.axis_size(a) > 1)
    scratch = []
    for axis in axes:
        size = lax.axis_size(axis)
        scratch += [pltpu.VMEM((size, *terms.shape), F32), DMA((size,)), DMA((size,))]
    return call(
        functools.partial(total_kernel, axes),
        identity,
        jax.ShapeDtypeStruct(terms.shape, F32),
        [pltpu.VMEM],
        pltpu.VMEM,
        scratch,
        16,
        terms,
    )


def head_total(terms):
    return total(terms.reshape(-1, 128), (CORE, TP, "z"), 3).reshape(terms.shape)


def all_total(terms):
    size = terms.shape[0]
    padded = jnp.pad(terms, (0, -size % 1024)).reshape(-1, 128)
    return total(padded, (CORE, TP, "y", "z", "ch"), 4).reshape(-1)[:size]


def columns(ref, slot, count):
    return ref.at[:, pl.ds(pl.multiple_of(slot * count, 128), count)]


def intake_kernel(nz, count, tok_ref, *refs):
    w_refs, refs = refs[:count], refs[count:]
    tok_out, refs = refs[0], refs[1:]
    o_refs, refs = refs[:count], refs[count:]
    tok_buf, refs = refs[0], refs[1:]
    bufs, refs = refs[:count], refs[count:]
    tl, tzs, tzr, txs, txr, tcs, tcr, wl, wzs, wzr, wys, wyr = refs
    iz, iy, ic, it = (lax.axis_index(a) for a in ("z", "y", CORE, TP))
    across, beside, behind = {TP: 1 - it}, {CORE: 1 - ic}, {"y": 1 - iy}
    greet(partners_of(("z", "y", TP, CORE)))
    sends = []

    def push(src, dst, send_sem, recv_sem, partner):
        copy = remote(src, dst, send_sem, recv_sem, partner)
        copy.start()
        sends.append(copy)

    def arrived(ref, sem):
        remote(ref, ref, sem, sem, across).wait_recv()

    for d in range(1, nz):
        push(tok_ref.at[it], tok_out.at[iz, ic, it], tzs.at[d], tzr.at[d], {"z": flip("z", d)})
    push(tok_ref, tok_out.at[iz, ic], tcs.at[0, 0], tcr.at[0, 0], beside)
    tok_load = pltpu.make_async_copy(tok_ref, tok_buf, tl.at[0])
    tok_load.start()
    widths = [o.shape[-1] for o in o_refs]
    loads = []
    for k, (w, o) in enumerate(zip(w_refs, o_refs)):
        own = columns(w, iz * 2 + ic, widths[k])
        push(own, o.at[iz, iy], wys.at[k, 0], wyr.at[k, 0], behind)
        for d in range(1, nz):
            other = flip("z", d)
            push(
                columns(w, other * 2 + ic, widths[k]),
                o.at[iz, iy],
                wzs.at[k, d],
                wzr.at[k, d],
                {"z": other},
            )
        load = pltpu.make_async_copy(own, bufs[k], wl.at[k])
        load.start()
        loads.append(load)
    tok_load.wait()
    stores = [pltpu.make_async_copy(tok_buf, tok_out.at[iz, ic], tl.at[1])]
    stores[0].start()
    for d in range(1, nz):
        block = tok_out.at[flip("z", d), ic, it]
        arrived(block, tzr.at[d])
        push(block, block, txs.at[d], txr.at[d], across)
        push(block, block, tcs.at[d, 0], tcr.at[d, 0], beside)

    def forward(k):
        for d in range(1, nz):
            block = o_refs[k].at[flip("z", d), iy]
            arrived(block, wzr.at[k, d])
            push(block, block, wys.at[k, d], wyr.at[k, d], behind)

    first = min(3, count)
    for k in range(first):
        forward(k)
    for d in range(1, nz):
        block = tok_out.at[flip("z", d), ic, 1 - it]
        arrived(block, txr.at[d])
        push(block, block, tcs.at[d, 1], tcr.at[d, 1], beside)
    for k, load in enumerate(loads):
        load.wait()
        store = pltpu.make_async_copy(bufs[k], o_refs[k].at[iz, iy], wl.at[k])
        store.start()
        stores.append(store)
    for k in range(first, count):
        forward(k)
    arrived(tok_out.at[iz, 1 - ic], tcr.at[0, 0])
    for d in range(1, nz):
        for half in range(2):
            side = it if half == 0 else 1 - it
            arrived(tok_out.at[flip("z", d), 1 - ic, side], tcr.at[d, half])
    for k in range(count):
        for d in range(nz):
            source = flip("z", d) if d else iz
            arrived(o_refs[k].at[source, 1 - iy], wyr.at[k, d])
    for copy in sends:
        copy.wait_send()
    for store in stores:
        store.wait()


def intake(token_rows, weights):
    nz = lax.axis_size("z")
    count = len(weights)
    own_rows, width = token_rows.shape
    rows = weights[0].shape[0]
    parts = [w.shape[1] // (2 * nz) for w in weights]
    piece = own_rows // 2
    out_shape = [jax.ShapeDtypeStruct((nz, 2, 2, piece, width), BF)] + [
        jax.ShapeDtypeStruct((nz, 2, rows, c), BF) for c in parts
    ]
    got = call(
        functools.partial(intake_kernel, nz, count),
        5,
        out_shape,
        [pl.ANY] * (count + 1),
        [pl.ANY] * (count + 1),
        [
            pltpu.VMEM((2, piece, width), BF),
            *[pltpu.VMEM((rows, c), BF) for c in parts],
            DMA((2,)),
            *[DMA((nz,)) for _ in range(4)],
            *[DMA((nz, 2)) for _ in range(2)],
            DMA((count,)),
            *[DMA((count, nz)) for _ in range(4)],
        ],
        16,
        token_rows.reshape(2, piece, width),
        *weights,
    )
    return got[0].reshape(-1, width), [g.reshape(-1, g.shape[-1]) for g in got[1:]]


def outlet_kernel(nz, count, *refs):
    g_refs, refs = refs[:count], refs[count:]
    o_refs, refs = refs[:count], refs[count:]
    own, refs = refs[:count], refs[count:]
    yin, refs = refs[:count], refs[count:]
    zout, refs = refs[:count], refs[count:]
    ls, ys, yr, zs, zr, cs, cr, os = refs
    iz, iy, ic = (lax.axis_index(a) for a in ("z", "y", CORE))
    beside, behind = {CORE: 1 - ic}, {"y": 1 - iy}
    greet(partners_of(("z", "y", CORE)))
    sends, loads, pairs, stores = [], {}, {}, []

    def push(src, dst, send_sem, recv_sem, partner):
        copy = remote(src, dst, send_sem, recv_sem, partner)
        copy.start()
        sends.append(copy)
        return copy

    order = [(k, d) for k in range(count) for d in range(nz - 1, -1, -1)]
    widths = [g.shape[-1] for g in g_refs]
    for k, d in order:
        target = flip("z", d) if d else iz
        pairs[k, d] = push(
            g_refs[k].at[target, 1 - iy], yin[k].at[d], ys.at[k, d], yr.at[k, d], behind
        )
        loads[k, d] = pltpu.make_async_copy(g_refs[k].at[target, iy], own[k].at[d], ls.at[k, d])
        loads[k, d].start()

    def relay(k, d):
        block = columns(o_refs[k], flip("z", d) * 2 + ic, widths[k])
        remote(block, block, zr.at[k, d], zr.at[k, d], beside).wait_recv()
        push(block, block, cs.at[k, d], cr.at[k, d], beside)

    for n, (k, d) in enumerate(order):
        loads[k, d].wait()
        pairs[k, d].wait_recv()
        zout[k][d] = (own[k][d].astype(F32) + yin[k][d].astype(F32)).astype(BF)
        mine = columns(o_refs[k], iz * 2 + ic, widths[k])
        if d:
            push(zout[k].at[d], mine, zs.at[k, d], zr.at[k, d], {"z": flip("z", d)})
        else:
            push(zout[k].at[d], mine, cs.at[k, d], cr.at[k, d], beside)
            store = pltpu.make_async_copy(zout[k].at[d], mine, os.at[k])
            store.start()
            stores.append(store)
            if k:
                for e in range(nz - 1, 0, -1):
                    relay(k - 1, e)
    for e in range(nz - 1, 0, -1):
        relay(count - 1, e)
    for k, d in order:
        source = flip("z", d) if d else iz
        block = columns(o_refs[k], source * 2 + 1 - ic, widths[k])
        remote(block, block, cr.at[k, d], cr.at[k, d], beside).wait_recv()
    for copy in sends:
        copy.wait_send()
    for store in stores:
        store.wait()


def outlet(grads, identity=6):
    nz = lax.axis_size("z")
    count = len(grads)
    parts = [g.shape[1] for g in grads]
    blocks = [g.astype(BF).reshape(nz, 2, -1, g.shape[1]) for g in grads]
    rows = blocks[0].shape[2]
    got = call(
        functools.partial(outlet_kernel, nz, count),
        identity,
        [jax.ShapeDtypeStruct((rows, 2 * nz * c), BF) for c in parts],
        [pl.ANY] * count,
        [pl.ANY] * count,
        [
            *[pltpu.VMEM((nz, rows, c), BF) for _ in range(3) for c in parts],
            *[DMA((count, nz)) for _ in range(7)],
            DMA((count,)),
        ],
        32,
        *blocks,
    )
    if lax.axis_size("ch") > 1:
        got = lax.psum(tuple(got), "ch")
    return [g.astype(F32) for g in got]


class Kernel:
    def __init__(self):
        self.ins, self.outs, self.scratch = [], [], []

    def inp(self, name, array, space=pl.ANY):
        self.ins.append((name, array, space))

    def out(self, name, shape, dtype, space=pl.ANY):
        self.outs.append((name, jax.ShapeDtypeStruct(shape, dtype), space))

    def mem(self, name, shape, dtype):
        self.scratch.append((name, pltpu.VMEM(shape, dtype)))

    def sem(self, name, *shape):
        self.scratch.append((name, DMA(shape)))

    def run(self, identity, body, limit):
        names = [n for n, *_ in self.ins + self.outs + self.scratch]

        def kernel(*refs):
            body(types.SimpleNamespace(**dict(zip(names, refs))))

        got = call(
            kernel,
            identity,
            [shape for _, shape, _ in self.outs],
            [space for *_, space in self.ins],
            [space for *_, space in self.outs],
            [made for _, made in self.scratch],
            limit,
            *[array for _, array, _ in self.ins],
        )
        return {n: g for (n, *_), g in zip(self.outs, got)}


class Flow:
    def __init__(self):
        self.sends, self.inner_sends = [], []
        self.iz, self.iy, self.ic, self.it = (
            lax.axis_index(a) for a in ("z", "y", CORE, TP)
        )
        self.across = {TP: 1 - self.it}
        self.beside = {CORE: 1 - self.ic}
        self.behind = {"y": 1 - self.iy}
        self.near, self.mid = {"z": flip("z", 1)}, {"z": 3 - self.iz}
        self.role = lax.rem((self.iz + 1) // 2, 2)
        self.inner = self.role == 1

    def at(self, d):
        return flip("z", d) if d else self.iz

    def line(self, s):
        side = self.iz // 2
        return (self.iz, self.near["z"], 2 - side, 3 - 3 * side)[s]

    def push(self, src, dst, send_sem, recv_sem, partner):
        copy = remote(src, dst, send_sem, recv_sem, partner)
        copy.start()
        self.sends.append(copy)
        return copy

    def push_inner(self, src, dst, send_sem, recv_sem, partner):
        copy = remote(src, dst, send_sem, recv_sem, partner)
        pl.when(self.inner)(copy.start)
        self.inner_sends.append(copy)

    def pass_on(self, s, block, send_sems, recv_sems):
        partner, number = ((self.mid, 3), (self.near, 2), (self.near, 3))[s - 1]
        self.push_inner(block, block, send_sems.at[s + 2], recv_sems.at[number], partner)

    def arrived(self, ref, sem):
        remote(ref, ref, sem, sem, self.across).wait_recv()

    def finish(self):
        for copy in self.sends:
            copy.wait_send()
        if self.inner_sends:

            @pl.when(self.inner)
            def _():
                for copy in self.inner_sends:
                    copy.wait_send()

        self.sends, self.inner_sends = [], []


def greet_line():
    flow = Flow()
    barrier = pltpu.get_barrier_semaphore()
    for partner in (flow.near, flow.across, flow.beside):
        pl.semaphore_signal(barrier, inc=1, device_id=partner, device_id_type=MESH)

    @pl.when(flow.inner)
    def _():
        pl.semaphore_signal(barrier, inc=1, device_id=flow.mid, device_id_type=MESH)

    pl.semaphore_wait(barrier, 3 + flow.role)


def stripe(ref, z, core, tp, piece):
    start = pl.multiple_of((core * 2 + tp) * piece, piece)
    return ref.at[z, pl.ds(start, piece)]


class Gather(Flow):
    @staticmethod
    def setup(k, name, rows, out=False, inside=False):
        piece, width = rows.shape
        if inside:
            k.mem(name + "_x", rows.shape, rows.dtype)
        else:
            k.inp(name + "_x", rows)
        (k.out if out else k.mem)(name, (4, 4 * piece, width), rows.dtype)
        k.sem(name + "_own")
        k.sem(name + "_zs", 6)
        for s in ("_zr", "_xs", "_xr"):
            k.sem(name + s, 4)
        k.sem(name + "_cs", 4, 2)
        k.sem(name + "_cr", 4, 2)

    def __init__(self, r, name):
        super().__init__()
        self.x, self.buf = getattr(r, name + "_x"), getattr(r, name)
        self.own_sem, self.zs, self.zr, self.xs, self.xr, self.cs, self.cr = (
            getattr(r, name + s) for s in ("_own", "_zs", "_zr", "_xs", "_xr", "_cs", "_cr")
        )
        self.piece = self.x.shape[0]

    def block(self, z, core, tp):
        return stripe(self.buf, z, core, tp, self.piece)

    def start(self):
        own = self.block(self.iz, self.ic, self.it)
        self.push(self.x, own, self.zs.at[1], self.zr.at[1], self.near)
        self.push_inner(self.x, own, self.zs.at[2], self.zr.at[2], self.mid)
        self.push(self.x, own, self.xs.at[0], self.xr.at[0], self.across)
        self.push(self.x, own, self.cs.at[0, 0], self.cr.at[0, 0], self.beside)
        self.local = pltpu.make_async_copy(self.x, own, self.own_sem)
        self.local.start()

    def from_across(self, s):
        block = self.block(self.line(s), self.ic, 1 - self.it)
        self.arrived(block, self.xr.at[s])
        self.push(block, block, self.cs.at[s, 1], self.cr.at[s, 1], self.beside)

    def advance(self, s):
        if s < 4:
            block = self.block(self.line(s), self.ic, self.it)
            self.arrived(block, self.zr.at[s])
            self.pass_on(s, block, self.zs, self.zr)
            self.push(block, block, self.xs.at[s], self.xr.at[s], self.across)
            self.push(block, block, self.cs.at[s, 0], self.cr.at[s, 0], self.beside)
        self.from_across(s - 1)

    def ready(self, s):
        if s == 0:
            self.local.wait()
        for half in range(2):
            side = self.it if half == 0 else 1 - self.it
            self.arrived(self.block(self.line(s), 1 - self.ic, side), self.cr.at[s, half])


class Scatter(Flow):
    @staticmethod
    def setup(k, name, piece, width, partial=None):
        if partial is None:
            k.mem(name + "_p", (4, 4 * piece, width), BF)
        else:
            k.inp(name + "_p", partial)
            k.mem(name + "_m", (4, 2 * piece, width), BF)
            k.sem(name + "_ls", 4)
        k.mem(name + "_c", (4, 2 * piece, width), BF)
        for s in ("_xo", "_xi", "_zo"):
            k.mem(name + s, (4, piece, width), BF)
        k.mem(name + "_zi", (6, piece, width), BF)
        for s in ("_cs", "_cr", "_xs", "_xr", "_zs"):
            k.sem(name + s, 4)
        k.sem(name + "_zr", 6)

    def __init__(self, r, name, out):
        super().__init__()
        self.out = out
        self.p, self.c, self.xo, self.xi, self.zo, self.zi = (
            getattr(r, name + s) for s in ("_p", "_c", "_xo", "_xi", "_zo", "_zi")
        )
        self.cs, self.cr, self.xs, self.xr, self.zs, self.zr = (
            getattr(r, name + s) for s in ("_cs", "_cr", "_xs", "_xr", "_zs", "_zr")
        )
        self.m, self.ls = getattr(r, name + "_m", None), getattr(r, name + "_ls", None)
        self.piece = self.xo.shape[1]
        self.core_copy, self.across_copy, self.loads = {}, {}, {}

    def rows(self, core):
        return pl.ds(pl.multiple_of(core * 2 * self.piece, 2 * self.piece), 2 * self.piece)

    def begin(self, s):
        part = s if self.m is None else self.line(s)
        self.core_copy[s] = self.push(
            self.p.at[part, self.rows(1 - self.ic)],
            self.c.at[s],
            self.cs.at[s],
            self.cr.at[s],
            self.beside,
        )
        if self.m is not None:
            self.loads[s] = pltpu.make_async_copy(
                self.p.at[part, self.rows(self.ic)], self.m.at[s], self.ls.at[s]
            )
            self.loads[s].start()

    def add(self, s, side):
        rows = pl.ds(pl.multiple_of(side * self.piece, self.piece), self.piece)
        if self.m is not None:
            own = self.m[s, rows]
        else:
            start = pl.multiple_of((self.ic * 2 + side) * self.piece, self.piece)
            own = self.p[s, pl.ds(start, self.piece)]
        return own.astype(F32) + self.c[s, rows].astype(F32)

    def cross(self, s):
        if s in self.loads:
            self.loads[s].wait()
        self.core_copy[s].wait_recv()
        self.xo[s] = self.add(s, 1 - self.it).astype(BF)
        self.across_copy[s] = self.push(
            self.xo.at[s], self.xi.at[s], self.xs.at[s], self.xr.at[s], self.across
        )

    def leave(self, s):
        self.across_copy[s].wait_recv()

        def value():
            return self.add(s, self.it) + self.xi[s].astype(F32)

        if s == 0:
            self.out[...] = value()
            return
        came = (None, 4, 2, 3)[s]

        @pl.when(self.inner)
        def _():
            self.arrived(self.zi.at[came], self.zr.at[came])
            self.zo[s] = (value() + self.zi[came].astype(F32)).astype(BF)

        @pl.when(self.role == 0)
        def _():
            self.zo[s] = value().astype(BF)

        place = s + self.role * (None, -1, 3, 1)[s]
        partner = self.near["z"]
        if s > 1:
            partner = partner + self.role * (self.mid["z"] - partner)
        self.push(
            self.zo.at[s], self.zi.at[place], self.zs.at[s], self.zr.at[place], {"z": partner}
        )

    def end(self):
        @pl.when(self.inner)
        def _():
            for place in (1, 5):
                self.arrived(self.zi.at[place], self.zr.at[place])
                self.out[...] += self.zi[place].astype(F32)

        @pl.when(self.role == 0)
        def _():
            self.arrived(self.zi.at[0], self.zr.at[0])
            self.out[...] += self.zi[0].astype(F32)


class Total(Flow):
    @staticmethod
    def setup(k, name, shape, axes):
        for axis in axes:
            size = lax.axis_size(axis)
            k.mem(f"{name}_{axis}", (size, *shape), F32)
            k.sem(f"{name}_{axis}_s", size)
            k.sem(f"{name}_{axis}_r", size)

    def __init__(self, r, name):
        super().__init__()
        self.r, self.name = r, name

    def send(self, axis, value):
        slots, ss, rs = (getattr(self.r, f"{self.name}_{axis}{s}") for s in ("", "_s", "_r"))
        me = lax.axis_index(axis)
        slots[me] = value
        self.copies = [
            self.push(slots.at[me], slots.at[me], ss.at[d], rs.at[d], {axis: flip(axis, d)})
            for d in range(1, lax.axis_size(axis))
        ]
        self.slots = slots

    def receive(self):
        for copy in self.copies:
            copy.wait_recv()
        value = self.slots[0]
        for n in range(1, self.slots.shape[0]):
            value = value + self.slots[n]
        return value


class Outlet(Flow):
    @staticmethod
    def setup(k, name, grads, nz, inside=False):
        for n, grad in enumerate(grads):
            rows, cols = grad.shape[0] // (2 * nz), grad.shape[1]
            if inside:
                k.mem(f"{name}_g{n}", (nz, 2, rows, cols), BF)
            else:
                k.inp(f"{name}_g{n}", grad.astype(BF).reshape(nz, 2, rows, cols))
                k.mem(f"{name}_own{n}", (nz, rows, cols), BF)
            k.out(f"{name}_o{n}", (rows, 2 * nz * cols), BF)
            for s in ("yin", "zout"):
                k.mem(f"{name}_{s}{n}", (nz, rows, cols), BF)
        for s in ("ls", "ys", "yr", "zs", "zr", "cs", "cr"):
            k.sem(f"{name}_{s}", len(grads), nz)
        k.sem(f"{name}_os", len(grads))

    def __init__(self, r, name, count, nz):
        super().__init__()
        self.nz, self.count = nz, count
        self.g, self.o, self.own, self.yin, self.zout = (
            [getattr(r, f"{name}_{s}{n}", None) for n in range(count)]
            for s in ("g", "o", "own", "yin", "zout")
        )
        self.ls, self.ys, self.yr, self.zs, self.zr, self.cs, self.cr, self.os = (
            getattr(r, f"{name}_{s}") for s in ("ls", "ys", "yr", "zs", "zr", "cs", "cr", "os")
        )
        self.loads, self.pairs, self.stores = {}, {}, []

    def slot(self, k, z, core):
        return columns(self.o[k], z * 2 + core, self.g[k].shape[-1])

    def start(self, k):
        for d in range(self.nz - 1, -1, -1):
            target = self.at(d)
            self.pairs[k, d] = self.push(
                self.g[k].at[target, 1 - self.iy],
                self.yin[k].at[d],
                self.ys.at[k, d],
                self.yr.at[k, d],
                self.behind,
            )
            if self.own[k] is not None:
                self.loads[k, d] = pltpu.make_async_copy(
                    self.g[k].at[target, self.iy], self.own[k].at[d], self.ls.at[k, d]
                )
                self.loads[k, d].start()

    def combine(self, k, blocks=(3, 2, 1, 0)):
        mine = self.slot(k, self.iz, self.ic)
        for d in blocks:
            self.pairs[k, d].wait_recv()
            if self.own[k] is not None:
                self.loads[k, d].wait()
                own = self.own[k][d]
            else:
                own = self.g[k][self.at(d), self.iy]
            self.zout[k][d] = (own.astype(F32) + self.yin[k][d].astype(F32)).astype(BF)
            src = self.zout[k].at[d]
            if d:
                self.push(src, mine, self.zs.at[k, d], self.zr.at[k, d], {"z": self.at(d)})
            else:
                self.push(src, mine, self.cs.at[k, d], self.cr.at[k, d], self.beside)
                store = pltpu.make_async_copy(src, mine, self.os.at[k])
                store.start()
                self.stores.append(store)

    def relay(self, k):
        for d in range(1, self.nz):
            block = self.slot(k, self.at(d), self.ic)
            self.arrived(block, self.zr.at[k, d])
            self.push(block, block, self.cs.at[k, d], self.cr.at[k, d], self.beside)

    def end(self):
        for k in range(self.count):
            for d in range(self.nz):
                self.arrived(self.slot(k, self.at(d), 1 - self.ic), self.cr.at[k, d])
        for store in self.stores:
            store.wait()
        self.finish()


def gather_line(rows):
    k = Kernel()
    Gather.setup(k, "all", rows, out=True)

    def body(r):
        greet_line()
        gather = Gather(r, "all")
        gather.start()
        for s in range(1, 5):
            gather.advance(s)
        for s in range(4):
            gather.ready(s)
        gather.finish()

    return k.run(1, body, 16)["all"].reshape(-1, rows.shape[1])


def scatter_line(partial):
    width = partial.shape[1]
    piece = partial.shape[0] // 16
    k = Kernel()
    Scatter.setup(k, "rs", piece, width, partial.astype(BF).reshape(4, 4 * piece, width))
    k.out("sum", (piece, width), F32, pltpu.VMEM)

    def body(r):
        greet_line()
        scatter = Scatter(r, "rs", r.sum)
        order = (3, 2, 1, 0)
        for s in order:
            scatter.begin(s)
        for s in order:
            scatter.cross(s)
        for s in order:
            scatter.leave(s)
        scatter.end()
        scatter.finish()

    return k.run(2, body, 32)["sum"]


def exact(a, b, dims):
    return lax.dot_general(
        a, b, (dims, ((), ())), precision=lax.Precision.HIGHEST, preferred_element_type=F32
    )


def picker(width):
    row = lax.broadcasted_iota(jnp.int32, (8, width), 0)
    part = lax.broadcasted_iota(jnp.int32, (8, width), 1) // HD
    return jnp.where(row == part, 1.0, 0.0).astype(F32)


def row_sums(first, second):
    both = jnp.concatenate([first, second], axis=1)
    return exact(picker(2 * HD), both, ((1,), (1,)))


def spread(sums, which):
    row = lax.broadcasted_iota(jnp.int32, (8, HD), 0)
    one = jnp.where(row == which, 1.0, 0.0).astype(F32)
    return exact(sums, one, ((0,), (0,)))


def softmax_rows(query, key, length):
    count = query.shape[0]
    row = lax.broadcasted_iota(jnp.int32, (count, count), 0)
    col = lax.broadcasted_iota(jnp.int32, (count, count), 1)
    scores = mm_nt(query, key) * (1.0 / math.sqrt(HD))
    scores = jnp.where((col <= row) & (col < length), scores, NEGATIVE)
    exponent = jnp.exp(scores - jnp.max(scores, axis=-1, keepdims=True))
    return exponent / jnp.sum(exponent, axis=-1, keepdims=True)


def load_all(pairs, sems):
    copies = []
    for n, (src, dst) in enumerate(pairs):
        copy = pltpu.make_async_copy(src, dst, sems.at[n])
        copy.start()
        copies.append(copy)
    return copies


def attention_back(
    branch, wide, wo, wqkv, saved, tokens_all, residual_grad, stream_rows, terms, gains, tables,
    seq_lengths,
):
    nz = lax.axis_size("z")
    piece, width = branch.shape
    rows = 4 * piece
    block = width // (2 * nz)
    padded = jnp.pad(terms, (0, -terms.shape[0] % 1024)).reshape(-1, 128)
    lanes = width // 128
    sum_axes = (CORE, TP, "y", "z")
    k = Kernel()
    Gather.setup(k, "ball", branch)
    Outlet.setup(k, "wide", wide, nz)
    slim = [jax.ShapeDtypeStruct((width, HD), BF)] * 4
    Outlet.setup(k, "slim", slim, nz, inside=True)
    Scatter.setup(k, "rs", piece, width)
    Total.setup(k, "tot", (nz, 8, rows), (CORE, TP, "z"))
    Total.setup(k, "sum", padded.shape, sum_axes)
    k.inp("wo", wo)
    k.inp("wqkv", wqkv)
    k.inp("tokens", tokens_all)
    k.mem("tokens_m", tokens_all.shape, BF)
    names = ("q", "k", "v", "att", "nq", "nk", "qs", "ks")
    for name, array in zip(names, saved):
        k.inp(name, array)
        k.mem(name + "_m", array.shape, array.dtype)
    k.mem("wo_m", wo.shape, BF)
    k.mem("wqkv_m", wqkv.shape, BF)
    k.inp("res", residual_grad)
    k.mem("res_m", (piece, width), F32)
    k.inp("stream", stream_rows)
    k.mem("stream_m", (piece, width), BF)
    k.sem("ld", len(names) + 5)
    k.inp("terms", padded, pltpu.VMEM)
    k.mem("terms_m", padded.shape, F32)
    k.out("terms_out", padded.shape, F32, pltpu.VMEM)
    k.inp("gains", gains, pltpu.VMEM)
    k.inp("tables", tables, pltpu.VMEM)
    k.inp("lens", seq_lengths, pltpu.SMEM)
    k.mem("wqk", (nz, 2, rows, HD), F32)
    k.mem("low", (nz, rows, 3 * HD), BF)
    k.mem("dots", (nz, 8, rows), F32)
    k.mem("norms", (2, HD), F32)
    k.mem("grad", (piece, width), F32)
    k.out("grad_out", (2, piece, width), F32)
    k.out("stream_out", (2, piece, width), BF)
    k.sem("xs", 2)
    k.sem("xr", 2)
    k.sem("ss", 2)

    def body(r):
        greet(partners_of(("z", "y", TP, CORE)))
        gather, outlet_flow = Gather(r, "ball"), Outlet(r, "wide", len(wide), nz)
        slim_flow, own = Outlet(r, "slim", len(slim), nz), Flow()
        scatter, total_flow = Scatter(r, "rs", r.grad), Total(r, "tot")
        sum_flow = Total(r, "sum")
        gather.start()
        for n in range(len(wide)):
            outlet_flow.start(n)
        names_in = ("wo", "wqkv", *names, "tokens", "res", "stream")
        loads = load_all([(getattr(r, n), getattr(r, n + "_m")) for n in names_in], r.ld)
        scale = 1.0 / math.sqrt(HD)
        cosine, sine = r.tables[0], r.tables[1]
        gather.advance(1)
        outlet_flow.combine(0, (3,))
        gather.advance(2)
        outlet_flow.combine(0, (2,))
        gather.advance(3)
        for copy in loads:
            copy.wait()
        r.norms[...] = jnp.zeros_like(r.norms)

        def compute(z):
            grad_low = mm(r.ball[z], r.wo_m[...]).astype(BF)
            query, key, value = r.q_m[z], r.k_m[z], r.v_m[z]
            probability = softmax_rows(query, key, r.lens[z])
            grad_prob = mm_nt(grad_low, value)
            row_dots = jnp.sum(probability * grad_prob, axis=-1, keepdims=True)
            grad_scores = (probability * (grad_prob - row_dots)).astype(BF)
            grad_q = rotate_back(mm(grad_scores, key) * scale, cosine, sine)
            grad_k = rotate_back(mm_tn(grad_scores, query) * scale, cosine, sine)
            grad_v = mm_tn(probability.astype(BF), grad_low)
            r.low[z, :, 2 * HD :] = grad_v.astype(BF)
            nq, nk = r.nq_m[z], r.nk_m[z]
            r.norms[0:1] += jnp.sum(grad_q * nq, axis=0, keepdims=True)
            r.norms[1:2] += jnp.sum(grad_k * nk, axis=0, keepdims=True)
            wq, wk = grad_q * r.gains[0:1], grad_k * r.gains[1:2]
            r.wqk[z, 0] = wq
            r.wqk[z, 1] = wk
            r.dots[z] = row_sums(wq * nq, wk * nk)

        def weight_blocks(left, right, place):
            @pl.loop(0, 2 * nz)
            def _(f):
                cols = pl.ds(pl.multiple_of(f * block, block), block)
                made = mm_tn(left[0, :, cols], right[0])
                for z in range(1, nz):
                    made = made + mm_tn(left[z, :, cols], right[z])
                made = made.astype(BF)
                for n, grad in enumerate(place):
                    grad[f // 2, lax.rem(f, 2)] = made[:, n * HD : (n + 1) * HD]

        for d in range(nz):
            if d == 0:
                gather.advance(4)
                outlet_flow.combine(0, (1, 0))
                own.push(
                    r.stream, r.stream_out.at[own.it], r.xs.at[0], r.xr.at[0], own.across
                )
            gather.ready(d)
            compute(gather.line(d))
        r.terms_m[...] = r.terms[...]
        slot = 2 * lanes + own.it * (lanes // 2) + own.iz * 2 + own.ic
        for n in range(2):
            r.terms_m[pl.ds(slot + n * lanes, 1)] = r.norms[n : n + 1]
        total_flow.send(CORE, r.dots[...])
        sum_flow.send(CORE, r.terms_m[...])
        value, other = total_flow.receive(), sum_flow.receive()
        total_flow.send(TP, value)
        sum_flow.send(TP, other)
        value, other = total_flow.receive(), sum_flow.receive()
        total_flow.send("z", value)
        sum_flow.send("y", other)
        outlet_flow.combine(1)
        weight_blocks(r.ball, r.att_m, [slim_flow.g[3]])
        slim_flow.start(3)
        r.dots[...] = total_flow.receive()
        order = list(range(nz - 1, -1, -1))
        for n, d in enumerate(order):
            z = gather.line(d)
            sums = r.dots[z] * (1.0 / width)
            for j, (normed, factor) in enumerate(((r.nq_m, r.qs_m), (r.nk_m, r.ks_m))):
                low = factor[z] * (r.wqk[z, j] - normed[z] * spread(sums, j))
                r.low[z, :, j * HD : (j + 1) * HD] = low.astype(BF)
            r.rs_p[d] = mm_nt(r.low[z], r.wqkv_m[...]).astype(BF)
            scatter.begin(d)
            if n:
                scatter.cross(order[n - 1])
            if n > 1:
                scatter.leave(order[n - 2])
        scatter.cross(0)
        scatter.leave(1)
        scatter.leave(0)
        outlet_flow.combine(2)
        weight_blocks(r.tokens_m, r.low, slim_flow.g[:3])
        for n in range(3):
            slim_flow.start(n)
        sum_flow.send("z", sum_flow.receive())
        slim_flow.combine(3)
        outlet_flow.relay(0)
        outlet_flow.relay(1)
        scatter.end()
        r.res_m[...] += r.grad[...]
        own.push(r.res_m, r.grad_out.at[own.it], r.xs.at[1], r.xr.at[1], own.across)
        stores = []
        for n, (src, out) in enumerate(((r.stream_m, r.stream_out), (r.res_m, r.grad_out))):
            stores.append(pltpu.make_async_copy(src, out.at[own.it], r.ss.at[n]))
            stores[-1].start()
        for n in range(3):
            slim_flow.combine(n)
        r.terms_out[...] = sum_flow.receive()
        outlet_flow.relay(2)
        slim_flow.relay(3)
        for n in range(3):
            slim_flow.relay(n)
        outlet_flow.end()
        slim_flow.end()
        for n, out in enumerate((r.stream_out, r.grad_out)):
            own.arrived(out.at[1 - own.it], r.xr.at[n])
        for flow in (gather, scatter, total_flow, sum_flow, own):
            flow.finish()
        for copy in stores:
            copy.wait()

    got = k.run(7, body, 60)
    return (
        [got[f"slim_o{n}"].astype(F32) for n in range(4)]
        + [got[f"wide_o{n}"].astype(F32) for n in range(len(wide))],
        got["grad_out"].reshape(-1, width),
        got["stream_out"].reshape(-1, width),
        got["terms_out"].reshape(-1)[: terms.shape[0]],
    )


def attention_front(token_rows, weights, gains, tables, seq_lengths, post_attention):
    nz = lax.axis_size("z")
    own_rows, width = token_rows.shape
    piece, rows = own_rows // 2, own_rows * 2
    w_rows = weights[0].shape[0]
    count = len(weights)
    parts = [w.shape[1] // (2 * nz) for w in weights]
    k = Kernel()
    Scatter.setup(k, "rs", piece, width)
    Total.setup(k, "tot", (nz, 8, rows), (CORE, TP, "z"))
    k.inp("tok", token_rows)
    for n, weight in enumerate(weights):
        k.inp(f"w{n}", weight)
    k.inp("gains", gains, pltpu.VMEM)
    k.inp("tables", tables, pltpu.VMEM)
    k.inp("lens", seq_lengths, pltpu.SMEM)
    k.mem("tall", (nz, rows, width), BF)
    k.mem("qkv", (nz, 2, w_rows, 3 * HD), BF)
    k.mem("wo", (nz, 2, w_rows, parts[3]), BF)
    for n in range(4, count):
        k.mem(f"b{n}", (w_rows, parts[n]), BF)
        k.out(f"o{n}", (nz, 2, w_rows, parts[n]), BF)
    k.mem("raw", (nz, rows, 3 * HD), F32)
    k.mem("dots", (nz, 8, rows), F32)
    saved = (("q", BF), ("k", BF), ("v", BF), ("nq", F32), ("nk", F32), ("qs", F32), ("ks", F32), ("att", BF))
    for name, kind in saved:
        k.mem(name + "_m", (nz, rows, HD), kind)
        k.out(name, (nz, rows, HD), kind)
    k.mem("branch", (piece, width), F32)
    k.inp("post", post_attention[None], pltpu.VMEM)
    for name in ("normed", "residual"):
        k.out(name, (piece, width), F32, pltpu.VMEM)
    k.out("scale", (piece, 128), F32, pltpu.VMEM)
    Gather.setup(k, "all", jax.ShapeDtypeStruct((piece, width), BF), inside=True)
    k.out("wide", (nz, rows, width), BF)
    k.out("tokens", (nz, rows, width), BF)
    k.out("qkv_out", (nz, 2, w_rows, 3 * HD), BF)
    k.out("wo_out", (nz, 2, w_rows, parts[3]), BF)
    k.sem("tl")
    k.sem("tzs", 6)
    for s in ("tzr", "txs", "txr"):
        k.sem(s, nz)
    k.sem("tcs", nz, 2)
    k.sem("tcr", nz, 2)
    k.sem("wl", 2, count)
    for s in ("wzs", "wzr", "wys", "wyr"):
        k.sem(s, count, nz)
    k.sem("st", len(saved) + 2, nz)
    k.sem("sw", 2)

    def body(r):
        greet(partners_of(("z", "y", TP, CORE)))
        flow = Flow()
        iz, iy, ic, it = flow.iz, flow.iy, flow.ic, flow.it
        scatter, total_flow = Scatter(r, "rs", r.branch), Total(r, "tot")
        gather = Gather(r, "all")

        def block(z, core, tp):
            return stripe(r.tall, z, core, tp, piece)

        def pair(z, core):
            start = pl.multiple_of(core * own_rows, own_rows)
            return r.tall.at[z, pl.ds(start, own_rows)]

        tok_half = r.tok.at[pl.ds(pl.multiple_of(it * piece, piece), piece)]
        flow.push(tok_half, block(iz, ic, it), r.tzs.at[1], r.tzr.at[1], flow.near)
        flow.push_inner(tok_half, block(iz, ic, it), r.tzs.at[2], r.tzr.at[2], flow.mid)
        flow.push(r.tok, pair(iz, ic), r.tcs.at[0, 0], r.tcr.at[0, 0], flow.beside)
        tok_load = pltpu.make_async_copy(r.tok, pair(iz, ic), r.tl)
        tok_load.start()
        loads = {}

        def landing(n, z, y):
            if n < 3:
                return r.qkv.at[z, y, :, n * HD : (n + 1) * HD]
            return r.wo.at[z, y] if n == 3 else getattr(r, f"o{n}").at[z, y]

        def bring(n, parts_of_z=(3, 2, 1), own_part=True):
            weight = getattr(r, f"w{n}")
            own = columns(weight, iz * 2 + ic, parts[n])
            for d in parts_of_z:
                other = flow.at(d)
                flow.push(
                    columns(weight, other * 2 + ic, parts[n]),
                    landing(n, iz, iy),
                    r.wzs.at[n, d],
                    r.wzr.at[n, d],
                    {"z": other},
                )
            if own_part:
                flow.push(own, landing(n, iz, iy), r.wys.at[n, 0], r.wyr.at[n, 0], flow.behind)
                dst = landing(n, iz, iy) if n < 4 else getattr(r, f"b{n}")
                loads[n] = pltpu.make_async_copy(own, dst, r.wl.at[0, n])
                loads[n].start()

        def forward(n, parts_of_z=(3, 2, 1)):
            for d in parts_of_z:
                here = landing(n, flow.at(d), iy)
                flow.arrived(here, r.wzr.at[n, d])
                flow.push(here, here, r.wys.at[n, d], r.wyr.at[n, d], flow.behind)

        def keep(n):
            loads[n].wait()
            copy = pltpu.make_async_copy(getattr(r, f"b{n}"), landing(n, iz, iy), r.wl.at[1, n])
            copy.start()
            stores.append(copy)

        def complete(n):
            for d in range(nz):
                flow.arrived(landing(n, flow.at(d), 1 - iy), r.wyr.at[n, d])

        bring(0)
        for d in range(1, nz):
            here = block(flow.line(d), ic, it)
            flow.arrived(here, r.tzr.at[d])
            flow.pass_on(d, here, r.tzs, r.tzr)
            flow.push(here, here, r.txs.at[d], r.txr.at[d], flow.across)
            flow.push(here, here, r.tcs.at[d, 0], r.tcr.at[d, 0], flow.beside)
            bring(d)
        bring(4)
        for d in range(1, nz):
            forward(d - 1)
            here = block(flow.line(d), ic, 1 - it)
            flow.arrived(here, r.txr.at[d])
            flow.push(here, here, r.tcs.at[d, 1], r.tcr.at[d, 1], flow.beside)
        stores = []

        def save(n, src, dst, d):
            copy = pltpu.make_async_copy(src, dst, r.st.at[n, d])
            copy.start()
            stores.append(copy)

        for n in range(4):
            loads[n].wait()
        for n in range(3):
            complete(n)
        tok_load.wait()
        for d in range(nz):
            z = flow.line(d)
            if d == 0:
                flow.arrived(pair(iz, 1 - ic), r.tcr.at[0, 0])
            else:
                for half in range(2):
                    side = it if half == 0 else 1 - it
                    flow.arrived(block(z, 1 - ic, side), r.tcr.at[d, half])
            save(0, r.tall.at[z], r.tokens.at[z], d)
            raw = mm(r.tall[z], r.qkv[...].reshape(2 * nz * w_rows, 3 * HD))
            r.raw[z] = raw
            query, key = raw[:, :HD], raw[:, HD : 2 * HD]
            r.dots[z] = row_sums(query * query, key * key)
        total_flow.send(CORE, r.dots[...])
        forward(3)
        value = total_flow.receive()
        total_flow.send(TP, value)
        value = total_flow.receive()
        total_flow.send("z", value)
        bring(5, (3,))
        for n in (4, 5):
            keep(n)
        complete(3)
        for n, (src, dst) in enumerate(((r.qkv, r.qkv_out), (r.wo, r.wo_out))):
            copy = pltpu.make_async_copy(src, dst, r.sw.at[n])
            copy.start()
            stores.append(copy)
        r.dots[...] = lax.rsqrt(total_flow.receive() * (1.0 / width) + EPSILON)
        cosine, sine = r.tables[0], r.tables[1]
        order = list(range(nz - 1, -1, -1))
        for n, d in enumerate(order):
            z = flow.line(d)
            sums = r.dots[z]
            r.qs_m[z] = spread(sums, 0)
            r.ks_m[z] = spread(sums, 1)
            r.nq_m[z] = r.raw[z, :, :HD] * r.qs_m[z]
            r.nk_m[z] = r.raw[z, :, HD : 2 * HD] * r.ks_m[z]
            query = rotate(r.nq_m[z] * r.gains[0:1], cosine, sine).astype(BF)
            key = rotate(r.nk_m[z] * r.gains[1:2], cosine, sine).astype(BF)
            value = r.raw[z, :, 2 * HD :].astype(BF)
            r.q_m[z] = query
            r.k_m[z] = key
            r.v_m[z] = value
            probability = softmax_rows(query, key, r.lens[z]).astype(BF)
            r.att_m[z] = mm(probability, value).astype(BF)
            for m, (name, _) in enumerate(saved):
                save(m + 1, getattr(r, name + "_m").at[z], getattr(r, name).at[z], d)
            wo = r.wo[...].reshape(2 * nz * w_rows, parts[3])
            r.rs_p[d] = mm_nt(r.att_m[z], wo).astype(BF)
            scatter.begin(d)
            if n:
                scatter.cross(order[n - 1])
            if n > 1:
                scatter.leave(order[n - 2])
            if n == 0:
                forward(4)
        scatter.cross(0)
        scatter.leave(1)
        bring(5, (2, 1), False)
        scatter.leave(0)
        forward(5, (3,))
        scatter.end()
        branch = r.branch[...]
        scale = lax.rsqrt(jnp.mean(branch * branch, axis=-1, keepdims=True) + EPSILON)
        r.normed[...] = branch * scale
        r.scale[...] = jnp.broadcast_to(scale, r.scale.shape)
        start = pl.multiple_of((ic * 2 + it) * piece, piece)
        mine = r.tall[iz, pl.ds(start, piece)].astype(F32)
        r.residual[...] = mine + r.normed[...] * r.post[...]
        r.all_x[...] = r.residual[...].astype(BF)
        gather.start()
        gather.advance(1)
        bring(6, (3, 2))
        forward(5, (2, 1))
        for d in range(2, 4):
            gather.advance(d)
        bring(6, (1,), False)
        gather.advance(4)
        keep(6)
        for d in range(nz):
            gather.ready(d)
            z = gather.line(d)
            save(len(saved) + 1, gather.buf.at[z], r.wide.at[z], d)
        forward(6)
        for n in range(4, count):
            complete(n)
        for f in (flow, scatter, total_flow, gather):
            f.finish()
        for copy in stores:
            copy.wait()

    return k.run(9, body, 60)


def local(
    tokens,
    lengths,
    weight_query,
    weight_key,
    weight_value,
    weight_out,
    weight_gate,
    weight_up,
    weight_down,
    post_attention,
    post_feedforward,
    query_norm,
    key_norm,
    cotangent,
):
    nz, ny, nch, ntp = (lax.axis_size(a) for a in ("z", "y", "ch", TP))
    iz, iy, ich, icore, itp = (lax.axis_index(a) for a in AXES)
    token_rows = tokens[0]
    own_rows, width = token_rows.shape
    piece = own_rows // ntp
    seq_rows = own_rows * 2
    total_rows = seq_rows * nz
    scale_factor = 1.0 / math.sqrt(HD)
    own_head = iz * 2 + icore
    qn = lax.dynamic_slice_in_dim(query_norm, own_head * HD, HD)
    kn = lax.dynamic_slice_in_dim(key_norm, own_head * HD, HD)
    seq_lengths = lax.dynamic_index_in_dim(lengths.reshape(nz, ny), iy, 1, keepdims=False)
    positions = ich * seq_rows + jnp.arange(seq_rows, dtype=jnp.int32)
    key_positions = jnp.arange(seq_rows * nch, dtype=jnp.int32)
    cosine, sine_table = rope_tables(positions)
    allowed = (key_positions[None, None, :] <= positions[None, :, None]) & (
        key_positions[None, None, :] < seq_lengths[:, None, None]
    )
    my_tokens = lax.dynamic_slice_in_dim(token_rows, itp * piece, piece, 0)
    my_cot = lax.dynamic_slice_in_dim(cotangent[0], itp * piece, piece, 0)
    my_pos = (ich * 2 + icore) * own_rows + itp * piece + jnp.arange(piece, dtype=jnp.int32)
    my_valid = (my_pos < lengths[iz * ny + iy]).astype(F32)[:, None]

    weights = (
        weight_query,
        weight_key,
        weight_value,
        weight_out,
        weight_gate,
        weight_up,
        weight_down,
    )
    fused = nch == 1 and nz == 4
    gather, scatter = (gather_line, scatter_line) if fused else (gather_rows, scatter_rows)
    by_seq = lambda a: a.reshape(nz, seq_rows, HD)
    gains, tables = jnp.stack([qn, kn]), jnp.stack([cosine, sine_table])
    if fused:
        front = attention_front(
            token_rows, weights, gains, tables, seq_lengths, post_attention
        )
        wg, wu, wd = (front[f"o{n}"].reshape(width, -1) for n in (4, 5, 6))
    else:
        tokens_all, (wq, wk, wv, wo, wg, wu, wd) = intake(token_rows, weights)
        query_raw = mm(tokens_all, wq)
        key_raw = mm(tokens_all, wk)
        value_raw = mm(tokens_all, wv)
        squares = head_total(
            jnp.stack([jnp.sum(query_raw * query_raw, axis=-1), jnp.sum(key_raw * key_raw, axis=-1)])
        )
        scales = lax.rsqrt(squares / width + EPSILON)
        query_scale = scales[0][:, None]
        key_scale = scales[1][:, None]
        queries = rotate(by_seq(query_raw * query_scale * qn), cosine, sine_table).astype(BF)
        keys = rotate(by_seq(key_raw * key_scale * kn), cosine, sine_table).astype(BF)
        values = by_seq(value_raw).astype(BF)
        if nch > 1:
            keys_full = lax.all_gather(keys, "ch", axis=1, tiled=True)
            values_full = lax.all_gather(values, "ch", axis=1, tiled=True)
        else:
            keys_full, values_full = keys, values
        scores = (
            jnp.einsum(SCORE, queries, keys_full, preferred_element_type=F32) * scale_factor
        )
        scores = jnp.where(allowed, scores, NEGATIVE)
        exponent = jnp.exp(scores - jnp.max(scores, axis=-1, keepdims=True))
        probability = exponent / jnp.sum(exponent, axis=-1, keepdims=True)
        probability_low = probability.astype(BF)
        attended = jnp.einsum(APPLY, probability_low, values_full, preferred_element_type=F32)
        attended_low = attended.reshape(total_rows, HD).astype(BF)
        branch_sum = scatter_rows(mm_nt(attended_low, wo))
    if fused:
        attn_normed, residual = front["normed"], front["residual"]
        attn_scale = front["scale"][:, :1]
        residual_all = front["wide"].reshape(-1, width)
    else:
        attn_scale = lax.rsqrt(jnp.mean(branch_sum * branch_sum, axis=-1, keepdims=True) + EPSILON)
        attn_normed = branch_sum * attn_scale
        residual = my_tokens.astype(F32) + attn_normed * post_attention
        residual_all = gather(residual.astype(BF))
    attention_branch = attn_normed * post_attention
    gate_value = mm(residual_all, wg)
    up_value = mm(residual_all, wu)
    sigmoid_gate = jax.nn.sigmoid(gate_value)
    silu_gate = gate_value * sigmoid_gate
    mixed_low = (silu_gate * up_value).astype(BF)
    down_sum = scatter(mm_nt(mixed_low, wd))
    ffn_scale = lax.rsqrt(jnp.mean(down_sum * down_sum, axis=-1, keepdims=True) + EPSILON)
    ffn_normed = down_sum * ffn_scale
    feedforward_branch = ffn_normed * post_feedforward
    stream = residual + feedforward_branch
    stat_terms = jnp.stack(
        [
            jnp.sum(my_valid * stream * stream),
            jnp.sum(my_valid * attention_branch * attention_branch),
            jnp.sum(my_valid * feedforward_branch * feedforward_branch),
        ]
    )
    grad_stream = my_cot * my_valid
    grad_post_ff = jnp.sum(grad_stream * ffn_normed, axis=0)
    scaled = grad_stream * post_feedforward
    grad_down_sum = ffn_scale * (
        scaled - ffn_normed * jnp.mean(scaled * ffn_normed, axis=-1, keepdims=True)
    )
    down_all = gather(grad_down_sum.astype(BF))
    grad_mixed = mm(down_all, wd)
    gate_low = (
        grad_mixed * up_value * sigmoid_gate * (1.0 + gate_value * (1.0 - sigmoid_gate))
    ).astype(BF)
    up_low = (grad_mixed * silu_gate).astype(BF)
    grad_wg = mm_tn(residual_all, gate_low)
    grad_wu = mm_tn(residual_all, up_low)
    grad_wd = mm_tn(down_all, mixed_low)
    grad_residual = grad_stream + scatter(mm_nt(gate_low, wg) + mm_nt(up_low, wu))
    grad_post_attn = jnp.sum(grad_residual * attn_normed, axis=0)
    scaled_attn = grad_residual * post_attention
    grad_branch = attn_scale * (
        scaled_attn - attn_normed * jnp.mean(scaled_attn * attn_normed, axis=-1, keepdims=True)
    )
    if not fused:
        branch_all = gather_rows(grad_branch.astype(BF))
        grad_att_low = mm(branch_all, wo).astype(BF)
        grad_wo = mm_tn(branch_all, attended_low)
        grad_att = by_seq(grad_att_low)
        grad_prob = jnp.einsum(SCORE, grad_att, values_full, preferred_element_type=F32)
        row_dots = jnp.sum(probability * grad_prob, axis=-1, keepdims=True)
        grad_scores = (probability * (grad_prob - row_dots)).astype(BF)
        grad_queries = (
            jnp.einsum(APPLY, grad_scores, keys_full, preferred_element_type=F32)
            * scale_factor
        )
        grad_keys = (
            jnp.einsum("bts,btd->bsd", grad_scores, queries, preferred_element_type=F32) * scale_factor
        )
        grad_values = jnp.einsum("bts,btd->bsd", probability_low, grad_att, preferred_element_type=F32)
        if nch > 1:
            grad_keys, grad_values = (
                lax.psum_scatter(g.astype(BF), "ch", scatter_dimension=1, tiled=True).astype(F32)
                for g in (grad_keys, grad_values)
            )
        value_grad_low = grad_values.reshape(total_rows, HD).astype(BF)
        grad_q_normed = rotate_back(grad_queries, cosine, sine_table).reshape(total_rows, HD)
        grad_k_normed = rotate_back(grad_keys, cosine, sine_table).reshape(total_rows, HD)
        query_weighted = grad_q_normed * qn
        key_weighted = grad_k_normed * kn
        dots = head_total(
            jnp.stack(
                [
                    jnp.sum(query_weighted * query_raw, axis=-1),
                    jnp.sum(key_weighted * key_raw, axis=-1),
                ]
            )
        )
        query_grad_low = (
            query_scale * (query_weighted - query_raw * query_scale**2 * (dots[0] / width)[:, None])
        ).astype(BF)
        key_grad_low = (
            key_scale * (key_weighted - key_raw * key_scale**2 * (dots[1] / width)[:, None])
        ).astype(BF)
        grad_qnorm = jnp.sum(grad_q_normed * query_raw * query_scale, axis=0)
        grad_knorm = jnp.sum(grad_k_normed * key_raw * key_scale, axis=0)
        grad_wq = mm_tn(tokens_all, query_grad_low)
        grad_wk = mm_tn(tokens_all, key_grad_low)
        grad_wv = mm_tn(tokens_all, value_grad_low)
        grad_rows = grad_residual + scatter_rows(
            mm_nt(query_grad_low, wq) + mm_nt(key_grad_low, wk) + mm_nt(value_grad_low, wv)
        )
    if fused:
        saved = tuple(front[n] for n in ("q", "k", "v", "att", "nq", "nk", "qs", "ks"))
        norms_wide = jnp.zeros((2 * width,), F32)
    else:
        slot = itp * (width // ntp) + own_head * HD
        zero_row = jnp.zeros((width,), F32)
        norms_wide = jnp.concatenate(
            [
                lax.dynamic_update_slice_in_dim(zero_row, grad_qnorm, slot, 0),
                lax.dynamic_update_slice_in_dim(zero_row, grad_knorm, slot, 0),
            ]
        )
    terms = jnp.concatenate([grad_post_attn, grad_post_ff, norms_wide, stat_terms])
    if fused:
        weight_grads, grad_input, output, summed = attention_back(
            grad_branch.astype(BF),
            (grad_wd, grad_wg, grad_wu),
            front["wo_out"].reshape(width, -1),
            front["qkv_out"].reshape(width, -1),
            saved,
            front["tokens"],
            grad_residual,
            stream.astype(BF),
            terms,
            gains,
            tables,
            seq_lengths,
        )
        weight_grads = [weight_grads[n] for n in (0, 1, 2, 3, 5, 6, 4)]
    else:
        weight_grads = outlet((grad_wq, grad_wk, grad_wv, grad_wo, grad_wg, grad_wu, grad_wd))
        grad_input = lax.all_gather(grad_rows, TP, axis=0, tiled=True)
        output = lax.all_gather(stream.astype(BF), TP, axis=0, tiled=True)
        summed = all_total(terms)
    half = width // ntp
    qn_sum = lax.dynamic_slice_in_dim(summed, 2 * width + itp * half, half)
    kn_sum = lax.dynamic_slice_in_dim(summed, 3 * width + itp * half, half)
    token_count = jnp.sum(lengths.astype(F32))
    root_means = jnp.sqrt(summed[4 * width :] / (token_count * width))
    return (
        output[None],
        grad_input[None],
        *weight_grads,
        summed[:width],
        summed[width : 2 * width],
        qn_sum,
        kn_sum,
        root_means,
    )


def solution(mesh):
    n_fsdp, n_ctx, n_tp = (mesh.shape[a] for a in ("fsdp", "ctx", TP))
    fine = Mesh(mesh.devices.reshape(n_fsdp // 2, 2, n_ctx // 2, 2, n_tp), AXES)
    fsdp, ctx = ("z", "y"), ("ch", CORE)
    rows = P(fsdp, ctx, None)
    weight = P(fsdp, TP)
    return jax.shard_map(
        local,
        mesh=fine,
        in_specs=(rows, P(), *([weight] * 7), P(), P(), P(TP), P(TP), rows),
        out_specs=(rows, rows, *([weight] * 7), P(), P(), P(TP), P(TP), P()),
        check_vma=False,
    )
```

```python
import functools
import math
import types

import jax
import jax.numpy as jnp
from jax import lax
from jax.experimental import pallas as pl
from jax.experimental.pallas import tpu as pltpu
from jax.sharding import Mesh, PartitionSpec as P

HD = 128
EPSILON = 1e-06
ROPE_BASE = 500000.0
NEGATIVE = -1e30
CORE, TP = "core", "tp"
SCORE = "btd,bsd->bts"
APPLY = "bts,bsd->btd"
AXES = ("z", "y", "ch", CORE, TP)
BF = jnp.bfloat16
F32 = jnp.float32


def rope_tables(positions):
    half_size = HD // 2
    exponent = jnp.arange(half_size, dtype=F32) * (2.0 / HD)
    frequency = jnp.power(ROPE_BASE, -exponent)
    angles = positions.astype(F32)[:, None] * frequency[None, :]
    cosine = jnp.cos(angles)
    sine_table = jnp.sin(angles)
    return (
        jnp.concatenate([cosine, cosine], axis=-1),
        jnp.concatenate([sine_table, sine_table], axis=-1),
    )


def rotate(values, cosine, sine_table):
    half_size = HD // 2
    turned = jnp.concatenate([-values[..., half_size:], values[..., :half_size]], axis=-1)
    return values * cosine + turned * sine_table


def rotate_back(grads_in, cosine, sine_table):
    half_size = HD // 2
    sin_part = grads_in * sine_table
    return grads_in * cosine + jnp.concatenate(
        [sin_part[..., half_size:], -sin_part[..., :half_size]], axis=-1
    )


def dot(former, latter, dims):
    return lax.dot_general(former, latter, (dims, ((), ())), preferred_element_type=F32)


def mm(a, b):
    return dot(a, b, ((1,), (0,)))


def mm_nt(a, b):
    return dot(a, b, ((1,), (1,)))


def mm_tn(a, b):
    return dot(a, b, ((0,), (0,)))


MESH = pl.DeviceIdType.MESH


def flip(axis, bits):
    me = lax.axis_index(axis)
    result, weight = me, 1
    while weight <= bits:
        if (bits // weight) % 2:
            result = result + weight * (1 - 2 * lax.rem(me // weight, 2))
        weight *= 2
    return result


def greet(partners):
    barrier = pltpu.get_barrier_semaphore()
    for partner in partners:
        pl.semaphore_signal(barrier, inc=1, device_id=partner, device_id_type=MESH)
    pl.semaphore_wait(barrier, len(partners))


def remote(src, dst, send_sem, recv_sem, partner):
    return pltpu.make_async_remote_copy(
        src_ref=src,
        dst_ref=dst,
        send_sem=send_sem,
        recv_sem=recv_sem,
        device_id=partner,
        device_id_type=MESH,
    )


def partners_of(axes):
    found = []
    for axis in axes:
        for bits in range(1, lax.axis_size(axis)):
            found.append({axis: flip(axis, bits)})
    return found


def call(kernel, identity, out_shape, in_spaces, out_spaces, scratch, limit, *operands):
    return pl.pallas_call(
        kernel,
        out_shape=out_shape,
        in_specs=[pl.BlockSpec(memory_space=s) for s in in_spaces],
        out_specs=jax.tree.map(lambda s: pl.BlockSpec(memory_space=s), out_spaces),
        scratch_shapes=scratch,
        compiler_params=pltpu.CompilerParams(
            collective_id=identity, has_side_effects=True, vmem_limit_bytes=limit * 2**20
        ),
    )(*operands)


DMA = pltpu.SemaphoreType.DMA


def gather_kernel(nz, x_ref, out_ref, own_sem, zs, zr, xs, xr, cs, cr):
    iz, ic, it = (lax.axis_index(a) for a in ("z", CORE, TP))
    greet(partners_of(("z", TP, CORE)))
    sends = []

    def push(src, where, send_sem, recv_sem, partner):
        copy = remote(src, out_ref.at[where], send_sem, recv_sem, partner)
        copy.start()
        sends.append(copy)

    across, beside = {TP: 1 - it}, {CORE: 1 - ic}
    own = (iz, ic, it)
    for d in range(1, nz):
        push(x_ref, own, zs.at[d], zr.at[d], {"z": flip("z", d)})
    push(x_ref, own, xs.at[0], xr.at[0], across)
    push(x_ref, own, cs.at[0, 0], cr.at[0, 0], beside)
    local_copy = pltpu.make_async_copy(x_ref, out_ref.at[own], own_sem)
    local_copy.start()

    def await_at(where, sem):
        remote(out_ref.at[where], out_ref.at[where], sem, sem, across).wait_recv()

    def from_across(d):
        where = (flip("z", d), ic, 1 - it)
        await_at(where, xr.at[d])
        push(out_ref.at[where], where, cs.at[d, 1], cr.at[d, 1], beside)

    for d in range(1, nz):
        where = (flip("z", d), ic, it)
        await_at(where, zr.at[d])
        push(out_ref.at[where], where, xs.at[d], xr.at[d], across)
        push(out_ref.at[where], where, cs.at[d, 0], cr.at[d, 0], beside)
        from_across(d - 1)
    from_across(nz - 1)
    for d in range(nz):
        for half in range(2):
            side = it if half == 0 else 1 - it
            await_at((flip("z", d), 1 - ic, side), cr.at[d, half])
    for copy in sends:
        copy.wait_send()
    local_copy.wait()


def gather_rows(rows):
    piece, width = rows.shape
    nz = lax.axis_size("z")
    out = call(
        functools.partial(gather_kernel, nz),
        1,
        jax.ShapeDtypeStruct((nz, 2, 2, piece, width), rows.dtype),
        [pl.ANY],
        pl.ANY,
        [DMA, DMA((nz,)), DMA((nz,)), DMA((nz,)), DMA((nz,)), DMA((nz, 2)), DMA((nz, 2))],
        16,
        rows,
    )
    return out.reshape(-1, width)


def scatter_kernel(
    nz, p_ref, out_ref, own, cin, xout, xin, zout, zin, ls, cs, cr, xs, xr, zs, zr
):
    iz, ic, it = (lax.axis_index(a) for a in ("z", CORE, TP))
    greet(partners_of(("z", TP, CORE)))
    across, beside = {TP: 1 - it}, {CORE: 1 - ic}
    order = list(range(nz - 1, -1, -1))
    loads, besides, acrosses, zeds = {}, {}, {}, {}
    for d in order:
        target = flip("z", d) if d else iz
        besides[d] = remote(p_ref.at[target, 1 - ic], cin.at[d], cs.at[d], cr.at[d], beside)
        besides[d].start()
        loads[d] = pltpu.make_async_copy(p_ref.at[target, ic], own.at[d], ls.at[d])
        loads[d].start()

    def add(d, side):
        return own[d, side].astype(F32) + cin[d, side].astype(F32)

    def after_across(d):
        acrosses[d].wait_recv()
        total = add(d, it) + xin[d].astype(F32)
        if d == 0:
            out_ref[...] = total
        else:
            zout[d] = total.astype(BF)
            zeds[d] = remote(zout.at[d], zin.at[d], zs.at[d], zr.at[d], {"z": flip("z", d)})
            zeds[d].start()

    for n, d in enumerate(order):
        loads[d].wait()
        besides[d].wait_recv()
        xout[d] = add(d, 1 - it).astype(BF)
        acrosses[d] = remote(xout.at[d], xin.at[d], xs.at[d], xr.at[d], across)
        acrosses[d].start()
        if n:
            after_across(order[n - 1])
    after_across(0)
    for d in order[:-1]:
        zeds[d].wait_recv()
        out_ref[...] += zin[d].astype(F32)
    for group in (besides, acrosses, zeds):
        for copy in group.values():
            copy.wait_send()


def scatter_rows(partial):
    nz = lax.axis_size("z")
    width = partial.shape[1]
    part = partial.astype(BF).reshape(nz, 2, 2, -1, width)
    piece = part.shape[3]
    sems = [DMA((nz,)) for _ in range(7)]
    return call(
        functools.partial(scatter_kernel, nz),
        2,
        jax.ShapeDtypeStruct((piece, width), F32),
        [pl.ANY],
        pltpu.VMEM,
        [
            pltpu.VMEM((nz, 2, piece, width), BF),
            pltpu.VMEM((nz, 2, piece, width), BF),
            *[pltpu.VMEM((nz, piece, width), BF) for _ in range(4)],
            *sems,
        ],
        32,
        part,
    )


def total_kernel(axes, x_ref, out_ref, *scratch):
    greet(partners_of(axes))
    value = x_ref[...]
    sends = []
    for stage, axis in enumerate(axes):
        slots, send_sems, recv_sems = scratch[3 * stage : 3 * stage + 3]
        size = lax.axis_size(axis)
        me = lax.axis_index(axis)
        slots[me] = value
        copies = []
        for d in range(1, size):
            copy = remote(
                slots.at[me], slots.at[me], send_sems.at[d], recv_sems.at[d], {axis: flip(axis, d)}
            )
            copy.start()
            copies.append(copy)
        for copy in copies:
            copy.wait_recv()
        value = slots[0]
        for n in range(1, size):
            value = value + slots[n]
        sends += copies
    out_ref[...] = value
    for copy in sends:
        copy.wait_send()


def total(terms, axes, identity):
    axes = tuple(a for a in axes if lax.axis_size(a) > 1)
    scratch = []
    for axis in axes:
        size = lax.axis_size(axis)
        scratch += [pltpu.VMEM((size, *terms.shape), F32), DMA((size,)), DMA((size,))]
    return call(
        functools.partial(total_kernel, axes),
        identity,
        jax.ShapeDtypeStruct(terms.shape, F32),
        [pltpu.VMEM],
        pltpu.VMEM,
        scratch,
        16,
        terms,
    )


def head_total(terms):
    return total(terms.reshape(-1, 128), (CORE, TP, "z"), 3).reshape(terms.shape)


def all_total(terms):
    size = terms.shape[0]
    padded = jnp.pad(terms, (0, -size % 1024)).reshape(-1, 128)
    return total(padded, (CORE, TP, "y", "z", "ch"), 4).reshape(-1)[:size]


def columns(ref, slot, count):
    return ref.at[:, pl.ds(pl.multiple_of(slot * count, 128), count)]


def intake_kernel(nz, count, tok_ref, *refs):
    w_refs, refs = refs[:count], refs[count:]
    tok_out, refs = refs[0], refs[1:]
    o_refs, refs = refs[:count], refs[count:]
    tok_buf, refs = refs[0], refs[1:]
    bufs, refs = refs[:count], refs[count:]
    tl, tzs, tzr, txs, txr, tcs, tcr, wl, wzs, wzr, wys, wyr = refs
    iz, iy, ic, it = (lax.axis_index(a) for a in ("z", "y", CORE, TP))
    across, beside, behind = {TP: 1 - it}, {CORE: 1 - ic}, {"y": 1 - iy}
    greet(partners_of(("z", "y", TP, CORE)))
    sends = []

    def push(src, dst, send_sem, recv_sem, partner):
        copy = remote(src, dst, send_sem, recv_sem, partner)
        copy.start()
        sends.append(copy)

    def arrived(ref, sem):
        remote(ref, ref, sem, sem, across).wait_recv()

    for d in range(1, nz):
        push(tok_ref.at[it], tok_out.at[iz, ic, it], tzs.at[d], tzr.at[d], {"z": flip("z", d)})
    push(tok_ref, tok_out.at[iz, ic], tcs.at[0, 0], tcr.at[0, 0], beside)
    tok_load = pltpu.make_async_copy(tok_ref, tok_buf, tl.at[0])
    tok_load.start()
    widths = [o.shape[-1] for o in o_refs]
    loads = []
    for k, (w, o) in enumerate(zip(w_refs, o_refs)):
        own = columns(w, iz * 2 + ic, widths[k])
        push(own, o.at[iz, iy], wys.at[k, 0], wyr.at[k, 0], behind)
        for d in range(1, nz):
            other = flip("z", d)
            push(
                columns(w, other * 2 + ic, widths[k]),
                o.at[iz, iy],
                wzs.at[k, d],
                wzr.at[k, d],
                {"z": other},
            )
        load = pltpu.make_async_copy(own, bufs[k], wl.at[k])
        load.start()
        loads.append(load)
    tok_load.wait()
    stores = [pltpu.make_async_copy(tok_buf, tok_out.at[iz, ic], tl.at[1])]
    stores[0].start()
    for d in range(1, nz):
        block = tok_out.at[flip("z", d), ic, it]
        arrived(block, tzr.at[d])
        push(block, block, txs.at[d], txr.at[d], across)
        push(block, block, tcs.at[d, 0], tcr.at[d, 0], beside)

    def forward(k):
        for d in range(1, nz):
            block = o_refs[k].at[flip("z", d), iy]
            arrived(block, wzr.at[k, d])
            push(block, block, wys.at[k, d], wyr.at[k, d], behind)

    first = min(3, count)
    for k in range(first):
        forward(k)
    for d in range(1, nz):
        block = tok_out.at[flip("z", d), ic, 1 - it]
        arrived(block, txr.at[d])
        push(block, block, tcs.at[d, 1], tcr.at[d, 1], beside)
    for k, load in enumerate(loads):
        load.wait()
        store = pltpu.make_async_copy(bufs[k], o_refs[k].at[iz, iy], wl.at[k])
        store.start()
        stores.append(store)
    for k in range(first, count):
        forward(k)
    arrived(tok_out.at[iz, 1 - ic], tcr.at[0, 0])
    for d in range(1, nz):
        for half in range(2):
            side = it if half == 0 else 1 - it
            arrived(tok_out.at[flip("z", d), 1 - ic, side], tcr.at[d, half])
    for k in range(count):
        for d in range(nz):
            source = flip("z", d) if d else iz
            arrived(o_refs[k].at[source, 1 - iy], wyr.at[k, d])
    for copy in sends:
        copy.wait_send()
    for store in stores:
        store.wait()


def intake(token_rows, weights):
    nz = lax.axis_size("z")
    count = len(weights)
    own_rows, width = token_rows.shape
    rows = weights[0].shape[0]
    parts = [w.shape[1] // (2 * nz) for w in weights]
    piece = own_rows // 2
    out_shape = [jax.ShapeDtypeStruct((nz, 2, 2, piece, width), BF)] + [
        jax.ShapeDtypeStruct((nz, 2, rows, c), BF) for c in parts
    ]
    got = call(
        functools.partial(intake_kernel, nz, count),
        5,
        out_shape,
        [pl.ANY] * (count + 1),
        [pl.ANY] * (count + 1),
        [
            pltpu.VMEM((2, piece, width), BF),
            *[pltpu.VMEM((rows, c), BF) for c in parts],
            DMA((2,)),
            *[DMA((nz,)) for _ in range(4)],
            *[DMA((nz, 2)) for _ in range(2)],
            DMA((count,)),
            *[DMA((count, nz)) for _ in range(4)],
        ],
        16,
        token_rows.reshape(2, piece, width),
        *weights,
    )
    return got[0].reshape(-1, width), [g.reshape(-1, g.shape[-1]) for g in got[1:]]


def outlet_kernel(nz, count, *refs):
    g_refs, refs = refs[:count], refs[count:]
    o_refs, refs = refs[:count], refs[count:]
    own, refs = refs[:count], refs[count:]
    yin, refs = refs[:count], refs[count:]
    zout, refs = refs[:count], refs[count:]
    ls, ys, yr, zs, zr, cs, cr, os = refs
    iz, iy, ic = (lax.axis_index(a) for a in ("z", "y", CORE))
    beside, behind = {CORE: 1 - ic}, {"y": 1 - iy}
    greet(partners_of(("z", "y", CORE)))
    sends, loads, pairs, stores = [], {}, {}, []

    def push(src, dst, send_sem, recv_sem, partner):
        copy = remote(src, dst, send_sem, recv_sem, partner)
        copy.start()
        sends.append(copy)
        return copy

    order = [(k, d) for k in range(count) for d in range(nz - 1, -1, -1)]
    widths = [g.shape[-1] for g in g_refs]
    for k, d in order:
        target = flip("z", d) if d else iz
        pairs[k, d] = push(
            g_refs[k].at[target, 1 - iy], yin[k].at[d], ys.at[k, d], yr.at[k, d], behind
        )
        loads[k, d] = pltpu.make_async_copy(g_refs[k].at[target, iy], own[k].at[d], ls.at[k, d])
        loads[k, d].start()

    def relay(k, d):
        block = columns(o_refs[k], flip("z", d) * 2 + ic, widths[k])
        remote(block, block, zr.at[k, d], zr.at[k, d], beside).wait_recv()
        push(block, block, cs.at[k, d], cr.at[k, d], beside)

    for n, (k, d) in enumerate(order):
        loads[k, d].wait()
        pairs[k, d].wait_recv()
        zout[k][d] = (own[k][d].astype(F32) + yin[k][d].astype(F32)).astype(BF)
        mine = columns(o_refs[k], iz * 2 + ic, widths[k])
        if d:
            push(zout[k].at[d], mine, zs.at[k, d], zr.at[k, d], {"z": flip("z", d)})
        else:
            push(zout[k].at[d], mine, cs.at[k, d], cr.at[k, d], beside)
            store = pltpu.make_async_copy(zout[k].at[d], mine, os.at[k])
            store.start()
            stores.append(store)
            if k:
                for e in range(nz - 1, 0, -1):
                    relay(k - 1, e)
    for e in range(nz - 1, 0, -1):
        relay(count - 1, e)
    for k, d in order:
        source = flip("z", d) if d else iz
        block = columns(o_refs[k], source * 2 + 1 - ic, widths[k])
        remote(block, block, cr.at[k, d], cr.at[k, d], beside).wait_recv()
    for copy in sends:
        copy.wait_send()
    for store in stores:
        store.wait()


def outlet(grads, identity=6):
    nz = lax.axis_size("z")
    count = len(grads)
    parts = [g.shape[1] for g in grads]
    blocks = [g.astype(BF).reshape(nz, 2, -1, g.shape[1]) for g in grads]
    rows = blocks[0].shape[2]
    got = call(
        functools.partial(outlet_kernel, nz, count),
        identity,
        [jax.ShapeDtypeStruct((rows, 2 * nz * c), BF) for c in parts],
        [pl.ANY] * count,
        [pl.ANY] * count,
        [
            *[pltpu.VMEM((nz, rows, c), BF) for _ in range(3) for c in parts],
            *[DMA((count, nz)) for _ in range(7)],
            DMA((count,)),
        ],
        32,
        *blocks,
    )
    if lax.axis_size("ch") > 1:
        got = lax.psum(tuple(got), "ch")
    return [g.astype(F32) for g in got]


class Kernel:
    def __init__(self):
        self.ins, self.outs, self.scratch = [], [], []

    def inp(self, name, array, space=pl.ANY):
        self.ins.append((name, array, space))

    def out(self, name, shape, dtype, space=pl.ANY):
        self.outs.append((name, jax.ShapeDtypeStruct(shape, dtype), space))

    def mem(self, name, shape, dtype):
        self.scratch.append((name, pltpu.VMEM(shape, dtype)))

    def sem(self, name, *shape):
        self.scratch.append((name, DMA(shape)))

    def run(self, identity, body, limit):
        names = [n for n, *_ in self.ins + self.outs + self.scratch]

        def kernel(*refs):
            body(types.SimpleNamespace(**dict(zip(names, refs))))

        got = call(
            kernel,
            identity,
            [shape for _, shape, _ in self.outs],
            [space for *_, space in self.ins],
            [space for *_, space in self.outs],
            [made for _, made in self.scratch],
            limit,
            *[array for _, array, _ in self.ins],
        )
        return {n: g for (n, *_), g in zip(self.outs, got)}


class Flow:
    def __init__(self):
        self.sends, self.inner_sends = [], []
        self.iz, self.iy, self.ic, self.it = (
            lax.axis_index(a) for a in ("z", "y", CORE, TP)
        )
        self.across = {TP: 1 - self.it}
        self.beside = {CORE: 1 - self.ic}
        self.behind = {"y": 1 - self.iy}
        self.near, self.mid = {"z": flip("z", 1)}, {"z": 3 - self.iz}
        self.role = lax.rem((self.iz + 1) // 2, 2)
        self.inner = self.role == 1

    def at(self, d):
        return flip("z", d) if d else self.iz

    def line(self, s):
        side = self.iz // 2
        return (self.iz, self.near["z"], 2 - side, 3 - 3 * side)[s]

    def push(self, src, dst, send_sem, recv_sem, partner):
        copy = remote(src, dst, send_sem, recv_sem, partner)
        copy.start()
        self.sends.append(copy)
        return copy

    def push_inner(self, src, dst, send_sem, recv_sem, partner):
        copy = remote(src, dst, send_sem, recv_sem, partner)
        pl.when(self.inner)(copy.start)
        self.inner_sends.append(copy)

    def pass_on(self, s, block, send_sems, recv_sems):
        partner, number = ((self.mid, 3), (self.near, 2), (self.near, 3))[s - 1]
        self.push_inner(block, block, send_sems.at[s + 2], recv_sems.at[number], partner)

    def arrived(self, ref, sem):
        remote(ref, ref, sem, sem, self.across).wait_recv()

    def finish(self):
        for copy in self.sends:
            copy.wait_send()
        if self.inner_sends:

            @pl.when(self.inner)
            def _():
                for copy in self.inner_sends:
                    copy.wait_send()

        self.sends, self.inner_sends = [], []


def greet_line(others=()):
    flow = Flow()
    barrier = pltpu.get_barrier_semaphore()
    for partner in (flow.near, flow.across, flow.beside, *others):
        pl.semaphore_signal(barrier, inc=1, device_id=partner, device_id_type=MESH)

    @pl.when(flow.inner)
    def _():
        pl.semaphore_signal(barrier, inc=1, device_id=flow.mid, device_id_type=MESH)

    pl.semaphore_wait(barrier, 3 + len(others) + flow.role)


def stripe(ref, z, core, tp, piece):
    start = pl.multiple_of((core * 2 + tp) * piece, piece)
    return ref.at[z, pl.ds(start, piece)]


class Gather(Flow):
    @staticmethod
    def setup(k, name, rows, out=False, inside=False):
        piece, width = rows.shape
        if inside:
            k.mem(name + "_x", rows.shape, rows.dtype)
        else:
            k.inp(name + "_x", rows)
        (k.out if out else k.mem)(name, (4, 4 * piece, width), rows.dtype)
        k.sem(name + "_own")
        k.sem(name + "_zs", 6)
        for s in ("_zr", "_xs", "_xr"):
            k.sem(name + s, 4)
        k.sem(name + "_cs", 4, 2)
        k.sem(name + "_cr", 4, 2)

    def __init__(self, r, name):
        super().__init__()
        self.x, self.buf = getattr(r, name + "_x"), getattr(r, name)
        self.own_sem, self.zs, self.zr, self.xs, self.xr, self.cs, self.cr = (
            getattr(r, name + s) for s in ("_own", "_zs", "_zr", "_xs", "_xr", "_cs", "_cr")
        )
        self.piece = self.x.shape[0]

    def block(self, z, core, tp):
        return stripe(self.buf, z, core, tp, self.piece)

    def start(self):
        own = self.block(self.iz, self.ic, self.it)
        self.push(self.x, own, self.zs.at[1], self.zr.at[1], self.near)
        self.push_inner(self.x, own, self.zs.at[2], self.zr.at[2], self.mid)
        self.push(self.x, own, self.xs.at[0], self.xr.at[0], self.across)
        self.push(self.x, own, self.cs.at[0, 0], self.cr.at[0, 0], self.beside)
        self.local = pltpu.make_async_copy(self.x, own, self.own_sem)
        self.local.start()

    def from_across(self, s):
        block = self.block(self.line(s), self.ic, 1 - self.it)
        self.arrived(block, self.xr.at[s])
        self.push(block, block, self.cs.at[s, 1], self.cr.at[s, 1], self.beside)

    def advance(self, s):
        if s < 4:
            block = self.block(self.line(s), self.ic, self.it)
            self.arrived(block, self.zr.at[s])
            self.pass_on(s, block, self.zs, self.zr)
            self.push(block, block, self.xs.at[s], self.xr.at[s], self.across)
            self.push(block, block, self.cs.at[s, 0], self.cr.at[s, 0], self.beside)
        self.from_across(s - 1)

    def ready(self, s):
        if s == 0:
            self.local.wait()
        for half in range(2):
            side = self.it if half == 0 else 1 - self.it
            self.arrived(self.block(self.line(s), 1 - self.ic, side), self.cr.at[s, half])


class Scatter(Flow):
    @staticmethod
    def setup(k, name, piece, width, partial=None):
        if partial is None:
            k.mem(name + "_p", (4, 4 * piece, width), BF)
        else:
            k.inp(name + "_p", partial)
            k.mem(name + "_m", (4, 2 * piece, width), BF)
            k.sem(name + "_ls", 4)
        k.mem(name + "_c", (4, 2 * piece, width), BF)
        for s in ("_xo", "_xi", "_zo"):
            k.mem(name + s, (4, piece, width), BF)
        k.mem(name + "_zi", (6, piece, width), BF)
        for s in ("_cs", "_cr", "_xs", "_xr", "_zs"):
            k.sem(name + s, 4)
        k.sem(name + "_zr", 6)

    def __init__(self, r, name, out):
        super().__init__()
        self.out = out
        self.p, self.c, self.xo, self.xi, self.zo, self.zi = (
            getattr(r, name + s) for s in ("_p", "_c", "_xo", "_xi", "_zo", "_zi")
        )
        self.cs, self.cr, self.xs, self.xr, self.zs, self.zr = (
            getattr(r, name + s) for s in ("_cs", "_cr", "_xs", "_xr", "_zs", "_zr")
        )
        self.m, self.ls = getattr(r, name + "_m", None), getattr(r, name + "_ls", None)
        self.piece = self.xo.shape[1]
        self.core_copy, self.across_copy, self.loads = {}, {}, {}

    def rows(self, core):
        return pl.ds(pl.multiple_of(core * 2 * self.piece, 2 * self.piece), 2 * self.piece)

    def begin(self, s):
        part = s if self.m is None else self.line(s)
        self.core_copy[s] = self.push(
            self.p.at[part, self.rows(1 - self.ic)],
            self.c.at[s],
            self.cs.at[s],
            self.cr.at[s],
            self.beside,
        )
        if self.m is not None:
            self.loads[s] = pltpu.make_async_copy(
                self.p.at[part, self.rows(self.ic)], self.m.at[s], self.ls.at[s]
            )
            self.loads[s].start()

    def add(self, s, side):
        rows = pl.ds(pl.multiple_of(side * self.piece, self.piece), self.piece)
        if self.m is not None:
            own = self.m[s, rows]
        else:
            start = pl.multiple_of((self.ic * 2 + side) * self.piece, self.piece)
            own = self.p[s, pl.ds(start, self.piece)]
        return own.astype(F32) + self.c[s, rows].astype(F32)

    def cross(self, s):
        if s in self.loads:
            self.loads[s].wait()
        self.core_copy[s].wait_recv()
        self.xo[s] = self.add(s, 1 - self.it).astype(BF)
        self.across_copy[s] = self.push(
            self.xo.at[s], self.xi.at[s], self.xs.at[s], self.xr.at[s], self.across
        )

    def leave(self, s):
        self.across_copy[s].wait_recv()

        def value():
            return self.add(s, self.it) + self.xi[s].astype(F32)

        if s == 0:
            self.out[...] = value()
            return
        came = (None, 4, 2, 3)[s]

        @pl.when(self.inner)
        def _():
            self.arrived(self.zi.at[came], self.zr.at[came])
            self.zo[s] = (value() + self.zi[came].astype(F32)).astype(BF)

        @pl.when(self.role == 0)
        def _():
            self.zo[s] = value().astype(BF)

        place = s + self.role * (None, -1, 3, 1)[s]
        partner = self.near["z"]
        if s > 1:
            partner = partner + self.role * (self.mid["z"] - partner)
        self.push(
            self.zo.at[s], self.zi.at[place], self.zs.at[s], self.zr.at[place], {"z": partner}
        )

    def end(self):
        @pl.when(self.inner)
        def _():
            for place in (1, 5):
                self.arrived(self.zi.at[place], self.zr.at[place])
                self.out[...] += self.zi[place].astype(F32)

        @pl.when(self.role == 0)
        def _():
            self.arrived(self.zi.at[0], self.zr.at[0])
            self.out[...] += self.zi[0].astype(F32)


class Total(Flow):
    @staticmethod
    def setup(k, name, shape, axes):
        for axis in axes:
            size = lax.axis_size(axis)
            k.mem(f"{name}_{axis}", (size, *shape), F32)
            k.sem(f"{name}_{axis}_s", size)
            k.sem(f"{name}_{axis}_r", size)

    def __init__(self, r, name):
        super().__init__()
        self.r, self.name = r, name

    def send(self, axis, value):
        slots, ss, rs = (getattr(self.r, f"{self.name}_{axis}{s}") for s in ("", "_s", "_r"))
        me = lax.axis_index(axis)
        slots[me] = value
        self.copies = [
            self.push(slots.at[me], slots.at[me], ss.at[d], rs.at[d], {axis: flip(axis, d)})
            for d in range(1, lax.axis_size(axis))
        ]
        self.slots = slots

    def receive(self):
        for copy in self.copies:
            copy.wait_recv()
        value = self.slots[0]
        for n in range(1, self.slots.shape[0]):
            value = value + self.slots[n]
        return value


class Outlet(Flow):
    @staticmethod
    def setup(k, name, grads, nz, inside=False):
        for n, grad in enumerate(grads):
            rows, cols = grad.shape[-2:]
            if inside:
                k.mem(f"{name}_g{n}", grad.shape, BF)
            else:
                k.inp(f"{name}_g{n}", grad)
            k.out(f"{name}_o{n}", (rows, 2 * nz * cols), BF)
            if grad.ndim == 3:
                continue
            for s in ("yin", "zout") if inside else ("yin", "zout", "own"):
                k.mem(f"{name}_{s}{n}", (nz, rows, cols), BF)
        for s in ("ls", "ys", "yr", "zs", "zr", "cs", "cr"):
            k.sem(f"{name}_{s}", len(grads), nz)
        k.sem(f"{name}_os", len(grads))

    def __init__(self, r, name, count, nz):
        super().__init__()
        self.nz, self.count = nz, count
        self.g, self.o, self.own, self.yin, self.zout = (
            [getattr(r, f"{name}_{s}{n}", None) for n in range(count)]
            for s in ("g", "o", "own", "yin", "zout")
        )
        self.ls, self.ys, self.yr, self.zs, self.zr, self.cs, self.cr, self.os = (
            getattr(r, f"{name}_{s}") for s in ("ls", "ys", "yr", "zs", "zr", "cs", "cr", "os")
        )
        self.loads, self.pairs, self.stores = {}, {}, []

    def slot(self, k, z, core):
        return columns(self.o[k], z * 2 + core, self.g[k].shape[-1])

    def start(self, k):
        if self.zout[k] is None:
            return
        for d in range(self.nz - 1, -1, -1):
            target = self.at(d)
            self.pairs[k, d] = self.push(
                self.g[k].at[target, 1 - self.iy],
                self.yin[k].at[d],
                self.ys.at[k, d],
                self.yr.at[k, d],
                self.behind,
            )
            if self.own[k] is not None:
                self.loads[k, d] = pltpu.make_async_copy(
                    self.g[k].at[target, self.iy], self.own[k].at[d], self.ls.at[k, d]
                )
                self.loads[k, d].start()

    def combine(self, k, blocks=(3, 2, 1, 0)):
        mine = self.slot(k, self.iz, self.ic)
        for d in blocks:
            if self.zout[k] is None:
                src = self.g[k].at[d]
            else:
                self.pairs[k, d].wait_recv()
                if self.own[k] is not None:
                    self.loads[k, d].wait()
                    own = self.own[k][d]
                else:
                    own = self.g[k][self.at(d), self.iy]
                self.zout[k][d] = (own.astype(F32) + self.yin[k][d].astype(F32)).astype(BF)
                src = self.zout[k].at[d]
            if d:
                self.push(src, mine, self.zs.at[k, d], self.zr.at[k, d], {"z": self.at(d)})
            else:
                self.push(src, mine, self.cs.at[k, d], self.cr.at[k, d], self.beside)
                store = pltpu.make_async_copy(src, mine, self.os.at[k])
                store.start()
                self.stores.append(store)

    def relay(self, k):
        for d in range(1, self.nz):
            block = self.slot(k, self.at(d), self.ic)
            self.arrived(block, self.zr.at[k, d])
            self.push(block, block, self.cs.at[k, d], self.cr.at[k, d], self.beside)

    def end(self):
        for k in range(self.count):
            for d in range(self.nz):
                self.arrived(self.slot(k, self.at(d), 1 - self.ic), self.cr.at[k, d])
        for store in self.stores:
            store.wait()
        self.finish()


def gather_line(rows):
    k = Kernel()
    Gather.setup(k, "all", rows, out=True)

    def body(r):
        greet_line()
        gather = Gather(r, "all")
        gather.start()
        for s in range(1, 5):
            gather.advance(s)
        for s in range(4):
            gather.ready(s)
        gather.finish()

    return k.run(1, body, 16)["all"].reshape(-1, rows.shape[1])


def scatter_line(partial):
    width = partial.shape[1]
    piece = partial.shape[0] // 16
    k = Kernel()
    Scatter.setup(k, "rs", piece, width, partial.astype(BF).reshape(4, 4 * piece, width))
    k.out("sum", (piece, width), F32, pltpu.VMEM)

    def body(r):
        greet_line()
        scatter = Scatter(r, "rs", r.sum)
        order = (3, 2, 1, 0)
        for s in order:
            scatter.begin(s)
        for s in order:
            scatter.cross(s)
        for s in order:
            scatter.leave(s)
        scatter.end()
        scatter.finish()

    return k.run(2, body, 32)["sum"]


def exact(a, b, dims):
    return lax.dot_general(
        a, b, (dims, ((), ())), precision=lax.Precision.HIGHEST, preferred_element_type=F32
    )


def picker(width):
    row = lax.broadcasted_iota(jnp.int32, (8, width), 0)
    part = lax.broadcasted_iota(jnp.int32, (8, width), 1) // HD
    return jnp.where(row == part, 1.0, 0.0).astype(F32)


def row_sums(first, second):
    both = jnp.concatenate([first, second], axis=1)
    return exact(picker(2 * HD), both, ((1,), (1,)))


def spread(sums, which):
    row = lax.broadcasted_iota(jnp.int32, (8, HD), 0)
    one = jnp.where(row == which, 1.0, 0.0).astype(F32)
    return exact(sums, one, ((0,), (0,)))


def softmax_rows(query, key, length):
    count = query.shape[0]
    row = lax.broadcasted_iota(jnp.int32, (count, count), 0)
    col = lax.broadcasted_iota(jnp.int32, (count, count), 1)
    scores = mm_nt(query, key) * (1.0 / math.sqrt(HD))
    scores = jnp.where((col <= row) & (col < length), scores, NEGATIVE)
    exponent = jnp.exp(scores - jnp.max(scores, axis=-1, keepdims=True))
    return exponent / jnp.sum(exponent, axis=-1, keepdims=True)


def weight_blocks(left, right, place):
    nz, parts = left.shape[0], 2 * left.shape[0]
    block, share = left.shape[2] // parts, right.shape[2] // len(place)

    @pl.loop(0, parts)
    def _(f):
        cols = pl.ds(pl.multiple_of(f * block, block), block)
        made = mm_tn(left[0, :, cols], right[0])
        for z in range(1, nz):
            made = made + mm_tn(left[z, :, cols], right[z])
        made = made.astype(BF)
        for n, grad in enumerate(place):
            grad[f // 2, lax.rem(f, 2)] = made[:, n * share : (n + 1) * share]


def scatter_back(partial, left, right):
    width, cols = partial.shape[1], right[0].shape[1]
    piece, rows = partial.shape[0] // 16, width // 8
    k = Kernel()
    Scatter.setup(k, "rs", piece, width, partial.astype(BF).reshape(4, 4 * piece, width))
    k.out("sum", (piece, width), F32, pltpu.VMEM)
    for n, array in enumerate((*left, *right)):
        array = array.reshape(4, 4 * piece, -1)
        k.inp(f"i{n}", array)
        k.mem(f"m{n}", array.shape, BF)
    for n in range(3):
        k.mem(f"g{n}", (4, 2, rows, cols), BF)
        k.out(f"o{n}", (4, 2, rows, cols) if n else (4, rows, cols), BF)
    k.mem("yin", (4, rows, cols), BF)
    k.mem("total", (4, rows, cols), BF)
    k.sem("ld", 5)
    for s in ("ys", "yr"):
        k.sem(s, 4)
    k.sem("os", 3)

    def body(r):
        flow, scatter = Flow(), Scatter(r, "rs", r.sum)
        greet_line((flow.behind,))
        order = (3, 2, 1, 0)
        for s in order:
            scatter.begin(s)
        loads = load_all(
            [(getattr(r, f"i{n}"), getattr(r, f"m{n}")) for n in (0, 2, 1, 3, 4)], r.ld
        )
        for s in order:
            scatter.cross(s)
        for n in (0, 1):
            loads[n].wait()
        weight_blocks(r.m0, r.m2, [r.g0])
        pairs = {}
        for d in order:
            pairs[d] = flow.push(
                r.g0.at[flow.at(d), 1 - flow.iy], r.yin.at[d], r.ys.at[d], r.yr.at[d], flow.behind
            )
        scatter.leave(3)
        stores = []

        def store(n, src, out):
            stores.append(pltpu.make_async_copy(src, out, r.os.at[n]))
            stores[-1].start()

        for n in (2, 3):
            loads[n].wait()
        weight_blocks(r.m1, r.m3, [r.g1])
        store(1, r.g1, r.o1)
        scatter.leave(2)
        loads[4].wait()
        weight_blocks(r.m1, r.m4, [r.g2])
        store(2, r.g2, r.o2)
        scatter.leave(1)
        scatter.leave(0)
        scatter.end()
        for d in order:
            pairs[d].wait_recv()
            own = r.g0[flow.at(d), flow.iy].astype(F32)
            r.total[d] = (own + r.yin[d].astype(F32)).astype(BF)
        store(0, r.total, r.o0)
        for f in (flow, scatter):
            f.finish()
        for copy in stores:
            copy.wait()

    got = k.run(3, body, 60)
    return got["sum"], [got[f"o{n}"] for n in range(3)]


def load_all(pairs, sems):
    copies = []
    for n, (src, dst) in enumerate(pairs):
        copy = pltpu.make_async_copy(src, dst, sems.at[n])
        copy.start()
        copies.append(copy)
    return copies


def attention_back(
    branch, wide, wo, wqkv, saved, tokens_all, residual_grad, stream_rows, terms, gains, tables,
    seq_lengths,
):
    nz = lax.axis_size("z")
    piece, width = branch.shape
    rows = 4 * piece
    padded = jnp.pad(terms, (0, -terms.shape[0] % 1024)).reshape(-1, 128)
    lanes = width // 128
    sum_axes = (CORE, TP, "y", "z")
    k = Kernel()
    Gather.setup(k, "ball", branch)
    Outlet.setup(k, "wide", wide, nz)
    slim = [jax.ShapeDtypeStruct((nz, 2, width // (2 * nz), HD), BF)] * 4
    Outlet.setup(k, "slim", slim, nz, inside=True)
    Scatter.setup(k, "rs", piece, width)
    Total.setup(k, "tot", (nz, 8, rows), (CORE, TP, "z"))
    Total.setup(k, "sum", padded.shape, sum_axes)
    k.inp("wo", wo)
    k.inp("wqkv", wqkv)
    k.inp("tokens", tokens_all)
    k.mem("tokens_m", tokens_all.shape, BF)
    names = ("q", "k", "v", "att", "nq", "nk", "qs", "ks")
    for name, array in zip(names, saved):
        k.inp(name, array)
        k.mem(name + "_m", array.shape, array.dtype)
    k.mem("wo_m", wo.shape, BF)
    k.mem("wqkv_m", wqkv.shape, BF)
    k.inp("res", residual_grad)
    k.mem("res_m", (piece, width), F32)
    k.inp("stream", stream_rows)
    k.mem("stream_m", (piece, width), BF)
    k.sem("ld", len(names) + 5)
    k.inp("terms", padded, pltpu.VMEM)
    k.mem("terms_m", padded.shape, F32)
    k.out("terms_out", padded.shape, F32, pltpu.VMEM)
    k.inp("gains", gains, pltpu.VMEM)
    k.inp("tables", tables, pltpu.VMEM)
    k.inp("lens", seq_lengths, pltpu.SMEM)
    k.mem("wqk", (nz, 2, rows, HD), F32)
    k.mem("low", (nz, rows, 3 * HD), BF)
    k.mem("dots", (nz, 8, rows), F32)
    k.mem("norms", (2, HD), F32)
    k.mem("grad", (piece, width), F32)
    k.mem("tail", (piece, width), BF)
    k.out("grad_out", (2, piece, width), BF)
    k.out("stream_out", (2, piece, width), BF)
    k.sem("xs", 2)
    k.sem("xr", 2)
    k.sem("ss", 2)

    def body(r):
        greet(partners_of(("z", "y", TP, CORE)))
        gather, outlet_flow = Gather(r, "ball"), Outlet(r, "wide", len(wide), nz)
        slim_flow, own = Outlet(r, "slim", len(slim), nz), Flow()
        scatter, total_flow = Scatter(r, "rs", r.grad), Total(r, "tot")
        sum_flow = Total(r, "sum")
        gather.start()
        for n in range(len(wide)):
            outlet_flow.start(n)
        names_in = ("wo", "wqkv", *names, "tokens", "res", "stream")
        loads = load_all([(getattr(r, n), getattr(r, n + "_m")) for n in names_in], r.ld)
        scale = 1.0 / math.sqrt(HD)
        cosine, sine = r.tables[0], r.tables[1]
        gather.advance(1)
        outlet_flow.combine(0, (3,))
        for copy in loads:
            copy.wait()
        r.norms[...] = jnp.zeros_like(r.norms)

        def compute(z):
            grad_low = mm(r.ball[z], r.wo_m[...]).astype(BF)
            query, key, value = r.q_m[z], r.k_m[z], r.v_m[z]
            probability = softmax_rows(query, key, r.lens[z])
            grad_prob = mm_nt(grad_low, value)
            row_dots = jnp.sum(probability * grad_prob, axis=-1, keepdims=True)
            grad_scores = (probability * (grad_prob - row_dots)).astype(BF)
            grad_q = rotate_back(mm(grad_scores, key) * scale, cosine, sine)
            grad_k = rotate_back(mm_tn(grad_scores, query) * scale, cosine, sine)
            grad_v = mm_tn(probability.astype(BF), grad_low)
            r.low[z, :, 2 * HD :] = grad_v.astype(BF)
            nq, nk = r.nq_m[z], r.nk_m[z]
            r.norms[0:1] += jnp.sum(grad_q * nq, axis=0, keepdims=True)
            r.norms[1:2] += jnp.sum(grad_k * nk, axis=0, keepdims=True)
            wq, wk = grad_q * r.gains[0:1], grad_k * r.gains[1:2]
            r.wqk[z, 0] = wq
            r.wqk[z, 1] = wk
            r.dots[z] = row_sums(wq * nq, wk * nk)

        for d in range(nz):
            gather.ready(d)
            compute(gather.line(d))
            if d + 2 <= nz:
                gather.advance(d + 2)
            if d == 0:
                outlet_flow.combine(0, (2,))
                own.push(
                    r.stream, r.stream_out.at[own.it], r.xs.at[0], r.xr.at[0], own.across
                )
            if d == 1:
                outlet_flow.combine(0, (1, 0))
        r.terms_m[...] = r.terms[...]
        slot = 2 * lanes + own.it * (lanes // 2) + own.iz * 2 + own.ic
        for n in range(2):
            r.terms_m[pl.ds(slot + n * lanes, 1)] = r.norms[n : n + 1]
        total_flow.send(CORE, r.dots[...])
        sum_flow.send(CORE, r.terms_m[...])
        value, other = total_flow.receive(), sum_flow.receive()
        total_flow.send(TP, value)
        sum_flow.send(TP, other)
        value, other = total_flow.receive(), sum_flow.receive()
        total_flow.send("z", value)
        sum_flow.send("y", other)
        outlet_flow.combine(1)
        weight_blocks(r.ball, r.att_m, [slim_flow.g[3]])
        slim_flow.start(3)
        r.dots[...] = total_flow.receive()
        order = list(range(nz - 1, -1, -1))
        for n, d in enumerate(order):
            z = gather.line(d)
            sums = r.dots[z] * (1.0 / width)
            for j, (normed, factor) in enumerate(((r.nq_m, r.qs_m), (r.nk_m, r.ks_m))):
                low = factor[z] * (r.wqk[z, j] - normed[z] * spread(sums, j))
                r.low[z, :, j * HD : (j + 1) * HD] = low.astype(BF)
            r.rs_p[d] = mm_nt(r.low[z], r.wqkv_m[...]).astype(BF)
            scatter.begin(d)
            if n:
                scatter.cross(order[n - 1])
        scatter.cross(0)
        outlet_flow.combine(2, (3,))
        scatter.leave(3)
        weight_blocks(r.tokens_m, r.low, slim_flow.g[:3])
        for n in range(3):
            slim_flow.start(n)
        scatter.leave(2)
        outlet_flow.combine(2, (2,))
        slim_flow.combine(3)
        scatter.leave(1)
        outlet_flow.combine(2, (1, 0))
        scatter.leave(0)
        sum_flow.send("z", sum_flow.receive())
        for n in range(3):
            slim_flow.combine(n)
        outlet_flow.relay(0)
        outlet_flow.relay(1)
        scatter.end()
        r.tail[...] = (r.res_m[...] + r.grad[...]).astype(BF)
        own.push(r.tail, r.grad_out.at[own.it], r.xs.at[1], r.xr.at[1], own.across)
        stores = []
        for n, (src, out) in enumerate(((r.stream_m, r.stream_out), (r.tail, r.grad_out))):
            stores.append(pltpu.make_async_copy(src, out.at[own.it], r.ss.at[n]))
            stores[-1].start()
        r.terms_out[...] = sum_flow.receive()
        outlet_flow.relay(2)
        slim_flow.relay(3)
        for n in range(3):
            slim_flow.relay(n)
        outlet_flow.end()
        slim_flow.end()
        for n, out in enumerate((r.stream_out, r.grad_out)):
            own.arrived(out.at[1 - own.it], r.xr.at[n])
        for flow in (gather, scatter, total_flow, sum_flow, own):
            flow.finish()
        for copy in stores:
            copy.wait()

    got = k.run(7, body, 60)
    return (
        [got[f"slim_o{n}"].astype(F32) for n in range(4)]
        + [got[f"wide_o{n}"].astype(F32) for n in range(len(wide))],
        got["grad_out"].reshape(-1, width).astype(F32),
        got["stream_out"].reshape(-1, width),
        got["terms_out"].reshape(-1)[: terms.shape[0]],
    )


def attention_front(token_rows, weights, gains, tables, seq_lengths, post_attention):
    nz = lax.axis_size("z")
    own_rows, width = token_rows.shape
    piece, rows = own_rows // 2, own_rows * 2
    w_rows = weights[0].shape[0]
    count = len(weights)
    parts = [w.shape[1] // (2 * nz) for w in weights]
    k = Kernel()
    Scatter.setup(k, "rs", piece, width)
    Total.setup(k, "tot", (nz, 8, rows), (CORE, TP, "z"))
    k.inp("tok", token_rows)
    for n, weight in enumerate(weights):
        k.inp(f"w{n}", weight)
    k.inp("gains", gains, pltpu.VMEM)
    k.inp("tables", tables, pltpu.VMEM)
    k.inp("lens", seq_lengths, pltpu.SMEM)
    k.mem("tall", (nz, rows, width), BF)
    k.mem("qkv", (nz, 2, w_rows, 3 * HD), BF)
    k.mem("wo", (nz, 2, w_rows, parts[3]), BF)
    for n in range(4, count):
        k.mem(f"b{n}", (w_rows, parts[n]), BF)
        k.out(f"o{n}", (nz, 2, w_rows, parts[n]), BF)
    k.mem("raw", (nz, rows, 3 * HD), F32)
    k.mem("dots", (nz, 8, rows), F32)
    saved = (("q", BF), ("k", BF), ("v", BF), ("nq", F32), ("nk", F32), ("qs", F32), ("ks", F32), ("att", BF))
    for name, kind in saved:
        k.mem(name + "_m", (nz, rows, HD), kind)
        k.out(name, (nz, rows, HD), kind)
    k.mem("branch", (piece, width), F32)
    k.inp("post", post_attention[None], pltpu.VMEM)
    for name in ("normed", "residual"):
        k.out(name, (piece, width), F32, pltpu.VMEM)
    k.out("scale", (piece, 128), F32, pltpu.VMEM)
    Gather.setup(k, "all", jax.ShapeDtypeStruct((piece, width), BF), inside=True)
    k.out("wide", (nz, rows, width), BF)
    k.out("tokens", (nz, rows, width), BF)
    k.out("qkv_out", (nz, 2, w_rows, 3 * HD), BF)
    k.out("wo_out", (nz, 2, w_rows, parts[3]), BF)
    k.sem("tl")
    k.sem("tzs", 6)
    for s in ("tzr", "txs", "txr"):
        k.sem(s, nz)
    k.sem("tcs", nz, 2)
    k.sem("tcr", nz, 2)
    k.sem("wl", 2, count)
    for s in ("wzs", "wzr", "wys", "wyr"):
        k.sem(s, count, nz)
    k.sem("st", len(saved) + 2, nz)
    k.sem("sw", 2)

    def body(r):
        greet(partners_of(("z", "y", TP, CORE)))
        flow = Flow()
        iz, iy, ic, it = flow.iz, flow.iy, flow.ic, flow.it
        scatter, total_flow = Scatter(r, "rs", r.branch), Total(r, "tot")
        gather = Gather(r, "all")

        def block(z, core, tp):
            return stripe(r.tall, z, core, tp, piece)

        def pair(z, core):
            start = pl.multiple_of(core * own_rows, own_rows)
            return r.tall.at[z, pl.ds(start, own_rows)]

        tok_half = r.tok.at[pl.ds(pl.multiple_of(it * piece, piece), piece)]
        flow.push(tok_half, block(iz, ic, it), r.tzs.at[1], r.tzr.at[1], flow.near)
        flow.push_inner(tok_half, block(iz, ic, it), r.tzs.at[2], r.tzr.at[2], flow.mid)
        flow.push(r.tok, pair(iz, ic), r.tcs.at[0, 0], r.tcr.at[0, 0], flow.beside)
        tok_load = pltpu.make_async_copy(r.tok, pair(iz, ic), r.tl)
        tok_load.start()
        loads = {}

        def landing(n, z, y):
            if n < 3:
                return r.qkv.at[z, y, :, n * HD : (n + 1) * HD]
            return r.wo.at[z, y] if n == 3 else getattr(r, f"o{n}").at[z, y]

        def bring(n, parts_of_z=(3, 2, 1), own_part=True):
            weight = getattr(r, f"w{n}")
            own = columns(weight, iz * 2 + ic, parts[n])
            for d in parts_of_z:
                other = flow.at(d)
                flow.push(
                    columns(weight, other * 2 + ic, parts[n]),
                    landing(n, iz, iy),
                    r.wzs.at[n, d],
                    r.wzr.at[n, d],
                    {"z": other},
                )
            if own_part:
                flow.push(own, landing(n, iz, iy), r.wys.at[n, 0], r.wyr.at[n, 0], flow.behind)
                dst = landing(n, iz, iy) if n < 4 else getattr(r, f"b{n}")
                loads[n] = pltpu.make_async_copy(own, dst, r.wl.at[0, n])
                loads[n].start()

        def forward(n, parts_of_z=(3, 2, 1)):
            for d in parts_of_z:
                here = landing(n, flow.at(d), iy)
                flow.arrived(here, r.wzr.at[n, d])
                flow.push(here, here, r.wys.at[n, d], r.wyr.at[n, d], flow.behind)

        def keep(n):
            loads[n].wait()
            copy = pltpu.make_async_copy(getattr(r, f"b{n}"), landing(n, iz, iy), r.wl.at[1, n])
            copy.start()
            stores.append(copy)

        def complete(n):
            for d in range(nz):
                flow.arrived(landing(n, flow.at(d), 1 - iy), r.wyr.at[n, d])

        bring(0)
        for d in range(1, nz):
            here = block(flow.line(d), ic, it)
            flow.arrived(here, r.tzr.at[d])
            flow.pass_on(d, here, r.tzs, r.tzr)
            flow.push(here, here, r.txs.at[d], r.txr.at[d], flow.across)
            flow.push(here, here, r.tcs.at[d, 0], r.tcr.at[d, 0], flow.beside)
            bring(d)
        bring(4)
        for d in range(1, nz):
            forward(d - 1)
            here = block(flow.line(d), ic, 1 - it)
            flow.arrived(here, r.txr.at[d])
            flow.push(here, here, r.tcs.at[d, 1], r.tcr.at[d, 1], flow.beside)
        stores = []

        def save(n, src, dst, d):
            copy = pltpu.make_async_copy(src, dst, r.st.at[n, d])
            copy.start()
            stores.append(copy)

        for n in range(4):
            loads[n].wait()
        for n in range(3):
            complete(n)
        tok_load.wait()
        for d in range(nz):
            z = flow.line(d)
            if d == 0:
                flow.arrived(pair(iz, 1 - ic), r.tcr.at[0, 0])
            else:
                for half in range(2):
                    side = it if half == 0 else 1 - it
                    flow.arrived(block(z, 1 - ic, side), r.tcr.at[d, half])
            save(0, r.tall.at[z], r.tokens.at[z], d)
            raw = mm(r.tall[z], r.qkv[...].reshape(2 * nz * w_rows, 3 * HD))
            r.raw[z] = raw
            query, key = raw[:, :HD], raw[:, HD : 2 * HD]
            r.dots[z] = row_sums(query * query, key * key)
        total_flow.send(CORE, r.dots[...])
        forward(3)
        value = total_flow.receive()
        total_flow.send(TP, value)
        value = total_flow.receive()
        total_flow.send("z", value)
        bring(5, (3,))
        for n in (4, 5):
            keep(n)
        complete(3)
        for n, (src, dst) in enumerate(((r.qkv, r.qkv_out), (r.wo, r.wo_out))):
            copy = pltpu.make_async_copy(src, dst, r.sw.at[n])
            copy.start()
            stores.append(copy)
        r.dots[...] = lax.rsqrt(total_flow.receive() * (1.0 / width) + EPSILON)
        cosine, sine = r.tables[0], r.tables[1]
        order = list(range(nz - 1, -1, -1))
        for n, d in enumerate(order):
            z = flow.line(d)
            sums = r.dots[z]
            r.qs_m[z] = spread(sums, 0)
            r.ks_m[z] = spread(sums, 1)
            r.nq_m[z] = r.raw[z, :, :HD] * r.qs_m[z]
            r.nk_m[z] = r.raw[z, :, HD : 2 * HD] * r.ks_m[z]
            query = rotate(r.nq_m[z] * r.gains[0:1], cosine, sine).astype(BF)
            key = rotate(r.nk_m[z] * r.gains[1:2], cosine, sine).astype(BF)
            value = r.raw[z, :, 2 * HD :].astype(BF)
            r.q_m[z] = query
            r.k_m[z] = key
            r.v_m[z] = value
            probability = softmax_rows(query, key, r.lens[z]).astype(BF)
            r.att_m[z] = mm(probability, value).astype(BF)
            for m, (name, _) in enumerate(saved):
                save(m + 1, getattr(r, name + "_m").at[z], getattr(r, name).at[z], d)
            wo = r.wo[...].reshape(2 * nz * w_rows, parts[3])
            r.rs_p[d] = mm_nt(r.att_m[z], wo).astype(BF)
            scatter.begin(d)
            if n:
                scatter.cross(order[n - 1])
            if n > 1:
                scatter.leave(order[n - 2])
            if n == 0:
                forward(4)
        scatter.cross(0)
        scatter.leave(1)
        bring(5, (2, 1), False)
        scatter.leave(0)
        forward(5, (3,))
        scatter.end()
        branch = r.branch[...]
        scale = lax.rsqrt(jnp.mean(branch * branch, axis=-1, keepdims=True) + EPSILON)
        r.normed[...] = branch * scale
        r.scale[...] = jnp.broadcast_to(scale, r.scale.shape)
        start = pl.multiple_of((ic * 2 + it) * piece, piece)
        mine = r.tall[iz, pl.ds(start, piece)].astype(F32)
        r.residual[...] = mine + r.normed[...] * r.post[...]
        r.all_x[...] = r.residual[...].astype(BF)
        gather.start()
        gather.advance(1)
        bring(6, (3, 2))
        forward(5, (2, 1))
        for d in range(2, 4):
            gather.advance(d)
        bring(6, (1,), False)
        gather.advance(4)
        keep(6)
        for d in range(nz):
            gather.ready(d)
            z = gather.line(d)
            save(len(saved) + 1, gather.buf.at[z], r.wide.at[z], d)
        forward(6)
        for n in range(4, count):
            complete(n)
        for f in (flow, scatter, total_flow, gather):
            f.finish()
        for copy in stores:
            copy.wait()

    return k.run(9, body, 60)


def local(
    tokens,
    lengths,
    weight_query,
    weight_key,
    weight_value,
    weight_out,
    weight_gate,
    weight_up,
    weight_down,
    post_attention,
    post_feedforward,
    query_norm,
    key_norm,
    cotangent,
):
    nz, ny, nch, ntp = (lax.axis_size(a) for a in ("z", "y", "ch", TP))
    iz, iy, ich, icore, itp = (lax.axis_index(a) for a in AXES)
    token_rows = tokens[0]
    own_rows, width = token_rows.shape
    piece = own_rows // ntp
    seq_rows = own_rows * 2
    total_rows = seq_rows * nz
    scale_factor = 1.0 / math.sqrt(HD)
    own_head = iz * 2 + icore
    qn = lax.dynamic_slice_in_dim(query_norm, own_head * HD, HD)
    kn = lax.dynamic_slice_in_dim(key_norm, own_head * HD, HD)
    seq_lengths = lax.dynamic_index_in_dim(lengths.reshape(nz, ny), iy, 1, keepdims=False)
    positions = ich * seq_rows + jnp.arange(seq_rows, dtype=jnp.int32)
    key_positions = jnp.arange(seq_rows * nch, dtype=jnp.int32)
    cosine, sine_table = rope_tables(positions)
    allowed = (key_positions[None, None, :] <= positions[None, :, None]) & (
        key_positions[None, None, :] < seq_lengths[:, None, None]
    )
    my_tokens = lax.dynamic_slice_in_dim(token_rows, itp * piece, piece, 0)
    my_cot = lax.dynamic_slice_in_dim(cotangent[0], itp * piece, piece, 0)
    my_pos = (ich * 2 + icore) * own_rows + itp * piece + jnp.arange(piece, dtype=jnp.int32)
    my_valid = (my_pos < lengths[iz * ny + iy]).astype(F32)[:, None]

    weights = (
        weight_query,
        weight_key,
        weight_value,
        weight_out,
        weight_gate,
        weight_up,
        weight_down,
    )
    fused = nch == 1 and nz == 4
    gather, scatter = (gather_line, scatter_line) if fused else (gather_rows, scatter_rows)
    by_seq = lambda a: a.reshape(nz, seq_rows, HD)
    gains, tables = jnp.stack([qn, kn]), jnp.stack([cosine, sine_table])
    if fused:
        front = attention_front(
            token_rows, weights, gains, tables, seq_lengths, post_attention
        )
        wg, wu, wd = (front[f"o{n}"].reshape(width, -1) for n in (4, 5, 6))
    else:
        tokens_all, (wq, wk, wv, wo, wg, wu, wd) = intake(token_rows, weights)
        query_raw = mm(tokens_all, wq)
        key_raw = mm(tokens_all, wk)
        value_raw = mm(tokens_all, wv)
        squares = head_total(
            jnp.stack([jnp.sum(query_raw * query_raw, axis=-1), jnp.sum(key_raw * key_raw, axis=-1)])
        )
        scales = lax.rsqrt(squares / width + EPSILON)
        query_scale = scales[0][:, None]
        key_scale = scales[1][:, None]
        queries = rotate(by_seq(query_raw * query_scale * qn), cosine, sine_table).astype(BF)
        keys = rotate(by_seq(key_raw * key_scale * kn), cosine, sine_table).astype(BF)
        values = by_seq(value_raw).astype(BF)
        if nch > 1:
            keys_full = lax.all_gather(keys, "ch", axis=1, tiled=True)
            values_full = lax.all_gather(values, "ch", axis=1, tiled=True)
        else:
            keys_full, values_full = keys, values
        scores = (
            jnp.einsum(SCORE, queries, keys_full, preferred_element_type=F32) * scale_factor
        )
        scores = jnp.where(allowed, scores, NEGATIVE)
        exponent = jnp.exp(scores - jnp.max(scores, axis=-1, keepdims=True))
        probability = exponent / jnp.sum(exponent, axis=-1, keepdims=True)
        probability_low = probability.astype(BF)
        attended = jnp.einsum(APPLY, probability_low, values_full, preferred_element_type=F32)
        attended_low = attended.reshape(total_rows, HD).astype(BF)
        branch_sum = scatter_rows(mm_nt(attended_low, wo))
    if fused:
        attn_normed, residual = front["normed"], front["residual"]
        attn_scale = front["scale"][:, :1]
        residual_all = front["wide"].reshape(-1, width)
    else:
        attn_scale = lax.rsqrt(jnp.mean(branch_sum * branch_sum, axis=-1, keepdims=True) + EPSILON)
        attn_normed = branch_sum * attn_scale
        residual = my_tokens.astype(F32) + attn_normed * post_attention
        residual_all = gather(residual.astype(BF))
    attention_branch = attn_normed * post_attention
    gate_value = mm(residual_all, wg)
    up_value = mm(residual_all, wu)
    sigmoid_gate = jax.nn.sigmoid(gate_value)
    silu_gate = gate_value * sigmoid_gate
    mixed_low = (silu_gate * up_value).astype(BF)
    down_sum = scatter(mm_nt(mixed_low, wd))
    ffn_scale = lax.rsqrt(jnp.mean(down_sum * down_sum, axis=-1, keepdims=True) + EPSILON)
    ffn_normed = down_sum * ffn_scale
    feedforward_branch = ffn_normed * post_feedforward
    stream = residual + feedforward_branch
    stat_terms = jnp.stack(
        [
            jnp.sum(my_valid * stream * stream),
            jnp.sum(my_valid * attention_branch * attention_branch),
            jnp.sum(my_valid * feedforward_branch * feedforward_branch),
        ]
    )
    grad_stream = my_cot * my_valid
    grad_post_ff = jnp.sum(grad_stream * ffn_normed, axis=0)
    scaled = grad_stream * post_feedforward
    grad_down_sum = ffn_scale * (
        scaled - ffn_normed * jnp.mean(scaled * ffn_normed, axis=-1, keepdims=True)
    )
    down_all = gather(grad_down_sum.astype(BF))
    grad_mixed = mm(down_all, wd)
    gate_low = (
        grad_mixed * up_value * sigmoid_gate * (1.0 + gate_value * (1.0 - sigmoid_gate))
    ).astype(BF)
    up_low = (grad_mixed * silu_gate).astype(BF)
    partial = mm_nt(gate_low, wg) + mm_nt(up_low, wu)
    if fused:
        back, wide_grads = scatter_back(
            partial, (down_all, residual_all), (mixed_low, gate_low, up_low)
        )
    else:
        grad_wg = mm_tn(residual_all, gate_low)
        grad_wu = mm_tn(residual_all, up_low)
        grad_wd = mm_tn(down_all, mixed_low)
        back = scatter(partial)
    grad_residual = grad_stream + back
    grad_post_attn = jnp.sum(grad_residual * attn_normed, axis=0)
    scaled_attn = grad_residual * post_attention
    grad_branch = attn_scale * (
        scaled_attn - attn_normed * jnp.mean(scaled_attn * attn_normed, axis=-1, keepdims=True)
    )
    if not fused:
        branch_all = gather_rows(grad_branch.astype(BF))
        grad_att_low = mm(branch_all, wo).astype(BF)
        grad_wo = mm_tn(branch_all, attended_low)
        grad_att = by_seq(grad_att_low)
        grad_prob = jnp.einsum(SCORE, grad_att, values_full, preferred_element_type=F32)
        row_dots = jnp.sum(probability * grad_prob, axis=-1, keepdims=True)
        grad_scores = (probability * (grad_prob - row_dots)).astype(BF)
        grad_queries = (
            jnp.einsum(APPLY, grad_scores, keys_full, preferred_element_type=F32)
            * scale_factor
        )
        grad_keys = (
            jnp.einsum("bts,btd->bsd", grad_scores, queries, preferred_element_type=F32) * scale_factor
        )
        grad_values = jnp.einsum("bts,btd->bsd", probability_low, grad_att, preferred_element_type=F32)
        if nch > 1:
            grad_keys, grad_values = (
                lax.psum_scatter(g.astype(BF), "ch", scatter_dimension=1, tiled=True).astype(F32)
                for g in (grad_keys, grad_values)
            )
        value_grad_low = grad_values.reshape(total_rows, HD).astype(BF)
        grad_q_normed = rotate_back(grad_queries, cosine, sine_table).reshape(total_rows, HD)
        grad_k_normed = rotate_back(grad_keys, cosine, sine_table).reshape(total_rows, HD)
        query_weighted = grad_q_normed * qn
        key_weighted = grad_k_normed * kn
        dots = head_total(
            jnp.stack(
                [
                    jnp.sum(query_weighted * query_raw, axis=-1),
                    jnp.sum(key_weighted * key_raw, axis=-1),
                ]
            )
        )
        query_grad_low = (
            query_scale * (query_weighted - query_raw * query_scale**2 * (dots[0] / width)[:, None])
        ).astype(BF)
        key_grad_low = (
            key_scale * (key_weighted - key_raw * key_scale**2 * (dots[1] / width)[:, None])
        ).astype(BF)
        grad_qnorm = jnp.sum(grad_q_normed * query_raw * query_scale, axis=0)
        grad_knorm = jnp.sum(grad_k_normed * key_raw * key_scale, axis=0)
        grad_wq = mm_tn(tokens_all, query_grad_low)
        grad_wk = mm_tn(tokens_all, key_grad_low)
        grad_wv = mm_tn(tokens_all, value_grad_low)
        grad_rows = grad_residual + scatter_rows(
            mm_nt(query_grad_low, wq) + mm_nt(key_grad_low, wk) + mm_nt(value_grad_low, wv)
        )
    if fused:
        saved = tuple(front[n] for n in ("q", "k", "v", "att", "nq", "nk", "qs", "ks"))
        norms_wide = jnp.zeros((2 * width,), F32)
    else:
        slot = itp * (width // ntp) + own_head * HD
        zero_row = jnp.zeros((width,), F32)
        norms_wide = jnp.concatenate(
            [
                lax.dynamic_update_slice_in_dim(zero_row, grad_qnorm, slot, 0),
                lax.dynamic_update_slice_in_dim(zero_row, grad_knorm, slot, 0),
            ]
        )
    terms = jnp.concatenate([grad_post_attn, grad_post_ff, norms_wide, stat_terms])
    if fused:
        weight_grads, grad_input, output, summed = attention_back(
            grad_branch.astype(BF),
            wide_grads,
            front["wo_out"].reshape(width, -1),
            front["qkv_out"].reshape(width, -1),
            saved,
            front["tokens"],
            grad_residual,
            stream.astype(BF),
            terms,
            gains,
            tables,
            seq_lengths,
        )
        weight_grads = [weight_grads[n] for n in (0, 1, 2, 3, 5, 6, 4)]
    else:
        weight_grads = outlet((grad_wq, grad_wk, grad_wv, grad_wo, grad_wg, grad_wu, grad_wd))
        grad_input = lax.all_gather(grad_rows, TP, axis=0, tiled=True)
        output = lax.all_gather(stream.astype(BF), TP, axis=0, tiled=True)
        summed = all_total(terms)
    half = width // ntp
    qn_sum = lax.dynamic_slice_in_dim(summed, 2 * width + itp * half, half)
    kn_sum = lax.dynamic_slice_in_dim(summed, 3 * width + itp * half, half)
    token_count = jnp.sum(lengths.astype(F32))
    root_means = jnp.sqrt(summed[4 * width :] / (token_count * width))
    return (
        output[None],
        grad_input[None],
        *weight_grads,
        summed[:width],
        summed[width : 2 * width],
        qn_sum,
        kn_sum,
        root_means,
    )


def solution(mesh):
    n_fsdp, n_ctx, n_tp = (mesh.shape[a] for a in ("fsdp", "ctx", TP))
    fine = Mesh(mesh.devices.reshape(n_fsdp // 2, 2, n_ctx // 2, 2, n_tp), AXES)
    fsdp, ctx = ("z", "y"), ("ch", CORE)
    rows = P(fsdp, ctx, None)
    weight = P(fsdp, TP)
    return jax.shard_map(
        local,
        mesh=fine,
        in_specs=(rows, P(), *([weight] * 7), P(), P(), P(TP), P(TP), rows),
        out_specs=(rows, rows, *([weight] * 7), P(), P(), P(TP), P(TP), P()),
        check_vma=False,
    )
```

```python
import functools
import math
import types

import jax
import jax.numpy as jnp
from jax import lax
from jax.experimental import pallas as pl
from jax.experimental.pallas import tpu as pltpu
from jax.sharding import Mesh, PartitionSpec as P

HD = 128
EPSILON = 1e-06
ROPE_BASE = 500000.0
NEGATIVE = -1e30
CORE, TP = "core", "tp"
SCORE = "btd,bsd->bts"
APPLY = "bts,bsd->btd"
AXES = ("z", "y", "ch", CORE, TP)
BF = jnp.bfloat16
F32 = jnp.float32


def rope_tables(positions):
    half_size = HD // 2
    exponent = jnp.arange(half_size, dtype=F32) * (2.0 / HD)
    frequency = jnp.power(ROPE_BASE, -exponent)
    angles = positions.astype(F32)[:, None] * frequency[None, :]
    cosine = jnp.cos(angles)
    sine_table = jnp.sin(angles)
    return (
        jnp.concatenate([cosine, cosine], axis=-1),
        jnp.concatenate([sine_table, sine_table], axis=-1),
    )


def rotate(values, cosine, sine_table):
    half_size = HD // 2
    turned = jnp.concatenate([-values[..., half_size:], values[..., :half_size]], axis=-1)
    return values * cosine + turned * sine_table


def rotate_back(grads_in, cosine, sine_table):
    half_size = HD // 2
    sin_part = grads_in * sine_table
    return grads_in * cosine + jnp.concatenate(
        [sin_part[..., half_size:], -sin_part[..., :half_size]], axis=-1
    )


def dot(former, latter, dims):
    return lax.dot_general(former, latter, (dims, ((), ())), preferred_element_type=F32)


def mm(a, b):
    return dot(a, b, ((1,), (0,)))


def mm_nt(a, b):
    return dot(a, b, ((1,), (1,)))


def mm_tn(a, b):
    return dot(a, b, ((0,), (0,)))


MESH = pl.DeviceIdType.MESH


def flip(axis, bits):
    me = lax.axis_index(axis)
    result, weight = me, 1
    while weight <= bits:
        if (bits // weight) % 2:
            result = result + weight * (1 - 2 * lax.rem(me // weight, 2))
        weight *= 2
    return result


def greet(partners):
    barrier = pltpu.get_barrier_semaphore()
    for partner in partners:
        pl.semaphore_signal(barrier, inc=1, device_id=partner, device_id_type=MESH)
    pl.semaphore_wait(barrier, len(partners))


def remote(src, dst, send_sem, recv_sem, partner):
    return pltpu.make_async_remote_copy(
        src_ref=src,
        dst_ref=dst,
        send_sem=send_sem,
        recv_sem=recv_sem,
        device_id=partner,
        device_id_type=MESH,
    )


def partners_of(axes):
    found = []
    for axis in axes:
        for bits in range(1, lax.axis_size(axis)):
            found.append({axis: flip(axis, bits)})
    return found


def call(kernel, identity, out_shape, in_spaces, out_spaces, scratch, limit, *operands):
    return pl.pallas_call(
        kernel,
        out_shape=out_shape,
        in_specs=[pl.BlockSpec(memory_space=s) for s in in_spaces],
        out_specs=jax.tree.map(lambda s: pl.BlockSpec(memory_space=s), out_spaces),
        scratch_shapes=scratch,
        compiler_params=pltpu.CompilerParams(
            collective_id=identity, has_side_effects=True, vmem_limit_bytes=limit * 2**20
        ),
    )(*operands)


DMA = pltpu.SemaphoreType.DMA


def gather_kernel(nz, x_ref, out_ref, own_sem, zs, zr, xs, xr, cs, cr):
    iz, ic, it = (lax.axis_index(a) for a in ("z", CORE, TP))
    greet(partners_of(("z", TP, CORE)))
    sends = []

    def push(src, where, send_sem, recv_sem, partner):
        copy = remote(src, out_ref.at[where], send_sem, recv_sem, partner)
        copy.start()
        sends.append(copy)

    across, beside = {TP: 1 - it}, {CORE: 1 - ic}
    own = (iz, ic, it)
    for d in range(1, nz):
        push(x_ref, own, zs.at[d], zr.at[d], {"z": flip("z", d)})
    push(x_ref, own, xs.at[0], xr.at[0], across)
    push(x_ref, own, cs.at[0, 0], cr.at[0, 0], beside)
    local_copy = pltpu.make_async_copy(x_ref, out_ref.at[own], own_sem)
    local_copy.start()

    def await_at(where, sem):
        remote(out_ref.at[where], out_ref.at[where], sem, sem, across).wait_recv()

    def from_across(d):
        where = (flip("z", d), ic, 1 - it)
        await_at(where, xr.at[d])
        push(out_ref.at[where], where, cs.at[d, 1], cr.at[d, 1], beside)

    for d in range(1, nz):
        where = (flip("z", d), ic, it)
        await_at(where, zr.at[d])
        push(out_ref.at[where], where, xs.at[d], xr.at[d], across)
        push(out_ref.at[where], where, cs.at[d, 0], cr.at[d, 0], beside)
        from_across(d - 1)
    from_across(nz - 1)
    for d in range(nz):
        for half in range(2):
            side = it if half == 0 else 1 - it
            await_at((flip("z", d), 1 - ic, side), cr.at[d, half])
    for copy in sends:
        copy.wait_send()
    local_copy.wait()


def gather_rows(rows):
    piece, width = rows.shape
    nz = lax.axis_size("z")
    out = call(
        functools.partial(gather_kernel, nz),
        1,
        jax.ShapeDtypeStruct((nz, 2, 2, piece, width), rows.dtype),
        [pl.ANY],
        pl.ANY,
        [DMA, DMA((nz,)), DMA((nz,)), DMA((nz,)), DMA((nz,)), DMA((nz, 2)), DMA((nz, 2))],
        16,
        rows,
    )
    return out.reshape(-1, width)


def scatter_kernel(
    nz, p_ref, out_ref, own, cin, xout, xin, zout, zin, ls, cs, cr, xs, xr, zs, zr
):
    iz, ic, it = (lax.axis_index(a) for a in ("z", CORE, TP))
    greet(partners_of(("z", TP, CORE)))
    across, beside = {TP: 1 - it}, {CORE: 1 - ic}
    order = list(range(nz - 1, -1, -1))
    loads, besides, acrosses, zeds = {}, {}, {}, {}
    for d in order:
        target = flip("z", d) if d else iz
        besides[d] = remote(p_ref.at[target, 1 - ic], cin.at[d], cs.at[d], cr.at[d], beside)
        besides[d].start()
        loads[d] = pltpu.make_async_copy(p_ref.at[target, ic], own.at[d], ls.at[d])
        loads[d].start()

    def add(d, side):
        return own[d, side].astype(F32) + cin[d, side].astype(F32)

    def after_across(d):
        acrosses[d].wait_recv()
        total = add(d, it) + xin[d].astype(F32)
        if d == 0:
            out_ref[...] = total
        else:
            zout[d] = total.astype(BF)
            zeds[d] = remote(zout.at[d], zin.at[d], zs.at[d], zr.at[d], {"z": flip("z", d)})
            zeds[d].start()

    for n, d in enumerate(order):
        loads[d].wait()
        besides[d].wait_recv()
        xout[d] = add(d, 1 - it).astype(BF)
        acrosses[d] = remote(xout.at[d], xin.at[d], xs.at[d], xr.at[d], across)
        acrosses[d].start()
        if n:
            after_across(order[n - 1])
    after_across(0)
    for d in order[:-1]:
        zeds[d].wait_recv()
        out_ref[...] += zin[d].astype(F32)
    for group in (besides, acrosses, zeds):
        for copy in group.values():
            copy.wait_send()


def scatter_rows(partial):
    nz = lax.axis_size("z")
    width = partial.shape[1]
    part = partial.astype(BF).reshape(nz, 2, 2, -1, width)
    piece = part.shape[3]
    sems = [DMA((nz,)) for _ in range(7)]
    return call(
        functools.partial(scatter_kernel, nz),
        2,
        jax.ShapeDtypeStruct((piece, width), F32),
        [pl.ANY],
        pltpu.VMEM,
        [
            pltpu.VMEM((nz, 2, piece, width), BF),
            pltpu.VMEM((nz, 2, piece, width), BF),
            *[pltpu.VMEM((nz, piece, width), BF) for _ in range(4)],
            *sems,
        ],
        32,
        part,
    )


def total_kernel(axes, x_ref, out_ref, *scratch):
    greet(partners_of(axes))
    value = x_ref[...]
    sends = []
    for stage, axis in enumerate(axes):
        slots, send_sems, recv_sems = scratch[3 * stage : 3 * stage + 3]
        size = lax.axis_size(axis)
        me = lax.axis_index(axis)
        slots[me] = value
        copies = []
        for d in range(1, size):
            copy = remote(
                slots.at[me], slots.at[me], send_sems.at[d], recv_sems.at[d], {axis: flip(axis, d)}
            )
            copy.start()
            copies.append(copy)
        for copy in copies:
            copy.wait_recv()
        value = slots[0]
        for n in range(1, size):
            value = value + slots[n]
        sends += copies
    out_ref[...] = value
    for copy in sends:
        copy.wait_send()


def total(terms, axes, identity):
    axes = tuple(a for a in axes if lax.axis_size(a) > 1)
    scratch = []
    for axis in axes:
        size = lax.axis_size(axis)
        scratch += [pltpu.VMEM((size, *terms.shape), F32), DMA((size,)), DMA((size,))]
    return call(
        functools.partial(total_kernel, axes),
        identity,
        jax.ShapeDtypeStruct(terms.shape, F32),
        [pltpu.VMEM],
        pltpu.VMEM,
        scratch,
        16,
        terms,
    )


def head_total(terms):
    return total(terms.reshape(-1, 128), (CORE, TP, "z"), 3).reshape(terms.shape)


def all_total(terms):
    size = terms.shape[0]
    padded = jnp.pad(terms, (0, -size % 1024)).reshape(-1, 128)
    return total(padded, (CORE, TP, "y", "z", "ch"), 4).reshape(-1)[:size]


def columns(ref, slot, count):
    return ref.at[:, pl.ds(pl.multiple_of(slot * count, 128), count)]


def intake_kernel(nz, count, tok_ref, *refs):
    w_refs, refs = refs[:count], refs[count:]
    tok_out, refs = refs[0], refs[1:]
    o_refs, refs = refs[:count], refs[count:]
    tok_buf, refs = refs[0], refs[1:]
    bufs, refs = refs[:count], refs[count:]
    tl, tzs, tzr, txs, txr, tcs, tcr, wl, wzs, wzr, wys, wyr = refs
    iz, iy, ic, it = (lax.axis_index(a) for a in ("z", "y", CORE, TP))
    across, beside, behind = {TP: 1 - it}, {CORE: 1 - ic}, {"y": 1 - iy}
    greet(partners_of(("z", "y", TP, CORE)))
    sends = []

    def push(src, dst, send_sem, recv_sem, partner):
        copy = remote(src, dst, send_sem, recv_sem, partner)
        copy.start()
        sends.append(copy)

    def arrived(ref, sem):
        remote(ref, ref, sem, sem, across).wait_recv()

    for d in range(1, nz):
        push(tok_ref.at[it], tok_out.at[iz, ic, it], tzs.at[d], tzr.at[d], {"z": flip("z", d)})
    push(tok_ref, tok_out.at[iz, ic], tcs.at[0, 0], tcr.at[0, 0], beside)
    tok_load = pltpu.make_async_copy(tok_ref, tok_buf, tl.at[0])
    tok_load.start()
    widths = [o.shape[-1] for o in o_refs]
    loads = []
    for k, (w, o) in enumerate(zip(w_refs, o_refs)):
        own = columns(w, iz * 2 + ic, widths[k])
        push(own, o.at[iz, iy], wys.at[k, 0], wyr.at[k, 0], behind)
        for d in range(1, nz):
            other = flip("z", d)
            push(
                columns(w, other * 2 + ic, widths[k]),
                o.at[iz, iy],
                wzs.at[k, d],
                wzr.at[k, d],
                {"z": other},
            )
        load = pltpu.make_async_copy(own, bufs[k], wl.at[k])
        load.start()
        loads.append(load)
    tok_load.wait()
    stores = [pltpu.make_async_copy(tok_buf, tok_out.at[iz, ic], tl.at[1])]
    stores[0].start()
    for d in range(1, nz):
        block = tok_out.at[flip("z", d), ic, it]
        arrived(block, tzr.at[d])
        push(block, block, txs.at[d], txr.at[d], across)
        push(block, block, tcs.at[d, 0], tcr.at[d, 0], beside)

    def forward(k):
        for d in range(1, nz):
            block = o_refs[k].at[flip("z", d), iy]
            arrived(block, wzr.at[k, d])
            push(block, block, wys.at[k, d], wyr.at[k, d], behind)

    first = min(3, count)
    for k in range(first):
        forward(k)
    for d in range(1, nz):
        block = tok_out.at[flip("z", d), ic, 1 - it]
        arrived(block, txr.at[d])
        push(block, block, tcs.at[d, 1], tcr.at[d, 1], beside)
    for k, load in enumerate(loads):
        load.wait()
        store = pltpu.make_async_copy(bufs[k], o_refs[k].at[iz, iy], wl.at[k])
        store.start()
        stores.append(store)
    for k in range(first, count):
        forward(k)
    arrived(tok_out.at[iz, 1 - ic], tcr.at[0, 0])
    for d in range(1, nz):
        for half in range(2):
            side = it if half == 0 else 1 - it
            arrived(tok_out.at[flip("z", d), 1 - ic, side], tcr.at[d, half])
    for k in range(count):
        for d in range(nz):
            source = flip("z", d) if d else iz
            arrived(o_refs[k].at[source, 1 - iy], wyr.at[k, d])
    for copy in sends:
        copy.wait_send()
    for store in stores:
        store.wait()


def intake(token_rows, weights):
    nz = lax.axis_size("z")
    count = len(weights)
    own_rows, width = token_rows.shape
    rows = weights[0].shape[0]
    parts = [w.shape[1] // (2 * nz) for w in weights]
    piece = own_rows // 2
    out_shape = [jax.ShapeDtypeStruct((nz, 2, 2, piece, width), BF)] + [
        jax.ShapeDtypeStruct((nz, 2, rows, c), BF) for c in parts
    ]
    got = call(
        functools.partial(intake_kernel, nz, count),
        5,
        out_shape,
        [pl.ANY] * (count + 1),
        [pl.ANY] * (count + 1),
        [
            pltpu.VMEM((2, piece, width), BF),
            *[pltpu.VMEM((rows, c), BF) for c in parts],
            DMA((2,)),
            *[DMA((nz,)) for _ in range(4)],
            *[DMA((nz, 2)) for _ in range(2)],
            DMA((count,)),
            *[DMA((count, nz)) for _ in range(4)],
        ],
        16,
        token_rows.reshape(2, piece, width),
        *weights,
    )
    return got[0].reshape(-1, width), [g.reshape(-1, g.shape[-1]) for g in got[1:]]


def outlet_kernel(nz, count, *refs):
    g_refs, refs = refs[:count], refs[count:]
    o_refs, refs = refs[:count], refs[count:]
    own, refs = refs[:count], refs[count:]
    yin, refs = refs[:count], refs[count:]
    zout, refs = refs[:count], refs[count:]
    ls, ys, yr, zs, zr, cs, cr, os = refs
    iz, iy, ic = (lax.axis_index(a) for a in ("z", "y", CORE))
    beside, behind = {CORE: 1 - ic}, {"y": 1 - iy}
    greet(partners_of(("z", "y", CORE)))
    sends, loads, pairs, stores = [], {}, {}, []

    def push(src, dst, send_sem, recv_sem, partner):
        copy = remote(src, dst, send_sem, recv_sem, partner)
        copy.start()
        sends.append(copy)
        return copy

    order = [(k, d) for k in range(count) for d in range(nz - 1, -1, -1)]
    widths = [g.shape[-1] for g in g_refs]
    for k, d in order:
        target = flip("z", d) if d else iz
        pairs[k, d] = push(
            g_refs[k].at[target, 1 - iy], yin[k].at[d], ys.at[k, d], yr.at[k, d], behind
        )
        loads[k, d] = pltpu.make_async_copy(g_refs[k].at[target, iy], own[k].at[d], ls.at[k, d])
        loads[k, d].start()

    def relay(k, d):
        block = columns(o_refs[k], flip("z", d) * 2 + ic, widths[k])
        remote(block, block, zr.at[k, d], zr.at[k, d], beside).wait_recv()
        push(block, block, cs.at[k, d], cr.at[k, d], beside)

    for n, (k, d) in enumerate(order):
        loads[k, d].wait()
        pairs[k, d].wait_recv()
        zout[k][d] = (own[k][d].astype(F32) + yin[k][d].astype(F32)).astype(BF)
        mine = columns(o_refs[k], iz * 2 + ic, widths[k])
        if d:
            push(zout[k].at[d], mine, zs.at[k, d], zr.at[k, d], {"z": flip("z", d)})
        else:
            push(zout[k].at[d], mine, cs.at[k, d], cr.at[k, d], beside)
            store = pltpu.make_async_copy(zout[k].at[d], mine, os.at[k])
            store.start()
            stores.append(store)
            if k:
                for e in range(nz - 1, 0, -1):
                    relay(k - 1, e)
    for e in range(nz - 1, 0, -1):
        relay(count - 1, e)
    for k, d in order:
        source = flip("z", d) if d else iz
        block = columns(o_refs[k], source * 2 + 1 - ic, widths[k])
        remote(block, block, cr.at[k, d], cr.at[k, d], beside).wait_recv()
    for copy in sends:
        copy.wait_send()
    for store in stores:
        store.wait()


def outlet(grads, identity=6):
    nz = lax.axis_size("z")
    count = len(grads)
    parts = [g.shape[1] for g in grads]
    blocks = [g.astype(BF).reshape(nz, 2, -1, g.shape[1]) for g in grads]
    rows = blocks[0].shape[2]
    got = call(
        functools.partial(outlet_kernel, nz, count),
        identity,
        [jax.ShapeDtypeStruct((rows, 2 * nz * c), BF) for c in parts],
        [pl.ANY] * count,
        [pl.ANY] * count,
        [
            *[pltpu.VMEM((nz, rows, c), BF) for _ in range(3) for c in parts],
            *[DMA((count, nz)) for _ in range(7)],
            DMA((count,)),
        ],
        32,
        *blocks,
    )
    if lax.axis_size("ch") > 1:
        got = lax.psum(tuple(got), "ch")
    return [g.astype(F32) for g in got]


class Kernel:
    def __init__(self):
        self.ins, self.outs, self.scratch = [], [], []

    def inp(self, name, array, space=pl.ANY):
        self.ins.append((name, array, space))

    def out(self, name, shape, dtype, space=pl.ANY):
        self.outs.append((name, jax.ShapeDtypeStruct(shape, dtype), space))

    def mem(self, name, shape, dtype):
        self.scratch.append((name, pltpu.VMEM(shape, dtype)))

    def sem(self, name, *shape):
        self.scratch.append((name, DMA(shape)))

    def run(self, identity, body, limit):
        names = [n for n, *_ in self.ins + self.outs + self.scratch]

        def kernel(*refs):
            body(types.SimpleNamespace(**dict(zip(names, refs))))

        got = call(
            kernel,
            identity,
            [shape for _, shape, _ in self.outs],
            [space for *_, space in self.ins],
            [space for *_, space in self.outs],
            [made for _, made in self.scratch],
            limit,
            *[array for _, array, _ in self.ins],
        )
        return {n: g for (n, *_), g in zip(self.outs, got)}


class Flow:
    def __init__(self):
        self.sends, self.inner_sends = [], []
        self.iz, self.iy, self.ic, self.it = (
            lax.axis_index(a) for a in ("z", "y", CORE, TP)
        )
        self.across = {TP: 1 - self.it}
        self.beside = {CORE: 1 - self.ic}
        self.behind = {"y": 1 - self.iy}
        self.near, self.mid = {"z": flip("z", 1)}, {"z": 3 - self.iz}
        self.role = lax.rem((self.iz + 1) // 2, 2)
        self.inner = self.role == 1

    def at(self, d):
        return flip("z", d) if d else self.iz

    def line(self, s):
        side = self.iz // 2
        return (self.iz, self.near["z"], 2 - side, 3 - 3 * side)[s]

    def push(self, src, dst, send_sem, recv_sem, partner):
        copy = remote(src, dst, send_sem, recv_sem, partner)
        copy.start()
        self.sends.append(copy)
        return copy

    def push_inner(self, src, dst, send_sem, recv_sem, partner):
        copy = remote(src, dst, send_sem, recv_sem, partner)
        pl.when(self.inner)(copy.start)
        self.inner_sends.append(copy)

    def pass_on(self, s, block, send_sems, recv_sems):
        partner, number = ((self.mid, 3), (self.near, 2), (self.near, 3))[s - 1]
        self.push_inner(block, block, send_sems.at[s + 2], recv_sems.at[number], partner)

    def arrived(self, ref, sem):
        remote(ref, ref, sem, sem, self.across).wait_recv()

    def finish(self):
        for copy in self.sends:
            copy.wait_send()
        if self.inner_sends:

            @pl.when(self.inner)
            def _():
                for copy in self.inner_sends:
                    copy.wait_send()

        self.sends, self.inner_sends = [], []


def greet_line(others=()):
    flow = Flow()
    barrier = pltpu.get_barrier_semaphore()
    for partner in (flow.near, flow.across, flow.beside, *others):
        pl.semaphore_signal(barrier, inc=1, device_id=partner, device_id_type=MESH)

    @pl.when(flow.inner)
    def _():
        pl.semaphore_signal(barrier, inc=1, device_id=flow.mid, device_id_type=MESH)

    pl.semaphore_wait(barrier, 3 + len(others) + flow.role)


def stripe(ref, z, core, tp, piece):
    start = pl.multiple_of((core * 2 + tp) * piece, piece)
    return ref.at[z, pl.ds(start, piece)]


class Gather(Flow):
    @staticmethod
    def setup(k, name, rows, out=False, inside=False):
        piece, width = rows.shape
        if inside:
            k.mem(name + "_x", rows.shape, rows.dtype)
        else:
            k.inp(name + "_x", rows)
        (k.out if out else k.mem)(name, (4, 4 * piece, width), rows.dtype)
        k.sem(name + "_own")
        k.sem(name + "_zs", 6)
        for s in ("_zr", "_xs", "_xr"):
            k.sem(name + s, 4)
        k.sem(name + "_cs", 4, 2)
        k.sem(name + "_cr", 4, 2)

    def __init__(self, r, name):
        super().__init__()
        self.x, self.buf = getattr(r, name + "_x"), getattr(r, name)
        self.own_sem, self.zs, self.zr, self.xs, self.xr, self.cs, self.cr = (
            getattr(r, name + s) for s in ("_own", "_zs", "_zr", "_xs", "_xr", "_cs", "_cr")
        )
        self.piece = self.x.shape[0]

    def block(self, z, core, tp):
        return stripe(self.buf, z, core, tp, self.piece)

    def start(self):
        own = self.block(self.iz, self.ic, self.it)
        self.push(self.x, own, self.zs.at[1], self.zr.at[1], self.near)
        self.push_inner(self.x, own, self.zs.at[2], self.zr.at[2], self.mid)
        self.push(self.x, own, self.xs.at[0], self.xr.at[0], self.across)
        self.push(self.x, own, self.cs.at[0, 0], self.cr.at[0, 0], self.beside)
        self.local = pltpu.make_async_copy(self.x, own, self.own_sem)
        self.local.start()

    def from_across(self, s):
        block = self.block(self.line(s), self.ic, 1 - self.it)
        self.arrived(block, self.xr.at[s])
        self.push(block, block, self.cs.at[s, 1], self.cr.at[s, 1], self.beside)

    def advance(self, s):
        if s < 4:
            block = self.block(self.line(s), self.ic, self.it)
            self.arrived(block, self.zr.at[s])
            self.pass_on(s, block, self.zs, self.zr)
            self.push(block, block, self.xs.at[s], self.xr.at[s], self.across)
            self.push(block, block, self.cs.at[s, 0], self.cr.at[s, 0], self.beside)
        self.from_across(s - 1)

    def ready(self, s):
        if s == 0:
            self.local.wait()
        for half in range(2):
            side = self.it if half == 0 else 1 - self.it
            self.arrived(self.block(self.line(s), 1 - self.ic, side), self.cr.at[s, half])


class Scatter(Flow):
    @staticmethod
    def setup(k, name, piece, width, partial=None):
        if partial is None:
            k.mem(name + "_p", (4, 4 * piece, width), BF)
        else:
            k.inp(name + "_p", partial)
            k.mem(name + "_m", (4, 2 * piece, width), BF)
            k.sem(name + "_ls", 4)
        k.mem(name + "_c", (4, 2 * piece, width), BF)
        for s in ("_xo", "_xi", "_zo"):
            k.mem(name + s, (4, piece, width), BF)
        k.mem(name + "_zi", (6, piece, width), BF)
        for s in ("_cs", "_cr", "_xs", "_xr", "_zs"):
            k.sem(name + s, 4)
        k.sem(name + "_zr", 6)

    def __init__(self, r, name, out):
        super().__init__()
        self.out = out
        self.p, self.c, self.xo, self.xi, self.zo, self.zi = (
            getattr(r, name + s) for s in ("_p", "_c", "_xo", "_xi", "_zo", "_zi")
        )
        self.cs, self.cr, self.xs, self.xr, self.zs, self.zr = (
            getattr(r, name + s) for s in ("_cs", "_cr", "_xs", "_xr", "_zs", "_zr")
        )
        self.m, self.ls = getattr(r, name + "_m", None), getattr(r, name + "_ls", None)
        self.piece = self.xo.shape[1]
        self.core_copy, self.across_copy, self.loads = {}, {}, {}

    def rows(self, core):
        return pl.ds(pl.multiple_of(core * 2 * self.piece, 2 * self.piece), 2 * self.piece)

    def begin(self, s):
        part = s if self.m is None else self.line(s)
        self.core_copy[s] = self.push(
            self.p.at[part, self.rows(1 - self.ic)],
            self.c.at[s],
            self.cs.at[s],
            self.cr.at[s],
            self.beside,
        )
        if self.m is not None:
            self.loads[s] = pltpu.make_async_copy(
                self.p.at[part, self.rows(self.ic)], self.m.at[s], self.ls.at[s]
            )
            self.loads[s].start()

    def add(self, s, side):
        rows = pl.ds(pl.multiple_of(side * self.piece, self.piece), self.piece)
        if self.m is not None:
            own = self.m[s, rows]
        else:
            start = pl.multiple_of((self.ic * 2 + side) * self.piece, self.piece)
            own = self.p[s, pl.ds(start, self.piece)]
        return own.astype(F32) + self.c[s, rows].astype(F32)

    def cross(self, s):
        if s in self.loads:
            self.loads[s].wait()
        self.core_copy[s].wait_recv()
        self.xo[s] = self.add(s, 1 - self.it).astype(BF)
        self.across_copy[s] = self.push(
            self.xo.at[s], self.xi.at[s], self.xs.at[s], self.xr.at[s], self.across
        )

    def leave(self, s):
        self.across_copy[s].wait_recv()

        def value():
            return self.add(s, self.it) + self.xi[s].astype(F32)

        if s == 0:
            self.out[...] = value()
            return
        came = (None, 4, 2, 3)[s]

        @pl.when(self.inner)
        def _():
            self.arrived(self.zi.at[came], self.zr.at[came])
            self.zo[s] = (value() + self.zi[came].astype(F32)).astype(BF)

        @pl.when(self.role == 0)
        def _():
            self.zo[s] = value().astype(BF)

        place = s + self.role * (None, -1, 3, 1)[s]
        partner = self.near["z"]
        if s > 1:
            partner = partner + self.role * (self.mid["z"] - partner)
        self.push(
            self.zo.at[s], self.zi.at[place], self.zs.at[s], self.zr.at[place], {"z": partner}
        )

    def end(self):
        @pl.when(self.inner)
        def _():
            for place in (1, 5):
                self.arrived(self.zi.at[place], self.zr.at[place])
                self.out[...] += self.zi[place].astype(F32)

        @pl.when(self.role == 0)
        def _():
            self.arrived(self.zi.at[0], self.zr.at[0])
            self.out[...] += self.zi[0].astype(F32)


class Total(Flow):
    @staticmethod
    def setup(k, name, shape, axes):
        for axis in axes:
            size = lax.axis_size(axis)
            k.mem(f"{name}_{axis}", (size, *shape), F32)
            k.sem(f"{name}_{axis}_s", size)
            k.sem(f"{name}_{axis}_r", size)

    def __init__(self, r, name):
        super().__init__()
        self.r, self.name = r, name

    def send(self, axis, value):
        slots, ss, rs = (getattr(self.r, f"{self.name}_{axis}{s}") for s in ("", "_s", "_r"))
        me = lax.axis_index(axis)
        slots[me] = value
        self.copies = [
            self.push(slots.at[me], slots.at[me], ss.at[d], rs.at[d], {axis: flip(axis, d)})
            for d in range(1, lax.axis_size(axis))
        ]
        self.slots = slots

    def receive(self):
        for copy in self.copies:
            copy.wait_recv()
        value = self.slots[0]
        for n in range(1, self.slots.shape[0]):
            value = value + self.slots[n]
        return value


class Outlet(Flow):
    @staticmethod
    def setup(k, name, grads, nz, inside=False):
        for n, grad in enumerate(grads):
            rows, cols = grad.shape[-2:]
            if inside:
                k.mem(f"{name}_g{n}", grad.shape, BF)
            else:
                k.inp(f"{name}_g{n}", grad)
            k.out(f"{name}_o{n}", (rows, 2 * nz * cols), BF)
            if grad.ndim == 3:
                continue
            for s in ("yin", "zout") if inside else ("yin", "zout", "own"):
                k.mem(f"{name}_{s}{n}", (nz, rows, cols), BF)
        for s in ("ls", "ys", "yr", "zs", "zr", "cs", "cr"):
            k.sem(f"{name}_{s}", len(grads), nz)
        k.sem(f"{name}_os", len(grads))

    def __init__(self, r, name, count, nz):
        super().__init__()
        self.nz, self.count = nz, count
        self.g, self.o, self.own, self.yin, self.zout = (
            [getattr(r, f"{name}_{s}{n}", None) for n in range(count)]
            for s in ("g", "o", "own", "yin", "zout")
        )
        self.ls, self.ys, self.yr, self.zs, self.zr, self.cs, self.cr, self.os = (
            getattr(r, f"{name}_{s}") for s in ("ls", "ys", "yr", "zs", "zr", "cs", "cr", "os")
        )
        self.loads, self.pairs, self.stores = {}, {}, []

    def slot(self, k, z, core):
        return columns(self.o[k], z * 2 + core, self.g[k].shape[-1])

    def start(self, k):
        if self.zout[k] is None:
            return
        for d in range(self.nz - 1, -1, -1):
            target = self.at(d)
            self.pairs[k, d] = self.push(
                self.g[k].at[target, 1 - self.iy],
                self.yin[k].at[d],
                self.ys.at[k, d],
                self.yr.at[k, d],
                self.behind,
            )
            if self.own[k] is not None:
                self.loads[k, d] = pltpu.make_async_copy(
                    self.g[k].at[target, self.iy], self.own[k].at[d], self.ls.at[k, d]
                )
                self.loads[k, d].start()

    def combine(self, k, blocks=(3, 2, 1, 0)):
        mine = self.slot(k, self.iz, self.ic)
        for d in blocks:
            if self.zout[k] is None:
                src = self.g[k].at[d]
            else:
                self.pairs[k, d].wait_recv()
                if self.own[k] is not None:
                    self.loads[k, d].wait()
                    own = self.own[k][d]
                else:
                    own = self.g[k][self.at(d), self.iy]
                self.zout[k][d] = (own.astype(F32) + self.yin[k][d].astype(F32)).astype(BF)
                src = self.zout[k].at[d]
            if d:
                self.push(src, mine, self.zs.at[k, d], self.zr.at[k, d], {"z": self.at(d)})
            else:
                self.push(src, mine, self.cs.at[k, d], self.cr.at[k, d], self.beside)
                store = pltpu.make_async_copy(src, mine, self.os.at[k])
                store.start()
                self.stores.append(store)

    def relay(self, k):
        for d in range(1, self.nz):
            block = self.slot(k, self.at(d), self.ic)
            self.arrived(block, self.zr.at[k, d])
            self.push(block, block, self.cs.at[k, d], self.cr.at[k, d], self.beside)

    def end(self):
        for k in range(self.count):
            for d in range(self.nz):
                self.arrived(self.slot(k, self.at(d), 1 - self.ic), self.cr.at[k, d])
        for store in self.stores:
            store.wait()
        self.finish()


def gather_line(rows):
    k = Kernel()
    Gather.setup(k, "all", rows, out=True)

    def body(r):
        greet_line()
        gather = Gather(r, "all")
        gather.start()
        for s in range(1, 5):
            gather.advance(s)
        for s in range(4):
            gather.ready(s)
        gather.finish()

    return k.run(1, body, 16)["all"].reshape(-1, rows.shape[1])


def scatter_line(partial):
    width = partial.shape[1]
    piece = partial.shape[0] // 16
    k = Kernel()
    Scatter.setup(k, "rs", piece, width, partial.astype(BF).reshape(4, 4 * piece, width))
    k.out("sum", (piece, width), F32, pltpu.VMEM)

    def body(r):
        greet_line()
        scatter = Scatter(r, "rs", r.sum)
        order = (3, 2, 1, 0)
        for s in order:
            scatter.begin(s)
        for s in order:
            scatter.cross(s)
        for s in order:
            scatter.leave(s)
        scatter.end()
        scatter.finish()

    return k.run(2, body, 32)["sum"]


def exact(a, b, dims):
    return lax.dot_general(
        a, b, (dims, ((), ())), precision=lax.Precision.HIGHEST, preferred_element_type=F32
    )


def picker(width):
    row = lax.broadcasted_iota(jnp.int32, (8, width), 0)
    part = lax.broadcasted_iota(jnp.int32, (8, width), 1) // HD
    return jnp.where(row == part, 1.0, 0.0).astype(F32)


def row_sums(first, second):
    both = jnp.concatenate([first, second], axis=1)
    return exact(picker(2 * HD), both, ((1,), (1,)))


def spread(sums, which):
    row = lax.broadcasted_iota(jnp.int32, (8, HD), 0)
    one = jnp.where(row == which, 1.0, 0.0).astype(F32)
    return exact(sums, one, ((0,), (0,)))


def softmax_rows(query, key, length):
    count = query.shape[0]
    row = lax.broadcasted_iota(jnp.int32, (count, count), 0)
    col = lax.broadcasted_iota(jnp.int32, (count, count), 1)
    scores = mm_nt(query, key) * (1.0 / math.sqrt(HD))
    scores = jnp.where((col <= row) & (col < length), scores, NEGATIVE)
    exponent = jnp.exp(scores - jnp.max(scores, axis=-1, keepdims=True))
    return exponent / jnp.sum(exponent, axis=-1, keepdims=True)


def weight_blocks(left, right, place):
    nz, parts = left.shape[0], 2 * left.shape[0]
    block, share = left.shape[2] // parts, right.shape[2] // len(place)

    @pl.loop(0, parts)
    def _(f):
        cols = pl.ds(pl.multiple_of(f * block, block), block)
        made = mm_tn(left[0, :, cols], right[0])
        for z in range(1, nz):
            made = made + mm_tn(left[z, :, cols], right[z])
        made = made.astype(BF)
        for n, grad in enumerate(place):
            grad[f // 2, lax.rem(f, 2)] = made[:, n * share : (n + 1) * share]


def scatter_back(partial, left, right):
    width, cols = partial.shape[1], right[0].shape[1]
    piece, rows = partial.shape[0] // 16, width // 8
    k = Kernel()
    Scatter.setup(k, "rs", piece, width, partial.astype(BF).reshape(4, 4 * piece, width))
    k.out("sum", (piece, width), F32, pltpu.VMEM)
    for n, array in enumerate((*left, *right)):
        array = array.reshape(4, 4 * piece, -1)
        k.inp(f"i{n}", array)
        k.mem(f"m{n}", array.shape, BF)
    for n in range(3):
        k.mem(f"g{n}", (4, 2, rows, cols), BF)
        k.out(f"o{n}", (4, 2, rows, cols) if n else (4, rows, cols), BF)
    k.mem("yin", (4, rows, cols), BF)
    k.mem("total", (4, rows, cols), BF)
    k.sem("ld", 5)
    for s in ("ys", "yr"):
        k.sem(s, 4)
    k.sem("os", 3)

    def body(r):
        flow, scatter = Flow(), Scatter(r, "rs", r.sum)
        greet_line((flow.behind,))
        order = (3, 2, 1, 0)
        for s in order:
            scatter.begin(s)
        loads = load_all(
            [(getattr(r, f"i{n}"), getattr(r, f"m{n}")) for n in (0, 2, 1, 3, 4)], r.ld
        )
        for s in order:
            scatter.cross(s)
        for n in (0, 1):
            loads[n].wait()
        weight_blocks(r.m0, r.m2, [r.g0])
        pairs = {}
        for d in order:
            pairs[d] = flow.push(
                r.g0.at[flow.at(d), 1 - flow.iy], r.yin.at[d], r.ys.at[d], r.yr.at[d], flow.behind
            )
        scatter.leave(3)
        stores = []

        def store(n, src, out):
            stores.append(pltpu.make_async_copy(src, out, r.os.at[n]))
            stores[-1].start()

        for n in (2, 3):
            loads[n].wait()
        weight_blocks(r.m1, r.m3, [r.g1])
        store(1, r.g1, r.o1)
        scatter.leave(2)
        loads[4].wait()
        weight_blocks(r.m1, r.m4, [r.g2])
        store(2, r.g2, r.o2)
        scatter.leave(1)
        scatter.leave(0)
        scatter.end()
        for d in order:
            pairs[d].wait_recv()
            own = r.g0[flow.at(d), flow.iy].astype(F32)
            r.total[d] = (own + r.yin[d].astype(F32)).astype(BF)
        store(0, r.total, r.o0)
        for f in (flow, scatter):
            f.finish()
        for copy in stores:
            copy.wait()

    got = k.run(3, body, 60)
    return got["sum"], [got[f"o{n}"] for n in range(3)]


def load_all(pairs, sems):
    copies = []
    for n, (src, dst) in enumerate(pairs):
        copy = pltpu.make_async_copy(src, dst, sems.at[n])
        copy.start()
        copies.append(copy)
    return copies


def attention_back(
    branch, wide, wo, wqkv, saved, tokens_all, residual_grad, stream_rows, terms, gains, tables,
    seq_lengths,
):
    nz = lax.axis_size("z")
    piece, width = branch.shape
    rows = 4 * piece
    padded = jnp.pad(terms, (0, -terms.shape[0] % 1024)).reshape(-1, 128)
    lanes = width // 128
    sum_axes = (CORE, TP, "y", "z")
    k = Kernel()
    Gather.setup(k, "ball", branch)
    Outlet.setup(k, "wide", wide, nz)
    slim = [jax.ShapeDtypeStruct((nz, 2, width // (2 * nz), HD), BF)] * 4
    Outlet.setup(k, "slim", slim, nz, inside=True)
    Scatter.setup(k, "rs", piece, width)
    Total.setup(k, "tot", (nz, 8, rows), (CORE, TP, "z"))
    Total.setup(k, "sum", padded.shape, sum_axes)
    k.inp("wo", wo)
    k.inp("wqkv", wqkv)
    k.inp("tokens", tokens_all)
    k.mem("tokens_m", tokens_all.shape, BF)
    names = ("q", "k", "v", "att", "nq", "nk", "qs", "ks")
    for name, array in zip(names, saved):
        k.inp(name, array)
        k.mem(name + "_m", array.shape, array.dtype)
    k.mem("wo_m", wo.shape, BF)
    k.mem("wqkv_m", wqkv.shape, BF)
    k.inp("res", residual_grad)
    k.mem("res_m", (piece, width), F32)
    k.inp("stream", stream_rows)
    k.mem("stream_m", (piece, width), BF)
    k.sem("ld", len(names) + 5)
    k.inp("terms", padded, pltpu.VMEM)
    k.mem("terms_m", padded.shape, F32)
    k.out("terms_out", padded.shape, F32, pltpu.VMEM)
    k.inp("gains", gains, pltpu.VMEM)
    k.inp("tables", tables, pltpu.VMEM)
    k.inp("lens", seq_lengths, pltpu.SMEM)
    k.mem("wqk", (nz, 2, rows, HD), F32)
    k.mem("low", (nz, rows, 3 * HD), BF)
    k.mem("dots", (nz, 8, rows), F32)
    k.mem("norms", (2, HD), F32)
    k.mem("grad", (piece, width), F32)
    k.mem("tail", (piece, width), BF)
    k.out("grad_out", (2, piece, width), BF)
    k.out("stream_out", (2, piece, width), BF)
    k.sem("xs", 2)
    k.sem("xr", 2)
    k.sem("ss", 2)

    def body(r):
        greet(partners_of(("z", "y", TP, CORE)))
        gather, outlet_flow = Gather(r, "ball"), Outlet(r, "wide", len(wide), nz)
        slim_flow, own = Outlet(r, "slim", len(slim), nz), Flow()
        scatter, total_flow = Scatter(r, "rs", r.grad), Total(r, "tot")
        sum_flow = Total(r, "sum")
        gather.start()
        for n in range(len(wide)):
            outlet_flow.start(n)
        names_in = ("wo", "wqkv", *names, "tokens", "res", "stream")
        loads = load_all([(getattr(r, n), getattr(r, n + "_m")) for n in names_in], r.ld)
        scale = 1.0 / math.sqrt(HD)
        cosine, sine = r.tables[0], r.tables[1]
        gather.advance(1)
        outlet_flow.combine(0, (3,))
        for copy in loads:
            copy.wait()
        r.norms[...] = jnp.zeros_like(r.norms)

        def compute(z):
            grad_low = mm(r.ball[z], r.wo_m[...]).astype(BF)
            query, key, value = r.q_m[z], r.k_m[z], r.v_m[z]
            probability = softmax_rows(query, key, r.lens[z])
            grad_prob = mm_nt(grad_low, value)
            row_dots = jnp.sum(probability * grad_prob, axis=-1, keepdims=True)
            grad_scores = (probability * (grad_prob - row_dots)).astype(BF)
            grad_q = rotate_back(mm(grad_scores, key) * scale, cosine, sine)
            grad_k = rotate_back(mm_tn(grad_scores, query) * scale, cosine, sine)
            grad_v = mm_tn(probability.astype(BF), grad_low)
            r.low[z, :, 2 * HD :] = grad_v.astype(BF)
            nq, nk = r.nq_m[z], r.nk_m[z]
            r.norms[0:1] += jnp.sum(grad_q * nq, axis=0, keepdims=True)
            r.norms[1:2] += jnp.sum(grad_k * nk, axis=0, keepdims=True)
            wq, wk = grad_q * r.gains[0:1], grad_k * r.gains[1:2]
            r.wqk[z, 0] = wq
            r.wqk[z, 1] = wk
            r.dots[z] = row_sums(wq * nq, wk * nk)

        for d in range(nz):
            gather.ready(d)
            compute(gather.line(d))
            if d + 2 <= nz:
                gather.advance(d + 2)
            if d == 0:
                outlet_flow.combine(0, (2,))
                own.push(
                    r.stream, r.stream_out.at[own.it], r.xs.at[0], r.xr.at[0], own.across
                )
            if d == 1:
                outlet_flow.combine(0, (1, 0))
        r.terms_m[...] = r.terms[...]
        slot = 2 * lanes + own.it * (lanes // 2) + own.iz * 2 + own.ic
        for n in range(2):
            r.terms_m[pl.ds(slot + n * lanes, 1)] = r.norms[n : n + 1]
        total_flow.send(CORE, r.dots[...])
        sum_flow.send(CORE, r.terms_m[...])
        value, other = total_flow.receive(), sum_flow.receive()
        total_flow.send(TP, value)
        sum_flow.send(TP, other)
        value, other = total_flow.receive(), sum_flow.receive()
        total_flow.send("z", value)
        sum_flow.send("y", other)
        outlet_flow.combine(1)
        weight_blocks(r.ball, r.att_m, [slim_flow.g[3]])
        slim_flow.start(3)
        r.dots[...] = total_flow.receive()
        order = list(range(nz - 1, -1, -1))
        for n, d in enumerate(order):
            z = gather.line(d)
            sums = r.dots[z] * (1.0 / width)
            for j, (normed, factor) in enumerate(((r.nq_m, r.qs_m), (r.nk_m, r.ks_m))):
                low = factor[z] * (r.wqk[z, j] - normed[z] * spread(sums, j))
                r.low[z, :, j * HD : (j + 1) * HD] = low.astype(BF)
            r.rs_p[d] = mm_nt(r.low[z], r.wqkv_m[...]).astype(BF)
            scatter.begin(d)
            if n:
                scatter.cross(order[n - 1])
        scatter.cross(0)
        outlet_flow.combine(2, (3,))
        scatter.leave(3)
        weight_blocks(r.tokens_m, r.low, slim_flow.g[:3])
        for n in range(3):
            slim_flow.start(n)
        scatter.leave(2)
        outlet_flow.combine(2, (2,))
        slim_flow.combine(3)
        scatter.leave(1)
        outlet_flow.combine(2, (1, 0))
        scatter.leave(0)
        sum_flow.send("z", sum_flow.receive())
        for n in range(3):
            slim_flow.combine(n)
        outlet_flow.relay(0)
        outlet_flow.relay(1)
        scatter.end()
        r.tail[...] = (r.res_m[...] + r.grad[...]).astype(BF)
        own.push(r.tail, r.grad_out.at[own.it], r.xs.at[1], r.xr.at[1], own.across)
        stores = []
        for n, (src, out) in enumerate(((r.stream_m, r.stream_out), (r.tail, r.grad_out))):
            stores.append(pltpu.make_async_copy(src, out.at[own.it], r.ss.at[n]))
            stores[-1].start()
        r.terms_out[...] = sum_flow.receive()
        outlet_flow.relay(2)
        slim_flow.relay(3)
        for n in range(3):
            slim_flow.relay(n)
        outlet_flow.end()
        slim_flow.end()
        for n, out in enumerate((r.stream_out, r.grad_out)):
            own.arrived(out.at[1 - own.it], r.xr.at[n])
        for flow in (gather, scatter, total_flow, sum_flow, own):
            flow.finish()
        for copy in stores:
            copy.wait()

    got = k.run(7, body, 60)
    return (
        [got[f"slim_o{n}"].astype(F32) for n in range(4)]
        + [got[f"wide_o{n}"].astype(F32) for n in range(len(wide))],
        got["grad_out"].reshape(-1, width).astype(F32),
        got["stream_out"].reshape(-1, width),
        got["terms_out"].reshape(-1)[: terms.shape[0]],
    )


def attention_front(token_rows, weights, gains, tables, seq_lengths, post_attention):
    nz = lax.axis_size("z")
    own_rows, width = token_rows.shape
    piece, rows = own_rows // 2, own_rows * 2
    w_rows = weights[0].shape[0]
    count = len(weights)
    parts = [w.shape[1] // (2 * nz) for w in weights]
    k = Kernel()
    Scatter.setup(k, "rs", piece, width)
    Total.setup(k, "tot", (nz, 8, rows), (CORE, TP, "z"))
    k.inp("tok", token_rows)
    for n, weight in enumerate(weights):
        k.inp(f"w{n}", weight)
    k.inp("gains", gains, pltpu.VMEM)
    k.inp("tables", tables, pltpu.VMEM)
    k.inp("lens", seq_lengths, pltpu.SMEM)
    k.mem("tall", (nz, rows, width), BF)
    k.mem("qkv", (nz, 2, w_rows, 3 * HD), BF)
    k.mem("wo", (nz, 2, w_rows, parts[3]), BF)
    for n in range(4, count):
        k.mem(f"b{n}", (w_rows, parts[n]), BF)
        k.out(f"o{n}", (nz, 2, w_rows, parts[n]), BF)
    k.mem("raw", (nz, rows, 3 * HD), F32)
    k.mem("dots", (nz, 8, rows), F32)
    saved = (("q", BF), ("k", BF), ("v", BF), ("nq", F32), ("nk", F32), ("qs", F32), ("ks", F32), ("att", BF))
    for name, kind in saved:
        k.mem(name + "_m", (nz, rows, HD), kind)
        k.out(name, (nz, rows, HD), kind)
    k.mem("branch", (piece, width), F32)
    k.inp("post", post_attention[None], pltpu.VMEM)
    for name in ("normed", "residual"):
        k.out(name, (piece, width), F32, pltpu.VMEM)
    k.out("scale", (piece, 128), F32, pltpu.VMEM)
    Gather.setup(k, "all", jax.ShapeDtypeStruct((piece, width), BF), inside=True)
    k.out("wide", (nz, rows, width), BF)
    k.out("tokens", (nz, rows, width), BF)
    k.out("qkv_out", (nz, 2, w_rows, 3 * HD), BF)
    k.out("wo_out", (nz, 2, w_rows, parts[3]), BF)
    k.sem("tl")
    k.sem("tzs", 6)
    for s in ("tzr", "txs", "txr"):
        k.sem(s, nz)
    k.sem("tcs", nz, 2)
    k.sem("tcr", nz, 2)
    k.sem("wl", 2, count)
    for s in ("wzs", "wzr", "wys", "wyr"):
        k.sem(s, count, nz)
    k.sem("st", len(saved) + 2, nz)
    k.sem("sw", 2)

    def body(r):
        greet(partners_of(("z", "y", TP, CORE)))
        flow = Flow()
        iz, iy, ic, it = flow.iz, flow.iy, flow.ic, flow.it
        scatter, total_flow = Scatter(r, "rs", r.branch), Total(r, "tot")
        gather = Gather(r, "all")

        def block(z, core, tp):
            return stripe(r.tall, z, core, tp, piece)

        def pair(z, core):
            start = pl.multiple_of(core * own_rows, own_rows)
            return r.tall.at[z, pl.ds(start, own_rows)]

        tok_half = r.tok.at[pl.ds(pl.multiple_of(it * piece, piece), piece)]
        flow.push(tok_half, block(iz, ic, it), r.tzs.at[1], r.tzr.at[1], flow.near)
        flow.push_inner(tok_half, block(iz, ic, it), r.tzs.at[2], r.tzr.at[2], flow.mid)
        flow.push(r.tok, pair(iz, ic), r.tcs.at[0, 0], r.tcr.at[0, 0], flow.beside)
        tok_load = pltpu.make_async_copy(r.tok, pair(iz, ic), r.tl)
        tok_load.start()
        loads = {}

        def landing(n, z, y):
            if n < 3:
                return r.qkv.at[z, y, :, n * HD : (n + 1) * HD]
            return r.wo.at[z, y] if n == 3 else getattr(r, f"o{n}").at[z, y]

        def bring(n, parts_of_z=(3, 2, 1), own_part=True):
            weight = getattr(r, f"w{n}")
            own = columns(weight, iz * 2 + ic, parts[n])
            for d in parts_of_z:
                other = flow.at(d)
                flow.push(
                    columns(weight, other * 2 + ic, parts[n]),
                    landing(n, iz, iy),
                    r.wzs.at[n, d],
                    r.wzr.at[n, d],
                    {"z": other},
                )
            if own_part:
                flow.push(own, landing(n, iz, iy), r.wys.at[n, 0], r.wyr.at[n, 0], flow.behind)
                dst = landing(n, iz, iy) if n < 4 else getattr(r, f"b{n}")
                loads[n] = pltpu.make_async_copy(own, dst, r.wl.at[0, n])
                loads[n].start()

        def forward(n, parts_of_z=(3, 2, 1)):
            for d in parts_of_z:
                here = landing(n, flow.at(d), iy)
                flow.arrived(here, r.wzr.at[n, d])
                flow.push(here, here, r.wys.at[n, d], r.wyr.at[n, d], flow.behind)

        def keep(n):
            loads[n].wait()
            copy = pltpu.make_async_copy(getattr(r, f"b{n}"), landing(n, iz, iy), r.wl.at[1, n])
            copy.start()
            stores.append(copy)

        def complete(n):
            for d in range(nz):
                flow.arrived(landing(n, flow.at(d), 1 - iy), r.wyr.at[n, d])

        bring(0)
        for d in range(1, nz):
            here = block(flow.line(d), ic, it)
            flow.arrived(here, r.tzr.at[d])
            flow.pass_on(d, here, r.tzs, r.tzr)
            flow.push(here, here, r.txs.at[d], r.txr.at[d], flow.across)
            flow.push(here, here, r.tcs.at[d, 0], r.tcr.at[d, 0], flow.beside)
            bring(d)
        bring(4)
        for d in range(1, nz):
            forward(d - 1)
            here = block(flow.line(d), ic, 1 - it)
            flow.arrived(here, r.txr.at[d])
            flow.push(here, here, r.tcs.at[d, 1], r.tcr.at[d, 1], flow.beside)
        stores = []

        def save(n, src, dst, d):
            copy = pltpu.make_async_copy(src, dst, r.st.at[n, d])
            copy.start()
            stores.append(copy)

        for n in range(4):
            loads[n].wait()
        for n in range(3):
            complete(n)
        tok_load.wait()
        for d in range(nz):
            z = flow.line(d)
            if d == 0:
                flow.arrived(pair(iz, 1 - ic), r.tcr.at[0, 0])
            else:
                for half in range(2):
                    side = it if half == 0 else 1 - it
                    flow.arrived(block(z, 1 - ic, side), r.tcr.at[d, half])
            save(0, r.tall.at[z], r.tokens.at[z], d)
            raw = mm(r.tall[z], r.qkv[...].reshape(2 * nz * w_rows, 3 * HD))
            r.raw[z] = raw
            query, key = raw[:, :HD], raw[:, HD : 2 * HD]
            r.dots[z] = row_sums(query * query, key * key)
        total_flow.send(CORE, r.dots[...])
        forward(3)
        value = total_flow.receive()
        total_flow.send(TP, value)
        value = total_flow.receive()
        total_flow.send("z", value)
        bring(5)
        bring(6)
        for n in (4, 5):
            keep(n)
        complete(3)
        for n, (src, dst) in enumerate(((r.qkv, r.qkv_out), (r.wo, r.wo_out))):
            copy = pltpu.make_async_copy(src, dst, r.sw.at[n])
            copy.start()
            stores.append(copy)
        r.dots[...] = lax.rsqrt(total_flow.receive() * (1.0 / width) + EPSILON)
        cosine, sine = r.tables[0], r.tables[1]
        order = list(range(nz - 1, -1, -1))
        for n, d in enumerate(order):
            z = flow.line(d)
            sums = r.dots[z]
            r.qs_m[z] = spread(sums, 0)
            r.ks_m[z] = spread(sums, 1)
            r.nq_m[z] = r.raw[z, :, :HD] * r.qs_m[z]
            r.nk_m[z] = r.raw[z, :, HD : 2 * HD] * r.ks_m[z]
            query = rotate(r.nq_m[z] * r.gains[0:1], cosine, sine).astype(BF)
            key = rotate(r.nk_m[z] * r.gains[1:2], cosine, sine).astype(BF)
            value = r.raw[z, :, 2 * HD :].astype(BF)
            r.q_m[z] = query
            r.k_m[z] = key
            r.v_m[z] = value
            probability = softmax_rows(query, key, r.lens[z]).astype(BF)
            r.att_m[z] = mm(probability, value).astype(BF)
            for m, (name, _) in enumerate(saved):
                save(m + 1, getattr(r, name + "_m").at[z], getattr(r, name).at[z], d)
            wo = r.wo[...].reshape(2 * nz * w_rows, parts[3])
            r.rs_p[d] = mm_nt(r.att_m[z], wo).astype(BF)
            scatter.begin(d)
            if n:
                scatter.cross(order[n - 1])
            if n > 1:
                scatter.leave(order[n - 2])
            if n == 0:
                forward(4)
        scatter.cross(0)
        forward(5, (3, 2))
        scatter.leave(1)
        scatter.leave(0)
        forward(5, (1,))
        scatter.end()
        branch = r.branch[...]
        scale = lax.rsqrt(jnp.mean(branch * branch, axis=-1, keepdims=True) + EPSILON)
        r.normed[...] = branch * scale
        r.scale[...] = jnp.broadcast_to(scale, r.scale.shape)
        start = pl.multiple_of((ic * 2 + it) * piece, piece)
        mine = r.tall[iz, pl.ds(start, piece)].astype(F32)
        r.residual[...] = mine + r.normed[...] * r.post[...]
        r.all_x[...] = r.residual[...].astype(BF)
        gather.start()
        forward(6, (3,))
        gather.advance(1)
        forward(6, (2,))
        gather.advance(2)
        forward(6, (1,))
        gather.advance(3)
        gather.advance(4)
        keep(6)
        for d in range(nz):
            gather.ready(d)
            z = gather.line(d)
            save(len(saved) + 1, gather.buf.at[z], r.wide.at[z], d)
        for n in range(4, count):
            complete(n)
        for f in (flow, scatter, total_flow, gather):
            f.finish()
        for copy in stores:
            copy.wait()

    return k.run(9, body, 60)


def local(
    tokens,
    lengths,
    weight_query,
    weight_key,
    weight_value,
    weight_out,
    weight_gate,
    weight_up,
    weight_down,
    post_attention,
    post_feedforward,
    query_norm,
    key_norm,
    cotangent,
):
    nz, ny, nch, ntp = (lax.axis_size(a) for a in ("z", "y", "ch", TP))
    iz, iy, ich, icore, itp = (lax.axis_index(a) for a in AXES)
    token_rows = tokens[0]
    own_rows, width = token_rows.shape
    piece = own_rows // ntp
    seq_rows = own_rows * 2
    total_rows = seq_rows * nz
    scale_factor = 1.0 / math.sqrt(HD)
    own_head = iz * 2 + icore
    qn = lax.dynamic_slice_in_dim(query_norm, own_head * HD, HD)
    kn = lax.dynamic_slice_in_dim(key_norm, own_head * HD, HD)
    seq_lengths = lax.dynamic_index_in_dim(lengths.reshape(nz, ny), iy, 1, keepdims=False)
    positions = ich * seq_rows + jnp.arange(seq_rows, dtype=jnp.int32)
    key_positions = jnp.arange(seq_rows * nch, dtype=jnp.int32)
    cosine, sine_table = rope_tables(positions)
    allowed = (key_positions[None, None, :] <= positions[None, :, None]) & (
        key_positions[None, None, :] < seq_lengths[:, None, None]
    )
    my_tokens = lax.dynamic_slice_in_dim(token_rows, itp * piece, piece, 0)
    my_cot = lax.dynamic_slice_in_dim(cotangent[0], itp * piece, piece, 0)
    my_pos = (ich * 2 + icore) * own_rows + itp * piece + jnp.arange(piece, dtype=jnp.int32)
    my_valid = (my_pos < lengths[iz * ny + iy]).astype(F32)[:, None]

    weights = (
        weight_query,
        weight_key,
        weight_value,
        weight_out,
        weight_gate,
        weight_up,
        weight_down,
    )
    fused = nch == 1 and nz == 4
    gather, scatter = (gather_line, scatter_line) if fused else (gather_rows, scatter_rows)
    by_seq = lambda a: a.reshape(nz, seq_rows, HD)
    gains, tables = jnp.stack([qn, kn]), jnp.stack([cosine, sine_table])
    if fused:
        front = attention_front(
            token_rows, weights, gains, tables, seq_lengths, post_attention
        )
        wg, wu, wd = (front[f"o{n}"].reshape(width, -1) for n in (4, 5, 6))
    else:
        tokens_all, (wq, wk, wv, wo, wg, wu, wd) = intake(token_rows, weights)
        query_raw = mm(tokens_all, wq)
        key_raw = mm(tokens_all, wk)
        value_raw = mm(tokens_all, wv)
        squares = head_total(
            jnp.stack([jnp.sum(query_raw * query_raw, axis=-1), jnp.sum(key_raw * key_raw, axis=-1)])
        )
        scales = lax.rsqrt(squares / width + EPSILON)
        query_scale = scales[0][:, None]
        key_scale = scales[1][:, None]
        queries = rotate(by_seq(query_raw * query_scale * qn), cosine, sine_table).astype(BF)
        keys = rotate(by_seq(key_raw * key_scale * kn), cosine, sine_table).astype(BF)
        values = by_seq(value_raw).astype(BF)
        if nch > 1:
            keys_full = lax.all_gather(keys, "ch", axis=1, tiled=True)
            values_full = lax.all_gather(values, "ch", axis=1, tiled=True)
        else:
            keys_full, values_full = keys, values
        scores = (
            jnp.einsum(SCORE, queries, keys_full, preferred_element_type=F32) * scale_factor
        )
        scores = jnp.where(allowed, scores, NEGATIVE)
        exponent = jnp.exp(scores - jnp.max(scores, axis=-1, keepdims=True))
        probability = exponent / jnp.sum(exponent, axis=-1, keepdims=True)
        probability_low = probability.astype(BF)
        attended = jnp.einsum(APPLY, probability_low, values_full, preferred_element_type=F32)
        attended_low = attended.reshape(total_rows, HD).astype(BF)
        branch_sum = scatter_rows(mm_nt(attended_low, wo))
    if fused:
        attn_normed, residual = front["normed"], front["residual"]
        attn_scale = front["scale"][:, :1]
        residual_all = front["wide"].reshape(-1, width)
    else:
        attn_scale = lax.rsqrt(jnp.mean(branch_sum * branch_sum, axis=-1, keepdims=True) + EPSILON)
        attn_normed = branch_sum * attn_scale
        residual = my_tokens.astype(F32) + attn_normed * post_attention
        residual_all = gather(residual.astype(BF))
    attention_branch = attn_normed * post_attention
    gate_value = mm(residual_all, wg)
    up_value = mm(residual_all, wu)
    sigmoid_gate = jax.nn.sigmoid(gate_value)
    silu_gate = gate_value * sigmoid_gate
    mixed_low = (silu_gate * up_value).astype(BF)
    down_sum = scatter(mm_nt(mixed_low, wd))
    ffn_scale = lax.rsqrt(jnp.mean(down_sum * down_sum, axis=-1, keepdims=True) + EPSILON)
    ffn_normed = down_sum * ffn_scale
    feedforward_branch = ffn_normed * post_feedforward
    stream = residual + feedforward_branch
    stat_terms = jnp.stack(
        [
            jnp.sum(my_valid * stream * stream),
            jnp.sum(my_valid * attention_branch * attention_branch),
            jnp.sum(my_valid * feedforward_branch * feedforward_branch),
        ]
    )
    grad_stream = my_cot * my_valid
    grad_post_ff = jnp.sum(grad_stream * ffn_normed, axis=0)
    scaled = grad_stream * post_feedforward
    grad_down_sum = ffn_scale * (
        scaled - ffn_normed * jnp.mean(scaled * ffn_normed, axis=-1, keepdims=True)
    )
    down_all = gather(grad_down_sum.astype(BF))
    grad_mixed = mm(down_all, wd)
    gate_low = (
        grad_mixed * up_value * sigmoid_gate * (1.0 + gate_value * (1.0 - sigmoid_gate))
    ).astype(BF)
    up_low = (grad_mixed * silu_gate).astype(BF)
    partial = mm_nt(gate_low, wg) + mm_nt(up_low, wu)
    if fused:
        back, wide_grads = scatter_back(
            partial, (down_all, residual_all), (mixed_low, gate_low, up_low)
        )
    else:
        grad_wg = mm_tn(residual_all, gate_low)
        grad_wu = mm_tn(residual_all, up_low)
        grad_wd = mm_tn(down_all, mixed_low)
        back = scatter(partial)
    grad_residual = grad_stream + back
    grad_post_attn = jnp.sum(grad_residual * attn_normed, axis=0)
    scaled_attn = grad_residual * post_attention
    grad_branch = attn_scale * (
        scaled_attn - attn_normed * jnp.mean(scaled_attn * attn_normed, axis=-1, keepdims=True)
    )
    if not fused:
        branch_all = gather_rows(grad_branch.astype(BF))
        grad_att_low = mm(branch_all, wo).astype(BF)
        grad_wo = mm_tn(branch_all, attended_low)
        grad_att = by_seq(grad_att_low)
        grad_prob = jnp.einsum(SCORE, grad_att, values_full, preferred_element_type=F32)
        row_dots = jnp.sum(probability * grad_prob, axis=-1, keepdims=True)
        grad_scores = (probability * (grad_prob - row_dots)).astype(BF)
        grad_queries = (
            jnp.einsum(APPLY, grad_scores, keys_full, preferred_element_type=F32)
            * scale_factor
        )
        grad_keys = (
            jnp.einsum("bts,btd->bsd", grad_scores, queries, preferred_element_type=F32) * scale_factor
        )
        grad_values = jnp.einsum("bts,btd->bsd", probability_low, grad_att, preferred_element_type=F32)
        if nch > 1:
            grad_keys, grad_values = (
                lax.psum_scatter(g.astype(BF), "ch", scatter_dimension=1, tiled=True).astype(F32)
                for g in (grad_keys, grad_values)
            )
        value_grad_low = grad_values.reshape(total_rows, HD).astype(BF)
        grad_q_normed = rotate_back(grad_queries, cosine, sine_table).reshape(total_rows, HD)
        grad_k_normed = rotate_back(grad_keys, cosine, sine_table).reshape(total_rows, HD)
        query_weighted = grad_q_normed * qn
        key_weighted = grad_k_normed * kn
        dots = head_total(
            jnp.stack(
                [
                    jnp.sum(query_weighted * query_raw, axis=-1),
                    jnp.sum(key_weighted * key_raw, axis=-1),
                ]
            )
        )
        query_grad_low = (
            query_scale * (query_weighted - query_raw * query_scale**2 * (dots[0] / width)[:, None])
        ).astype(BF)
        key_grad_low = (
            key_scale * (key_weighted - key_raw * key_scale**2 * (dots[1] / width)[:, None])
        ).astype(BF)
        grad_qnorm = jnp.sum(grad_q_normed * query_raw * query_scale, axis=0)
        grad_knorm = jnp.sum(grad_k_normed * key_raw * key_scale, axis=0)
        grad_wq = mm_tn(tokens_all, query_grad_low)
        grad_wk = mm_tn(tokens_all, key_grad_low)
        grad_wv = mm_tn(tokens_all, value_grad_low)
        grad_rows = grad_residual + scatter_rows(
            mm_nt(query_grad_low, wq) + mm_nt(key_grad_low, wk) + mm_nt(value_grad_low, wv)
        )
    if fused:
        saved = tuple(front[n] for n in ("q", "k", "v", "att", "nq", "nk", "qs", "ks"))
        norms_wide = jnp.zeros((2 * width,), F32)
    else:
        slot = itp * (width // ntp) + own_head * HD
        zero_row = jnp.zeros((width,), F32)
        norms_wide = jnp.concatenate(
            [
                lax.dynamic_update_slice_in_dim(zero_row, grad_qnorm, slot, 0),
                lax.dynamic_update_slice_in_dim(zero_row, grad_knorm, slot, 0),
            ]
        )
    terms = jnp.concatenate([grad_post_attn, grad_post_ff, norms_wide, stat_terms])
    if fused:
        weight_grads, grad_input, output, summed = attention_back(
            grad_branch.astype(BF),
            wide_grads,
            front["wo_out"].reshape(width, -1),
            front["qkv_out"].reshape(width, -1),
            saved,
            front["tokens"],
            grad_residual,
            stream.astype(BF),
            terms,
            gains,
            tables,
            seq_lengths,
        )
        weight_grads = [weight_grads[n] for n in (0, 1, 2, 3, 5, 6, 4)]
    else:
        weight_grads = outlet((grad_wq, grad_wk, grad_wv, grad_wo, grad_wg, grad_wu, grad_wd))
        grad_input = lax.all_gather(grad_rows, TP, axis=0, tiled=True)
        output = lax.all_gather(stream.astype(BF), TP, axis=0, tiled=True)
        summed = all_total(terms)
    half = width // ntp
    qn_sum = lax.dynamic_slice_in_dim(summed, 2 * width + itp * half, half)
    kn_sum = lax.dynamic_slice_in_dim(summed, 3 * width + itp * half, half)
    token_count = jnp.sum(lengths.astype(F32))
    root_means = jnp.sqrt(summed[4 * width :] / (token_count * width))
    return (
        output[None],
        grad_input[None],
        *weight_grads,
        summed[:width],
        summed[width : 2 * width],
        qn_sum,
        kn_sum,
        root_means,
    )


def solution(mesh):
    n_fsdp, n_ctx, n_tp = (mesh.shape[a] for a in ("fsdp", "ctx", TP))
    fine = Mesh(mesh.devices.reshape(n_fsdp // 2, 2, n_ctx // 2, 2, n_tp), AXES)
    fsdp, ctx = ("z", "y"), ("ch", CORE)
    rows = P(fsdp, ctx, None)
    weight = P(fsdp, TP)
    return jax.shard_map(
        local,
        mesh=fine,
        in_specs=(rows, P(), *([weight] * 7), P(), P(), P(TP), P(TP), rows),
        out_specs=(rows, rows, *([weight] * 7), P(), P(), P(TP), P(TP), P()),
        check_vma=False,
    )
```

```python
import functools
import math
import types

import jax
import jax.numpy as jnp
from jax import lax
from jax.experimental import pallas as pl
from jax.experimental.pallas import tpu as pltpu
from jax.sharding import Mesh, PartitionSpec as P

HD = 128
EPSILON = 1e-06
ROPE_BASE = 500000.0
NEGATIVE = -1e30
CORE, TP = "core", "tp"
SCORE = "btd,bsd->bts"
APPLY = "bts,bsd->btd"
AXES = ("z", "y", "ch", CORE, TP)
BF = jnp.bfloat16
F32 = jnp.float32


def rope_tables(positions):
    half_size = HD // 2
    exponent = jnp.arange(half_size, dtype=F32) * (2.0 / HD)
    frequency = jnp.power(ROPE_BASE, -exponent)
    angles = positions.astype(F32)[:, None] * frequency[None, :]
    cosine = jnp.cos(angles)
    sine_table = jnp.sin(angles)
    return (
        jnp.concatenate([cosine, cosine], axis=-1),
        jnp.concatenate([sine_table, sine_table], axis=-1),
    )


def rotate(values, cosine, sine_table):
    half_size = HD // 2
    turned = jnp.concatenate([-values[..., half_size:], values[..., :half_size]], axis=-1)
    return values * cosine + turned * sine_table


def rotate_back(grads_in, cosine, sine_table):
    half_size = HD // 2
    sin_part = grads_in * sine_table
    return grads_in * cosine + jnp.concatenate(
        [sin_part[..., half_size:], -sin_part[..., :half_size]], axis=-1
    )


def dot(former, latter, dims):
    return lax.dot_general(former, latter, (dims, ((), ())), preferred_element_type=F32)


def mm(a, b):
    return dot(a, b, ((1,), (0,)))


def mm_nt(a, b):
    return dot(a, b, ((1,), (1,)))


def mm_tn(a, b):
    return dot(a, b, ((0,), (0,)))


MESH = pl.DeviceIdType.MESH


def flip(axis, bits):
    me = lax.axis_index(axis)
    result, weight = me, 1
    while weight <= bits:
        if (bits // weight) % 2:
            result = result + weight * (1 - 2 * lax.rem(me // weight, 2))
        weight *= 2
    return result


def greet(partners):
    barrier = pltpu.get_barrier_semaphore()
    for partner in partners:
        pl.semaphore_signal(barrier, inc=1, device_id=partner, device_id_type=MESH)
    pl.semaphore_wait(barrier, len(partners))


def remote(src, dst, send_sem, recv_sem, partner):
    return pltpu.make_async_remote_copy(
        src_ref=src,
        dst_ref=dst,
        send_sem=send_sem,
        recv_sem=recv_sem,
        device_id=partner,
        device_id_type=MESH,
    )


def partners_of(axes):
    found = []
    for axis in axes:
        for bits in range(1, lax.axis_size(axis)):
            found.append({axis: flip(axis, bits)})
    return found


def call(kernel, identity, out_shape, in_spaces, out_spaces, scratch, limit, *operands):
    return pl.pallas_call(
        kernel,
        out_shape=out_shape,
        in_specs=[pl.BlockSpec(memory_space=s) for s in in_spaces],
        out_specs=jax.tree.map(lambda s: pl.BlockSpec(memory_space=s), out_spaces),
        scratch_shapes=scratch,
        compiler_params=pltpu.CompilerParams(
            collective_id=identity, has_side_effects=True, vmem_limit_bytes=limit * 2**20
        ),
    )(*operands)


DMA = pltpu.SemaphoreType.DMA


def gather_kernel(nz, x_ref, out_ref, own_sem, zs, zr, xs, xr, cs, cr):
    iz, ic, it = (lax.axis_index(a) for a in ("z", CORE, TP))
    greet(partners_of(("z", TP, CORE)))
    sends = []

    def push(src, where, send_sem, recv_sem, partner):
        copy = remote(src, out_ref.at[where], send_sem, recv_sem, partner)
        copy.start()
        sends.append(copy)

    across, beside = {TP: 1 - it}, {CORE: 1 - ic}
    own = (iz, ic, it)
    for d in range(1, nz):
        push(x_ref, own, zs.at[d], zr.at[d], {"z": flip("z", d)})
    push(x_ref, own, xs.at[0], xr.at[0], across)
    push(x_ref, own, cs.at[0, 0], cr.at[0, 0], beside)
    local_copy = pltpu.make_async_copy(x_ref, out_ref.at[own], own_sem)
    local_copy.start()

    def await_at(where, sem):
        remote(out_ref.at[where], out_ref.at[where], sem, sem, across).wait_recv()

    def from_across(d):
        where = (flip("z", d), ic, 1 - it)
        await_at(where, xr.at[d])
        push(out_ref.at[where], where, cs.at[d, 1], cr.at[d, 1], beside)

    for d in range(1, nz):
        where = (flip("z", d), ic, it)
        await_at(where, zr.at[d])
        push(out_ref.at[where], where, xs.at[d], xr.at[d], across)
        push(out_ref.at[where], where, cs.at[d, 0], cr.at[d, 0], beside)
        from_across(d - 1)
    from_across(nz - 1)
    for d in range(nz):
        for half in range(2):
            side = it if half == 0 else 1 - it
            await_at((flip("z", d), 1 - ic, side), cr.at[d, half])
    for copy in sends:
        copy.wait_send()
    local_copy.wait()


def gather_rows(rows):
    piece, width = rows.shape
    nz = lax.axis_size("z")
    out = call(
        functools.partial(gather_kernel, nz),
        1,
        jax.ShapeDtypeStruct((nz, 2, 2, piece, width), rows.dtype),
        [pl.ANY],
        pl.ANY,
        [DMA, DMA((nz,)), DMA((nz,)), DMA((nz,)), DMA((nz,)), DMA((nz, 2)), DMA((nz, 2))],
        16,
        rows,
    )
    return out.reshape(-1, width)


def scatter_kernel(
    nz, p_ref, out_ref, own, cin, xout, xin, zout, zin, ls, cs, cr, xs, xr, zs, zr
):
    iz, ic, it = (lax.axis_index(a) for a in ("z", CORE, TP))
    greet(partners_of(("z", TP, CORE)))
    across, beside = {TP: 1 - it}, {CORE: 1 - ic}
    order = list(range(nz - 1, -1, -1))
    loads, besides, acrosses, zeds = {}, {}, {}, {}
    for d in order:
        target = flip("z", d) if d else iz
        besides[d] = remote(p_ref.at[target, 1 - ic], cin.at[d], cs.at[d], cr.at[d], beside)
        besides[d].start()
        loads[d] = pltpu.make_async_copy(p_ref.at[target, ic], own.at[d], ls.at[d])
        loads[d].start()

    def add(d, side):
        return own[d, side].astype(F32) + cin[d, side].astype(F32)

    def after_across(d):
        acrosses[d].wait_recv()
        total = add(d, it) + xin[d].astype(F32)
        if d == 0:
            out_ref[...] = total
        else:
            zout[d] = total.astype(BF)
            zeds[d] = remote(zout.at[d], zin.at[d], zs.at[d], zr.at[d], {"z": flip("z", d)})
            zeds[d].start()

    for n, d in enumerate(order):
        loads[d].wait()
        besides[d].wait_recv()
        xout[d] = add(d, 1 - it).astype(BF)
        acrosses[d] = remote(xout.at[d], xin.at[d], xs.at[d], xr.at[d], across)
        acrosses[d].start()
        if n:
            after_across(order[n - 1])
    after_across(0)
    for d in order[:-1]:
        zeds[d].wait_recv()
        out_ref[...] += zin[d].astype(F32)
    for group in (besides, acrosses, zeds):
        for copy in group.values():
            copy.wait_send()


def scatter_rows(partial):
    nz = lax.axis_size("z")
    width = partial.shape[1]
    part = partial.astype(BF).reshape(nz, 2, 2, -1, width)
    piece = part.shape[3]
    sems = [DMA((nz,)) for _ in range(7)]
    return call(
        functools.partial(scatter_kernel, nz),
        2,
        jax.ShapeDtypeStruct((piece, width), F32),
        [pl.ANY],
        pltpu.VMEM,
        [
            pltpu.VMEM((nz, 2, piece, width), BF),
            pltpu.VMEM((nz, 2, piece, width), BF),
            *[pltpu.VMEM((nz, piece, width), BF) for _ in range(4)],
            *sems,
        ],
        32,
        part,
    )


def total_kernel(axes, x_ref, out_ref, *scratch):
    greet(partners_of(axes))
    value = x_ref[...]
    sends = []
    for stage, axis in enumerate(axes):
        slots, send_sems, recv_sems = scratch[3 * stage : 3 * stage + 3]
        size = lax.axis_size(axis)
        me = lax.axis_index(axis)
        slots[me] = value
        copies = []
        for d in range(1, size):
            copy = remote(
                slots.at[me], slots.at[me], send_sems.at[d], recv_sems.at[d], {axis: flip(axis, d)}
            )
            copy.start()
            copies.append(copy)
        for copy in copies:
            copy.wait_recv()
        value = slots[0]
        for n in range(1, size):
            value = value + slots[n]
        sends += copies
    out_ref[...] = value
    for copy in sends:
        copy.wait_send()


def total(terms, axes, identity):
    axes = tuple(a for a in axes if lax.axis_size(a) > 1)
    scratch = []
    for axis in axes:
        size = lax.axis_size(axis)
        scratch += [pltpu.VMEM((size, *terms.shape), F32), DMA((size,)), DMA((size,))]
    return call(
        functools.partial(total_kernel, axes),
        identity,
        jax.ShapeDtypeStruct(terms.shape, F32),
        [pltpu.VMEM],
        pltpu.VMEM,
        scratch,
        16,
        terms,
    )


def head_total(terms):
    return total(terms.reshape(-1, 128), (CORE, TP, "z"), 3).reshape(terms.shape)


def all_total(terms):
    size = terms.shape[0]
    padded = jnp.pad(terms, (0, -size % 1024)).reshape(-1, 128)
    return total(padded, (CORE, TP, "y", "z", "ch"), 4).reshape(-1)[:size]


def columns(ref, slot, count):
    return ref.at[:, pl.ds(pl.multiple_of(slot * count, 128), count)]


def intake_kernel(nz, count, tok_ref, *refs):
    w_refs, refs = refs[:count], refs[count:]
    tok_out, refs = refs[0], refs[1:]
    o_refs, refs = refs[:count], refs[count:]
    tok_buf, refs = refs[0], refs[1:]
    bufs, refs = refs[:count], refs[count:]
    tl, tzs, tzr, txs, txr, tcs, tcr, wl, wzs, wzr, wys, wyr = refs
    iz, iy, ic, it = (lax.axis_index(a) for a in ("z", "y", CORE, TP))
    across, beside, behind = {TP: 1 - it}, {CORE: 1 - ic}, {"y": 1 - iy}
    greet(partners_of(("z", "y", TP, CORE)))
    sends = []

    def push(src, dst, send_sem, recv_sem, partner):
        copy = remote(src, dst, send_sem, recv_sem, partner)
        copy.start()
        sends.append(copy)

    def arrived(ref, sem):
        remote(ref, ref, sem, sem, across).wait_recv()

    for d in range(1, nz):
        push(tok_ref.at[it], tok_out.at[iz, ic, it], tzs.at[d], tzr.at[d], {"z": flip("z", d)})
    push(tok_ref, tok_out.at[iz, ic], tcs.at[0, 0], tcr.at[0, 0], beside)
    tok_load = pltpu.make_async_copy(tok_ref, tok_buf, tl.at[0])
    tok_load.start()
    widths = [o.shape[-1] for o in o_refs]
    loads = []
    for k, (w, o) in enumerate(zip(w_refs, o_refs)):
        own = columns(w, iz * 2 + ic, widths[k])
        push(own, o.at[iz, iy], wys.at[k, 0], wyr.at[k, 0], behind)
        for d in range(1, nz):
            other = flip("z", d)
            push(
                columns(w, other * 2 + ic, widths[k]),
                o.at[iz, iy],
                wzs.at[k, d],
                wzr.at[k, d],
                {"z": other},
            )
        load = pltpu.make_async_copy(own, bufs[k], wl.at[k])
        load.start()
        loads.append(load)
    tok_load.wait()
    stores = [pltpu.make_async_copy(tok_buf, tok_out.at[iz, ic], tl.at[1])]
    stores[0].start()
    for d in range(1, nz):
        block = tok_out.at[flip("z", d), ic, it]
        arrived(block, tzr.at[d])
        push(block, block, txs.at[d], txr.at[d], across)
        push(block, block, tcs.at[d, 0], tcr.at[d, 0], beside)

    def forward(k):
        for d in range(1, nz):
            block = o_refs[k].at[flip("z", d), iy]
            arrived(block, wzr.at[k, d])
            push(block, block, wys.at[k, d], wyr.at[k, d], behind)

    first = min(3, count)
    for k in range(first):
        forward(k)
    for d in range(1, nz):
        block = tok_out.at[flip("z", d), ic, 1 - it]
        arrived(block, txr.at[d])
        push(block, block, tcs.at[d, 1], tcr.at[d, 1], beside)
    for k, load in enumerate(loads):
        load.wait()
        store = pltpu.make_async_copy(bufs[k], o_refs[k].at[iz, iy], wl.at[k])
        store.start()
        stores.append(store)
    for k in range(first, count):
        forward(k)
    arrived(tok_out.at[iz, 1 - ic], tcr.at[0, 0])
    for d in range(1, nz):
        for half in range(2):
            side = it if half == 0 else 1 - it
            arrived(tok_out.at[flip("z", d), 1 - ic, side], tcr.at[d, half])
    for k in range(count):
        for d in range(nz):
            source = flip("z", d) if d else iz
            arrived(o_refs[k].at[source, 1 - iy], wyr.at[k, d])
    for copy in sends:
        copy.wait_send()
    for store in stores:
        store.wait()


def intake(token_rows, weights):
    nz = lax.axis_size("z")
    count = len(weights)
    own_rows, width = token_rows.shape
    rows = weights[0].shape[0]
    parts = [w.shape[1] // (2 * nz) for w in weights]
    piece = own_rows // 2
    out_shape = [jax.ShapeDtypeStruct((nz, 2, 2, piece, width), BF)] + [
        jax.ShapeDtypeStruct((nz, 2, rows, c), BF) for c in parts
    ]
    got = call(
        functools.partial(intake_kernel, nz, count),
        5,
        out_shape,
        [pl.ANY] * (count + 1),
        [pl.ANY] * (count + 1),
        [
            pltpu.VMEM((2, piece, width), BF),
            *[pltpu.VMEM((rows, c), BF) for c in parts],
            DMA((2,)),
            *[DMA((nz,)) for _ in range(4)],
            *[DMA((nz, 2)) for _ in range(2)],
            DMA((count,)),
            *[DMA((count, nz)) for _ in range(4)],
        ],
        16,
        token_rows.reshape(2, piece, width),
        *weights,
    )
    return got[0].reshape(-1, width), [g.reshape(-1, g.shape[-1]) for g in got[1:]]


def outlet_kernel(nz, count, *refs):
    g_refs, refs = refs[:count], refs[count:]
    o_refs, refs = refs[:count], refs[count:]
    own, refs = refs[:count], refs[count:]
    yin, refs = refs[:count], refs[count:]
    zout, refs = refs[:count], refs[count:]
    ls, ys, yr, zs, zr, cs, cr, os = refs
    iz, iy, ic = (lax.axis_index(a) for a in ("z", "y", CORE))
    beside, behind = {CORE: 1 - ic}, {"y": 1 - iy}
    greet(partners_of(("z", "y", CORE)))
    sends, loads, pairs, stores = [], {}, {}, []

    def push(src, dst, send_sem, recv_sem, partner):
        copy = remote(src, dst, send_sem, recv_sem, partner)
        copy.start()
        sends.append(copy)
        return copy

    order = [(k, d) for k in range(count) for d in range(nz - 1, -1, -1)]
    widths = [g.shape[-1] for g in g_refs]
    for k, d in order:
        target = flip("z", d) if d else iz
        pairs[k, d] = push(
            g_refs[k].at[target, 1 - iy], yin[k].at[d], ys.at[k, d], yr.at[k, d], behind
        )
        loads[k, d] = pltpu.make_async_copy(g_refs[k].at[target, iy], own[k].at[d], ls.at[k, d])
        loads[k, d].start()

    def relay(k, d):
        block = columns(o_refs[k], flip("z", d) * 2 + ic, widths[k])
        remote(block, block, zr.at[k, d], zr.at[k, d], beside).wait_recv()
        push(block, block, cs.at[k, d], cr.at[k, d], beside)

    for n, (k, d) in enumerate(order):
        loads[k, d].wait()
        pairs[k, d].wait_recv()
        zout[k][d] = (own[k][d].astype(F32) + yin[k][d].astype(F32)).astype(BF)
        mine = columns(o_refs[k], iz * 2 + ic, widths[k])
        if d:
            push(zout[k].at[d], mine, zs.at[k, d], zr.at[k, d], {"z": flip("z", d)})
        else:
            push(zout[k].at[d], mine, cs.at[k, d], cr.at[k, d], beside)
            store = pltpu.make_async_copy(zout[k].at[d], mine, os.at[k])
            store.start()
            stores.append(store)
            if k:
                for e in range(nz - 1, 0, -1):
                    relay(k - 1, e)
    for e in range(nz - 1, 0, -1):
        relay(count - 1, e)
    for k, d in order:
        source = flip("z", d) if d else iz
        block = columns(o_refs[k], source * 2 + 1 - ic, widths[k])
        remote(block, block, cr.at[k, d], cr.at[k, d], beside).wait_recv()
    for copy in sends:
        copy.wait_send()
    for store in stores:
        store.wait()


def outlet(grads, identity=6):
    nz = lax.axis_size("z")
    count = len(grads)
    parts = [g.shape[1] for g in grads]
    blocks = [g.astype(BF).reshape(nz, 2, -1, g.shape[1]) for g in grads]
    rows = blocks[0].shape[2]
    got = call(
        functools.partial(outlet_kernel, nz, count),
        identity,
        [jax.ShapeDtypeStruct((rows, 2 * nz * c), BF) for c in parts],
        [pl.ANY] * count,
        [pl.ANY] * count,
        [
            *[pltpu.VMEM((nz, rows, c), BF) for _ in range(3) for c in parts],
            *[DMA((count, nz)) for _ in range(7)],
            DMA((count,)),
        ],
        32,
        *blocks,
    )
    if lax.axis_size("ch") > 1:
        got = lax.psum(tuple(got), "ch")
    return [g.astype(F32) for g in got]


class Kernel:
    def __init__(self):
        self.ins, self.outs, self.scratch = [], [], []

    def inp(self, name, array, space=pl.ANY):
        self.ins.append((name, array, space))

    def out(self, name, shape, dtype, space=pl.ANY):
        self.outs.append((name, jax.ShapeDtypeStruct(shape, dtype), space))

    def mem(self, name, shape, dtype):
        self.scratch.append((name, pltpu.VMEM(shape, dtype)))

    def sem(self, name, *shape):
        self.scratch.append((name, DMA(shape)))

    def run(self, identity, body, limit):
        names = [n for n, *_ in self.ins + self.outs + self.scratch]

        def kernel(*refs):
            body(types.SimpleNamespace(**dict(zip(names, refs))))

        got = call(
            kernel,
            identity,
            [shape for _, shape, _ in self.outs],
            [space for *_, space in self.ins],
            [space for *_, space in self.outs],
            [made for _, made in self.scratch],
            limit,
            *[array for _, array, _ in self.ins],
        )
        return {n: g for (n, *_), g in zip(self.outs, got)}


class Flow:
    def __init__(self):
        self.sends, self.inner_sends = [], []
        self.iz, self.iy, self.ic, self.it = (
            lax.axis_index(a) for a in ("z", "y", CORE, TP)
        )
        self.across = {TP: 1 - self.it}
        self.beside = {CORE: 1 - self.ic}
        self.behind = {"y": 1 - self.iy}
        self.near, self.mid = {"z": flip("z", 1)}, {"z": 3 - self.iz}
        self.role = lax.rem((self.iz + 1) // 2, 2)
        self.inner = self.role == 1

    def at(self, d):
        return flip("z", d) if d else self.iz

    def line(self, s):
        side = self.iz // 2
        return (self.iz, self.near["z"], 2 - side, 3 - 3 * side)[s]

    def push(self, src, dst, send_sem, recv_sem, partner):
        copy = remote(src, dst, send_sem, recv_sem, partner)
        copy.start()
        self.sends.append(copy)
        return copy

    def push_inner(self, src, dst, send_sem, recv_sem, partner):
        copy = remote(src, dst, send_sem, recv_sem, partner)
        pl.when(self.inner)(copy.start)
        self.inner_sends.append(copy)

    def pass_on(self, s, block, send_sems, recv_sems):
        partner, number = ((self.mid, 3), (self.near, 2), (self.near, 3))[s - 1]
        self.push_inner(block, block, send_sems.at[s + 2], recv_sems.at[number], partner)

    def arrived(self, ref, sem):
        remote(ref, ref, sem, sem, self.across).wait_recv()

    def finish(self):
        for copy in self.sends:
            copy.wait_send()
        if self.inner_sends:

            @pl.when(self.inner)
            def _():
                for copy in self.inner_sends:
                    copy.wait_send()

        self.sends, self.inner_sends = [], []


def greet_line(others=()):
    flow = Flow()
    barrier = pltpu.get_barrier_semaphore()
    for partner in (flow.near, flow.across, flow.beside, *others):
        pl.semaphore_signal(barrier, inc=1, device_id=partner, device_id_type=MESH)

    @pl.when(flow.inner)
    def _():
        pl.semaphore_signal(barrier, inc=1, device_id=flow.mid, device_id_type=MESH)

    pl.semaphore_wait(barrier, 3 + len(others) + flow.role)


def stripe(ref, z, core, tp, piece):
    start = pl.multiple_of((core * 2 + tp) * piece, piece)
    return ref.at[z, pl.ds(start, piece)]


class Gather(Flow):
    @staticmethod
    def setup(k, name, rows, out=False, inside=False):
        piece, width = rows.shape
        if inside:
            k.mem(name + "_x", rows.shape, rows.dtype)
        else:
            k.inp(name + "_x", rows)
        (k.out if out else k.mem)(name, (4, 4 * piece, width), rows.dtype)
        k.sem(name + "_own")
        k.sem(name + "_zs", 6)
        for s in ("_zr", "_xs", "_xr"):
            k.sem(name + s, 4)
        k.sem(name + "_cs", 4, 2)
        k.sem(name + "_cr", 4, 2)

    def __init__(self, r, name):
        super().__init__()
        self.x, self.buf = getattr(r, name + "_x"), getattr(r, name)
        self.own_sem, self.zs, self.zr, self.xs, self.xr, self.cs, self.cr = (
            getattr(r, name + s) for s in ("_own", "_zs", "_zr", "_xs", "_xr", "_cs", "_cr")
        )
        self.piece = self.x.shape[0]

    def block(self, z, core, tp):
        return stripe(self.buf, z, core, tp, self.piece)

    def start(self):
        own = self.block(self.iz, self.ic, self.it)
        self.push(self.x, own, self.zs.at[1], self.zr.at[1], self.near)
        self.push_inner(self.x, own, self.zs.at[2], self.zr.at[2], self.mid)
        self.push(self.x, own, self.xs.at[0], self.xr.at[0], self.across)
        self.push(self.x, own, self.cs.at[0, 0], self.cr.at[0, 0], self.beside)
        self.local = pltpu.make_async_copy(self.x, own, self.own_sem)
        self.local.start()

    def from_across(self, s):
        block = self.block(self.line(s), self.ic, 1 - self.it)
        self.arrived(block, self.xr.at[s])
        self.push(block, block, self.cs.at[s, 1], self.cr.at[s, 1], self.beside)

    def advance(self, s):
        if s < 4:
            block = self.block(self.line(s), self.ic, self.it)
            self.arrived(block, self.zr.at[s])
            self.pass_on(s, block, self.zs, self.zr)
            self.push(block, block, self.xs.at[s], self.xr.at[s], self.across)
            self.push(block, block, self.cs.at[s, 0], self.cr.at[s, 0], self.beside)
        self.from_across(s - 1)

    def ready(self, s):
        if s == 0:
            self.local.wait()
        for half in range(2):
            side = self.it if half == 0 else 1 - self.it
            self.arrived(self.block(self.line(s), 1 - self.ic, side), self.cr.at[s, half])


class Scatter(Flow):
    @staticmethod
    def setup(k, name, piece, width, partial=None):
        if partial is None:
            k.mem(name + "_p", (4, 4 * piece, width), BF)
        else:
            k.inp(name + "_p", partial)
            k.mem(name + "_m", (4, 2 * piece, width), BF)
            k.sem(name + "_ls", 4)
        k.mem(name + "_c", (4, 2 * piece, width), BF)
        for s in ("_xo", "_xi", "_zo"):
            k.mem(name + s, (4, piece, width), BF)
        k.mem(name + "_zi", (6, piece, width), BF)
        for s in ("_cs", "_cr", "_xs", "_xr", "_zs"):
            k.sem(name + s, 4)
        k.sem(name + "_zr", 6)

    def __init__(self, r, name, out):
        super().__init__()
        self.out = out
        self.p, self.c, self.xo, self.xi, self.zo, self.zi = (
            getattr(r, name + s) for s in ("_p", "_c", "_xo", "_xi", "_zo", "_zi")
        )
        self.cs, self.cr, self.xs, self.xr, self.zs, self.zr = (
            getattr(r, name + s) for s in ("_cs", "_cr", "_xs", "_xr", "_zs", "_zr")
        )
        self.m, self.ls = getattr(r, name + "_m", None), getattr(r, name + "_ls", None)
        self.piece = self.xo.shape[1]
        self.core_copy, self.across_copy, self.loads = {}, {}, {}

    def rows(self, core):
        return pl.ds(pl.multiple_of(core * 2 * self.piece, 2 * self.piece), 2 * self.piece)

    def begin(self, s):
        part = s if self.m is None else self.line(s)
        self.core_copy[s] = self.push(
            self.p.at[part, self.rows(1 - self.ic)],
            self.c.at[s],
            self.cs.at[s],
            self.cr.at[s],
            self.beside,
        )
        if self.m is not None:
            self.loads[s] = pltpu.make_async_copy(
                self.p.at[part, self.rows(self.ic)], self.m.at[s], self.ls.at[s]
            )
            self.loads[s].start()

    def add(self, s, side):
        rows = pl.ds(pl.multiple_of(side * self.piece, self.piece), self.piece)
        if self.m is not None:
            own = self.m[s, rows]
        else:
            start = pl.multiple_of((self.ic * 2 + side) * self.piece, self.piece)
            own = self.p[s, pl.ds(start, self.piece)]
        return own.astype(F32) + self.c[s, rows].astype(F32)

    def cross(self, s):
        if s in self.loads:
            self.loads[s].wait()
        self.core_copy[s].wait_recv()
        self.xo[s] = self.add(s, 1 - self.it).astype(BF)
        self.across_copy[s] = self.push(
            self.xo.at[s], self.xi.at[s], self.xs.at[s], self.xr.at[s], self.across
        )

    def leave(self, s):
        self.across_copy[s].wait_recv()

        def value():
            return self.add(s, self.it) + self.xi[s].astype(F32)

        if s == 0:
            self.out[...] = value()
            return
        came = (None, 4, 2, 3)[s]

        @pl.when(self.inner)
        def _():
            self.arrived(self.zi.at[came], self.zr.at[came])
            self.zo[s] = (value() + self.zi[came].astype(F32)).astype(BF)

        @pl.when(self.role == 0)
        def _():
            self.zo[s] = value().astype(BF)

        place = s + self.role * (None, -1, 3, 1)[s]
        partner = self.near["z"]
        if s > 1:
            partner = partner + self.role * (self.mid["z"] - partner)
        self.push(
            self.zo.at[s], self.zi.at[place], self.zs.at[s], self.zr.at[place], {"z": partner}
        )

    def end(self):
        @pl.when(self.inner)
        def _():
            for place in (1, 5):
                self.arrived(self.zi.at[place], self.zr.at[place])
                self.out[...] += self.zi[place].astype(F32)

        @pl.when(self.role == 0)
        def _():
            self.arrived(self.zi.at[0], self.zr.at[0])
            self.out[...] += self.zi[0].astype(F32)


class Total(Flow):
    @staticmethod
    def setup(k, name, shape, axes):
        for axis in axes:
            size = lax.axis_size(axis)
            k.mem(f"{name}_{axis}", (size, *shape), F32)
            k.sem(f"{name}_{axis}_s", size)
            k.sem(f"{name}_{axis}_r", size)

    def __init__(self, r, name):
        super().__init__()
        self.r, self.name = r, name

    def send(self, axis, value):
        slots, ss, rs = (getattr(self.r, f"{self.name}_{axis}{s}") for s in ("", "_s", "_r"))
        me = lax.axis_index(axis)
        slots[me] = value
        self.copies = [
            self.push(slots.at[me], slots.at[me], ss.at[d], rs.at[d], {axis: flip(axis, d)})
            for d in range(1, lax.axis_size(axis))
        ]
        self.slots = slots

    def receive(self):
        for copy in self.copies:
            copy.wait_recv()
        value = self.slots[0]
        for n in range(1, self.slots.shape[0]):
            value = value + self.slots[n]
        return value


class Outlet(Flow):
    @staticmethod
    def setup(k, name, grads, nz, inside=False):
        for n, grad in enumerate(grads):
            rows, cols = grad.shape[-2:]
            if inside:
                k.mem(f"{name}_g{n}", grad.shape, BF)
            else:
                k.inp(f"{name}_g{n}", grad)
            k.out(f"{name}_o{n}", (rows, 2 * nz * cols), BF)
            if grad.ndim == 3:
                continue
            for s in ("yin", "zout") if inside else ("yin", "zout", "own"):
                k.mem(f"{name}_{s}{n}", (nz, rows, cols), BF)
        for s in ("ls", "ys", "yr", "zs", "zr", "cs", "cr"):
            k.sem(f"{name}_{s}", len(grads), nz)
        k.sem(f"{name}_os", len(grads))

    def __init__(self, r, name, count, nz):
        super().__init__()
        self.nz, self.count = nz, count
        self.g, self.o, self.own, self.yin, self.zout = (
            [getattr(r, f"{name}_{s}{n}", None) for n in range(count)]
            for s in ("g", "o", "own", "yin", "zout")
        )
        self.ls, self.ys, self.yr, self.zs, self.zr, self.cs, self.cr, self.os = (
            getattr(r, f"{name}_{s}") for s in ("ls", "ys", "yr", "zs", "zr", "cs", "cr", "os")
        )
        self.loads, self.pairs, self.stores = {}, {}, []

    def slot(self, k, z, core):
        return columns(self.o[k], z * 2 + core, self.g[k].shape[-1])

    def start(self, k):
        if self.zout[k] is None:
            return
        for d in range(self.nz - 1, -1, -1):
            target = self.at(d)
            self.pairs[k, d] = self.push(
                self.g[k].at[target, 1 - self.iy],
                self.yin[k].at[d],
                self.ys.at[k, d],
                self.yr.at[k, d],
                self.behind,
            )
            if self.own[k] is not None:
                self.loads[k, d] = pltpu.make_async_copy(
                    self.g[k].at[target, self.iy], self.own[k].at[d], self.ls.at[k, d]
                )
                self.loads[k, d].start()

    def combine(self, k, blocks=(3, 2, 1, 0)):
        mine = self.slot(k, self.iz, self.ic)
        for d in blocks:
            if self.zout[k] is None:
                src = self.g[k].at[d]
            else:
                self.pairs[k, d].wait_recv()
                if self.own[k] is not None:
                    self.loads[k, d].wait()
                    own = self.own[k][d]
                else:
                    own = self.g[k][self.at(d), self.iy]
                self.zout[k][d] = (own.astype(F32) + self.yin[k][d].astype(F32)).astype(BF)
                src = self.zout[k].at[d]
            if d:
                self.push(src, mine, self.zs.at[k, d], self.zr.at[k, d], {"z": self.at(d)})
            else:
                self.push(src, mine, self.cs.at[k, d], self.cr.at[k, d], self.beside)
                store = pltpu.make_async_copy(src, mine, self.os.at[k])
                store.start()
                self.stores.append(store)

    def relay(self, k):
        for d in range(1, self.nz):
            block = self.slot(k, self.at(d), self.ic)
            self.arrived(block, self.zr.at[k, d])
            self.push(block, block, self.cs.at[k, d], self.cr.at[k, d], self.beside)

    def end(self):
        for k in range(self.count):
            for d in range(self.nz):
                self.arrived(self.slot(k, self.at(d), 1 - self.ic), self.cr.at[k, d])
        for store in self.stores:
            store.wait()
        self.finish()


def gather_line(rows):
    k = Kernel()
    Gather.setup(k, "all", rows, out=True)

    def body(r):
        greet_line()
        gather = Gather(r, "all")
        gather.start()
        for s in range(1, 5):
            gather.advance(s)
        for s in range(4):
            gather.ready(s)
        gather.finish()

    return k.run(1, body, 16)["all"].reshape(-1, rows.shape[1])


def scatter_line(partial):
    width = partial.shape[1]
    piece = partial.shape[0] // 16
    k = Kernel()
    Scatter.setup(k, "rs", piece, width, partial.astype(BF).reshape(4, 4 * piece, width))
    k.out("sum", (piece, width), F32, pltpu.VMEM)

    def body(r):
        greet_line()
        scatter = Scatter(r, "rs", r.sum)
        order = (3, 2, 1, 0)
        for s in order:
            scatter.begin(s)
        for s in order:
            scatter.cross(s)
        for s in order:
            scatter.leave(s)
        scatter.end()
        scatter.finish()

    return k.run(2, body, 32)["sum"]


def exact(a, b, dims):
    return lax.dot_general(
        a, b, (dims, ((), ())), precision=lax.Precision.HIGHEST, preferred_element_type=F32
    )


def picker(width):
    row = lax.broadcasted_iota(jnp.int32, (8, width), 0)
    part = lax.broadcasted_iota(jnp.int32, (8, width), 1) // HD
    return jnp.where(row == part, 1.0, 0.0).astype(F32)


def row_sums(first, second):
    both = jnp.concatenate([first, second], axis=1)
    return exact(picker(2 * HD), both, ((1,), (1,)))


def spread(sums, which):
    row = lax.broadcasted_iota(jnp.int32, (8, HD), 0)
    one = jnp.where(row == which, 1.0, 0.0).astype(F32)
    return exact(sums, one, ((0,), (0,)))


def softmax_rows(query, key, length):
    count = query.shape[0]
    row = lax.broadcasted_iota(jnp.int32, (count, count), 0)
    col = lax.broadcasted_iota(jnp.int32, (count, count), 1)
    scores = mm_nt(query, key) * (1.0 / math.sqrt(HD))
    scores = jnp.where((col <= row) & (col < length), scores, NEGATIVE)
    exponent = jnp.exp(scores - jnp.max(scores, axis=-1, keepdims=True))
    return exponent / jnp.sum(exponent, axis=-1, keepdims=True)


def weight_blocks(left, right, place):
    nz, parts = left.shape[0], 2 * left.shape[0]
    block, share = left.shape[2] // parts, right.shape[2] // len(place)

    @pl.loop(0, parts)
    def _(f):
        cols = pl.ds(pl.multiple_of(f * block, block), block)
        made = mm_tn(left[0, :, cols], right[0])
        for z in range(1, nz):
            made = made + mm_tn(left[z, :, cols], right[z])
        made = made.astype(BF)
        for n, grad in enumerate(place):
            grad[f // 2, lax.rem(f, 2)] = made[:, n * share : (n + 1) * share]


def scatter_back(partial, left, right):
    width, cols = partial.shape[1], right[0].shape[1]
    piece, rows = partial.shape[0] // 16, width // 8
    k = Kernel()
    Scatter.setup(k, "rs", piece, width, partial.astype(BF).reshape(4, 4 * piece, width))
    k.out("sum", (piece, width), F32, pltpu.VMEM)
    for n, array in enumerate((*left, *right)):
        array = array.reshape(4, 4 * piece, -1)
        k.inp(f"i{n}", array)
        k.mem(f"m{n}", array.shape, BF)
    for n in range(3):
        k.mem(f"g{n}", (4, 2, rows, cols), BF)
        k.out(f"o{n}", (4, 2, rows, cols) if n else (4, rows, cols), BF)
    k.mem("yin", (4, rows, cols), BF)
    k.mem("total", (4, rows, cols), BF)
    k.sem("ld", 5)
    for s in ("ys", "yr"):
        k.sem(s, 4)
    k.sem("os", 3)

    def body(r):
        flow, scatter = Flow(), Scatter(r, "rs", r.sum)
        greet_line((flow.behind,))
        order = (3, 2, 1, 0)
        for s in order:
            scatter.begin(s)
        loads = load_all(
            [(getattr(r, f"i{n}"), getattr(r, f"m{n}")) for n in (0, 2, 1, 3, 4)], r.ld
        )
        for s in order:
            scatter.cross(s)
        for n in (0, 1):
            loads[n].wait()
        weight_blocks(r.m0, r.m2, [r.g0])
        pairs = {}
        for d in order:
            pairs[d] = flow.push(
                r.g0.at[flow.at(d), 1 - flow.iy], r.yin.at[d], r.ys.at[d], r.yr.at[d], flow.behind
            )
        scatter.leave(3)
        stores = []

        def store(n, src, out):
            stores.append(pltpu.make_async_copy(src, out, r.os.at[n]))
            stores[-1].start()

        for n in (2, 3):
            loads[n].wait()
        weight_blocks(r.m1, r.m3, [r.g1])
        store(1, r.g1, r.o1)
        scatter.leave(2)
        loads[4].wait()
        weight_blocks(r.m1, r.m4, [r.g2])
        store(2, r.g2, r.o2)
        scatter.leave(1)
        scatter.leave(0)
        scatter.end()
        for d in order:
            pairs[d].wait_recv()
            own = r.g0[flow.at(d), flow.iy].astype(F32)
            r.total[d] = (own + r.yin[d].astype(F32)).astype(BF)
        store(0, r.total, r.o0)
        for f in (flow, scatter):
            f.finish()
        for copy in stores:
            copy.wait()

    got = k.run(3, body, 60)
    return got["sum"], [got[f"o{n}"] for n in range(3)]


def load_all(pairs, sems):
    copies = []
    for n, (src, dst) in enumerate(pairs):
        copy = pltpu.make_async_copy(src, dst, sems.at[n])
        copy.start()
        copies.append(copy)
    return copies


def widen(arrays):
    count = len(arrays)
    parts = [4 if a.shape[0] % 64 == 0 else 2 for a in arrays]

    def kernel(*refs):
        ins, outs, bufs, wides = (refs[n * count : (n + 1) * count] for n in range(4))
        load_sems, store_sems = refs[4 * count :]
        loads, stores = {}, []
        chunks = [(n, p) for n in range(count) for p in range(parts[n])]

        def rows(n, p):
            size = arrays[n].shape[0] // parts[n]
            return pl.ds(p * size, size)

        for n, p in chunks:
            loads[n, p] = pltpu.make_async_copy(
                ins[n].at[rows(n, p)], bufs[n].at[rows(n, p)], load_sems.at[n, p]
            )
            loads[n, p].start()
        for n, p in chunks:
            loads[n, p].wait()
            size = arrays[n].shape[0] // parts[n]

            @pl.loop(0, size // 8)
            def _(i):
                where = pl.ds(pl.multiple_of(p * size + i * 8, 8), 8)
                wides[n][where] = bufs[n][where].astype(F32)

            stores.append(
                pltpu.make_async_copy(
                    wides[n].at[rows(n, p)], outs[n].at[rows(n, p)], store_sems.at[n, p]
                )
            )
            stores[-1].start()
        for copy in stores:
            copy.wait()

    hold = [pl.BlockSpec(memory_space=pl.ANY)] * count
    return pl.pallas_call(
        kernel,
        out_shape=[jax.ShapeDtypeStruct(a.shape, F32) for a in arrays],
        in_specs=hold,
        out_specs=hold,
        scratch_shapes=[
            *[pltpu.VMEM(a.shape, BF) for a in arrays],
            *[pltpu.VMEM(a.shape, F32) for a in arrays],
            DMA((count, 4)),
            DMA((count, 4)),
        ],
        compiler_params=pltpu.CompilerParams(vmem_limit_bytes=63 * 2**20),
    )(*arrays)


def attention_back(
    branch, wide, wo, wqkv, saved, tokens_all, residual_grad, stream_rows, terms, gains, tables,
    seq_lengths,
):
    nz = lax.axis_size("z")
    piece, width = branch.shape
    rows = 4 * piece
    padded = jnp.pad(terms, (0, -terms.shape[0] % 1024)).reshape(-1, 128)
    lanes = width // 128
    sum_axes = (CORE, TP, "y", "z")
    k = Kernel()
    Gather.setup(k, "ball", branch)
    Outlet.setup(k, "wide", wide, nz)
    slim = [jax.ShapeDtypeStruct((nz, 2, width // (2 * nz), HD), BF)] * 4
    Outlet.setup(k, "slim", slim, nz, inside=True)
    Scatter.setup(k, "rs", piece, width)
    Total.setup(k, "tot", (nz, 8, rows), (CORE, TP, "z"))
    Total.setup(k, "sum", padded.shape, sum_axes)
    k.inp("wo", wo)
    k.inp("wqkv", wqkv)
    k.inp("tokens", tokens_all)
    k.mem("tokens_m", tokens_all.shape, BF)
    names = ("q", "k", "v", "att", "nq", "nk", "qs", "ks")
    for name, array in zip(names, saved):
        k.inp(name, array)
        k.mem(name + "_m", array.shape, array.dtype)
    k.mem("wo_m", wo.shape, BF)
    k.mem("wqkv_m", wqkv.shape, BF)
    k.inp("res", residual_grad)
    k.mem("res_m", (piece, width), F32)
    k.inp("stream", stream_rows)
    k.mem("stream_m", (piece, width), BF)
    k.sem("ld", len(names) + 5)
    k.inp("terms", padded, pltpu.VMEM)
    k.mem("terms_m", padded.shape, F32)
    k.out("terms_out", padded.shape, F32, pltpu.VMEM)
    k.inp("gains", gains, pltpu.VMEM)
    k.inp("tables", tables, pltpu.VMEM)
    k.inp("lens", seq_lengths, pltpu.SMEM)
    k.mem("wqk", (nz, 2, rows, HD), F32)
    k.mem("low", (nz, rows, 3 * HD), BF)
    k.mem("dots", (nz, 8, rows), F32)
    k.mem("norms", (2, HD), F32)
    k.mem("grad", (piece, width), F32)
    k.mem("tail", (piece, width), BF)
    k.out("grad_out", (2, piece, width), BF)
    k.out("stream_out", (2, piece, width), BF)
    k.sem("xs", 2)
    k.sem("xr", 2)
    k.sem("ss", 2)

    def body(r):
        greet(partners_of(("z", "y", TP, CORE)))
        gather, outlet_flow = Gather(r, "ball"), Outlet(r, "wide", len(wide), nz)
        slim_flow, own = Outlet(r, "slim", len(slim), nz), Flow()
        scatter, total_flow = Scatter(r, "rs", r.grad), Total(r, "tot")
        sum_flow = Total(r, "sum")
        gather.start()
        for n in range(len(wide)):
            outlet_flow.start(n)
        names_in = ("wo", "wqkv", *names, "tokens", "res", "stream")
        loads = load_all([(getattr(r, n), getattr(r, n + "_m")) for n in names_in], r.ld)
        scale = 1.0 / math.sqrt(HD)
        cosine, sine = r.tables[0], r.tables[1]
        gather.advance(1)
        outlet_flow.combine(0, (3,))
        for copy in loads:
            copy.wait()
        r.norms[...] = jnp.zeros_like(r.norms)

        def compute(z):
            grad_low = mm(r.ball[z], r.wo_m[...]).astype(BF)
            query, key, value = r.q_m[z], r.k_m[z], r.v_m[z]
            probability = softmax_rows(query, key, r.lens[z])
            grad_prob = mm_nt(grad_low, value)
            row_dots = jnp.sum(probability * grad_prob, axis=-1, keepdims=True)
            grad_scores = (probability * (grad_prob - row_dots)).astype(BF)
            grad_q = rotate_back(mm(grad_scores, key) * scale, cosine, sine)
            grad_k = rotate_back(mm_tn(grad_scores, query) * scale, cosine, sine)
            grad_v = mm_tn(probability.astype(BF), grad_low)
            r.low[z, :, 2 * HD :] = grad_v.astype(BF)
            nq, nk = r.nq_m[z], r.nk_m[z]
            r.norms[0:1] += jnp.sum(grad_q * nq, axis=0, keepdims=True)
            r.norms[1:2] += jnp.sum(grad_k * nk, axis=0, keepdims=True)
            wq, wk = grad_q * r.gains[0:1], grad_k * r.gains[1:2]
            r.wqk[z, 0] = wq
            r.wqk[z, 1] = wk
            r.dots[z] = row_sums(wq * nq, wk * nk)

        for d in range(nz):
            gather.ready(d)
            compute(gather.line(d))
            if d + 2 <= nz:
                gather.advance(d + 2)
            if d == 0:
                outlet_flow.combine(0, (2,))
                own.push(
                    r.stream, r.stream_out.at[own.it], r.xs.at[0], r.xr.at[0], own.across
                )
            if d == 1:
                outlet_flow.combine(0, (1, 0))
        r.terms_m[...] = r.terms[...]
        slot = 2 * lanes + own.it * (lanes // 2) + own.iz * 2 + own.ic
        for n in range(2):
            r.terms_m[pl.ds(slot + n * lanes, 1)] = r.norms[n : n + 1]
        total_flow.send(CORE, r.dots[...])
        sum_flow.send(CORE, r.terms_m[...])
        value, other = total_flow.receive(), sum_flow.receive()
        total_flow.send(TP, value)
        sum_flow.send(TP, other)
        value, other = total_flow.receive(), sum_flow.receive()
        total_flow.send("z", value)
        sum_flow.send("y", other)
        outlet_flow.combine(1)
        outlet_flow.combine(2)
        weight_blocks(r.ball, r.att_m, [slim_flow.g[3]])
        slim_flow.start(3)
        r.dots[...] = total_flow.receive()
        order = list(range(nz - 1, -1, -1))
        for n, d in enumerate(order):
            z = gather.line(d)
            sums = r.dots[z] * (1.0 / width)
            for j, (normed, factor) in enumerate(((r.nq_m, r.qs_m), (r.nk_m, r.ks_m))):
                low = factor[z] * (r.wqk[z, j] - normed[z] * spread(sums, j))
                r.low[z, :, j * HD : (j + 1) * HD] = low.astype(BF)
            r.rs_p[d] = mm_nt(r.low[z], r.wqkv_m[...]).astype(BF)
            scatter.begin(d)
            if n:
                scatter.cross(order[n - 1])
        scatter.cross(0)
        scatter.leave(3)
        weight_blocks(r.tokens_m, r.low, slim_flow.g[:3])
        for n in range(3):
            slim_flow.start(n)
        outlet_flow.relay(0)
        slim_flow.combine(3)
        scatter.leave(2)
        scatter.leave(1)
        outlet_flow.relay(1)
        scatter.leave(0)
        sum_flow.send("z", sum_flow.receive())
        for n in range(3):
            slim_flow.combine(n)
        scatter.end()
        r.tail[...] = (r.res_m[...] + r.grad[...]).astype(BF)
        own.push(r.tail, r.grad_out.at[own.it], r.xs.at[1], r.xr.at[1], own.across)
        stores = []
        for n, (src, out) in enumerate(((r.stream_m, r.stream_out), (r.tail, r.grad_out))):
            stores.append(pltpu.make_async_copy(src, out.at[own.it], r.ss.at[n]))
            stores[-1].start()
        r.terms_out[...] = sum_flow.receive()
        outlet_flow.relay(2)
        slim_flow.relay(3)
        for n in range(3):
            slim_flow.relay(n)
        outlet_flow.end()
        slim_flow.end()
        for n, out in enumerate((r.stream_out, r.grad_out)):
            own.arrived(out.at[1 - own.it], r.xr.at[n])
        for flow in (gather, scatter, total_flow, sum_flow, own):
            flow.finish()
        for copy in stores:
            copy.wait()

    got = k.run(7, body, 60)
    *made, grad_input = widen(
        [got[f"slim_o{n}"] for n in range(4)]
        + [got[f"wide_o{n}"] for n in range(len(wide))]
        + [got["grad_out"].reshape(-1, width)]
    )
    return (
        made,
        grad_input,
        got["stream_out"].reshape(-1, width),
        got["terms_out"].reshape(-1)[: terms.shape[0]],
    )


def attention_front(token_rows, weights, gains, tables, seq_lengths, post_attention):
    nz = lax.axis_size("z")
    own_rows, width = token_rows.shape
    piece, rows = own_rows // 2, own_rows * 2
    w_rows = weights[0].shape[0]
    count = len(weights)
    parts = [w.shape[1] // (2 * nz) for w in weights]
    k = Kernel()
    Scatter.setup(k, "rs", piece, width)
    Total.setup(k, "tot", (nz, 8, rows), (CORE, TP, "z"))
    k.inp("tok", token_rows)
    for n, weight in enumerate(weights):
        k.inp(f"w{n}", weight)
    k.inp("gains", gains, pltpu.VMEM)
    k.inp("tables", tables, pltpu.VMEM)
    k.inp("lens", seq_lengths, pltpu.SMEM)
    k.mem("tall", (nz, rows, width), BF)
    k.mem("qkv", (nz, 2, w_rows, 3 * HD), BF)
    k.mem("wo", (nz, 2, w_rows, parts[3]), BF)
    for n in range(4, count):
        k.mem(f"b{n}", (w_rows, parts[n]), BF)
        k.out(f"o{n}", (nz, 2, w_rows, parts[n]), BF)
    k.mem("raw", (nz, rows, 3 * HD), F32)
    k.mem("dots", (nz, 8, rows), F32)
    saved = (("q", BF), ("k", BF), ("v", BF), ("nq", F32), ("nk", F32), ("qs", F32), ("ks", F32), ("att", BF))
    for name, kind in saved:
        k.mem(name + "_m", (nz, rows, HD), kind)
        k.out(name, (nz, rows, HD), kind)
    k.mem("branch", (piece, width), F32)
    k.inp("post", post_attention[None], pltpu.VMEM)
    for name in ("normed", "residual"):
        k.out(name, (piece, width), F32, pltpu.VMEM)
    k.out("scale", (piece, 128), F32, pltpu.VMEM)
    Gather.setup(k, "all", jax.ShapeDtypeStruct((piece, width), BF), inside=True)
    k.out("wide", (nz, rows, width), BF)
    k.out("tokens", (nz, rows, width), BF)
    k.out("qkv_out", (nz, 2, w_rows, 3 * HD), BF)
    k.out("wo_out", (nz, 2, w_rows, parts[3]), BF)
    k.sem("tl")
    k.sem("tzs", 6)
    for s in ("tzr", "txs", "txr"):
        k.sem(s, nz)
    k.sem("tcs", nz, 2)
    k.sem("tcr", nz, 2)
    k.sem("wl", 2, count)
    for s in ("wzs", "wzr", "wys", "wyr"):
        k.sem(s, count, nz)
    k.sem("st", len(saved) + 2, nz)
    k.sem("sw", 2)

    def body(r):
        greet(partners_of(("z", "y", TP, CORE)))
        flow = Flow()
        iz, iy, ic, it = flow.iz, flow.iy, flow.ic, flow.it
        scatter, total_flow = Scatter(r, "rs", r.branch), Total(r, "tot")
        gather = Gather(r, "all")

        def block(z, core, tp):
            return stripe(r.tall, z, core, tp, piece)

        def pair(z, core):
            start = pl.multiple_of(core * own_rows, own_rows)
            return r.tall.at[z, pl.ds(start, own_rows)]

        tok_half = r.tok.at[pl.ds(pl.multiple_of(it * piece, piece), piece)]
        flow.push(tok_half, block(iz, ic, it), r.tzs.at[1], r.tzr.at[1], flow.near)
        flow.push_inner(tok_half, block(iz, ic, it), r.tzs.at[2], r.tzr.at[2], flow.mid)
        flow.push(r.tok, pair(iz, ic), r.tcs.at[0, 0], r.tcr.at[0, 0], flow.beside)
        tok_load = pltpu.make_async_copy(r.tok, pair(iz, ic), r.tl)
        tok_load.start()
        loads = {}

        def landing(n, z, y):
            if n < 3:
                return r.qkv.at[z, y, :, n * HD : (n + 1) * HD]
            return r.wo.at[z, y] if n == 3 else getattr(r, f"o{n}").at[z, y]

        def bring(n, parts_of_z=(3, 2, 1), own_part=True):
            weight = getattr(r, f"w{n}")
            own = columns(weight, iz * 2 + ic, parts[n])
            for d in parts_of_z:
                other = flow.at(d)
                flow.push(
                    columns(weight, other * 2 + ic, parts[n]),
                    landing(n, iz, iy),
                    r.wzs.at[n, d],
                    r.wzr.at[n, d],
                    {"z": other},
                )
            if own_part:
                flow.push(own, landing(n, iz, iy), r.wys.at[n, 0], r.wyr.at[n, 0], flow.behind)
                dst = landing(n, iz, iy) if n < 4 else getattr(r, f"b{n}")
                loads[n] = pltpu.make_async_copy(own, dst, r.wl.at[0, n])
                loads[n].start()

        def forward(n, parts_of_z=(3, 2, 1)):
            for d in parts_of_z:
                here = landing(n, flow.at(d), iy)
                flow.arrived(here, r.wzr.at[n, d])
                flow.push(here, here, r.wys.at[n, d], r.wyr.at[n, d], flow.behind)

        def keep(n):
            loads[n].wait()
            copy = pltpu.make_async_copy(getattr(r, f"b{n}"), landing(n, iz, iy), r.wl.at[1, n])
            copy.start()
            stores.append(copy)

        def complete(n):
            for d in range(nz):
                flow.arrived(landing(n, flow.at(d), 1 - iy), r.wyr.at[n, d])

        bring(0)
        for d in range(1, nz):
            here = block(flow.line(d), ic, it)
            flow.arrived(here, r.tzr.at[d])
            flow.pass_on(d, here, r.tzs, r.tzr)
            flow.push(here, here, r.txs.at[d], r.txr.at[d], flow.across)
            flow.push(here, here, r.tcs.at[d, 0], r.tcr.at[d, 0], flow.beside)
            bring(d)
        bring(4)
        for d in range(1, nz):
            forward(d - 1)
            here = block(flow.line(d), ic, 1 - it)
            flow.arrived(here, r.txr.at[d])
            flow.push(here, here, r.tcs.at[d, 1], r.tcr.at[d, 1], flow.beside)
        stores = []

        def save(n, src, dst, d):
            copy = pltpu.make_async_copy(src, dst, r.st.at[n, d])
            copy.start()
            stores.append(copy)

        for n in range(4):
            loads[n].wait()
        for n in range(3):
            complete(n)
        tok_load.wait()
        for d in range(nz):
            z = flow.line(d)
            if d == 0:
                flow.arrived(pair(iz, 1 - ic), r.tcr.at[0, 0])
            else:
                for half in range(2):
                    side = it if half == 0 else 1 - it
                    flow.arrived(block(z, 1 - ic, side), r.tcr.at[d, half])
            save(0, r.tall.at[z], r.tokens.at[z], d)
            raw = mm(r.tall[z], r.qkv[...].reshape(2 * nz * w_rows, 3 * HD))
            r.raw[z] = raw
            query, key = raw[:, :HD], raw[:, HD : 2 * HD]
            r.dots[z] = row_sums(query * query, key * key)
        total_flow.send(CORE, r.dots[...])
        forward(3)
        value = total_flow.receive()
        total_flow.send(TP, value)
        value = total_flow.receive()
        total_flow.send("z", value)
        bring(5)
        bring(6)
        for n in (4, 5):
            keep(n)
        complete(3)
        for n, (src, dst) in enumerate(((r.qkv, r.qkv_out), (r.wo, r.wo_out))):
            copy = pltpu.make_async_copy(src, dst, r.sw.at[n])
            copy.start()
            stores.append(copy)
        r.dots[...] = lax.rsqrt(total_flow.receive() * (1.0 / width) + EPSILON)
        cosine, sine = r.tables[0], r.tables[1]
        order = list(range(nz - 1, -1, -1))
        for n, d in enumerate(order):
            z = flow.line(d)
            sums = r.dots[z]
            r.qs_m[z] = spread(sums, 0)
            r.ks_m[z] = spread(sums, 1)
            r.nq_m[z] = r.raw[z, :, :HD] * r.qs_m[z]
            r.nk_m[z] = r.raw[z, :, HD : 2 * HD] * r.ks_m[z]
            query = rotate(r.nq_m[z] * r.gains[0:1], cosine, sine).astype(BF)
            key = rotate(r.nk_m[z] * r.gains[1:2], cosine, sine).astype(BF)
            value = r.raw[z, :, 2 * HD :].astype(BF)
            r.q_m[z] = query
            r.k_m[z] = key
            r.v_m[z] = value
            probability = softmax_rows(query, key, r.lens[z]).astype(BF)
            r.att_m[z] = mm(probability, value).astype(BF)
            for m, (name, _) in enumerate(saved):
                save(m + 1, getattr(r, name + "_m").at[z], getattr(r, name).at[z], d)
            wo = r.wo[...].reshape(2 * nz * w_rows, parts[3])
            r.rs_p[d] = mm_nt(r.att_m[z], wo).astype(BF)
            scatter.begin(d)
            if n:
                scatter.cross(order[n - 1])
            if n > 1:
                scatter.leave(order[n - 2])
            if n == 0:
                forward(4)
        scatter.cross(0)
        forward(5, (3, 2))
        scatter.leave(1)
        scatter.leave(0)
        forward(5, (1,))
        scatter.end()
        branch = r.branch[...]
        scale = lax.rsqrt(jnp.mean(branch * branch, axis=-1, keepdims=True) + EPSILON)
        r.normed[...] = branch * scale
        r.scale[...] = jnp.broadcast_to(scale, r.scale.shape)
        start = pl.multiple_of((ic * 2 + it) * piece, piece)
        mine = r.tall[iz, pl.ds(start, piece)].astype(F32)
        r.residual[...] = mine + r.normed[...] * r.post[...]
        r.all_x[...] = r.residual[...].astype(BF)
        gather.start()
        forward(6, (3,))
        gather.advance(1)
        forward(6, (2,))
        gather.advance(2)
        forward(6, (1,))
        gather.advance(3)
        gather.advance(4)
        keep(6)
        for d in range(nz):
            gather.ready(d)
            z = gather.line(d)
            save(len(saved) + 1, gather.buf.at[z], r.wide.at[z], d)
        for n in range(4, count):
            complete(n)
        for f in (flow, scatter, total_flow, gather):
            f.finish()
        for copy in stores:
            copy.wait()

    return k.run(9, body, 60)


def local(
    tokens,
    lengths,
    weight_query,
    weight_key,
    weight_value,
    weight_out,
    weight_gate,
    weight_up,
    weight_down,
    post_attention,
    post_feedforward,
    query_norm,
    key_norm,
    cotangent,
):
    nz, ny, nch, ntp = (lax.axis_size(a) for a in ("z", "y", "ch", TP))
    iz, iy, ich, icore, itp = (lax.axis_index(a) for a in AXES)
    token_rows = tokens[0]
    own_rows, width = token_rows.shape
    piece = own_rows // ntp
    seq_rows = own_rows * 2
    total_rows = seq_rows * nz
    scale_factor = 1.0 / math.sqrt(HD)
    own_head = iz * 2 + icore
    qn = lax.dynamic_slice_in_dim(query_norm, own_head * HD, HD)
    kn = lax.dynamic_slice_in_dim(key_norm, own_head * HD, HD)
    seq_lengths = lax.dynamic_index_in_dim(lengths.reshape(nz, ny), iy, 1, keepdims=False)
    positions = ich * seq_rows + jnp.arange(seq_rows, dtype=jnp.int32)
    key_positions = jnp.arange(seq_rows * nch, dtype=jnp.int32)
    cosine, sine_table = rope_tables(positions)
    allowed = (key_positions[None, None, :] <= positions[None, :, None]) & (
        key_positions[None, None, :] < seq_lengths[:, None, None]
    )
    my_tokens = lax.dynamic_slice_in_dim(token_rows, itp * piece, piece, 0)
    my_cot = lax.dynamic_slice_in_dim(cotangent[0], itp * piece, piece, 0)
    my_pos = (ich * 2 + icore) * own_rows + itp * piece + jnp.arange(piece, dtype=jnp.int32)
    my_valid = (my_pos < lengths[iz * ny + iy]).astype(F32)[:, None]

    weights = (
        weight_query,
        weight_key,
        weight_value,
        weight_out,
        weight_gate,
        weight_up,
        weight_down,
    )
    fused = nch == 1 and nz == 4
    gather, scatter = (gather_line, scatter_line) if fused else (gather_rows, scatter_rows)
    by_seq = lambda a: a.reshape(nz, seq_rows, HD)
    gains, tables = jnp.stack([qn, kn]), jnp.stack([cosine, sine_table])
    if fused:
        front = attention_front(
            token_rows, weights, gains, tables, seq_lengths, post_attention
        )
        wg, wu, wd = (front[f"o{n}"].reshape(width, -1) for n in (4, 5, 6))
    else:
        tokens_all, (wq, wk, wv, wo, wg, wu, wd) = intake(token_rows, weights)
        query_raw = mm(tokens_all, wq)
        key_raw = mm(tokens_all, wk)
        value_raw = mm(tokens_all, wv)
        squares = head_total(
            jnp.stack([jnp.sum(query_raw * query_raw, axis=-1), jnp.sum(key_raw * key_raw, axis=-1)])
        )
        scales = lax.rsqrt(squares / width + EPSILON)
        query_scale = scales[0][:, None]
        key_scale = scales[1][:, None]
        queries = rotate(by_seq(query_raw * query_scale * qn), cosine, sine_table).astype(BF)
        keys = rotate(by_seq(key_raw * key_scale * kn), cosine, sine_table).astype(BF)
        values = by_seq(value_raw).astype(BF)
        if nch > 1:
            keys_full = lax.all_gather(keys, "ch", axis=1, tiled=True)
            values_full = lax.all_gather(values, "ch", axis=1, tiled=True)
        else:
            keys_full, values_full = keys, values
        scores = (
            jnp.einsum(SCORE, queries, keys_full, preferred_element_type=F32) * scale_factor
        )
        scores = jnp.where(allowed, scores, NEGATIVE)
        exponent = jnp.exp(scores - jnp.max(scores, axis=-1, keepdims=True))
        probability = exponent / jnp.sum(exponent, axis=-1, keepdims=True)
        probability_low = probability.astype(BF)
        attended = jnp.einsum(APPLY, probability_low, values_full, preferred_element_type=F32)
        attended_low = attended.reshape(total_rows, HD).astype(BF)
        branch_sum = scatter_rows(mm_nt(attended_low, wo))
    if fused:
        attn_normed, residual = front["normed"], front["residual"]
        attn_scale = front["scale"][:, :1]
        residual_all = front["wide"].reshape(-1, width)
    else:
        attn_scale = lax.rsqrt(jnp.mean(branch_sum * branch_sum, axis=-1, keepdims=True) + EPSILON)
        attn_normed = branch_sum * attn_scale
        residual = my_tokens.astype(F32) + attn_normed * post_attention
        residual_all = gather(residual.astype(BF))
    attention_branch = attn_normed * post_attention
    gate_value = mm(residual_all, wg)
    up_value = mm(residual_all, wu)
    sigmoid_gate = jax.nn.sigmoid(gate_value)
    silu_gate = gate_value * sigmoid_gate
    mixed_low = (silu_gate * up_value).astype(BF)
    down_sum = scatter(mm_nt(mixed_low, wd))
    ffn_scale = lax.rsqrt(jnp.mean(down_sum * down_sum, axis=-1, keepdims=True) + EPSILON)
    ffn_normed = down_sum * ffn_scale
    feedforward_branch = ffn_normed * post_feedforward
    stream = residual + feedforward_branch
    stat_terms = jnp.stack(
        [
            jnp.sum(my_valid * stream * stream),
            jnp.sum(my_valid * attention_branch * attention_branch),
            jnp.sum(my_valid * feedforward_branch * feedforward_branch),
        ]
    )
    grad_stream = my_cot * my_valid
    grad_post_ff = jnp.sum(grad_stream * ffn_normed, axis=0)
    scaled = grad_stream * post_feedforward
    grad_down_sum = ffn_scale * (
        scaled - ffn_normed * jnp.mean(scaled * ffn_normed, axis=-1, keepdims=True)
    )
    down_all = gather(grad_down_sum.astype(BF))
    grad_mixed = mm(down_all, wd)
    gate_low = (
        grad_mixed * up_value * sigmoid_gate * (1.0 + gate_value * (1.0 - sigmoid_gate))
    ).astype(BF)
    up_low = (grad_mixed * silu_gate).astype(BF)
    partial = mm_nt(gate_low, wg) + mm_nt(up_low, wu)
    if fused:
        back, wide_grads = scatter_back(
            partial, (down_all, residual_all), (mixed_low, gate_low, up_low)
        )
    else:
        grad_wg = mm_tn(residual_all, gate_low)
        grad_wu = mm_tn(residual_all, up_low)
        grad_wd = mm_tn(down_all, mixed_low)
        back = scatter(partial)
    grad_residual = grad_stream + back
    grad_post_attn = jnp.sum(grad_residual * attn_normed, axis=0)
    scaled_attn = grad_residual * post_attention
    grad_branch = attn_scale * (
        scaled_attn - attn_normed * jnp.mean(scaled_attn * attn_normed, axis=-1, keepdims=True)
    )
    if not fused:
        branch_all = gather_rows(grad_branch.astype(BF))
        grad_att_low = mm(branch_all, wo).astype(BF)
        grad_wo = mm_tn(branch_all, attended_low)
        grad_att = by_seq(grad_att_low)
        grad_prob = jnp.einsum(SCORE, grad_att, values_full, preferred_element_type=F32)
        row_dots = jnp.sum(probability * grad_prob, axis=-1, keepdims=True)
        grad_scores = (probability * (grad_prob - row_dots)).astype(BF)
        grad_queries = (
            jnp.einsum(APPLY, grad_scores, keys_full, preferred_element_type=F32)
            * scale_factor
        )
        grad_keys = (
            jnp.einsum("bts,btd->bsd", grad_scores, queries, preferred_element_type=F32) * scale_factor
        )
        grad_values = jnp.einsum("bts,btd->bsd", probability_low, grad_att, preferred_element_type=F32)
        if nch > 1:
            grad_keys, grad_values = (
                lax.psum_scatter(g.astype(BF), "ch", scatter_dimension=1, tiled=True).astype(F32)
                for g in (grad_keys, grad_values)
            )
        value_grad_low = grad_values.reshape(total_rows, HD).astype(BF)
        grad_q_normed = rotate_back(grad_queries, cosine, sine_table).reshape(total_rows, HD)
        grad_k_normed = rotate_back(grad_keys, cosine, sine_table).reshape(total_rows, HD)
        query_weighted = grad_q_normed * qn
        key_weighted = grad_k_normed * kn
        dots = head_total(
            jnp.stack(
                [
                    jnp.sum(query_weighted * query_raw, axis=-1),
                    jnp.sum(key_weighted * key_raw, axis=-1),
                ]
            )
        )
        query_grad_low = (
            query_scale * (query_weighted - query_raw * query_scale**2 * (dots[0] / width)[:, None])
        ).astype(BF)
        key_grad_low = (
            key_scale * (key_weighted - key_raw * key_scale**2 * (dots[1] / width)[:, None])
        ).astype(BF)
        grad_qnorm = jnp.sum(grad_q_normed * query_raw * query_scale, axis=0)
        grad_knorm = jnp.sum(grad_k_normed * key_raw * key_scale, axis=0)
        grad_wq = mm_tn(tokens_all, query_grad_low)
        grad_wk = mm_tn(tokens_all, key_grad_low)
        grad_wv = mm_tn(tokens_all, value_grad_low)
        grad_rows = grad_residual + scatter_rows(
            mm_nt(query_grad_low, wq) + mm_nt(key_grad_low, wk) + mm_nt(value_grad_low, wv)
        )
    if fused:
        saved = tuple(front[n] for n in ("q", "k", "v", "att", "nq", "nk", "qs", "ks"))
        norms_wide = jnp.zeros((2 * width,), F32)
    else:
        slot = itp * (width // ntp) + own_head * HD
        zero_row = jnp.zeros((width,), F32)
        norms_wide = jnp.concatenate(
            [
                lax.dynamic_update_slice_in_dim(zero_row, grad_qnorm, slot, 0),
                lax.dynamic_update_slice_in_dim(zero_row, grad_knorm, slot, 0),
            ]
        )
    terms = jnp.concatenate([grad_post_attn, grad_post_ff, norms_wide, stat_terms])
    if fused:
        weight_grads, grad_input, output, summed = attention_back(
            grad_branch.astype(BF),
            wide_grads,
            front["wo_out"].reshape(width, -1),
            front["qkv_out"].reshape(width, -1),
            saved,
            front["tokens"],
            grad_residual,
            stream.astype(BF),
            terms,
            gains,
            tables,
            seq_lengths,
        )
        weight_grads = [weight_grads[n] for n in (0, 1, 2, 3, 5, 6, 4)]
    else:
        weight_grads = outlet((grad_wq, grad_wk, grad_wv, grad_wo, grad_wg, grad_wu, grad_wd))
        grad_input = lax.all_gather(grad_rows, TP, axis=0, tiled=True)
        output = lax.all_gather(stream.astype(BF), TP, axis=0, tiled=True)
        summed = all_total(terms)
    half = width // ntp
    qn_sum = lax.dynamic_slice_in_dim(summed, 2 * width + itp * half, half)
    kn_sum = lax.dynamic_slice_in_dim(summed, 3 * width + itp * half, half)
    token_count = jnp.sum(lengths.astype(F32))
    root_means = jnp.sqrt(summed[4 * width :] / (token_count * width))
    return (
        output[None],
        grad_input[None],
        *weight_grads,
        summed[:width],
        summed[width : 2 * width],
        qn_sum,
        kn_sum,
        root_means,
    )


def solution(mesh):
    n_fsdp, n_ctx, n_tp = (mesh.shape[a] for a in ("fsdp", "ctx", TP))
    fine = Mesh(mesh.devices.reshape(n_fsdp // 2, 2, n_ctx // 2, 2, n_tp), AXES)
    fsdp, ctx = ("z", "y"), ("ch", CORE)
    rows = P(fsdp, ctx, None)
    weight = P(fsdp, TP)
    return jax.shard_map(
        local,
        mesh=fine,
        in_specs=(rows, P(), *([weight] * 7), P(), P(), P(TP), P(TP), rows),
        out_specs=(rows, rows, *([weight] * 7), P(), P(), P(TP), P(TP), P()),
        check_vma=False,
    )
```
